32 devices in a mesh: seg: 2 (over y), chan: 8 (over z, core), tm: 2 (over x).
Axes of the slice: x: 2, y: 2, z: 4, core: 2. Of those that a mesh axis runs over, the one named last changes fastest.
Arguments:
- traces: bfloat16 [1024, 12288], P(('seg', 'chan'), 'tm'), parts along dimension 0, may hold values from -14 to 14
- filter_taps: float32 [512, 33], P('chan'), may hold values from -1 to 1
- source_counts: int32 [8], replicated, may hold values from 1 to 36, 96 in all
- source_channel: int32 [8, 36], replicated, may hold values from 0 to 63
- block_sources: int32 [8, 12], P('chan'), may hold values from 0 to 95
Outputs:
- stacked: float32 [1024, 12, 1024], P(('seg', 'chan', 'tm')), parts along dimension 0
The draws below stay inside these ranges and needn't reach their ends.
There are 2 independent parts, one for each index of `seg`. The reference program is written for one: setup_inputs(seed, part) draws one part's arguments, and reference() takes and returns one part's arrays. A program takes and returns all parts, laid end to end along the dimension named above; an argument that names none is the same for every part. Nothing has to cross between parts.
Inputs may be any that keep to these rules, and one draw needn't show every extreme that they name: `source_counts`: the entries sum to 96 and the largest is exactly 36. `source_channel`: only the first source_counts[h] entries of row h name virtual sources.
All inputs are finite; a program needn't handle non-finite values.
Results may differ from the reference program's by a relative error of at most 0.0072.
Values may be sent and summed in bfloat16 or wider, within the bound.
No kernel may reach another device: no remote copies, remote signals or barrier semaphores. Data moves between devices by JAX's collectives and lax.ppermute only.
A program may use at most 64 MiB of HBM per device.

```python
import math
import jax
import jax.numpy as jnp
import numpy as np
from jax import lax

TILE = 64
NFFT = 4096
NF = 512
F0 = 8
TAPS = 33
PAIRS = 12
CH_DEV = 64
CHANNELS = 512
NTILE = 8
HOP = 2048
SAMPLES = 12288
SRC_MOST = 36
NVS = 96
N_CHAN = 8


def draw_traces(key, part):
    noise_key, scale_key = jax.random.split(key, 2)
    channel_scale = jnp.exp(jax.random.uniform(scale_key, (CHANNELS, 1), jnp.float32, -1.2, 1.2))
    values = channel_scale * jnp.clip(jax.random.normal(noise_key, (CHANNELS, SAMPLES), jnp.float32), -4.0, 4.0)
    return values.astype(jnp.bfloat16)


def set_ends(result, stream_key, least, high):
    place = [jax.random.randint(jax.random.fold_in(stream_key, axis), (), 0, length) for axis, length in enumerate(result.shape)]
    longest = result.shape.index(max(result.shape))
    next_to = place[:longest] + [(place[longest] + 1) % result.shape[longest]] + place[longest + 1:]
    return result.at[tuple(place)].set(least).at[tuple(next_to)].set(high)


def block_levels(key, dims, cuts, low, largest):
    def one(axis_at, blocks):
        steps = jax.random.uniform(jax.random.fold_in(jax.random.fold_in(key, 6), axis_at), (blocks,), jnp.float32, low / len(cuts), largest / len(cuts))
        return jnp.repeat(jnp.exp(steps), dims[axis_at] // blocks).reshape((-1,) + (1,) * (len(dims) - axis_at - 1))

    loudness = one(*cuts[0])
    for cut in cuts[1:]:
        loudness = loudness * one(*cut)
    return loudness


def rank_bounds(count, skew):
    portions = [(1 << 20) // math.isqrt(grade ** skew) + 1 for grade in range(1, count + 1)]
    width = 1 + sum(portions) // (1 << 30)
    return np.cumsum(np.array([max(1, weight // width) for weight in portions]))


def skewed_ids(stream_key, dims, count, slope):
    listing = rank_bounds(count, slope)
    lot = jax.random.randint(jax.random.fold_in(stream_key, 1), dims, 0, int(listing[count - 1]))
    standing = jnp.searchsorted(jnp.asarray(listing, jnp.int32), lot, side="right")
    return jax.random.permutation(jax.random.fold_in(stream_key, 2), count)[standing].astype(jnp.int32)


def profile(count, total, most, lean):
    weights = [(1 << 20) // math.isqrt(rank ** lean) + 1 for rank in range(2, count + 1)]
    rest, given = total - most - (count - 1), [1] * (count - 1)
    while rest > 0:
        free = [i for i in range(count - 1) if given[i] < most]
        mass, left = sum([weights[i] for i in free]), rest
        for i in free:
            more = min(most - given[i], max(1, left * weights[i] // mass), rest)
            given[i] = given[i] + more
            rest = rest - more
    return np.array([most] + given)


def uneven_parts(key, number_of, total, bound, slope):
    if number_of == 2:
        one = jax.random.randint(key, (), max(1, total - bound), min(bound, total - 1) + 1)
        return jnp.stack([one, total - one])
    sizes = jnp.asarray(profile(number_of, total, bound, slope), jnp.int32)
    couples = (number_of - 1) // 2
    donor, receiver = sizes[1:1 + 2 * couples:2], sizes[2:2 + 2 * couples:2]
    slack = jnp.minimum(donor - 1, bound - receiver)
    shifted = jax.random.randint(jax.random.fold_in(key, 1), (couples,), 0, 1 << 20) % (slack + 1)
    sizes = sizes.at[1:1 + 2 * couples:2].set(donor - shifted).at[2:2 + 2 * couples:2].set(receiver + shifted)
    return sizes[jax.random.permutation(jax.random.fold_in(key, 2), number_of)]


def gaussian(own_key, dims, deviation, bound, cuts=(), held_as=jnp.bfloat16):
    entries = deviation * jax.random.normal(own_key, dims, jnp.float32)
    if cuts:
        entries = entries * block_levels(own_key, dims, cuts, -0.22, 0.18)
    return jnp.clip(entries, -bound, bound).astype(held_as)


def setup_inputs(seed: int = 0, part: int = 0) -> dict:
    key_of = jax.random.split(jax.random.key(seed), 6)
    part_keys = jax.random.split(jax.random.fold_in(key_of[5], part), 6)
    traces = draw_traces(jax.random.fold_in(jax.random.fold_in(key_of[5], part), 71), part)
    filter_taps = gaussian(key_of[1], (CHANNELS, TAPS), TAPS ** -0.5, 1.0, ((0, 8),), jnp.float32)
    source_counts = uneven_parts(key_of[2], N_CHAN, NVS, SRC_MOST, 2).astype(jnp.int32)
    source_channel = set_ends(jax.random.randint(key_of[3], (N_CHAN, SRC_MOST), 0, CH_DEV), jax.random.fold_in(key_of[3], 1), 0, CH_DEV - 1).astype(jnp.int32)
    block_sources = set_ends(skewed_ids(key_of[4], (NTILE, PAIRS), NVS, 2), jax.random.fold_in(key_of[4], 3), 0, NVS - 1).astype(jnp.int32)
    return dict(traces=traces, filter_taps=filter_taps, source_counts=source_counts, source_channel=source_channel, block_sources=block_sources)


def transform_table():
    sample_index = jnp.arange(NFFT, dtype=jnp.int32)[:, None]
    frequency = F0 + jnp.arange(NF, dtype=jnp.int32)[None, :]
    phase_index = (frequency * sample_index % NFFT).astype(jnp.int32)
    angles = phase_index.astype(jnp.float32) * jnp.float32(2.0 * math.pi / NFFT)
    cosine = jnp.cos(angles).astype(jnp.bfloat16)
    sine_part = (-jnp.sin(angles)).astype(jnp.bfloat16)
    return jnp.concatenate([cosine, sine_part], axis=1)

def apply_filter(extended, filter_taps):
    tap_count = filter_taps.shape[1]
    length = extended.shape[1] - (tap_count - 1)
    summed = jnp.zeros((extended.shape[0], length), jnp.float32)
    for tap_index in range(tap_count):
        first_sample = tap_count - 1 - tap_index
        summed = summed + filter_taps[:, tap_index:tap_index + 1] * extended[:, first_sample:first_sample + length]
    return summed.astype(jnp.bfloat16)

def intersecting(filtered, hop_length):
    channel_count = filtered.shape[0]
    pieces = filtered.reshape(channel_count, -1, hop_length)
    return jnp.concatenate([pieces[:, :-1], pieces[:, 1:]], axis=2)

def whiten(spectra):
    half_width = spectra.shape[-1] // 2
    real_part = spectra[..., :half_width]
    imag_part = spectra[..., half_width:]
    powers = real_part * real_part + imag_part * imag_part
    widths = [(0, 0)] * (powers.ndim - 1) + [(2, 2)]
    padded = jnp.pad(powers, widths)
    smooth = (padded[..., 0:half_width] + padded[..., 1:half_width + 1] + padded[..., 2:half_width + 2] + padded[..., 3:half_width + 3] + padded[..., 4:half_width + 4]) / 5.0
    mean_power = lax.optimization_barrier(jnp.mean(powers, axis=-1, keepdims=True))
    scaling = lax.rsqrt(smooth + 0.1 * mean_power + 1e-06)
    return jnp.concatenate([real_part * scaling, imag_part * scaling], axis=-1).astype(jnp.bfloat16)

def correlate(receivers, sources, factor):
    half_width = receivers.shape[-1] // 2
    receiver_real = receivers[..., :half_width]
    receiver_imag = receivers[..., half_width:]
    source_real = sources[..., :half_width]
    source_imag = sources[..., half_width:]
    real_sum = lax.optimization_barrier(jnp.sum(source_real * receiver_real + source_imag * receiver_imag, axis=-2))
    imag_sum = lax.optimization_barrier(jnp.sum(source_real * receiver_imag - source_imag * receiver_real, axis=-2))
    return jnp.concatenate([real_sum, imag_sum], axis=-1) * factor

def source_rows(source_counts, source_channel, wanted):
    offsets = (jnp.cumsum(source_counts) - source_counts).astype(jnp.int32)
    home_group = (lax.optimization_barrier(jnp.sum((wanted[..., None] >= offsets).astype(jnp.int32), axis=-1)) - 1).astype(jnp.int32)
    slot_index = (wanted - offsets[home_group]).astype(jnp.int32)
    local_channel = source_channel[home_group, slot_index].astype(jnp.int32)
    return (home_group, slot_index, local_channel)

def reference(traces, filter_taps, source_counts, source_channel, block_sources):
    transform = transform_table()
    window_count = SAMPLES // HOP
    factor = 1.0 / window_count

    def tile_spectra(tile_index):
        first_row = (tile_index * TILE).astype(jnp.int32)
        raw_tile = lax.dynamic_slice_in_dim(traces, first_row, TILE, 0).astype(jnp.float32)
        tile_taps = lax.dynamic_slice_in_dim(filter_taps, first_row, TILE, 0).astype(jnp.float32)
        extended = jnp.pad(raw_tile, ((0, 0), (HOP + TAPS - 1, 0)))
        filtered = apply_filter(extended, tile_taps)
        windows = intersecting(filtered, HOP).reshape(TILE * window_count, NFFT)
        spectra = jnp.dot(windows.astype(jnp.float32), transform.astype(jnp.float32), preferred_element_type=jnp.float32)
        return whiten(spectra).reshape(TILE, window_count, 2 * NF)
    whitened = lax.map(tile_spectra, jnp.arange(NTILE, dtype=jnp.int32))
    home_group, slot_index, local_channel = source_rows(source_counts, source_channel, block_sources)
    global_source = (home_group * CH_DEV + local_channel).astype(jnp.int32)
    all_channels = whitened.reshape(CHANNELS, window_count, 2 * NF)
    sources = all_channels[global_source]

    def tile_stack(tile_pair):
        receivers, source = tile_pair
        return correlate(receivers.astype(jnp.float32)[:, None], source.astype(jnp.float32)[None], factor)
    stacked = lax.map(tile_stack, (whitened, sources))
    return stacked.reshape(CHANNELS, PAIRS, 2 * NF)
```

```python
import functools

import jax
import jax.numpy as jnp
import numpy as np
from jax import lax
from jax.experimental import pallas as pl
from jax.experimental.pallas import tpu as pltpu
from jax.sharding import PartitionSpec as P

NFFT = 4096
NF = 512
F0 = 8
STEP = 32
F32 = jnp.float32
BF16 = jnp.bfloat16


def angle_factors():
    bins = F0 + np.arange(NF)
    row = np.arange(STEP)[:, None]
    coarse = (bins * row * STEP % NFFT) * (2.0 * np.pi / NFFT)
    fine = (bins * row % NFFT) * (2.0 * np.pi / NFFT)
    parts = [np.cos(coarse), np.sin(coarse), np.cos(fine), np.sin(fine)]
    return np.stack(parts).astype(np.float32)


def split_two(x):
    high = x.astype(BF16)
    low = (x - high.astype(F32)).astype(BF16)
    return high, low


def dot(a, b):
    return jnp.dot(a, b, preferred_element_type=F32)


def dot_three(x, table_high, table_low):
    high, low = split_two(x)
    return dot(high, table_high) + dot(low, table_high) + dot(high, table_low)


def spectra_kernel(
    shape,
    where,
    counts,
    slots,
    *refs,
):
    channels, windows, tap_count, pairs, block_rows, chips, times = shape
    wanted = refs[:chips]
    traces, halo, taps, factors = refs[chips : chips + 4]
    keep, send = refs[chips + 4 : chips + 6]
    blocks = refs[chips + 6 : chips + 6 + times]
    high, low, chosen, spectra, white = refs[chips + 6 + times :]
    quarter = NFFT // 4
    half = NFFT // 2

    def make_table(a, carry):
        cos_a = factors[0, pl.ds(a, 1), :]
        sin_a = factors[1, pl.ds(a, 1), :]
        cos_b = factors[2]
        sin_b = factors[3]
        rows = pl.ds(pl.multiple_of(a * STEP, STEP), STEP)
        h, l = split_two(cos_a * cos_b - sin_a * sin_b)
        high[rows, :NF] = h
        low[rows, :NF] = l
        h, l = split_two(-(sin_a * cos_b + cos_a * sin_b))
        high[rows, NF:] = h
        low[rows, NF:] = l
        return carry

    lax.fori_loop(0, quarter // STEP, make_table, 0)

    group = where[0]
    first = jnp.int32(0)
    for g in range(counts.shape[0]):
        first = first + jnp.where(g < group, counts[g], 0)
    owned = counts[group]
    width = windows * channels
    column = lax.broadcasted_iota(jnp.int32, (1, width), 1)
    base = 2 * chips * block_rows
    chosen[:base, :] = jnp.zeros((base, width), F32)
    for core in range(2):
        for d in range(chips):
            for p in range(pairs):
                slot = wanted[d][core, p] - first
                mine = (slot >= 0) & (slot < owned)
                channel = slots[group, jnp.where(mine, slot, 0)]
                at = jnp.where(mine, channel, -width)
                row = (core * chips + d) * block_rows + p
                for w in range(windows):
                    r = row + w * pairs
                    chosen[r : r + 1, :] = (column == at + w * channels).astype(F32)
    part = channels // times
    for d in range(times):
        start = (where[1] ^ d) * part
        for w in range(windows):
            r = base + (d * windows + w) * part
            line = lax.broadcasted_iota(jnp.int32, (part, width), 0)
            col = lax.broadcasted_iota(jnp.int32, (part, width), 1)
            chosen[r : r + part, :] = (col == line + start + w * channels).astype(F32)

    filter_taps = taps[...]
    h, l = split_two(filter_taps)
    t_rows = high[:tap_count, :]
    response = dot(h, t_rows) + dot(l, t_rows) + dot(h, low[:tap_count, :])
    lag = tap_count - 1
    tile = halo.shape[1] - half
    ends = [halo[:, :tile], halo[:, half : half + tile]]
    for b in range(1, windows + 1):
        ends.append(traces[:, b * half - tile : b * half])
    lane = lax.broadcasted_iota(jnp.int32, (channels, tile), 1)
    edges = []
    for w in range(windows):
        apart = ends[w].astype(F32) - ends[w + 2].astype(F32)
        total = jnp.zeros((channels, tile), F32)
        for k in range(1, tap_count):
            turned = pltpu.roll(apart, k, 1)
            total = total + filter_taps[:, k : k + 1] * jnp.where(lane < k, turned, 0.0)
        edges.append(total[:, :lag])
    edge = dot_three(jnp.concatenate(edges, axis=0), high[:lag, :], low[:lag, :])
    spectra[...] = edge

    samples = [halo[:, tile : tile + quarter], halo[:, tile + quarter :]]
    for q in range(traces.shape[1] // quarter):
        samples.append(traces[:, q * quarter : (q + 1) * quarter])
    x = jnp.concatenate(samples, axis=0)
    chunk = 256
    turn = lax.broadcasted_iota(jnp.int32, (1, chunk), 1) % 4
    odd = (turn % 2) == 1
    sign = jnp.where(odd, -1.0, 1.0)
    sign_r = jnp.where(turn < 2, 1.0, -1.0)
    sign_i = jnp.where((turn == 0) | (turn == 3), 1.0, -1.0)
    for f in range(0, NF, chunk):
        re = slice(f, f + chunk)
        im = slice(NF + f, NF + f + chunk)
        dr = dot(x, high[:, re]) + dot(x, low[:, re])
        di = dot(x, high[:, im]) + dot(x, low[:, im])
        hr, hi = [], []
        for b in range(windows + 1):
            even_rows = slice(2 * b * channels, (2 * b + 1) * channels)
            odd_rows = slice((2 * b + 1) * channels, (2 * b + 2) * channels)
            br, bi = dr[odd_rows], di[odd_rows]
            hr.append(dr[even_rows] + sign_r * jnp.where(odd, bi, br))
            hi.append(di[even_rows] + sign_i * jnp.where(odd, br, bi))
        pr, pi = response[:, re], response[:, im]
        for w in range(windows):
            rows = slice(w * channels, (w + 1) * channels)
            xr = hr[w] + sign * hr[w + 1]
            xi = hi[w] + sign * hi[w + 1]
            spectra[rows, re] = spectra[rows, re] + (xr * pr - xi * pi)
            spectra[rows, im] = spectra[rows, im] + (xr * pi + xi * pr)

    rows_at_once = 16
    place = lax.broadcasted_iota(jnp.int32, (rows_at_once, NF), 1)

    def whiten(i, carry):
        rows = pl.ds(pl.multiple_of(i * rows_at_once, rows_at_once), rows_at_once)
        re = spectra[rows, :NF]
        im = spectra[rows, NF:]
        power = re * re + im * im
        smooth = power
        for s in (1, 2):
            smooth = smooth + jnp.where(place >= s, pltpu.roll(power, s, 1), 0.0)
            smooth = smooth + jnp.where(place < NF - s, pltpu.roll(power, NF - s, 1), 0.0)
        mean = jnp.mean(power, axis=1, keepdims=True)
        scaling = lax.rsqrt(smooth / 5.0 + 0.1 * mean + 1e-06)
        white[rows, :NF] = (re * scaling).astype(BF16)
        white[rows, NF:] = (im * scaling).astype(BF16)
        return carry

    lax.fori_loop(0, width // rows_at_once, whiten, 0)

    picks = chosen[...].astype(BF16)
    for f in range(0, 2 * NF, chunk):
        cols = slice(f, f + chunk)
        out = dot(picks, white[:, cols]).astype(BF16)
        keep[:, cols] = out[: base // 2]
        send[:, cols] = out[base // 2 : base]
        for d in range(times):
            r = base + d * windows * part
            blocks[d][:, cols] = out[r : r + windows * part]


def correlate_kernel(windows, pairs, factor, *refs):
    count = (len(refs) - 2) // 2
    receivers = refs[:count]
    sources = refs[count : 2 * count]
    out = refs[2 * count]
    held = refs[2 * count + 1]

    @pl.when(pl.program_id(0) == 0)
    def _():
        for d in range(count):
            for w in range(windows):
                rows = sources[d][w * pairs : (w + 1) * pairs, :]
                held[d * windows + w, :pairs, :] = rows.astype(F32) * factor

    for c in range(out.shape[0]):
        for f in range(0, NF, 128):
            re = slice(f, f + 128)
            im = slice(NF + f, NF + f + 128)
            total_r = jnp.zeros((pairs, 128), F32)
            total_i = jnp.zeros((pairs, 128), F32)
            for d in range(count):
                for w in range(windows):
                    rr = receivers[d][w, c : c + 1, re].astype(F32)
                    ri = receivers[d][w, c : c + 1, im].astype(F32)
                    sr = held[d * windows + w, :pairs, re]
                    si = held[d * windows + w, :pairs, im]
                    total_r = total_r + (sr * rr + si * ri)
                    total_i = total_i + (sr * ri - si * rr)
            out[c, :, re] = total_r
            out[c, :, im] = total_i


def shards(traces, filter_taps, source_counts, source_channel, block_sources):
    channels, samples = traces.shape
    tap_count = filter_taps.shape[1]
    pairs = block_sources.shape[1]
    half = NFFT // 2
    windows = samples // half
    groups = lax.axis_size("chan")
    times = lax.axis_size("tm")
    chips = groups // 2
    part = channels // times
    block_rows = -(-windows * pairs // 8) * 8

    def across(x, axis, distance):
        size = lax.axis_size(axis)
        return lax.ppermute(x, axis, [(i, i ^ distance) for i in range(size)])

    tail = traces[:, samples - half - 128 :]
    halo = lax.ppermute(tail, "tm", [(i - 1, i) for i in range(1, times)])
    both = jnp.concatenate([block_sources, across(block_sources, "chan", 1)], axis=0)
    wanted = [both] + [across(both, "chan", 2 * d) for d in range(1, chips)]
    where = jnp.stack([lax.axis_index("chan"), lax.axis_index("tm")]).astype(jnp.int32)

    shape = (channels, windows, tap_count, pairs, block_rows, chips, times)
    smem = pl.BlockSpec(memory_space=pltpu.SMEM)
    vmem = pl.BlockSpec(memory_space=pltpu.VMEM)
    width = windows * channels
    all_rows = 2 * chips * block_rows + width
    outs = pl.pallas_call(
        functools.partial(spectra_kernel, shape),
        out_shape=[jax.ShapeDtypeStruct((chips * block_rows, 2 * NF), BF16)] * 2
        + [jax.ShapeDtypeStruct((windows * part, 2 * NF), BF16)] * times,
        in_specs=[smem] * (3 + chips) + [vmem] * 4,
        out_specs=[vmem] * (2 + times),
        scratch_shapes=[
            pltpu.VMEM((NFFT // 4, 2 * NF), BF16),
            pltpu.VMEM((NFFT // 4, 2 * NF), BF16),
            pltpu.VMEM((all_rows, width), F32),
            pltpu.VMEM((width, 2 * NF), F32),
            pltpu.VMEM((width, 2 * NF), BF16),
        ],
        name="spectra",
    )(
        where,
        source_counts,
        source_channel,
        *wanted,
        traces,
        halo,
        filter_taps,
        jnp.asarray(angle_factors()),
    )
    keep, send, blocks = outs[0], outs[1], outs[2:]
    gathered = keep + across(send, "chan", 1)
    pieces = [gathered[d * block_rows : (d + 1) * block_rows] for d in range(chips)]
    mine = pieces[0]
    for d in range(1, chips):
        mine = mine + across(pieces[d], "chan", 2 * d)
    receivers = [blocks[0]] + [across(blocks[d], "tm", d) for d in range(1, times)]
    receivers = [r.reshape(windows, part, 2 * NF) for r in receivers]
    sources = [mine] + [across(mine, "tm", d) for d in range(1, times)]

    step = 8
    factor = 1.0 / (windows * times)
    return pl.pallas_call(
        functools.partial(correlate_kernel, windows, pairs, factor),
        out_shape=jax.ShapeDtypeStruct((part, pairs, 2 * NF), F32),
        grid=(part // step,),
        in_specs=[pl.BlockSpec((windows, step, 2 * NF), lambda i: (0, i, 0))] * times
        + [pl.BlockSpec((block_rows, 2 * NF), lambda i: (0, 0))] * times,
        out_specs=pl.BlockSpec((step, pairs, 2 * NF), lambda i: (i, 0, 0)),
        scratch_shapes=[pltpu.VMEM((windows * times, -(-pairs // 8) * 8, 2 * NF), F32)],
        name="correlate",
    )(*receivers, *sources)


def solution(mesh):
    in_specs = (P(("seg", "chan"), "tm"), P("chan", None), P(), P(), P("chan", None))
    out_specs = P(("seg", "chan", "tm"), None, None)
    return jax.shard_map(shards, mesh=mesh, in_specs=in_specs, out_specs=out_specs, check_vma=False)
```

```python
import functools

import jax
import jax.numpy as jnp
import ml_dtypes
import numpy as np
from jax import lax
from jax.experimental import pallas as pl
from jax.experimental.pallas import tpu as pltpu
from jax.sharding import PartitionSpec as P

NFFT = 4096
NF = 512
F0 = 8
PIECE = NFFT // 8
HALF = NFFT // 2
CHUNK = 256
F32 = jnp.float32
BF16 = jnp.bfloat16
LIMIT = 24 * 1024 * 1024


def piece_table():
    bins = F0 + np.arange(NF)
    angle = (bins * np.arange(PIECE)[:, None] % NFFT) * (2.0 * np.pi / NFFT)
    exact = np.concatenate([np.cos(angle), -np.sin(angle)], axis=1)
    high = exact.astype(ml_dtypes.bfloat16)
    low = (exact - high.astype(np.float64)).astype(ml_dtypes.bfloat16)
    return np.concatenate([high, low], axis=0)


def split_two(x):
    high = x.astype(BF16)
    low = (x - high.astype(F32)).astype(BF16)
    return high, low


def dot(a, b):
    return jnp.dot(a, b, preferred_element_type=F32)


def dot_three(x, table, rows):
    high, low = split_two(x)
    first = table[:rows, :]
    return dot(high, first) + dot(low, first) + dot(high, table[PIECE : PIECE + rows, :])


class Turns:
    def __init__(self):
        lane = lax.broadcasted_iota(jnp.int32, (1, CHUNK), 1)
        turn = lane % 4
        self.odd = (turn % 2) == 1
        self.sign = jnp.where(self.odd, -1.0, 1.0)
        self.real = jnp.where(turn < 2, 1.0, -1.0)
        self.imag = jnp.where((turn == 0) | (turn == 3), 1.0, -1.0)
        eighth = lane % 8
        root = np.float32(np.sqrt(0.5))
        self.cos = jnp.where(turn % 4 == 0, 1.0, jnp.where(turn == 2, 0.0, root))
        self.cos = jnp.where((eighth > 2) & (eighth < 6), -self.cos, self.cos)
        self.sin = jnp.where(turn == 2, 1.0, jnp.where(turn == 0, 0.0, root))
        self.sin = jnp.where(eighth < 4, -self.sin, self.sin)

    def quarter(self, ar, ai, br, bi):
        return (
            ar + self.real * jnp.where(self.odd, bi, br),
            ai + self.imag * jnp.where(self.odd, br, bi),
        )

    def half(self, re, im):
        ar, ai = self.quarter(re[0], im[0], re[2], im[2])
        br, bi = self.quarter(re[1], im[1], re[3], im[3])
        return ar + (br * self.cos - bi * self.sin), ai + (br * self.sin + bi * self.cos)


def half_spectra(x, table, channels, halves, turns, f):
    re = slice(f, f + CHUNK)
    im = slice(NF + f, NF + f + CHUNK)
    both = jnp.concatenate([x, x], axis=1)
    dr = dot(both, table[:, re])
    di = dot(both, table[:, im])
    out = []
    for b in range(halves):
        rows = [slice((4 * b + e) * channels, (4 * b + e + 1) * channels) for e in range(4)]
        out.append(turns.half([dr[r] for r in rows], [di[r] for r in rows]))
    return out


def turned_taps(taps, square):
    count, channels = taps.shape
    square[...] = jnp.zeros_like(square)
    square[:count, :channels] = taps[...]
    return square[...].T[:channels, :]


def end_terms(filter_taps, tap_count, before, after):
    lag = tap_count - 1
    channels = before[0].shape[0]
    apart = [b.astype(F32) - a.astype(F32) for b, a in zip(before, after)]
    width = apart[0].shape[1]
    lane = lax.broadcasted_iota(jnp.int32, (channels, width), 1)
    totals = [jnp.zeros((channels, width), F32) for _ in apart]
    for k in range(1, tap_count):
        tap = jnp.where(lane < k, filter_taps[:, k : k + 1], 0.0)
        for i, a in enumerate(apart):
            totals[i] = totals[i] + tap * pltpu.roll(a, k, 1)
    return [t[:, :lag] for t in totals]


def whiten_rows(re, im):
    rows = re.shape[0]
    place = lax.broadcasted_iota(jnp.int32, (rows, NF), 1)
    power = re * re + im * im
    smooth = power
    for s in (1, 2):
        smooth = smooth + jnp.where(place >= s, pltpu.roll(power, s, 1), 0.0)
        smooth = smooth + jnp.where(place < NF - s, pltpu.roll(power, NF - s, 1), 0.0)
    mean = jnp.mean(power, axis=1, keepdims=True)
    scaling = lax.rsqrt(smooth / 5.0 + 0.1 * mean + 1e-06)
    return (re * scaling).astype(BF16), (im * scaling).astype(BF16)


ROWS = 16


def whiten_all(spectra, white, count):
    def step(i, carry):
        rows = pl.ds(pl.multiple_of(i * ROWS, ROWS), ROWS)
        re, im = whiten_rows(spectra[rows, :NF], spectra[rows, NF:])
        white[rows, :NF] = re
        white[rows, NF:] = im
        return carry

    lax.fori_loop(0, count // ROWS, step, 0)


def own_kernel(windows, traces, taps, table, part, white, response, square, spectra):
    channels, samples = traces.shape
    tap_count = taps.shape[0]
    filter_taps = turned_taps(taps, square)
    response[...] = dot_three(filter_taps[:, :tap_count], table, tap_count)
    tile = 128
    last = windows - 1
    start = (last - 1) * HALF
    before = [traces[:, start - tile : start]]
    after = [traces[:, samples - tile :]]
    edge = end_terms(filter_taps, tap_count, before, after)[0]
    spectra[...] = dot_three(edge, table, tap_count - 1)
    pieces = samples // PIECE
    x = jnp.concatenate([traces[:, q * PIECE : (q + 1) * PIECE] for q in range(pieces)], axis=0)
    turns = Turns()
    for f in range(0, NF, CHUNK):
        re = slice(f, f + CHUNK)
        im = slice(NF + f, NF + f + CHUNK)
        halves = half_spectra(x, table, channels, windows, turns, f)
        pr, pi = response[:, re], response[:, im]
        for w in range(windows):
            xr, xi = halves[w]
            xr, xi = turns.sign * xr, turns.sign * xi
            if w > 0:
                xr, xi = xr + halves[w - 1][0], xi + halves[w - 1][1]
            yr = xr * pr - xi * pi
            yi = xr * pi + xi * pr
            if w < last:
                rows = slice(w * channels, (w + 1) * channels)
                part[rows, re] = yr
                part[rows, im] = yi
            else:
                spectra[:, re] = spectra[:, re] + yr
                spectra[:, im] = spectra[:, im] + yi
    whiten_all(spectra, white, channels)


def picks_kernel(shape, where, counts, slots, *refs):
    channels, windows, pairs, block_rows, chips, times = shape
    wanted, picks, chosen = refs[:chips], refs[chips], refs[chips + 1]
    group = where[0]
    first = jnp.int32(0)
    for g in range(counts.shape[0]):
        first = first + jnp.where(g < group, counts[g], 0)
    owned = counts[group]
    width = windows * channels
    column = lax.broadcasted_iota(jnp.int32, (1, width), 1) % channels
    base = 2 * chips * block_rows
    chosen[...] = jnp.zeros_like(chosen)
    for core in range(2):
        for d in range(chips):
            for p in range(pairs):
                slot = wanted[d][core, p] - first
                mine = (slot >= 0) & (slot < owned)
                channel = slots[group, jnp.where(mine, slot, 0)]
                line = (column == jnp.where(mine, channel, -1)).astype(F32)
                row = (core * chips + d) * block_rows + p
                for w in range(windows):
                    chosen[row + w * pairs : row + w * pairs + 1, :] = line
    block = lax.broadcasted_iota(jnp.int32, (block_rows, width), 0)
    window = lax.broadcasted_iota(jnp.int32, (block_rows, width), 1) // channels
    inside = (block >= window * pairs) & (block < (window + 1) * pairs)
    for b in range(2 * chips):
        rows = slice(b * block_rows, (b + 1) * block_rows)
        picks[rows, :] = jnp.where(inside, chosen[rows, :], 0.0).astype(BF16)
    part = channels // times
    count = windows * channels
    row = lax.broadcasted_iota(jnp.int32, (count, width), 0)
    col = lax.broadcasted_iota(jnp.int32, (count, width), 1)
    distance = row // (windows * part)
    line = (where[1] ^ distance) * part + row % part
    at = (row // part) % windows * channels + line
    picks[base : base + count, :] = (col == at).astype(F32).astype(BF16)


def rest_kernel(
    shape, traces, halo, taps, table, part, own_white, response, picks, *refs
):
    channels, windows, pairs, block_rows, chips, times = shape
    keep, send = refs[:2]
    blocks = refs[2 : 2 + times]
    square, spectra, white = refs[2 + times :]
    tap_count = taps.shape[0]
    filter_taps = turned_taps(taps, square)
    tile = halo.shape[1] - HALF
    before = [halo[:, :tile], halo[:, HALF:]]
    for b in range(1, windows - 2):
        before.append(traces[:, b * HALF - tile : b * HALF])
    after = [traces[:, (w + 1) * HALF - tile : (w + 1) * HALF] for w in range(windows - 1)]
    edges = end_terms(filter_taps, tap_count, before, after)
    spectra[...] = part[...] + dot_three(jnp.concatenate(edges, axis=0), table, tap_count - 1)
    x = jnp.concatenate(
        [halo[:, tile + q * PIECE : tile + (q + 1) * PIECE] for q in range(HALF // PIECE)],
        axis=0,
    )
    turns = Turns()
    for f in range(0, NF, CHUNK):
        re = slice(f, f + CHUNK)
        im = slice(NF + f, NF + f + CHUNK)
        xr, xi = half_spectra(x, table, channels, 1, turns, f)[0]
        pr, pi = response[:, re], response[:, im]
        spectra[:channels, re] = spectra[:channels, re] + (xr * pr - xi * pi)
        spectra[:channels, im] = spectra[:channels, im] + (xr * pi + xi * pr)
    count = (windows - 1) * channels
    whiten_all(spectra, white, count)
    white[count:, :] = own_white[...]
    base = 2 * chips * block_rows
    rows = windows * channels // times
    choose = picks[...]
    for f in range(0, 2 * NF, CHUNK):
        cols = slice(f, f + CHUNK)
        out = dot(choose, white[:, cols]).astype(BF16)
        keep[:, cols] = out[: base // 2]
        send[:, cols] = out[base // 2 : base]
        for d in range(times):
            blocks[d][:, cols] = out[base + d * rows : base + (d + 1) * rows]


def correlate_kernel(windows, factor, count, has_total, *refs):
    receivers = refs[:count]
    sources = refs[count : 2 * count]
    total = refs[2 * count] if has_total else None
    out, line_r, line_s = refs[2 * count + has_total :]
    step, part = out.shape[0], out.shape[1]
    pairs = line_s.shape[0]

    @pl.when(pl.program_id(0) == 0)
    def _():
        for d in range(count):
            for w in range(windows):
                at = d * windows + w
                line_r[at] = receivers[d][w].astype(F32) * factor
                rows = sources[d][w * pairs : (w + 1) * pairs, :].astype(F32)
                for p in range(pairs):
                    line_s[p, at : at + 1, :] = rows[p : p + 1, :]

    start = pl.program_id(0) * step
    for i in range(step):
        for f in range(0, NF, 128):
            re = slice(f, f + 128)
            im = slice(NF + f, NF + f + 128)
            if has_total:
                total_r, total_i = total[i, :, re], total[i, :, im]
            else:
                total_r = jnp.zeros((part, 128), F32)
                total_i = jnp.zeros((part, 128), F32)
            for at in range(count * windows):
                rr = line_r[at, :, re]
                ri = line_r[at, :, im]
                sr = line_s[start + i, at : at + 1, re]
                si = line_s[start + i, at : at + 1, im]
                total_r = total_r + (sr * rr + si * ri)
                total_i = total_i + (sr * ri - si * rr)
            out[i, :, re] = total_r
            out[i, :, im] = total_i


def correlate(receivers, sources, total, pairs, factor):
    windows, part, width = receivers[0].shape
    count = len(receivers)
    step = next(s for s in (2, 1) if pairs % s == 0)
    block = pl.BlockSpec((step, part, width), lambda i: (i, 0, 0))
    extra = [] if total is None else [total]
    return pl.pallas_call(
        functools.partial(correlate_kernel, windows, factor, count, len(extra)),
        out_shape=jax.ShapeDtypeStruct((pairs, part, width), F32),
        grid=(pairs // step,),
        in_specs=[pl.BlockSpec(r.shape, lambda i: (0, 0, 0)) for r in receivers]
        + [pl.BlockSpec(s.shape, lambda i: (0, 0)) for s in sources]
        + [block] * len(extra),
        out_specs=block,
        scratch_shapes=[
            pltpu.VMEM((count * windows, part, width), F32),
            pltpu.VMEM((pairs, -(-count * windows // 8) * 8, width), F32),
        ],
        compiler_params=pltpu.CompilerParams(vmem_limit_bytes=LIMIT),
        name="correlate",
    )(*receivers, *sources, *extra)


def shards(traces, filter_taps, source_counts, source_channel, block_sources):
    channels, samples = traces.shape
    tap_count = filter_taps.shape[1]
    pairs = block_sources.shape[1]
    windows = samples // HALF
    groups = lax.axis_size("chan")
    times = lax.axis_size("tm")
    chips = groups // 2
    part = channels // times
    block_rows = -(-windows * pairs // 8) * 8

    def across(x, axis, distance):
        size = lax.axis_size(axis)
        return lax.ppermute(x, axis, [(i, i ^ distance) for i in range(size)])

    tail = traces[:, samples - HALF - 128 :]
    halo = lax.ppermute(tail, "tm", [(i - 1, i) for i in range(1, times)])
    both = jnp.concatenate([block_sources, across(block_sources, "chan", 1)], axis=0)
    wanted = [both] + [across(both, "chan", 2 * d) for d in range(1, chips)]
    where = jnp.stack([lax.axis_index("chan"), lax.axis_index("tm")]).astype(jnp.int32)

    shape = (channels, windows, pairs, block_rows, chips, times)
    smem = pl.BlockSpec(memory_space=pltpu.SMEM)
    vmem = pl.BlockSpec(memory_space=pltpu.VMEM)
    params = pltpu.CompilerParams(vmem_limit_bytes=LIMIT)
    width = windows * channels
    all_rows = 2 * chips * block_rows + width
    taps = filter_taps.T
    table = jnp.asarray(piece_table())
    part_spectra, own_white, response = pl.pallas_call(
        functools.partial(own_kernel, windows),
        out_shape=[
            jax.ShapeDtypeStruct((width - channels, 2 * NF), F32),
            jax.ShapeDtypeStruct((channels, 2 * NF), BF16),
            jax.ShapeDtypeStruct((channels, 2 * NF), F32),
        ],
        in_specs=[vmem] * 3,
        out_specs=[vmem] * 3,
        scratch_shapes=[pltpu.VMEM((128, 128), F32), pltpu.VMEM((channels, 2 * NF), F32)],
        compiler_params=params,
        name="own",
    )(traces, taps, table)
    picks = pl.pallas_call(
        functools.partial(picks_kernel, shape),
        out_shape=jax.ShapeDtypeStruct((all_rows, width), BF16),
        in_specs=[smem] * (3 + chips),
        out_specs=vmem,
        scratch_shapes=[pltpu.VMEM((2 * chips * block_rows, width), F32)],
        compiler_params=params,
        name="picks",
    )(where, source_counts, source_channel, *wanted)
    outs = pl.pallas_call(
        functools.partial(rest_kernel, shape),
        out_shape=[jax.ShapeDtypeStruct((chips * block_rows, 2 * NF), BF16)] * 2
        + [jax.ShapeDtypeStruct((windows * part, 2 * NF), BF16)] * times,
        in_specs=[vmem] * 8,
        out_specs=[vmem] * (2 + times),
        scratch_shapes=[
            pltpu.VMEM((128, 128), F32),
            pltpu.VMEM((width - channels, 2 * NF), F32),
            pltpu.VMEM((width, 2 * NF), BF16),
        ],
        compiler_params=params,
        name="rest",
    )(traces, halo, taps, table, part_spectra, own_white, response, picks)
    keep, send, blocks = outs[0], outs[1], outs[2:]
    gathered = keep + across(send, "chan", 1)
    pieces = [gathered[d * block_rows : (d + 1) * block_rows] for d in range(chips)]
    mine = pieces[0]
    for d in range(1, chips):
        mine = mine + across(pieces[d], "chan", 2 * d)
    receivers = [blocks[0]] + [across(blocks[d], "tm", d) for d in range(1, times)]
    receivers = [r.reshape(windows, part, 2 * NF) for r in receivers]
    sources = [mine] + [across(mine, "tm", d) for d in range(1, times)]

    factor = 1.0 / (windows * times)
    total = correlate(receivers[:1], sources[:1], None, pairs, factor)
    if times > 1:
        total = correlate(receivers[1:], sources[1:], total, pairs, factor)
    return total.transpose(1, 0, 2)


def solution(mesh):
    in_specs = (P(("seg", "chan"), "tm"), P("chan", None), P(), P(), P("chan", None))
    out_specs = P(("seg", "chan", "tm"), None, None)
    return jax.shard_map(shards, mesh=mesh, in_specs=in_specs, out_specs=out_specs, check_vma=False)
```

```python
import functools

import jax
import jax.numpy as jnp
import ml_dtypes
import numpy as np
from jax import lax
from jax.experimental import pallas as pl
from jax.experimental.pallas import tpu as pltpu
from jax.sharding import PartitionSpec as P


NFFT = 4096
NF = 512
F0 = 8
PIECE = NFFT // 8
HALF = NFFT // 2
CHUNK = 256
F32 = jnp.float32
BF16 = jnp.bfloat16
LIMIT = 24 * 1024 * 1024


def piece_table():
    bins = F0 + np.arange(NF)
    angle = (bins * np.arange(PIECE)[:, None] % NFFT) * (2.0 * np.pi / NFFT)
    exact = np.concatenate([np.cos(angle), -np.sin(angle)], axis=1)
    high = exact.astype(ml_dtypes.bfloat16)
    low = (exact - high.astype(np.float64)).astype(ml_dtypes.bfloat16)
    return np.concatenate([high, low], axis=0)


def split_two(x):
    high = x.astype(BF16)
    low = (x - high.astype(F32)).astype(BF16)
    return high, low


def dot(a, b):
    return jnp.dot(a, b, preferred_element_type=F32)


def dot_three(x, table, rows, cols):
    high, low = x
    first = table[:rows, cols]
    return dot(high, first) + dot(low, first) + dot(high, table[PIECE : PIECE + rows, cols])


class Turns:
    def __init__(self):
        lane = lax.broadcasted_iota(jnp.int32, (1, CHUNK), 1)
        turn = lane % 4
        self.odd = (turn % 2) == 1
        self.sign = jnp.where(self.odd, -1.0, 1.0)
        self.real = jnp.where(turn < 2, 1.0, -1.0)
        self.imag = jnp.where((turn == 0) | (turn == 3), 1.0, -1.0)
        eighth = lane % 8
        root = np.float32(np.sqrt(0.5))
        self.cos = jnp.where(turn % 4 == 0, 1.0, jnp.where(turn == 2, 0.0, root))
        self.cos = jnp.where((eighth > 2) & (eighth < 6), -self.cos, self.cos)
        self.sin = jnp.where(turn == 2, 1.0, jnp.where(turn == 0, 0.0, root))
        self.sin = jnp.where(eighth < 4, -self.sin, self.sin)

    def quarter(self, ar, ai, br, bi):
        return (
            ar + self.real * jnp.where(self.odd, bi, br),
            ai + self.imag * jnp.where(self.odd, br, bi),
        )

    def half(self, re, im):
        ar, ai = self.quarter(re[0], im[0], re[2], im[2])
        br, bi = self.quarter(re[1], im[1], re[3], im[3])
        return ar + (br * self.cos - bi * self.sin), ai + (br * self.sin + bi * self.cos)


def half_spectra(x, table, channels, halves, turns, f):
    re = slice(f, f + CHUNK)
    im = slice(NF + f, NF + f + CHUNK)
    both = jnp.concatenate([x, x], axis=1)
    dr = dot(both, table[:, re])
    di = dot(both, table[:, im])
    out = []
    for b in range(halves):
        rows = [slice((4 * b + e) * channels, (4 * b + e + 1) * channels) for e in range(4)]
        out.append(turns.half([dr[r] for r in rows], [di[r] for r in rows]))
    return out


def end_terms(taps_wide, shifted, tap_count, ends):
    lag = tap_count - 1
    apart = ends.T
    size = apart.shape[0]
    shifted[...] = jnp.zeros_like(shifted)
    shifted[:tap_count, :] = taps_wide
    total = jnp.zeros((lag, apart.shape[1]), F32)
    for j in range(1, tap_count):
        total = total + shifted[j : j + lag, :] * apart[size - j : size - j + 1, :]
    return total.T


def whiten_rows(re, im):
    rows = re.shape[0]
    place = lax.broadcasted_iota(jnp.int32, (rows, NF), 1)
    power = re * re + im * im
    smooth = power
    for s in (1, 2):
        smooth = smooth + jnp.where(place >= s, pltpu.roll(power, s, 1), 0.0)
        smooth = smooth + jnp.where(place < NF - s, pltpu.roll(power, NF - s, 1), 0.0)
    total = jnp.sum(power, axis=1, keepdims=True)
    scaling = lax.rsqrt(smooth * 0.2 + (total * (0.1 / NF) + 1e-06))
    return (re * scaling).astype(BF16), (im * scaling).astype(BF16)


ROWS = 16


def whiten_all(spectra, white, count):
    def step(i, carry):
        rows = pl.ds(pl.multiple_of(i * ROWS, ROWS), ROWS)
        re, im = whiten_rows(spectra[rows, :NF], spectra[rows, NF:])
        white[rows, :NF] = re
        white[rows, NF:] = im
        return carry

    lax.fori_loop(0, count // ROWS, step, 0, unroll=2)


def own_kernel(
    windows,
    traces_in,
    taps_in,
    table_in,
    part,
    white,
    response,
    ends,
    taps,
    table,
    traces,
    square,
    shifted,
    spectra,
    sems,
):
    channels, samples = traces.shape
    tap_count = taps.shape[0]
    copies = [
        pltpu.make_async_copy(taps_in, taps, sems.at[0]),
        pltpu.make_async_copy(traces_in, traces, sems.at[1]),
    ]
    order = [c for f in range(0, NF, CHUNK) for c in (f, NF + f)]
    for i, c in enumerate(order):
        cols = slice(c, c + CHUNK)
        copies.append(
            pltpu.make_async_copy(table_in.at[:, cols], table.at[:, cols], sems.at[2 + i])
        )
    for copy in copies:
        copy.start()
    copies[0].wait()
    square[...] = jnp.zeros_like(square)
    square[:tap_count, :channels] = taps[...]
    filter_taps = split_two(square[...].T[:channels, :tap_count])
    copies[1].wait()
    tile = 128
    last = windows - 1
    for b in range(1, windows):
        ends[:, (b - 1) * tile : b * tile] = traces[:, b * HALF - tile : b * HALF]
    start = (last - 1) * HALF
    apart = traces[:, start - tile : start].astype(F32) - traces[:, samples - tile :].astype(F32)
    edge = split_two(end_terms(taps[...], shifted, tap_count, apart))
    pieces = samples // PIECE
    x = jnp.concatenate([traces[:, q * PIECE : (q + 1) * PIECE] for q in range(pieces)], axis=0)
    turns = Turns()
    for i, f in enumerate(range(0, NF, CHUNK)):
        re = slice(f, f + CHUNK)
        im = slice(NF + f, NF + f + CHUNK)
        copies[2 + 2 * i].wait()
        copies[3 + 2 * i].wait()
        pr = dot_three(filter_taps, table, tap_count, re)
        pi = dot_three(filter_taps, table, tap_count, im)
        response[:, re] = pr
        response[:, im] = pi
        halves = half_spectra(x, table, channels, windows, turns, f)
        for w in range(windows):
            xr, xi = halves[w]
            xr, xi = turns.sign * xr, turns.sign * xi
            if w > 0:
                xr, xi = xr + halves[w - 1][0], xi + halves[w - 1][1]
            yr = xr * pr - xi * pi
            yi = xr * pi + xi * pr
            if w < last:
                rows = slice(w * channels, (w + 1) * channels)
                part[rows, re] = yr
                part[rows, im] = yi
            else:
                spectra[:, re] = yr + dot_three(edge, table, tap_count - 1, re)
                spectra[:, im] = yi + dot_three(edge, table, tap_count - 1, im)
    whiten_all(spectra, white, channels)


def mark_picks(shape, where, counts, slots, wanted, chosen):
    channels, windows, pairs, block_rows, chips, _ = shape
    group = where[0]
    first = jnp.int32(0)
    for g in range(counts.shape[0]):
        first = first + jnp.where(g < group, counts[g], 0)
    owned = counts[group]
    width = windows * channels
    lane = lax.broadcasted_iota(jnp.int32, (1, width), 1)
    columns = [jnp.where(lane // channels == w, lane % channels, -2) for w in range(windows)]
    unused = block_rows - windows * pairs
    for core in range(2):
        for d in range(chips):
            base = (core * chips + d) * block_rows
            for p in range(pairs):
                slot = wanted[d][core, p] - first
                mine = (slot >= 0) & (slot < owned)
                channel = slots[group, jnp.where(mine, slot, 0)]
                channel = jnp.where(mine, channel, -1)
                for w in range(windows):
                    row = base + w * pairs + p
                    chosen[row : row + 1, :] = (columns[w] == channel).astype(F32)
            if unused:
                chosen[base + windows * pairs : base + block_rows, :] = jnp.zeros(
                    (unused, width), F32
                )


def rest_kernel(shape, where, counts, slots, *refs):
    channels, windows, _, block_rows, chips, times = shape
    wanted = refs[:chips]
    halo, ends, taps, table, part, own_white, response = refs[chips : chips + 7]
    keep, send = refs[chips + 7 : chips + 9]
    blocks = refs[chips + 9 : chips + 9 + times]
    shifted, spectra, white, chosen = refs[chips + 9 + times :]
    tap_count = taps.shape[0]
    tile = halo.shape[1] - HALF
    rest = windows - 1

    before = [halo[:, :tile], halo[:, HALF:]]
    before += [ends[:, (b - 1) * tile : b * tile] for b in range(1, windows - 2)]
    after = [ends[:, w * tile : (w + 1) * tile] for w in range(rest)]
    apart = jnp.concatenate([b.astype(F32) - a.astype(F32) for b, a in zip(before, after)], axis=0)
    taps_wide = jnp.concatenate([taps[...]] * rest, axis=1)
    edge = split_two(end_terms(taps_wide, shifted, tap_count, apart))
    x = jnp.concatenate(
        [halo[:, tile + q * PIECE : tile + (q + 1) * PIECE] for q in range(HALF // PIECE)],
        axis=0,
    )
    mark_picks(shape, where, counts, slots, wanted, chosen)
    turns = Turns()
    for f in range(0, NF, CHUNK):
        re = slice(f, f + CHUNK)
        im = slice(NF + f, NF + f + CHUNK)
        xr, xi = half_spectra(x, table, channels, 1, turns, f)[0]
        pr, pi = response[:, re], response[:, im]
        er = dot_three(edge, table, tap_count - 1, re)
        ei = dot_three(edge, table, tap_count - 1, im)
        spectra[:channels, re] = part[:channels, re] + er[:channels] + (xr * pr - xi * pi)
        spectra[:channels, im] = part[:channels, im] + ei[:channels] + (xr * pi + xi * pr)
        spectra[channels:, re] = part[channels:, re] + er[channels:]
        spectra[channels:, im] = part[channels:, im] + ei[channels:]
    count = rest * channels
    whiten_all(spectra, white, count)
    white[count:, :] = own_white[...]
    base = 2 * chips * block_rows
    size = channels // times
    choose = chosen[...].astype(BF16)
    for f in range(0, 2 * NF, CHUNK):
        cols = slice(f, f + CHUNK)
        out = dot(choose, white[:, cols]).astype(BF16)
        keep[:, cols] = out[: base // 2]
        send[:, cols] = out[base // 2 :]
    for d in range(times):
        line = (where[1] ^ d) * size
        for w in range(windows):
            if size % ROWS == 0:
                at = pl.multiple_of(w * channels + line, ROWS)
                blocks[d][w * size : (w + 1) * size, :] = white[pl.ds(at, size), :]
            else:
                row = lax.broadcasted_iota(jnp.int32, (size, channels), 0)
                col = lax.broadcasted_iota(jnp.int32, (size, channels), 1)
                move = (col == row + line).astype(F32).astype(BF16)
                moved = dot(move, white[w * channels : (w + 1) * channels, :])
                blocks[d][w * size : (w + 1) * size, :] = moved.astype(BF16)


def correlate_kernel(windows, factor, count, has_total, *refs):
    receivers = refs[:count]
    sources = refs[count : 2 * count]
    total = refs[2 * count] if has_total else None
    out, line_r, line_s = refs[2 * count + has_total :]
    step, part = out.shape[0], out.shape[1]
    pairs = line_s.shape[0]

    @pl.when(pl.program_id(0) == 0)
    def _():
        for d in range(count):
            for w in range(windows):
                at = d * windows + w
                line_r[at] = receivers[d][w].astype(F32) * factor
                rows = sources[d][w * pairs : (w + 1) * pairs, :].astype(F32)
                for p in range(pairs):
                    line_s[p, at : at + 1, :] = rows[p : p + 1, :]

    start = pl.program_id(0) * step
    for i in range(step):
        for f in range(0, NF, 128):
            re = slice(f, f + 128)
            im = slice(NF + f, NF + f + 128)
            if has_total:
                total_r, total_i = total[start + i, :, re], total[start + i, :, im]
            else:
                total_r = jnp.zeros((part, 128), F32)
                total_i = jnp.zeros((part, 128), F32)
            for at in range(count * windows):
                rr = line_r[at, :, re]
                ri = line_r[at, :, im]
                sr = line_s[start + i, at : at + 1, re]
                si = line_s[start + i, at : at + 1, im]
                total_r = total_r + (sr * rr + si * ri)
                total_i = total_i + (sr * ri - si * rr)
            out[i, :, re] = total_r
            out[i, :, im] = total_i


def correlate(receivers, sources, total, pairs, factor):
    windows, part, width = receivers[0].shape
    count = len(receivers)
    step = next(s for s in (2, 1) if pairs % s == 0)
    block = pl.BlockSpec((step, part, width), lambda i: (i, 0, 0))
    extra = [] if total is None else [total]
    return pl.pallas_call(
        functools.partial(correlate_kernel, windows, factor, count, len(extra)),
        out_shape=jax.ShapeDtypeStruct((pairs, part, width), F32),
        grid=(pairs // step,),
        in_specs=[pl.BlockSpec(memory_space=pltpu.VMEM)] * (2 * count + len(extra)),
        out_specs=block,
        scratch_shapes=[
            pltpu.VMEM((count * windows, part, width), F32),
            pltpu.VMEM((pairs, -(-count * windows // 8) * 8, width), F32),
        ],
        compiler_params=pltpu.CompilerParams(vmem_limit_bytes=LIMIT),
        name="correlate",
    )(*receivers, *sources, *extra)


def shards(traces, filter_taps, source_counts, source_channel, block_sources):
    channels, samples = traces.shape
    tap_count = filter_taps.shape[1]
    pairs = block_sources.shape[1]
    windows = samples // HALF
    groups = lax.axis_size("chan")
    times = lax.axis_size("tm")
    chips = groups // 2
    part = channels // times
    block_rows = -(-windows * pairs // 8) * 8

    def across(x, axis, distance):
        size = lax.axis_size(axis)
        return lax.ppermute(x, axis, [(i, i ^ distance) for i in range(size)])

    tail = traces[:, samples - HALF - 128 :]
    halo = lax.ppermute(tail, "tm", [(i - 1, i) for i in range(1, times)])
    both = jnp.concatenate([block_sources, across(block_sources, "chan", 1)], axis=0)
    wanted = [both]
    for d in range(1, chips):
        wanted.append(across(both, "chan", 2 * d))
    where = jnp.stack([lax.axis_index("chan"), lax.axis_index("tm")]).astype(jnp.int32)

    shape = (channels, windows, pairs, block_rows, chips, times)
    smem = pl.BlockSpec(memory_space=pltpu.SMEM)
    vmem = pl.BlockSpec(memory_space=pltpu.VMEM)
    params = pltpu.CompilerParams(vmem_limit_bytes=LIMIT)
    width = windows * channels
    taps = filter_taps.T
    table = jnp.asarray(piece_table())
    own = pl.pallas_call(
        functools.partial(own_kernel, windows),
        out_shape=[
            jax.ShapeDtypeStruct((width - channels, 2 * NF), F32),
            jax.ShapeDtypeStruct((channels, 2 * NF), BF16),
            jax.ShapeDtypeStruct((channels, 2 * NF), F32),
            jax.ShapeDtypeStruct((channels, (windows - 1) * 128), BF16),
            jax.ShapeDtypeStruct(taps.shape, F32),
            jax.ShapeDtypeStruct(table.shape, BF16),
        ],
        in_specs=[pl.BlockSpec(memory_space=pltpu.HBM)] * 3,
        out_specs=[vmem] * 6,
        scratch_shapes=[
            pltpu.VMEM(traces.shape, BF16),
            pltpu.VMEM((128, 128), F32),
            pltpu.VMEM((2 * tap_count + 6, channels), F32),
            pltpu.VMEM((channels, 2 * NF), F32),
            pltpu.SemaphoreType.DMA((2 + 2 * NF // CHUNK,)),
        ],
        compiler_params=params,
        name="own",
    )(*(pltpu.with_memory_space_constraint(a, pltpu.HBM) for a in (traces, taps, table)))
    part_spectra, own_white, response, ends, taps, table = own
    outs = pl.pallas_call(
        functools.partial(rest_kernel, shape),
        out_shape=[jax.ShapeDtypeStruct((chips * block_rows, 2 * NF), BF16)] * 2
        + [jax.ShapeDtypeStruct((windows * part, 2 * NF), BF16)] * times,
        in_specs=[smem] * (3 + chips) + [vmem] * 7,
        out_specs=[vmem] * (2 + times),
        scratch_shapes=[
            pltpu.VMEM((2 * tap_count + 6, width - channels), F32),
            pltpu.VMEM((width - channels, 2 * NF), F32),
            pltpu.VMEM((width, 2 * NF), BF16),
            pltpu.VMEM((2 * chips * block_rows, width), F32),
        ],
        compiler_params=params,
        name="rest",
    )(
        where,
        source_counts,
        source_channel,
        *wanted,
        halo,
        ends,
        taps,
        table,
        part_spectra,
        own_white,
        response,
    )
    keep, send, blocks = outs[0], outs[1], outs[2:]
    gathered = keep + across(send, "chan", 1)
    pieces = [gathered[d * block_rows : (d + 1) * block_rows] for d in range(chips)]
    mine = pieces[0]
    for d in range(1, chips):
        mine = mine + across(pieces[d], "chan", 2 * d)
    receivers = [blocks[0]] + [across(blocks[d], "tm", d) for d in range(1, times)]
    receivers = [r.reshape(windows, part, 2 * NF) for r in receivers]
    sources = [mine] + [across(mine, "tm", d) for d in range(1, times)]

    factor = 1.0 / (windows * times)
    total = correlate(receivers[:1], sources[:1], None, pairs, factor)
    if times > 1:
        total = correlate(receivers[1:], sources[1:], total, pairs, factor)
    return total.transpose(1, 0, 2)


def solution(mesh):
    in_specs = (P(("seg", "chan"), "tm"), P("chan", None), P(), P(), P("chan", None))
    out_specs = P(("seg", "chan", "tm"), None, None)
    return jax.shard_map(shards, mesh=mesh, in_specs=in_specs, out_specs=out_specs, check_vma=False)
```

```python
import functools

import jax
import jax.numpy as jnp
import ml_dtypes
import numpy as np
from jax import lax
from jax.experimental import pallas as pl
from jax.experimental.pallas import tpu as pltpu
from jax.sharding import PartitionSpec as P


NFFT = 4096
NF = 512
F0 = 8
PIECE = NFFT // 8
HALF = NFFT // 2
CHUNK = 256
F32 = jnp.float32
BF16 = jnp.bfloat16
LIMIT = 24 * 1024 * 1024


def piece_table():
    bins = F0 + np.arange(NF)
    angle = (bins * np.arange(PIECE)[:, None] % NFFT) * (2.0 * np.pi / NFFT)
    exact = np.concatenate([np.cos(angle), -np.sin(angle)], axis=1)
    high = exact.astype(ml_dtypes.bfloat16)
    low = (exact - high.astype(np.float64)).astype(ml_dtypes.bfloat16)
    return np.concatenate([high, low], axis=0)


def split_two(x):
    high = x.astype(BF16)
    low = (x - high.astype(F32)).astype(BF16)
    return high, low


def dot(a, b):
    return jnp.dot(a, b, preferred_element_type=F32)


def dot_three(x, table, rows, cols):
    high, low = x
    first = table[:rows, cols]
    return dot(high, first) + dot(low, first) + dot(high, table[PIECE : PIECE + rows, cols])


class Turns:
    def __init__(self):
        lane = lax.broadcasted_iota(jnp.int32, (1, CHUNK), 1)
        turn = lane % 4
        self.odd = (turn % 2) == 1
        self.sign = jnp.where(self.odd, -1.0, 1.0)
        self.real = jnp.where(turn < 2, 1.0, -1.0)
        self.imag = jnp.where((turn == 0) | (turn == 3), 1.0, -1.0)
        eighth = lane % 8
        root = np.float32(np.sqrt(0.5))
        self.cos = jnp.where(turn % 4 == 0, 1.0, jnp.where(turn == 2, 0.0, root))
        self.cos = jnp.where((eighth > 2) & (eighth < 6), -self.cos, self.cos)
        self.sin = jnp.where(turn == 2, 1.0, jnp.where(turn == 0, 0.0, root))
        self.sin = jnp.where(eighth < 4, -self.sin, self.sin)

    def quarter(self, ar, ai, br, bi):
        return (
            ar + self.real * jnp.where(self.odd, bi, br),
            ai + self.imag * jnp.where(self.odd, br, bi),
        )

    def half(self, re, im):
        ar, ai = self.quarter(re[0], im[0], re[2], im[2])
        br, bi = self.quarter(re[1], im[1], re[3], im[3])
        return ar + (br * self.cos - bi * self.sin), ai + (br * self.sin + bi * self.cos)


def half_spectra(x, table, channels, halves, turns, f):
    re = slice(f, f + CHUNK)
    im = slice(NF + f, NF + f + CHUNK)
    both = jnp.concatenate([x, x], axis=1)
    dr = dot(both, table[:, re])
    di = dot(both, table[:, im])
    out = []
    for b in range(halves):
        rows = [slice((4 * b + e) * channels, (4 * b + e + 1) * channels) for e in range(4)]
        out.append(turns.half([dr[r] for r in rows], [di[r] for r in rows]))
    return out


def end_terms(taps_wide, shifted, tap_count, ends):
    lag = tap_count - 1
    apart = ends.T
    size = apart.shape[0]
    shifted[...] = jnp.zeros_like(shifted)
    shifted[:tap_count, :] = taps_wide
    total = jnp.zeros((lag, apart.shape[1]), F32)
    for j in range(1, tap_count):
        total = total + shifted[j : j + lag, :] * apart[size - j : size - j + 1, :]
    return total.T


def whiten_rows(re, im):
    rows = re.shape[0]
    place = lax.broadcasted_iota(jnp.int32, (rows, NF), 1)
    power = re * re + im * im
    smooth = power
    for s in (1, 2):
        smooth = smooth + jnp.where(place >= s, pltpu.roll(power, s, 1), 0.0)
        smooth = smooth + jnp.where(place < NF - s, pltpu.roll(power, NF - s, 1), 0.0)
    total = jnp.sum(power, axis=1, keepdims=True)
    scaling = lax.rsqrt(smooth * 0.2 + (total * (0.1 / NF) + 1e-06))
    return (re * scaling).astype(BF16), (im * scaling).astype(BF16)


ROWS = 16


def whiten_all(spectra, white, count):
    def step(i, carry):
        rows = pl.ds(pl.multiple_of(i * ROWS, ROWS), ROWS)
        re, im = whiten_rows(spectra[rows, :NF], spectra[rows, NF:])
        white[rows, :NF] = re
        white[rows, NF:] = im
        return carry

    lax.fori_loop(0, count // ROWS, step, 0, unroll=2)


def head_kernel(traces_in, taps_in, table_in, tail, traces, taps, table, sems):
    start = traces.shape[1] - tail.shape[1]
    copies = [
        pltpu.make_async_copy(traces_in.at[:, start:], tail, sems.at[0]),
        pltpu.make_async_copy(traces_in, traces, sems.at[1]),
        pltpu.make_async_copy(taps_in, taps, sems.at[2]),
        pltpu.make_async_copy(table_in, table, sems.at[3]),
    ]
    for copy in copies:
        copy.start()
    for copy in copies:
        copy.wait()


def own_kernel(windows, traces, taps, table, part, white, response, ends, square, shifted, spectra):
    channels, samples = traces.shape
    tap_count = taps.shape[0]
    square[...] = jnp.zeros_like(square)
    square[:tap_count, :channels] = taps[...]
    filter_taps = split_two(square[...].T[:channels, :tap_count])
    tile = 128
    last = windows - 1
    for b in range(1, windows):
        ends[:, (b - 1) * tile : b * tile] = traces[:, b * HALF - tile : b * HALF]
    start = (last - 1) * HALF
    apart = traces[:, start - tile : start].astype(F32) - traces[:, samples - tile :].astype(F32)
    edge = split_two(end_terms(taps[...], shifted, tap_count, apart))
    pieces = samples // PIECE
    x = jnp.concatenate([traces[:, q * PIECE : (q + 1) * PIECE] for q in range(pieces)], axis=0)
    turns = Turns()
    for f in range(0, NF, CHUNK):
        re = slice(f, f + CHUNK)
        im = slice(NF + f, NF + f + CHUNK)
        pr = dot_three(filter_taps, table, tap_count, re)
        pi = dot_three(filter_taps, table, tap_count, im)
        response[:, re] = pr
        response[:, im] = pi
        halves = half_spectra(x, table, channels, windows, turns, f)
        for w in range(windows):
            xr, xi = halves[w]
            xr, xi = turns.sign * xr, turns.sign * xi
            if w > 0:
                xr, xi = xr + halves[w - 1][0], xi + halves[w - 1][1]
            yr = xr * pr - xi * pi
            yi = xr * pi + xi * pr
            if w < last:
                rows = slice(w * channels, (w + 1) * channels)
                part[rows, re] = yr
                part[rows, im] = yi
            else:
                spectra[:, re] = yr + dot_three(edge, table, tap_count - 1, re)
                spectra[:, im] = yi + dot_three(edge, table, tap_count - 1, im)
    whiten_all(spectra, white, channels)


def mark_picks(shape, where, counts, slots, wanted, chosen):
    channels, windows, pairs, block_rows, chips, _ = shape
    group = where[0]
    first = jnp.int32(0)
    for g in range(counts.shape[0]):
        first = first + jnp.where(g < group, counts[g], 0)
    owned = counts[group]
    width = windows * channels
    lane = lax.broadcasted_iota(jnp.int32, (1, width), 1)
    columns = [jnp.where(lane // channels == w, lane % channels, -2) for w in range(windows)]
    unused = block_rows - windows * pairs
    per = wanted[0].shape[0]
    for core in range(2):
        for d in range(chips):
            base = (core * chips + d) * block_rows
            for p in range(pairs):
                slot = wanted[2 * d // per][(2 * d + core) % per, p] - first
                mine = (slot >= 0) & (slot < owned)
                channel = slots[group, jnp.where(mine, slot, 0)]
                channel = jnp.where(mine, channel, -1)
                for w in range(windows):
                    row = base + w * pairs + p
                    chosen[row : row + 1, :] = (columns[w] == channel).astype(F32)
            if unused:
                chosen[base + windows * pairs : base + block_rows, :] = jnp.zeros(
                    (unused, width), F32
                )


def rest_kernel(shape, where, counts, slots, *refs):
    channels, windows, _, block_rows, chips, times = shape
    wanted = refs[:2] if chips > 1 else refs[:1]
    refs = refs[len(wanted) :]
    halo, ends, taps, table, part, own_white, response = refs[:7]
    keep, send = refs[7:9]
    blocks = refs[9 : 9 + times]
    shifted, spectra, white, chosen = refs[9 + times :]
    tap_count = taps.shape[0]
    tile = halo.shape[1] - HALF
    rest = windows - 1

    before = [halo[:, :tile], halo[:, HALF:]]
    before += [ends[:, (b - 1) * tile : b * tile] for b in range(1, windows - 2)]
    after = [ends[:, w * tile : (w + 1) * tile] for w in range(rest)]
    apart = jnp.concatenate([b.astype(F32) - a.astype(F32) for b, a in zip(before, after)], axis=0)
    taps_wide = jnp.concatenate([taps[...]] * rest, axis=1)
    edge = split_two(end_terms(taps_wide, shifted, tap_count, apart))
    x = jnp.concatenate(
        [halo[:, tile + q * PIECE : tile + (q + 1) * PIECE] for q in range(HALF // PIECE)],
        axis=0,
    )
    mark_picks(shape, where, counts, slots, wanted, chosen)
    turns = Turns()
    for f in range(0, NF, CHUNK):
        re = slice(f, f + CHUNK)
        im = slice(NF + f, NF + f + CHUNK)
        xr, xi = half_spectra(x, table, channels, 1, turns, f)[0]
        pr, pi = response[:, re], response[:, im]
        er = dot_three(edge, table, tap_count - 1, re)
        ei = dot_three(edge, table, tap_count - 1, im)
        spectra[:channels, re] = part[:channels, re] + er[:channels] + (xr * pr - xi * pi)
        spectra[:channels, im] = part[:channels, im] + ei[:channels] + (xr * pi + xi * pr)
        spectra[channels:, re] = part[channels:, re] + er[channels:]
        spectra[channels:, im] = part[channels:, im] + ei[channels:]
    count = rest * channels
    whiten_all(spectra, white, count)
    white[count:, :] = own_white[...]
    base = 2 * chips * block_rows
    size = channels // times
    choose = chosen[...].astype(BF16)
    for f in range(0, 2 * NF, CHUNK):
        cols = slice(f, f + CHUNK)
        out = dot(choose, white[:, cols]).astype(BF16)
        keep[:, cols] = out[: base // 2]
        send[:, cols] = out[base // 2 :]
    for d in range(times):
        line = (where[1] ^ d) * size
        for w in range(windows):
            if size % ROWS == 0:
                at = pl.multiple_of(w * channels + line, ROWS)
                blocks[d][w * size : (w + 1) * size, :] = white[pl.ds(at, size), :]
            else:
                row = lax.broadcasted_iota(jnp.int32, (size, channels), 0)
                col = lax.broadcasted_iota(jnp.int32, (size, channels), 1)
                move = (col == row + line).astype(F32).astype(BF16)
                moved = dot(move, white[w * channels : (w + 1) * channels, :])
                blocks[d][w * size : (w + 1) * size, :] = moved.astype(BF16)


def correlate_kernel(windows, factor, count, *refs):
    receivers = refs[:count]
    sources = refs[count : 2 * count]
    last = len(refs) == 2 * count + 6
    total = refs[2 * count] if last else None
    out, line_r, line_s = refs[2 * count + last : 2 * count + last + 3]
    held, sems = refs[-2:] if last else (out, None)
    pairs, part = out.shape[0], out.shape[1]
    for d in range(count):
        for w in range(windows):
            at = d * windows + w
            line_r[at] = receivers[d][w].astype(F32) * factor
            rows = sources[d][w * pairs : (w + 1) * pairs, :].astype(F32)
            for p in range(pairs):
                line_s[p, at : at + 1, :] = rows[p : p + 1, :]

    def copy(p):
        return pltpu.make_async_copy(held.at[p], out.at[p], sems.at[p])

    def one(p, carry):
        for f in range(0, NF, 128):
            re = slice(f, f + 128)
            im = slice(NF + f, NF + f + 128)
            if last:
                total_r, total_i = total[p, :, re], total[p, :, im]
            else:
                total_r = jnp.zeros((part, 128), F32)
                total_i = jnp.zeros((part, 128), F32)
            for at in range(count * windows):
                rr = line_r[at, :, re]
                ri = line_r[at, :, im]
                sr = line_s[p, at : at + 1, re]
                si = line_s[p, at : at + 1, im]
                total_r = total_r + (sr * rr + si * ri)
                total_i = total_i + (sr * ri - si * rr)
            held[p, :, re] = total_r
            held[p, :, im] = total_i
        if last:
            copy(p).start()
        return carry

    lax.fori_loop(0, pairs, one, 0)
    if last:
        for p in range(pairs):
            copy(p).wait()


def correlate(receivers, sources, total, pairs, factor):
    windows, part, width = receivers[0].shape
    count = len(receivers)
    vmem = pl.BlockSpec(memory_space=pltpu.VMEM)
    shape = (pairs, part, width)
    last = total is not None
    scratch = [
        pltpu.VMEM((count * windows, part, width), F32),
        pltpu.VMEM((pairs, -(-count * windows // 8) * 8, width), F32),
    ]
    if last:
        scratch += [pltpu.VMEM(shape, F32), pltpu.SemaphoreType.DMA((pairs,))]
    return pl.pallas_call(
        functools.partial(correlate_kernel, windows, factor, count),
        out_shape=jax.ShapeDtypeStruct(shape, F32),
        in_specs=[vmem] * (2 * count + last),
        out_specs=pl.BlockSpec(memory_space=pltpu.HBM) if last else vmem,
        scratch_shapes=scratch,
        compiler_params=pltpu.CompilerParams(vmem_limit_bytes=LIMIT),
        name="correlate",
    )(*receivers, *sources, *([total] if last else []))


def shards(traces, filter_taps, source_counts, source_channel, block_sources):
    channels, samples = traces.shape
    tap_count = filter_taps.shape[1]
    pairs = block_sources.shape[1]
    windows = samples // HALF
    groups = lax.axis_size("chan")
    times = lax.axis_size("tm")
    chips = groups // 2
    part = channels // times
    block_rows = -(-windows * pairs // 8) * 8

    def across(x, axis, distance):
        size = lax.axis_size(axis)
        return lax.ppermute(x, axis, [(i, i ^ distance) for i in range(size)])

    smem = pl.BlockSpec(memory_space=pltpu.SMEM)
    vmem = pl.BlockSpec(memory_space=pltpu.VMEM)
    hbm = pl.BlockSpec(memory_space=pltpu.HBM)
    params = pltpu.CompilerParams(vmem_limit_bytes=LIMIT)
    bits = [1 << b for b in range(chips.bit_length() - 1)]

    other = across(block_sources, "chan", 1)
    inputs = (traces, filter_taps.T, jnp.asarray(piece_table()))
    tail, traces, taps, table = pl.pallas_call(
        head_kernel,
        out_shape=[jax.ShapeDtypeStruct((channels, HALF + 128), BF16)]
        + [jax.ShapeDtypeStruct(a.shape, a.dtype) for a in inputs],
        in_specs=[hbm] * 3,
        out_specs=[vmem] * 4,
        scratch_shapes=[pltpu.SemaphoreType.DMA((4,))],
        compiler_params=params,
        name="head",
    )(*(pltpu.with_memory_space_constraint(a, pltpu.HBM) for a in inputs))
    halo = lax.ppermute(tail, "tm", [(i - 1, i) for i in range(1, times)])
    wanted = [jnp.concatenate([block_sources, other], axis=0)]
    for bit in bits:
        known = jnp.concatenate(wanted, axis=0)
        wanted = [known, across(known, "chan", 2 * bit)]
    where = jnp.stack([lax.axis_index("chan"), lax.axis_index("tm")]).astype(jnp.int32)

    shape = (channels, windows, pairs, block_rows, chips, times)
    width = windows * channels
    own = pl.pallas_call(
        functools.partial(own_kernel, windows),
        out_shape=[
            jax.ShapeDtypeStruct((width - channels, 2 * NF), F32),
            jax.ShapeDtypeStruct((channels, 2 * NF), BF16),
            jax.ShapeDtypeStruct((channels, 2 * NF), F32),
            jax.ShapeDtypeStruct((channels, (windows - 1) * 128), BF16),
        ],
        in_specs=[vmem] * 3,
        out_specs=[vmem] * 4,
        scratch_shapes=[
            pltpu.VMEM((128, 128), F32),
            pltpu.VMEM((2 * tap_count + 6, channels), F32),
            pltpu.VMEM((channels, 2 * NF), F32),
        ],
        compiler_params=params,
        name="own",
    )(traces, taps, table)
    part_spectra, own_white, response, ends = own
    outs = pl.pallas_call(
        functools.partial(rest_kernel, shape),
        out_shape=[jax.ShapeDtypeStruct((chips * block_rows, 2 * NF), BF16)] * 2
        + [jax.ShapeDtypeStruct((windows * part, 2 * NF), BF16)] * times,
        in_specs=[smem] * (3 + len(wanted)) + [vmem] * 7,
        out_specs=[vmem] * (2 + times),
        scratch_shapes=[
            pltpu.VMEM((2 * tap_count + 6, width - channels), F32),
            pltpu.VMEM((width - channels, 2 * NF), F32),
            pltpu.VMEM((width, 2 * NF), BF16),
            pltpu.VMEM((2 * chips * block_rows, width), F32),
        ],
        compiler_params=params,
        name="rest",
    )(
        where,
        source_counts,
        source_channel,
        *wanted,
        halo,
        ends,
        taps,
        table,
        part_spectra,
        own_white,
        response,
    )
    keep, send, blocks = outs[0], outs[1], outs[2:]
    gathered = keep + across(send, "chan", 1)
    pieces = [gathered[d * block_rows : (d + 1) * block_rows] for d in range(chips)]
    for bit in bits:
        onward = [d for d in range(2 * bit, chips) if d & (2 * bit - 1) == bit]
        if onward:
            block = jnp.concatenate([pieces[d] for d in onward], axis=0)
            block = across(block, "chan", 2 * bit)
            for i, d in enumerate(onward):
                rows = slice(i * block_rows, (i + 1) * block_rows)
                pieces[d ^ bit] = pieces[d ^ bit] + block[rows]
    mine = pieces[0]
    for bit in bits:
        mine = mine + across(pieces[bit], "chan", 2 * bit)
    receivers = [blocks[0]]
    for d in range(1, times):
        receivers.append(across(blocks[d], "tm", d))
    receivers = [r.reshape(windows, part, 2 * NF) for r in receivers]
    sources = [mine] + [across(mine, "tm", d) for d in range(1, times)]

    factor = 1.0 / (windows * times)
    total = correlate(receivers[:1], sources[:1], None, pairs, factor)
    if times > 1:
        total = correlate(receivers[1:], sources[1:], total, pairs, factor)
    return total.transpose(1, 0, 2)


def solution(mesh):
    in_specs = (P(("seg", "chan"), "tm"), P("chan", None), P(), P(), P("chan", None))
    out_specs = P(("seg", "chan", "tm"), None, None)
    return jax.shard_map(shards, mesh=mesh, in_specs=in_specs, out_specs=out_specs, check_vma=False)
```

```python
import functools

import jax
import jax.numpy as jnp
import ml_dtypes
import numpy as np
from jax import lax
from jax.experimental import pallas as pl
from jax.experimental.pallas import tpu as pltpu
from jax.sharding import PartitionSpec as P


NFFT = 4096
NF = 512
F0 = 8
PIECE = NFFT // 8
HALF = NFFT // 2
CHUNK = 256
F32 = jnp.float32
BF16 = jnp.bfloat16
LIMIT = 24 * 1024 * 1024


def piece_table():
    bins = F0 + np.arange(NF)
    angle = (bins * np.arange(PIECE)[:, None] % NFFT) * (2.0 * np.pi / NFFT)
    exact = np.concatenate([np.cos(angle), -np.sin(angle)], axis=1)
    high = exact.astype(ml_dtypes.bfloat16)
    low = (exact - high.astype(np.float64)).astype(ml_dtypes.bfloat16)
    return np.concatenate([high, low], axis=0)


def split_two(x):
    high = x.astype(BF16)
    low = (x - high.astype(F32)).astype(BF16)
    return high, low


def dot(a, b):
    return jnp.dot(a, b, preferred_element_type=F32)


def stacked_parts(x):
    high, low = split_two(x)
    high = high.astype(F32)
    return jnp.concatenate([high, low.astype(F32), high], axis=0)


def stacked_rows(table, rows, cols):
    first = table[:rows, cols]
    return jnp.concatenate([first, first, table[PIECE : PIECE + rows, cols]], axis=0)


class Turns:
    def __init__(self):
        lane = lax.broadcasted_iota(jnp.int32, (1, CHUNK), 1)
        turn = lane % 4
        self.odd = (turn % 2) == 1
        self.sign = jnp.where(self.odd, -1.0, 1.0)
        self.real = jnp.where(turn < 2, 1.0, -1.0)
        self.imag = jnp.where((turn == 0) | (turn == 3), 1.0, -1.0)
        eighth = lane % 8
        root = np.float32(np.sqrt(0.5))
        self.cos = jnp.where(turn % 4 == 0, 1.0, jnp.where(turn == 2, 0.0, root))
        self.cos = jnp.where((eighth > 2) & (eighth < 6), -self.cos, self.cos)
        self.sin = jnp.where(turn == 2, 1.0, jnp.where(turn == 0, 0.0, root))
        self.sin = jnp.where(eighth < 4, -self.sin, self.sin)

    def quarter(self, ar, ai, br, bi):
        return (
            ar + self.real * jnp.where(self.odd, bi, br),
            ai + self.imag * jnp.where(self.odd, br, bi),
        )

    def half(self, re, im):
        ar, ai = self.quarter(re[0], im[0], re[2], im[2])
        br, bi = self.quarter(re[1], im[1], re[3], im[3])
        return ar + (br * self.cos - bi * self.sin), ai + (br * self.sin + bi * self.cos)


def half_spectra(x, table, channels, halves, turns, f):
    re = slice(f, f + CHUNK)
    im = slice(NF + f, NF + f + CHUNK)
    both = jnp.concatenate([x, x], axis=1)
    dr = dot(both, table[:, re])
    di = dot(both, table[:, im])
    out = []
    for b in range(halves):
        rows = [slice((4 * b + e) * channels, (4 * b + e + 1) * channels) for e in range(4)]
        out.append(turns.half([dr[r] for r in rows], [di[r] for r in rows]))
    return out


def end_terms(taps_wide, shifted, tap_count, ends):
    lag = tap_count - 1
    apart = ends.T
    size = apart.shape[0]
    shifted[...] = jnp.zeros_like(shifted)
    shifted[:tap_count, :] = taps_wide
    total = jnp.zeros((lag, apart.shape[1]), F32)
    for j in range(1, tap_count):
        total = total + shifted[j : j + lag, :] * apart[size - j : size - j + 1, :]
    return stacked_parts(total).T.astype(BF16)


def whiten_rows(re, im):
    rows = re.shape[0]
    place = lax.broadcasted_iota(jnp.int32, (rows, NF), 1)
    power = re * re + im * im
    smooth = power
    for s in (1, 2):
        smooth = smooth + jnp.where(place >= s, pltpu.roll(power, s, 1), 0.0)
        smooth = smooth + jnp.where(place < NF - s, pltpu.roll(power, NF - s, 1), 0.0)
    total = jnp.sum(power, axis=1, keepdims=True)
    scaling = lax.rsqrt(smooth * 0.2 + (total * (0.1 / NF) + 1e-06))
    return (re * scaling).astype(BF16), (im * scaling).astype(BF16)


ROWS = 16


def whiten_all(spectra, white, count):
    def step(i, carry):
        rows = pl.ds(pl.multiple_of(i * ROWS, ROWS), ROWS)
        re, im = whiten_rows(spectra[rows, :NF], spectra[rows, NF:])
        white[rows, :NF] = re
        white[rows, NF:] = im
        return carry

    lax.fori_loop(0, count // ROWS, step, 0, unroll=2)


def head_kernel(traces_in, taps_in, table_in, tail, traces, taps, table, sems):
    start = traces.shape[1] - tail.shape[1]
    copies = [
        pltpu.make_async_copy(traces_in.at[:, start:], tail, sems.at[0]),
        pltpu.make_async_copy(traces_in, traces, sems.at[1]),
        pltpu.make_async_copy(taps_in, taps, sems.at[2]),
        pltpu.make_async_copy(table_in, table, sems.at[3]),
    ]
    for copy in copies:
        copy.start()
    for copy in copies:
        copy.wait()


def own_kernel(windows, traces, taps, table, part, white, response, ends, square, shifted, spectra):
    channels, samples = traces.shape
    tap_count = taps.shape[0]
    square[...] = jnp.zeros_like(square)
    high, low = split_two(taps[...])
    high = high.astype(F32)
    lines = square.shape[0] // 3
    for i, value in enumerate((high, low.astype(F32), high)):
        square[i * lines : i * lines + tap_count, :channels] = value
    filter_taps = square[...].T[:channels].astype(BF16)
    tile = 128
    last = windows - 1
    for b in range(1, windows):
        ends[:, (b - 1) * tile : b * tile] = traces[:, b * HALF - tile : b * HALF]
    start = (last - 1) * HALF
    apart = traces[:, start - tile : start].astype(F32) - traces[:, samples - tile :].astype(F32)
    edge = end_terms(taps[...], shifted, tap_count, apart)
    pieces = samples // PIECE
    x = jnp.concatenate([traces[:, q * PIECE : (q + 1) * PIECE] for q in range(pieces)], axis=0)
    turns = Turns()
    for f in range(0, NF, CHUNK):
        re = slice(f, f + CHUNK)
        im = slice(NF + f, NF + f + CHUNK)
        pr = dot(filter_taps, stacked_rows(table, lines, re))
        pi = dot(filter_taps, stacked_rows(table, lines, im))
        response[:, re] = pr
        response[:, im] = pi
        halves = half_spectra(x, table, channels, windows, turns, f)
        for w in range(windows):
            xr, xi = halves[w]
            xr, xi = turns.sign * xr, turns.sign * xi
            if w > 0:
                xr, xi = xr + halves[w - 1][0], xi + halves[w - 1][1]
            yr = xr * pr - xi * pi
            yi = xr * pi + xi * pr
            if w < last:
                rows = slice(w * channels, (w + 1) * channels)
                part[rows, re] = yr
                part[rows, im] = yi
            else:
                spectra[:, re] = yr + dot(edge, stacked_rows(table, tap_count - 1, re))
                spectra[:, im] = yi + dot(edge, stacked_rows(table, tap_count - 1, im))
    whiten_all(spectra, white, channels)


def part_rows(windows, pairs):
    return [-(-w * pairs // 8) * 8 for w in (windows - 1, 1)]


def picks_kernel(shape, where, counts, slots, *refs):
    channels, windows, pairs, chips = shape
    wanted, picks, chosen = refs[:-2], refs[-2], refs[-1]
    group = where[0]
    first = jnp.int32(0)
    for g in range(counts.shape[0]):
        first = first + jnp.where(g < group, counts[g], 0)
    owned = counts[group]
    width = windows * channels
    lane = lax.broadcasted_iota(jnp.int32, (1, width), 1)
    columns = [jnp.where(lane // channels == w, lane % channels, -2) for w in range(windows)]
    sizes = part_rows(windows, pairs)
    per = wanted[0].shape[0]
    chosen[...] = jnp.zeros_like(chosen)
    for core in range(2):
        for d in range(chips):
            base = (core * chips + d) * sum(sizes)
            tail = base + sizes[0]
            for p in range(pairs):
                slot = wanted[2 * d // per][(2 * d + core) % per, p] - first
                mine = (slot >= 0) & (slot < owned)
                channel = slots[group, jnp.where(mine, slot, 0)]
                channel = jnp.where(mine, channel, -1)
                for w in range(windows):
                    row = (base + w * pairs if w < windows - 1 else tail) + p
                    chosen[row : row + 1, :] = (columns[w] == channel).astype(F32)
    picks[...] = chosen[...].astype(BF16)


def rest_kernel(
    windows, times, where, halo, ends, taps, table, part, own_white, response, picks, *refs
):
    keep, send = refs[:2]
    blocks = refs[2 : 2 + times]
    shifted, spectra, white = refs[2 + times :]
    channels = response.shape[0]
    tap_count = taps.shape[0]
    tile = halo.shape[1] - HALF
    rest = windows - 1

    before = [halo[:, :tile], halo[:, HALF:]]
    before += [ends[:, (b - 1) * tile : b * tile] for b in range(1, windows - 2)]
    after = [ends[:, w * tile : (w + 1) * tile] for w in range(rest)]
    apart = jnp.concatenate([b.astype(F32) - a.astype(F32) for b, a in zip(before, after)], axis=0)
    taps_wide = jnp.concatenate([taps[...]] * rest, axis=1)
    edge = end_terms(taps_wide, shifted, tap_count, apart)
    x = jnp.concatenate(
        [halo[:, tile + q * PIECE : tile + (q + 1) * PIECE] for q in range(HALF // PIECE)],
        axis=0,
    )
    turns = Turns()
    for f in range(0, NF, CHUNK):
        re = slice(f, f + CHUNK)
        im = slice(NF + f, NF + f + CHUNK)
        xr, xi = half_spectra(x, table, channels, 1, turns, f)[0]
        pr, pi = response[:, re], response[:, im]
        er = dot(edge, stacked_rows(table, tap_count - 1, re))
        ei = dot(edge, stacked_rows(table, tap_count - 1, im))
        spectra[:channels, re] = part[:channels, re] + er[:channels] + (xr * pr - xi * pi)
        spectra[:channels, im] = part[:channels, im] + ei[:channels] + (xr * pi + xi * pr)
        spectra[channels:, re] = part[channels:, re] + er[channels:]
        spectra[channels:, im] = part[channels:, im] + ei[channels:]
    count = rest * channels
    whiten_all(spectra, white, count)
    white[count:, :] = own_white[...]
    base = keep.shape[0]
    size = channels // times
    choose = picks[...]
    for f in range(0, 2 * NF, CHUNK):
        cols = slice(f, f + CHUNK)
        out = dot(choose, white[:, cols]).astype(BF16)
        keep[:, cols] = out[:base]
        send[:, cols] = out[base:]
    for d in range(times):
        line = (where[1] ^ d) * size
        for w in range(windows):
            if size % ROWS == 0:
                at = pl.multiple_of(w * channels + line, ROWS)
                blocks[d][w * size : (w + 1) * size, :] = white[pl.ds(at, size), :]
            else:
                row = lax.broadcasted_iota(jnp.int32, (size, channels), 0)
                col = lax.broadcasted_iota(jnp.int32, (size, channels), 1)
                move = (col == row + line).astype(F32).astype(BF16)
                moved = dot(move, white[w * channels : (w + 1) * channels, :])
                blocks[d][w * size : (w + 1) * size, :] = moved.astype(BF16)


def correlate_kernel(windows, factor, count, *refs):
    receivers = refs[:count]
    sources = refs[count : 3 * count]
    last = len(refs) == 3 * count + 6
    total = refs[3 * count] if last else None
    out, line_r, line_s = refs[3 * count + last : 3 * count + last + 3]
    held, sems = refs[-2:] if last else (out, None)
    pairs, part = out.shape[0], out.shape[1]
    for d in range(count):
        for w in range(windows):
            at = d * windows + w
            line_r[at] = receivers[d][w].astype(F32) * factor
            if w < windows - 1:
                rows = sources[2 * d][w * pairs : (w + 1) * pairs, :].astype(F32)
            else:
                rows = sources[2 * d + 1][:pairs, :].astype(F32)
            for p in range(pairs):
                line_s[p, at : at + 1, :] = rows[p : p + 1, :]

    def copy(p):
        return pltpu.make_async_copy(held.at[p], out.at[p], sems.at[p])

    def one(p, carry):
        for f in range(0, NF, 128):
            re = slice(f, f + 128)
            im = slice(NF + f, NF + f + 128)
            if last:
                total_r, total_i = total[p, :, re], total[p, :, im]
            else:
                total_r = jnp.zeros((part, 128), F32)
                total_i = jnp.zeros((part, 128), F32)
            for at in range(count * windows):
                rr = line_r[at, :, re]
                ri = line_r[at, :, im]
                sr = line_s[p, at : at + 1, re]
                si = line_s[p, at : at + 1, im]
                total_r = total_r + (sr * rr + si * ri)
                total_i = total_i + (sr * ri - si * rr)
            held[p, :, re] = total_r
            held[p, :, im] = total_i
        if last:
            copy(p).start()
        return carry

    lax.fori_loop(0, pairs, one, 0)
    if last:
        for p in range(pairs):
            copy(p).wait()


def correlate(receivers, sources, total, pairs, factor):
    windows, part, width = receivers[0].shape
    count = len(receivers)
    vmem = pl.BlockSpec(memory_space=pltpu.VMEM)
    shape = (pairs, part, width)
    last = total is not None
    scratch = [
        pltpu.VMEM((count * windows, part, width), F32),
        pltpu.VMEM((pairs, -(-count * windows // 8) * 8, width), F32),
    ]
    if last:
        scratch += [pltpu.VMEM(shape, F32), pltpu.SemaphoreType.DMA((pairs,))]
    return pl.pallas_call(
        functools.partial(correlate_kernel, windows, factor, count),
        out_shape=jax.ShapeDtypeStruct(shape, F32),
        in_specs=[vmem] * (3 * count + last),
        out_specs=pl.BlockSpec(memory_space=pltpu.HBM) if last else vmem,
        scratch_shapes=scratch,
        compiler_params=pltpu.CompilerParams(vmem_limit_bytes=LIMIT),
        name="correlate",
    )(*receivers, *(part for both in sources for part in both), *([total] if last else []))


def shards(traces, filter_taps, source_counts, source_channel, block_sources):
    channels, samples = traces.shape
    tap_count = filter_taps.shape[1]
    pairs = block_sources.shape[1]
    windows = samples // HALF
    groups = lax.axis_size("chan")
    times = lax.axis_size("tm")
    chips = groups // 2
    part = channels // times
    sizes = part_rows(windows, pairs)
    rows_out = chips * sum(sizes)

    def across(x, axis, distance):
        size = lax.axis_size(axis)
        return lax.ppermute(x, axis, [(i, i ^ distance) for i in range(size)])

    smem = pl.BlockSpec(memory_space=pltpu.SMEM)
    vmem = pl.BlockSpec(memory_space=pltpu.VMEM)
    hbm = pl.BlockSpec(memory_space=pltpu.HBM)
    params = pltpu.CompilerParams(vmem_limit_bytes=LIMIT)
    bits = [1 << b for b in range(chips.bit_length() - 1)]

    other = across(block_sources, "chan", 1)
    inputs = (traces, filter_taps.T, jnp.asarray(piece_table()))
    tail, traces, taps, table = pl.pallas_call(
        head_kernel,
        out_shape=[jax.ShapeDtypeStruct((channels, HALF + 128), BF16)]
        + [jax.ShapeDtypeStruct(a.shape, a.dtype) for a in inputs],
        in_specs=[hbm] * 3,
        out_specs=[vmem] * 4,
        scratch_shapes=[pltpu.SemaphoreType.DMA((4,))],
        compiler_params=params,
        name="head",
    )(*(pltpu.with_memory_space_constraint(a, pltpu.HBM) for a in inputs))
    halo = lax.ppermute(tail, "tm", [(i - 1, i) for i in range(1, times)])
    wanted = [jnp.concatenate([block_sources, other], axis=0)]
    for bit in bits:
        known = jnp.concatenate(wanted, axis=0)
        wanted = [known, across(known, "chan", 2 * bit)]
    where = jnp.stack([lax.axis_index("chan"), lax.axis_index("tm")]).astype(jnp.int32)

    shape = (channels, windows, pairs, chips)
    width = windows * channels
    own = pl.pallas_call(
        functools.partial(own_kernel, windows),
        out_shape=[
            jax.ShapeDtypeStruct((width - channels, 2 * NF), F32),
            jax.ShapeDtypeStruct((channels, 2 * NF), BF16),
            jax.ShapeDtypeStruct((channels, 2 * NF), F32),
            jax.ShapeDtypeStruct((channels, (windows - 1) * 128), BF16),
        ],
        in_specs=[vmem] * 3,
        out_specs=[vmem] * 4,
        scratch_shapes=[
            pltpu.VMEM((3 * (-(-tap_count // 16) * 16), 128), F32),
            pltpu.VMEM((2 * tap_count + 6, channels), F32),
            pltpu.VMEM((channels, 2 * NF), F32),
        ],
        compiler_params=params,
        name="own",
    )(traces, taps, table)
    part_spectra, own_white, response, ends = own
    picks = pl.pallas_call(
        functools.partial(picks_kernel, shape),
        out_shape=jax.ShapeDtypeStruct((2 * rows_out, width), BF16),
        in_specs=[smem] * (3 + len(wanted)),
        out_specs=vmem,
        scratch_shapes=[pltpu.VMEM((2 * rows_out, width), F32)],
        compiler_params=params,
        name="picks",
    )(where, source_counts, source_channel, *wanted)
    outs = pl.pallas_call(
        functools.partial(rest_kernel, windows, times),
        out_shape=[jax.ShapeDtypeStruct((rows_out, 2 * NF), BF16)] * 2
        + [jax.ShapeDtypeStruct((windows * part, 2 * NF), BF16)] * times,
        in_specs=[smem] + [vmem] * 8,
        out_specs=[vmem] * (2 + times),
        scratch_shapes=[
            pltpu.VMEM((2 * tap_count + 6, width - channels), F32),
            pltpu.VMEM((width - channels, 2 * NF), F32),
            pltpu.VMEM((width, 2 * NF), BF16),
        ],
        compiler_params=params,
        name="rest",
    )(where, halo, ends, taps, table, part_spectra, own_white, response, picks)
    keep, send, blocks = outs[0], outs[1], outs[2:]
    gathered = keep + across(send, "chan", 1)
    rows = sum(sizes)
    pieces = [gathered[d * rows : (d + 1) * rows] for d in range(chips)]
    pieces = list(lax.optimization_barrier(tuple(pieces)))
    for bit in bits:
        onward = [d for d in range(2 * bit, chips) if d & (2 * bit - 1) == bit]
        if onward:
            block = jnp.concatenate([pieces[d] for d in onward], axis=0)
            block = across(block, "chan", 2 * bit)
            for i, d in enumerate(onward):
                pieces[d ^ bit] = pieces[d ^ bit] + block[i * rows : (i + 1) * rows]
    mine = pieces[0]
    for bit in bits[:-1]:
        mine = mine + across(pieces[bit], "chan", 2 * bit)
    mine = [mine[: sizes[0]], mine[sizes[0] :]]
    if bits:
        last = pieces[bits[-1]]
        for i, x in enumerate((last[: sizes[0]], last[sizes[0] :])):
            mine[i] = mine[i] + across(x, "chan", 2 * bits[-1])
    receivers = [blocks[0]]
    for d in range(1, times):
        receivers.append(across(blocks[d], "tm", d))
    receivers = [r.reshape(windows, part, 2 * NF) for r in receivers]
    sources = [mine]
    for d in range(1, times):
        both = []
        for x in mine:
            both.append(across(x, "tm", d))
        sources.append(both)

    factor = 1.0 / (windows * times)
    total = correlate(receivers[:1], sources[:1], None, pairs, factor)
    if times > 1:
        total = correlate(receivers[1:], sources[1:], total, pairs, factor)
    return total.transpose(1, 0, 2)


def solution(mesh):
    in_specs = (P(("seg", "chan"), "tm"), P("chan", None), P(), P(), P("chan", None))
    out_specs = P(("seg", "chan", "tm"), None, None)
    return jax.shard_map(shards, mesh=mesh, in_specs=in_specs, out_specs=out_specs, check_vma=False)
```

```python
import functools

import jax
import jax.numpy as jnp
import ml_dtypes
import numpy as np
from jax import lax
from jax.experimental import pallas as pl
from jax.experimental.pallas import tpu as pltpu
from jax.sharding import PartitionSpec as P


NFFT = 4096
NF = 512
F0 = 8
PIECE = NFFT // 8
HALF = NFFT // 2
CHUNK = 256
F32 = jnp.float32
BF16 = jnp.bfloat16
LIMIT = 24 * 1024 * 1024
HINT = 10**10


def piece_table():
    bins = F0 + np.arange(NF)
    angle = (bins * np.arange(PIECE)[:, None] % NFFT) * (2.0 * np.pi / NFFT)
    exact = np.concatenate([np.cos(angle), -np.sin(angle)], axis=1)
    high = exact.astype(ml_dtypes.bfloat16)
    low = (exact - high.astype(np.float64)).astype(ml_dtypes.bfloat16)
    return np.concatenate([high, low], axis=0)


def split_two(x):
    high = x.astype(BF16)
    low = (x - high.astype(F32)).astype(BF16)
    return high, low


def dot(a, b):
    return jnp.dot(a, b, preferred_element_type=F32)


def stacked_parts(x):
    high, low = split_two(x)
    high = high.astype(F32)
    return jnp.concatenate([high, low.astype(F32), high], axis=0)


def stacked_rows(table, rows, cols):
    first = table[:rows, cols]
    return jnp.concatenate([first, first, table[PIECE : PIECE + rows, cols]], axis=0)


class Turns:
    def __init__(self):
        lane = lax.broadcasted_iota(jnp.int32, (1, CHUNK), 1)
        turn = lane % 4
        self.odd = (turn % 2) == 1
        self.sign = jnp.where(self.odd, -1.0, 1.0)
        self.real = jnp.where(turn < 2, 1.0, -1.0)
        self.imag = jnp.where((turn == 0) | (turn == 3), 1.0, -1.0)
        eighth = lane % 8
        root = np.float32(np.sqrt(0.5))
        self.cos = jnp.where(turn % 4 == 0, 1.0, jnp.where(turn == 2, 0.0, root))
        self.cos = jnp.where((eighth > 2) & (eighth < 6), -self.cos, self.cos)
        self.sin = jnp.where(turn == 2, 1.0, jnp.where(turn == 0, 0.0, root))
        self.sin = jnp.where(eighth < 4, -self.sin, self.sin)

    def quarter(self, ar, ai, br, bi):
        return (
            ar + self.real * jnp.where(self.odd, bi, br),
            ai + self.imag * jnp.where(self.odd, br, bi),
        )

    def half(self, re, im):
        ar, ai = self.quarter(re[0], im[0], re[2], im[2])
        br, bi = self.quarter(re[1], im[1], re[3], im[3])
        return ar + (br * self.cos - bi * self.sin), ai + (br * self.sin + bi * self.cos)


def half_spectra(x, table, channels, halves, turns, f):
    re = slice(f, f + CHUNK)
    im = slice(NF + f, NF + f + CHUNK)
    both = jnp.concatenate([x, x], axis=1)
    dr = dot(both, table[:, re])
    di = dot(both, table[:, im])
    out = []
    for b in range(halves):
        rows = [slice((4 * b + e) * channels, (4 * b + e + 1) * channels) for e in range(4)]
        out.append(turns.half([dr[r] for r in rows], [di[r] for r in rows]))
    return out


def end_terms(taps_wide, shifted, tap_count, ends):
    lag = tap_count - 1
    apart = ends.T
    size = apart.shape[0]
    shifted[...] = jnp.zeros_like(shifted)
    shifted[:tap_count, :] = taps_wide
    total = jnp.zeros((lag, apart.shape[1]), F32)
    for j in range(1, tap_count):
        total = total + shifted[j : j + lag, :] * apart[size - j : size - j + 1, :]
    return stacked_parts(total).T.astype(BF16)


def whiten_rows(re, im):
    rows = re.shape[0]
    place = lax.broadcasted_iota(jnp.int32, (rows, NF), 1)
    power = re * re + im * im
    smooth = power
    for s in (1, 2):
        smooth = smooth + jnp.where(place >= s, pltpu.roll(power, s, 1), 0.0)
        smooth = smooth + jnp.where(place < NF - s, pltpu.roll(power, NF - s, 1), 0.0)
    total = jnp.sum(power, axis=1, keepdims=True)
    scaling = lax.rsqrt(smooth * 0.2 + (total * (0.1 / NF) + 1e-06))
    return (re * scaling).astype(BF16), (im * scaling).astype(BF16)


ROWS = 16


def whiten_all(spectra, white, count):
    def step(i, carry):
        rows = pl.ds(pl.multiple_of(i * ROWS, ROWS), ROWS)
        re, im = whiten_rows(spectra[rows, :NF], spectra[rows, NF:])
        white[rows, :NF] = re
        white[rows, NF:] = im
        return carry

    lax.fori_loop(0, count // ROWS, step, 0, unroll=2)


def tail_kernel(traces, wanted, tail, ids, sems):
    start = traces.shape[1] - tail.shape[1]
    copies = [
        pltpu.make_async_copy(traces.at[:, start:], tail, sems.at[0]),
        pltpu.make_async_copy(wanted, ids, sems.at[1]),
    ]
    for copy in copies:
        copy.start()
    for copy in copies:
        copy.wait()


def pair_kernel(mine, other, out):
    out[:1, :] = mine[...]
    out[1:, :] = other[...]


def own_kernel(windows, traces, taps, table, part, white, response, ends, square, shifted, spectra):
    channels, samples = traces.shape
    tap_count = taps.shape[0]
    square[...] = jnp.zeros_like(square)
    high, low = split_two(taps[...])
    high = high.astype(F32)
    lines = square.shape[0] // 3
    for i, value in enumerate((high, low.astype(F32), high)):
        square[i * lines : i * lines + tap_count, :channels] = value
    filter_taps = square[...].T[:channels].astype(BF16)
    tile = 128
    last = windows - 1
    for b in range(1, windows):
        ends[:, (b - 1) * tile : b * tile] = traces[:, b * HALF - tile : b * HALF]
    start = (last - 1) * HALF
    apart = traces[:, start - tile : start].astype(F32) - traces[:, samples - tile :].astype(F32)
    edge = end_terms(taps[...], shifted, tap_count, apart)
    pieces = samples // PIECE
    x = jnp.concatenate([traces[:, q * PIECE : (q + 1) * PIECE] for q in range(pieces)], axis=0)
    turns = Turns()
    for f in range(0, NF, CHUNK):
        re = slice(f, f + CHUNK)
        im = slice(NF + f, NF + f + CHUNK)
        pr = dot(filter_taps, stacked_rows(table, lines, re))
        pi = dot(filter_taps, stacked_rows(table, lines, im))
        response[:, re] = pr
        response[:, im] = pi
        halves = half_spectra(x, table, channels, windows, turns, f)
        for w in range(windows):
            xr, xi = halves[w]
            xr, xi = turns.sign * xr, turns.sign * xi
            if w > 0:
                xr, xi = xr + halves[w - 1][0], xi + halves[w - 1][1]
            yr = xr * pr - xi * pi
            yi = xr * pi + xi * pr
            if w < last:
                rows = slice(w * channels, (w + 1) * channels)
                part[rows, re] = yr
                part[rows, im] = yi
            else:
                spectra[:, re] = yr + dot(edge, stacked_rows(table, tap_count - 1, re))
                spectra[:, im] = yi + dot(edge, stacked_rows(table, tap_count - 1, im))
    whiten_all(spectra, white, channels)


def part_rows(windows, pairs):
    return [-(-w * pairs // 8) * 8 for w in (windows - 1, 1)]


def picks_kernel(shape, where, counts, slots, *refs):
    channels, windows, pairs, chips = shape
    wanted, picks, chosen = refs[:-2], refs[-2], refs[-1]
    group = where[0]
    first = jnp.int32(0)
    for g in range(counts.shape[0]):
        first = first + jnp.where(g < group, counts[g], 0)
    owned = counts[group]
    width = windows * channels
    lane = lax.broadcasted_iota(jnp.int32, (1, width), 1)
    columns = [jnp.where(lane // channels == w, lane % channels, -2) for w in range(windows)]
    sizes = part_rows(windows, pairs)
    per = wanted[0].shape[0]
    chosen[...] = jnp.zeros_like(chosen)
    for core in range(2):
        for d in range(chips):
            base = (core * chips + d) * sum(sizes)
            tail = base + sizes[0]
            for p in range(pairs):
                slot = wanted[2 * d // per][(2 * d + core) % per, p] - first
                mine = (slot >= 0) & (slot < owned)
                channel = slots[group, jnp.where(mine, slot, 0)]
                channel = jnp.where(mine, channel, -1)
                for w in range(windows):
                    row = (base + w * pairs if w < windows - 1 else tail) + p
                    chosen[row : row + 1, :] = (columns[w] == channel).astype(F32)
    picks[...] = chosen[...].astype(BF16)


def rest_kernel(
    windows, times, where, halo, ends, taps, table, part, own_white, response, picks, *refs
):
    keep, send = refs[:2]
    blocks = refs[2 : 2 + times]
    shifted, spectra, white = refs[2 + times :]
    channels = response.shape[0]
    tap_count = taps.shape[0]
    tile = halo.shape[1] - HALF
    rest = windows - 1

    before = [halo[:, :tile], halo[:, HALF:]]
    before += [ends[:, (b - 1) * tile : b * tile] for b in range(1, windows - 2)]
    after = [ends[:, w * tile : (w + 1) * tile] for w in range(rest)]
    apart = jnp.concatenate([b.astype(F32) - a.astype(F32) for b, a in zip(before, after)], axis=0)
    taps_wide = jnp.concatenate([taps[...]] * rest, axis=1)
    edge = end_terms(taps_wide, shifted, tap_count, apart)
    x = jnp.concatenate(
        [halo[:, tile + q * PIECE : tile + (q + 1) * PIECE] for q in range(HALF // PIECE)],
        axis=0,
    )
    turns = Turns()
    for f in range(0, NF, CHUNK):
        re = slice(f, f + CHUNK)
        im = slice(NF + f, NF + f + CHUNK)
        xr, xi = half_spectra(x, table, channels, 1, turns, f)[0]
        pr, pi = response[:, re], response[:, im]
        er = dot(edge, stacked_rows(table, tap_count - 1, re))
        ei = dot(edge, stacked_rows(table, tap_count - 1, im))
        spectra[:channels, re] = part[:channels, re] + er[:channels] + (xr * pr - xi * pi)
        spectra[:channels, im] = part[:channels, im] + ei[:channels] + (xr * pi + xi * pr)
        spectra[channels:, re] = part[channels:, re] + er[channels:]
        spectra[channels:, im] = part[channels:, im] + ei[channels:]
    count = rest * channels
    whiten_all(spectra, white, count)
    white[count:, :] = own_white[...]
    base = keep.shape[0]
    size = channels // times
    choose = picks[...]
    for f in range(0, 2 * NF, CHUNK):
        cols = slice(f, f + CHUNK)
        out = dot(choose, white[:, cols]).astype(BF16)
        keep[:, cols] = out[:base]
        send[:, cols] = out[base:]
    for d in range(times):
        line = (where[1] ^ d) * size
        for w in range(windows):
            if size % ROWS == 0:
                at = pl.multiple_of(w * channels + line, ROWS)
                blocks[d][w * size : (w + 1) * size, :] = white[pl.ds(at, size), :]
            else:
                row = lax.broadcasted_iota(jnp.int32, (size, channels), 0)
                col = lax.broadcasted_iota(jnp.int32, (size, channels), 1)
                move = (col == row + line).astype(F32).astype(BF16)
                moved = dot(move, white[w * channels : (w + 1) * channels, :])
                blocks[d][w * size : (w + 1) * size, :] = moved.astype(BF16)


def correlate_kernel(windows, factor, count, *refs):
    receivers = refs[:count]
    sources = refs[count : 3 * count]
    last = len(refs) == 3 * count + 6
    total = refs[3 * count] if last else None
    out, line_r, line_s = refs[3 * count + last : 3 * count + last + 3]
    held, sems = refs[-2:] if last else (out, None)
    pairs, part = out.shape[0], out.shape[1]
    for d in range(count):
        for w in range(windows):
            at = d * windows + w
            line_r[at] = receivers[d][w].astype(F32) * factor
            if w < windows - 1:
                rows = sources[2 * d][w * pairs : (w + 1) * pairs, :].astype(F32)
            else:
                rows = sources[2 * d + 1][:pairs, :].astype(F32)
            for p in range(pairs):
                line_s[p, at : at + 1, :] = rows[p : p + 1, :]

    def copy(p):
        return pltpu.make_async_copy(held.at[p], out.at[p], sems.at[p])

    def one(p, carry):
        for f in range(0, NF, 128):
            re = slice(f, f + 128)
            im = slice(NF + f, NF + f + 128)
            if last:
                total_r, total_i = total[p, :, re], total[p, :, im]
            else:
                total_r = jnp.zeros((part, 128), F32)
                total_i = jnp.zeros((part, 128), F32)
            for at in range(count * windows):
                rr = line_r[at, :, re]
                ri = line_r[at, :, im]
                sr = line_s[p, at : at + 1, re]
                si = line_s[p, at : at + 1, im]
                total_r = total_r + (sr * rr + si * ri)
                total_i = total_i + (sr * ri - si * rr)
            held[p, :, re] = total_r
            held[p, :, im] = total_i
        if last:
            copy(p).start()
        return carry

    lax.fori_loop(0, pairs, one, 0)
    if last:
        for p in range(pairs):
            copy(p).wait()


def correlate(receivers, sources, total, pairs, factor):
    windows, part, width = receivers[0].shape
    count = len(receivers)
    vmem = pl.BlockSpec(memory_space=pltpu.VMEM)
    shape = (pairs, part, width)
    last = total is not None
    scratch = [
        pltpu.VMEM((count * windows, part, width), F32),
        pltpu.VMEM((pairs, -(-count * windows // 8) * 8, width), F32),
    ]
    if last:
        scratch += [pltpu.VMEM(shape, F32), pltpu.SemaphoreType.DMA((pairs,))]
    return pl.pallas_call(
        functools.partial(correlate_kernel, windows, factor, count),
        out_shape=jax.ShapeDtypeStruct(shape, F32),
        in_specs=[vmem] * (3 * count + last),
        out_specs=pl.BlockSpec(memory_space=pltpu.HBM) if last else vmem,
        scratch_shapes=scratch,
        compiler_params=pltpu.CompilerParams(vmem_limit_bytes=LIMIT),
        name="correlate",
    )(*receivers, *(part for both in sources for part in both), *([total] if last else []))


def shards(traces, filter_taps, source_counts, source_channel, block_sources):
    channels, samples = traces.shape
    tap_count = filter_taps.shape[1]
    pairs = block_sources.shape[1]
    windows = samples // HALF
    groups = lax.axis_size("chan")
    times = lax.axis_size("tm")
    chips = groups // 2
    part = channels // times
    sizes = part_rows(windows, pairs)
    rows_out = chips * sum(sizes)

    def across(x, axis, distance):
        size = lax.axis_size(axis)
        return lax.ppermute(x, axis, [(i, i ^ distance) for i in range(size)])

    smem = pl.BlockSpec(memory_space=pltpu.SMEM)
    vmem = pl.BlockSpec(memory_space=pltpu.VMEM)
    hbm = pl.BlockSpec(memory_space=pltpu.HBM)
    params = pltpu.CompilerParams(vmem_limit_bytes=LIMIT)
    bits = [1 << b for b in range(chips.bit_length() - 1)]

    tail, ids = pl.pallas_call(
        tail_kernel,
        out_shape=[
            jax.ShapeDtypeStruct((channels, HALF + 128), BF16),
            jax.ShapeDtypeStruct(block_sources.shape, jnp.int32),
        ],
        in_specs=[hbm] * 2,
        out_specs=[vmem] * 2,
        scratch_shapes=[pltpu.SemaphoreType.DMA((2,))],
        compiler_params=params,
        name="tail",
    )(*(pltpu.with_memory_space_constraint(a, pltpu.HBM) for a in (traces, block_sources)))
    halo = lax.ppermute(tail, "tm", [(i - 1, i) for i in range(1, times)])
    other = across(ids, "chan", 1)
    taps = filter_taps.T
    traces, taps, table = (
        pltpu.with_memory_space_constraint(a, pltpu.VMEM)
        for a in (traces, taps, jnp.asarray(piece_table()))
    )
    wanted = [
        pl.pallas_call(
            pair_kernel,
            out_shape=jax.ShapeDtypeStruct((2, pairs), jnp.int32),
            in_specs=[vmem] * 2,
            out_specs=vmem,
            compiler_params=params,
            cost_estimate=pl.CostEstimate(flops=HINT, bytes_accessed=8 * pairs, transcendentals=0),
            name="pair",
        )(ids, other)
    ]
    for bit in bits:
        known = jnp.concatenate(wanted, axis=0)
        wanted = [known, across(known, "chan", 2 * bit)]
    where = jnp.stack([lax.axis_index("chan"), lax.axis_index("tm")]).astype(jnp.int32)

    shape = (channels, windows, pairs, chips)
    width = windows * channels
    own = pl.pallas_call(
        functools.partial(own_kernel, windows),
        out_shape=[
            jax.ShapeDtypeStruct((width - channels, 2 * NF), F32),
            jax.ShapeDtypeStruct((channels, 2 * NF), BF16),
            jax.ShapeDtypeStruct((channels, 2 * NF), F32),
            jax.ShapeDtypeStruct((channels, (windows - 1) * 128), BF16),
        ],
        in_specs=[vmem] * 3,
        out_specs=[vmem] * 4,
        scratch_shapes=[
            pltpu.VMEM((3 * (-(-tap_count // 16) * 16), 128), F32),
            pltpu.VMEM((2 * tap_count + 6, channels), F32),
            pltpu.VMEM((channels, 2 * NF), F32),
        ],
        compiler_params=params,
        name="own",
    )(traces, taps, table)
    part_spectra, own_white, response, ends = own
    picks = pl.pallas_call(
        functools.partial(picks_kernel, shape),
        out_shape=jax.ShapeDtypeStruct((2 * rows_out, width), BF16),
        in_specs=[smem] * (3 + len(wanted)),
        out_specs=vmem,
        scratch_shapes=[pltpu.VMEM((2 * rows_out, width), F32)],
        compiler_params=params,
        name="picks",
    )(where, source_counts, source_channel, *wanted)
    outs = pl.pallas_call(
        functools.partial(rest_kernel, windows, times),
        out_shape=[jax.ShapeDtypeStruct((rows_out, 2 * NF), BF16)] * 2
        + [jax.ShapeDtypeStruct((windows * part, 2 * NF), BF16)] * times,
        in_specs=[smem] + [vmem] * 8,
        out_specs=[vmem] * (2 + times),
        scratch_shapes=[
            pltpu.VMEM((2 * tap_count + 6, width - channels), F32),
            pltpu.VMEM((width - channels, 2 * NF), F32),
            pltpu.VMEM((width, 2 * NF), BF16),
        ],
        compiler_params=params,
        name="rest",
    )(where, halo, ends, taps, table, part_spectra, own_white, response, picks)
    keep, send, blocks = outs[0], outs[1], outs[2:]
    gathered = keep + across(send, "chan", 1)
    rows = sum(sizes)
    pieces = [gathered[d * rows : (d + 1) * rows] for d in range(chips)]
    pieces = list(lax.optimization_barrier(tuple(pieces)))
    for bit in bits:
        onward = [d for d in range(2 * bit, chips) if d & (2 * bit - 1) == bit]
        if onward:
            block = jnp.concatenate([pieces[d] for d in onward], axis=0)
            block = across(block, "chan", 2 * bit)
            for i, d in enumerate(onward):
                pieces[d ^ bit] = pieces[d ^ bit] + block[i * rows : (i + 1) * rows]
    mine = pieces[0]
    for bit in bits[:-1]:
        mine = mine + across(pieces[bit], "chan", 2 * bit)
    mine = [mine[: sizes[0]], mine[sizes[0] :]]
    if bits:
        last = pieces[bits[-1]]
        for i, x in enumerate((last[: sizes[0]], last[sizes[0] :])):
            mine[i] = mine[i] + across(x, "chan", 2 * bits[-1])
    receivers = [blocks[0]]
    for d in range(1, times):
        receivers.append(across(blocks[d], "tm", d))
    receivers = [r.reshape(windows, part, 2 * NF) for r in receivers]
    sources = [mine]
    for d in range(1, times):
        both = []
        for x in mine:
            both.append(across(x, "tm", d))
        sources.append(both)

    factor = 1.0 / (windows * times)
    total = correlate(receivers[:1], sources[:1], None, pairs, factor)
    if times > 1:
        total = correlate(receivers[1:], sources[1:], total, pairs, factor)
    return total.transpose(1, 0, 2)


def solution(mesh):
    in_specs = (P(("seg", "chan"), "tm"), P("chan", None), P(), P(), P("chan", None))
    out_specs = P(("seg", "chan", "tm"), None, None)
    return jax.shard_map(shards, mesh=mesh, in_specs=in_specs, out_specs=out_specs, check_vma=False)
```

```python
import functools

import jax
import jax.numpy as jnp
import ml_dtypes
import numpy as np
from jax import lax
from jax.experimental import pallas as pl
from jax.experimental.pallas import tpu as pltpu
from jax.sharding import PartitionSpec as P


NFFT = 4096
NF = 512
F0 = 8
PIECE = NFFT // 8
HALF = NFFT // 2
CHUNK = 256
F32 = jnp.float32
BF16 = jnp.bfloat16
LIMIT = 24 * 1024 * 1024
HINT = 10**10


def piece_table():
    bins = F0 + np.arange(NF)
    angle = (bins * np.arange(PIECE)[:, None] % NFFT) * (2.0 * np.pi / NFFT)
    exact = np.concatenate([np.cos(angle), -np.sin(angle)], axis=1)
    high = exact.astype(ml_dtypes.bfloat16)
    low = (exact - high.astype(np.float64)).astype(ml_dtypes.bfloat16)
    return np.concatenate([high, low], axis=0)


def split_two(x):
    high = x.astype(BF16)
    low = (x - high.astype(F32)).astype(BF16)
    return high, low


def dot(a, b):
    return jnp.dot(a, b, preferred_element_type=F32)


def stacked_parts(x):
    high, low = split_two(x)
    high = high.astype(F32)
    return jnp.concatenate([high, low.astype(F32), high], axis=0)


def stacked_rows(table, rows, cols):
    first = table[:rows, cols]
    return jnp.concatenate([first, first, table[PIECE : PIECE + rows, cols]], axis=0)


class Turns:
    def __init__(self):
        lane = lax.broadcasted_iota(jnp.int32, (1, CHUNK), 1)
        turn = lane % 4
        self.odd = (turn % 2) == 1
        self.sign = jnp.where(self.odd, -1.0, 1.0)
        self.real = jnp.where(turn < 2, 1.0, -1.0)
        self.imag = jnp.where((turn == 0) | (turn == 3), 1.0, -1.0)
        eighth = lane % 8
        root = np.float32(np.sqrt(0.5))
        self.cos = jnp.where(turn % 4 == 0, 1.0, jnp.where(turn == 2, 0.0, root))
        self.cos = jnp.where((eighth > 2) & (eighth < 6), -self.cos, self.cos)
        self.sin = jnp.where(turn == 2, 1.0, jnp.where(turn == 0, 0.0, root))
        self.sin = jnp.where(eighth < 4, -self.sin, self.sin)

    def quarter(self, ar, ai, br, bi):
        return (
            ar + self.real * jnp.where(self.odd, bi, br),
            ai + self.imag * jnp.where(self.odd, br, bi),
        )

    def half(self, re, im):
        ar, ai = self.quarter(re[0], im[0], re[2], im[2])
        br, bi = self.quarter(re[1], im[1], re[3], im[3])
        return ar + (br * self.cos - bi * self.sin), ai + (br * self.sin + bi * self.cos)


def half_spectra(x, table, channels, halves, turns, f):
    re = slice(f, f + CHUNK)
    im = slice(NF + f, NF + f + CHUNK)
    both = jnp.concatenate([x, x], axis=1)
    dr = dot(both, table[:, re])
    di = dot(both, table[:, im])
    out = []
    for b in range(halves):
        rows = [slice((4 * b + e) * channels, (4 * b + e + 1) * channels) for e in range(4)]
        out.append(turns.half([dr[r] for r in rows], [di[r] for r in rows]))
    return out


def end_terms(taps_wide, shifted, tap_count, ends):
    lag = tap_count - 1
    apart = ends.T
    size = apart.shape[0]
    shifted[...] = jnp.zeros_like(shifted)
    shifted[:tap_count, :] = taps_wide
    total = jnp.zeros((lag, apart.shape[1]), F32)
    for j in range(1, tap_count):
        total = total + shifted[j : j + lag, :] * apart[size - j : size - j + 1, :]
    return stacked_parts(total).T.astype(BF16)


def whiten_rows(re, im):
    rows = re.shape[0]
    place = lax.broadcasted_iota(jnp.int32, (rows, NF), 1)
    power = re * re + im * im
    smooth = power
    for s in (1, 2):
        smooth = smooth + jnp.where(place >= s, pltpu.roll(power, s, 1), 0.0)
        smooth = smooth + jnp.where(place < NF - s, pltpu.roll(power, NF - s, 1), 0.0)
    total = jnp.sum(power, axis=1, keepdims=True)
    scaling = lax.rsqrt(smooth * 0.2 + (total * (0.1 / NF) + 1e-06))
    return (re * scaling).astype(BF16), (im * scaling).astype(BF16)


ROWS = 16


def whiten_all(spectra, white, count):
    def step(i, carry):
        rows = pl.ds(pl.multiple_of(i * ROWS, ROWS), ROWS)
        re, im = whiten_rows(spectra[rows, :NF], spectra[rows, NF:])
        white[rows, :NF] = re
        white[rows, NF:] = im
        return carry

    lax.fori_loop(0, count // ROWS, step, 0, unroll=2)


def tail_kernel(traces, wanted, tail, ids, sems):
    start = traces.shape[1] - tail.shape[1]
    copies = [
        pltpu.make_async_copy(traces.at[:, start:], tail, sems.at[0]),
        pltpu.make_async_copy(wanted, ids, sems.at[1]),
    ]
    for copy in copies:
        copy.start()
    for copy in copies:
        copy.wait()


def pair_kernel(mine, other, out):
    out[:1, :] = mine[...]
    out[1:, :] = other[...]


def own_chunk(windows, f, traces, table, lines, edge, part, response, last):
    channels, samples = traces.shape
    size = lines.shape[1] // 3
    lag = edge.shape[1] // 3
    pieces = samples // PIECE
    x = jnp.concatenate([traces[:, q * PIECE : (q + 1) * PIECE] for q in range(pieces)], axis=0)
    turns = Turns()
    re = slice(f, f + CHUNK)
    im = slice(NF + f, NF + f + CHUNK)
    pr = dot(lines[...], stacked_rows(table, size, re))
    pi = dot(lines[...], stacked_rows(table, size, im))
    response[:, :CHUNK] = pr
    response[:, CHUNK:] = pi
    halves = half_spectra(x, table, channels, windows, turns, f)
    for w in range(windows):
        xr, xi = halves[w]
        xr, xi = turns.sign * xr, turns.sign * xi
        if w > 0:
            xr, xi = xr + halves[w - 1][0], xi + halves[w - 1][1]
        yr = xr * pr - xi * pi
        yi = xr * pi + xi * pr
        if w < windows - 1:
            rows = slice(w * channels, (w + 1) * channels)
            part[rows, :CHUNK] = yr
            part[rows, CHUNK:] = yi
        else:
            last[:, :CHUNK] = yr + dot(edge[...], stacked_rows(table, lag, re))
            last[:, CHUNK:] = yi + dot(edge[...], stacked_rows(table, lag, im))


def first_kernel(
    windows, traces, taps, table, part, response, last, ends, edge, lines, square, shifted
):
    channels, samples = traces.shape
    tap_count = taps.shape[0]
    square[...] = jnp.zeros_like(square)
    high, low = split_two(taps[...])
    high = high.astype(F32)
    size = square.shape[0] // 3
    for i, value in enumerate((high, low.astype(F32), high)):
        square[i * size : i * size + tap_count, :channels] = value
    lines[...] = square[...].T[:channels].astype(BF16)
    tile = 128
    for b in range(1, windows):
        ends[:, (b - 1) * tile : b * tile] = traces[:, b * HALF - tile : b * HALF]
    start = (windows - 2) * HALF
    apart = traces[:, start - tile : start].astype(F32) - traces[:, samples - tile :].astype(F32)
    edge[...] = end_terms(taps[...], shifted, tap_count, apart)
    own_chunk(windows, 0, traces, table, lines, edge, part, response, last)


def second_kernel(
    windows, traces, table, lines, edge, first, part, response, white, second, spectra
):
    own_chunk(windows, CHUNK, traces, table, lines, edge, part, response, second)
    for i, half in enumerate((first, second)):
        spectra[:, i * CHUNK : (i + 1) * CHUNK] = half[:, :CHUNK]
        spectra[:, NF + i * CHUNK : NF + (i + 1) * CHUNK] = half[:, CHUNK:]
    whiten_all(spectra, white, white.shape[0])


def part_rows(windows, pairs):
    return [-(-w * pairs // 8) * 8 for w in (windows - 1, 1)]


def picks_kernel(shape, where, counts, slots, *refs):
    channels, windows, pairs, chips = shape
    wanted, picks, chosen = refs[:-2], refs[-2], refs[-1]
    group = where[0]
    first = jnp.int32(0)
    for g in range(counts.shape[0]):
        first = first + jnp.where(g < group, counts[g], 0)
    owned = counts[group]
    width = windows * channels
    lane = lax.broadcasted_iota(jnp.int32, (1, width), 1)
    columns = [jnp.where(lane // channels == w, lane % channels, -2) for w in range(windows)]
    sizes = part_rows(windows, pairs)
    per = wanted[0].shape[0]
    chosen[...] = jnp.zeros_like(chosen)
    for core in range(2):
        for d in range(chips):
            base = (core * chips + d) * sum(sizes)
            tail = base + sizes[0]
            for p in range(pairs):
                slot = wanted[2 * d // per][(2 * d + core) % per, p] - first
                mine = (slot >= 0) & (slot < owned)
                channel = slots[group, jnp.where(mine, slot, 0)]
                channel = jnp.where(mine, channel, -1)
                for w in range(windows):
                    row = (base + w * pairs if w < windows - 1 else tail) + p
                    chosen[row : row + 1, :] = (columns[w] == channel).astype(F32)
    picks[...] = chosen[...].astype(BF16)


def rest_kernel(
    windows, times, where, halo, ends, taps, table, part_a, part_b, response_a, response_b, *refs
):
    own_white, picks, keep, send = refs[:4]
    blocks = refs[4 : 4 + times]
    shifted, spectra, white = refs[4 + times :]
    channels = response_a.shape[0]
    tap_count = taps.shape[0]
    tile = halo.shape[1] - HALF
    rest = windows - 1

    before = [halo[:, :tile], halo[:, HALF:]]
    before += [ends[:, (b - 1) * tile : b * tile] for b in range(1, windows - 2)]
    after = [ends[:, w * tile : (w + 1) * tile] for w in range(rest)]
    apart = jnp.concatenate([b.astype(F32) - a.astype(F32) for b, a in zip(before, after)], axis=0)
    taps_wide = jnp.concatenate([taps[...]] * rest, axis=1)
    edge = end_terms(taps_wide, shifted, tap_count, apart)
    x = jnp.concatenate(
        [halo[:, tile + q * PIECE : tile + (q + 1) * PIECE] for q in range(HALF // PIECE)],
        axis=0,
    )
    turns = Turns()
    for f in range(0, NF, CHUNK):
        re = slice(f, f + CHUNK)
        im = slice(NF + f, NF + f + CHUNK)
        xr, xi = half_spectra(x, table, channels, 1, turns, f)[0]
        part, response = (part_b, response_b) if f else (part_a, response_a)
        pr, pi = response[:, :CHUNK], response[:, CHUNK:]
        er = dot(edge, stacked_rows(table, tap_count - 1, re))
        ei = dot(edge, stacked_rows(table, tap_count - 1, im))
        spectra[:channels, re] = part[:channels, :CHUNK] + er[:channels] + (xr * pr - xi * pi)
        spectra[:channels, im] = part[:channels, CHUNK:] + ei[:channels] + (xr * pi + xi * pr)
        spectra[channels:, re] = part[channels:, :CHUNK] + er[channels:]
        spectra[channels:, im] = part[channels:, CHUNK:] + ei[channels:]
    count = rest * channels
    whiten_all(spectra, white, count)
    white[count:, :] = own_white[...]
    base = keep.shape[0]
    size = channels // times
    choose = picks[...]
    for f in range(0, 2 * NF, CHUNK):
        cols = slice(f, f + CHUNK)
        out = dot(choose, white[:, cols]).astype(BF16)
        keep[:, cols] = out[:base]
        send[:, cols] = out[base:]
    for d in range(times):
        line = (where[1] ^ d) * size
        for w in range(windows):
            if size % ROWS == 0:
                at = pl.multiple_of(w * channels + line, ROWS)
                blocks[d][w * size : (w + 1) * size, :] = white[pl.ds(at, size), :]
            else:
                row = lax.broadcasted_iota(jnp.int32, (size, channels), 0)
                col = lax.broadcasted_iota(jnp.int32, (size, channels), 1)
                move = (col == row + line).astype(F32).astype(BF16)
                moved = dot(move, white[w * channels : (w + 1) * channels, :])
                blocks[d][w * size : (w + 1) * size, :] = moved.astype(BF16)


def correlate_kernel(windows, factor, count, *refs):
    receivers = refs[:count]
    sources = refs[count : 3 * count]
    last = len(refs) == 3 * count + 6
    total = refs[3 * count] if last else None
    out, line_r, line_s = refs[3 * count + last : 3 * count + last + 3]
    held, sems = refs[-2:] if last else (out, None)
    pairs, part = out.shape[0], out.shape[1]
    for d in range(count):
        for w in range(windows):
            at = d * windows + w
            line_r[at] = receivers[d][w].astype(F32) * factor
            if w < windows - 1:
                rows = sources[2 * d][w * pairs : (w + 1) * pairs, :].astype(F32)
            else:
                rows = sources[2 * d + 1][:pairs, :].astype(F32)
            for p in range(pairs):
                line_s[p, at : at + 1, :] = rows[p : p + 1, :]

    def copy(p):
        return pltpu.make_async_copy(held.at[p], out.at[p], sems.at[p])

    def one(p, carry):
        for f in range(0, NF, 128):
            re = slice(f, f + 128)
            im = slice(NF + f, NF + f + 128)
            if last:
                total_r, total_i = total[p, :, re], total[p, :, im]
            else:
                total_r = jnp.zeros((part, 128), F32)
                total_i = jnp.zeros((part, 128), F32)
            for at in range(count * windows):
                rr = line_r[at, :, re]
                ri = line_r[at, :, im]
                sr = line_s[p, at : at + 1, re]
                si = line_s[p, at : at + 1, im]
                total_r = total_r + (sr * rr + si * ri)
                total_i = total_i + (sr * ri - si * rr)
            held[p, :, re] = total_r
            held[p, :, im] = total_i
        if last:
            copy(p).start()
        return carry

    lax.fori_loop(0, pairs, one, 0)
    if last:
        for p in range(pairs):
            copy(p).wait()


def correlate(receivers, sources, total, pairs, factor):
    windows, part, width = receivers[0].shape
    count = len(receivers)
    vmem = pl.BlockSpec(memory_space=pltpu.VMEM)
    shape = (pairs, part, width)
    last = total is not None
    scratch = [
        pltpu.VMEM((count * windows, part, width), F32),
        pltpu.VMEM((pairs, -(-count * windows // 8) * 8, width), F32),
    ]
    if last:
        scratch += [pltpu.VMEM(shape, F32), pltpu.SemaphoreType.DMA((pairs,))]
    return pl.pallas_call(
        functools.partial(correlate_kernel, windows, factor, count),
        out_shape=jax.ShapeDtypeStruct(shape, F32),
        in_specs=[vmem] * (3 * count + last),
        out_specs=pl.BlockSpec(memory_space=pltpu.HBM) if last else vmem,
        scratch_shapes=scratch,
        compiler_params=pltpu.CompilerParams(vmem_limit_bytes=LIMIT),
        name="correlate",
    )(*receivers, *(part for both in sources for part in both), *([total] if last else []))


def shards(traces, filter_taps, source_counts, source_channel, block_sources):
    channels, samples = traces.shape
    tap_count = filter_taps.shape[1]
    pairs = block_sources.shape[1]
    windows = samples // HALF
    groups = lax.axis_size("chan")
    times = lax.axis_size("tm")
    chips = groups // 2
    part = channels // times
    sizes = part_rows(windows, pairs)
    rows_out = chips * sum(sizes)

    def across(x, axis, distance):
        size = lax.axis_size(axis)
        return lax.ppermute(x, axis, [(i, i ^ distance) for i in range(size)])

    smem = pl.BlockSpec(memory_space=pltpu.SMEM)
    vmem = pl.BlockSpec(memory_space=pltpu.VMEM)
    hbm = pl.BlockSpec(memory_space=pltpu.HBM)
    params = pltpu.CompilerParams(vmem_limit_bytes=LIMIT)
    bits = [1 << b for b in range(chips.bit_length() - 1)]

    other = across(block_sources, "chan", 1)
    tail, ids = pl.pallas_call(
        tail_kernel,
        out_shape=[
            jax.ShapeDtypeStruct((channels, HALF + 128), BF16),
            jax.ShapeDtypeStruct(block_sources.shape, jnp.int32),
        ],
        in_specs=[hbm] * 2,
        out_specs=[vmem] * 2,
        scratch_shapes=[pltpu.SemaphoreType.DMA((2,))],
        compiler_params=params,
        name="tail",
    )(*(pltpu.with_memory_space_constraint(a, pltpu.HBM) for a in (traces, block_sources)))
    halo = lax.ppermute(tail, "tm", [(i - 1, i) for i in range(1, times)])
    taps = filter_taps.T
    traces, taps, table = (
        pltpu.with_memory_space_constraint(a, pltpu.VMEM)
        for a in (traces, taps, jnp.asarray(piece_table()))
    )
    wanted = [
        pl.pallas_call(
            pair_kernel,
            out_shape=jax.ShapeDtypeStruct((2, pairs), jnp.int32),
            in_specs=[vmem] * 2,
            out_specs=vmem,
            compiler_params=params,
            cost_estimate=pl.CostEstimate(flops=HINT, bytes_accessed=8 * pairs, transcendentals=0),
            name="pair",
        )(ids, other)
    ]
    for bit in bits:
        known = jnp.concatenate(wanted, axis=0)
        wanted = [known, across(known, "chan", 2 * bit)]
    where = jnp.stack([lax.axis_index("chan"), lax.axis_index("tm")]).astype(jnp.int32)

    shape = (channels, windows, pairs, chips)
    width = windows * channels
    chunk_shapes = [
        jax.ShapeDtypeStruct((width - channels, 2 * CHUNK), F32),
        jax.ShapeDtypeStruct((channels, 2 * CHUNK), F32),
    ]
    size = -(-tap_count // 16) * 16
    part_a, response_a, last, ends, edge, lines = pl.pallas_call(
        functools.partial(first_kernel, windows),
        out_shape=chunk_shapes
        + [
            chunk_shapes[1],
            jax.ShapeDtypeStruct((channels, (windows - 1) * 128), BF16),
            jax.ShapeDtypeStruct((channels, 3 * (tap_count - 1)), BF16),
            jax.ShapeDtypeStruct((channels, 3 * size), BF16),
        ],
        in_specs=[vmem] * 3,
        out_specs=[vmem] * 6,
        scratch_shapes=[
            pltpu.VMEM((3 * size, 128), F32),
            pltpu.VMEM((2 * tap_count + 6, channels), F32),
        ],
        compiler_params=params,
        name="first",
    )(traces, taps, table)
    part_b, response_b, own_white = pl.pallas_call(
        functools.partial(second_kernel, windows),
        out_shape=chunk_shapes + [jax.ShapeDtypeStruct((channels, 2 * NF), BF16)],
        in_specs=[vmem] * 5,
        out_specs=[vmem] * 3,
        scratch_shapes=[
            pltpu.VMEM((channels, 2 * CHUNK), F32),
            pltpu.VMEM((channels, 2 * NF), F32),
        ],
        compiler_params=params,
        name="second",
    )(traces, table, lines, edge, last)
    picks = pl.pallas_call(
        functools.partial(picks_kernel, shape),
        out_shape=jax.ShapeDtypeStruct((2 * rows_out, width), BF16),
        in_specs=[smem] * (3 + len(wanted)),
        out_specs=vmem,
        scratch_shapes=[pltpu.VMEM((2 * rows_out, width), F32)],
        compiler_params=params,
        name="picks",
    )(where, source_counts, source_channel, *wanted)
    outs = pl.pallas_call(
        functools.partial(rest_kernel, windows, times),
        out_shape=[jax.ShapeDtypeStruct((rows_out, 2 * NF), BF16)] * 2
        + [jax.ShapeDtypeStruct((windows * part, 2 * NF), BF16)] * times,
        in_specs=[smem] + [vmem] * 10,
        out_specs=[vmem] * (2 + times),
        scratch_shapes=[
            pltpu.VMEM((2 * tap_count + 6, width - channels), F32),
            pltpu.VMEM((width - channels, 2 * NF), F32),
            pltpu.VMEM((width, 2 * NF), BF16),
        ],
        compiler_params=params,
        name="rest",
    )(
        where,
        halo,
        ends,
        taps,
        table,
        part_a,
        part_b,
        response_a,
        response_b,
        own_white,
        picks,
    )
    keep, send, blocks = outs[0], outs[1], outs[2:]
    gathered = keep + across(send, "chan", 1)
    rows = sum(sizes)
    pieces = [gathered[d * rows : (d + 1) * rows] for d in range(chips)]
    pieces = list(lax.optimization_barrier(tuple(pieces)))
    for bit in bits:
        onward = [d for d in range(2 * bit, chips) if d & (2 * bit - 1) == bit]
        if onward:
            block = jnp.concatenate([pieces[d] for d in onward], axis=0)
            block = across(block, "chan", 2 * bit)
            for i, d in enumerate(onward):
                pieces[d ^ bit] = pieces[d ^ bit] + block[i * rows : (i + 1) * rows]
    mine = pieces[0]
    for bit in bits[:-1]:
        mine = mine + across(pieces[bit], "chan", 2 * bit)
    mine = [mine[: sizes[0]], mine[sizes[0] :]]
    if bits:
        last = pieces[bits[-1]]
        for i, x in enumerate((last[: sizes[0]], last[sizes[0] :])):
            mine[i] = mine[i] + across(x, "chan", 2 * bits[-1])
    receivers = [blocks[0]]
    for d in range(1, times):
        receivers.append(across(blocks[d], "tm", d))
    receivers = [r.reshape(windows, part, 2 * NF) for r in receivers]
    sources = [mine]
    for d in range(1, times):
        both = []
        for x in mine:
            both.append(across(x, "tm", d))
        sources.append(both)

    factor = 1.0 / (windows * times)
    total = correlate(receivers[:1], sources[:1], None, pairs, factor)
    if times > 1:
        total = correlate(receivers[1:], sources[1:], total, pairs, factor)
    return total.transpose(1, 0, 2)


def solution(mesh):
    in_specs = (P(("seg", "chan"), "tm"), P("chan", None), P(), P(), P("chan", None))
    out_specs = P(("seg", "chan", "tm"), None, None)
    return jax.shard_map(shards, mesh=mesh, in_specs=in_specs, out_specs=out_specs, check_vma=False)
```

```python
import functools

import jax
import jax.numpy as jnp
import ml_dtypes
import numpy as np
from jax import lax
from jax.experimental import pallas as pl
from jax.experimental.pallas import tpu as pltpu
from jax.sharding import PartitionSpec as P


NFFT = 4096
NF = 512
F0 = 8
PIECE = NFFT // 8
HALF = NFFT // 2
CHUNK = 256
F32 = jnp.float32
BF16 = jnp.bfloat16
LIMIT = 24 * 1024 * 1024
HINT = 10**10


def piece_table():
    bins = F0 + np.arange(NF)
    angle = (bins * np.arange(PIECE)[:, None] % NFFT) * (2.0 * np.pi / NFFT)
    exact = np.concatenate([np.cos(angle), -np.sin(angle)], axis=1)
    high = exact.astype(ml_dtypes.bfloat16)
    low = (exact - high.astype(np.float64)).astype(ml_dtypes.bfloat16)
    return np.concatenate([high, low], axis=0)


def split_two(x):
    high = x.astype(BF16)
    low = (x - high.astype(F32)).astype(BF16)
    return high, low


def dot(a, b):
    return jnp.dot(a, b, preferred_element_type=F32)


def stacked_parts(x):
    high, low = split_two(x)
    high = high.astype(F32)
    return jnp.concatenate([high, low.astype(F32), high], axis=0)


def stacked_rows(table, rows, cols):
    first = table[:rows, cols]
    return jnp.concatenate([first, first, table[PIECE : PIECE + rows, cols]], axis=0)


class Turns:
    def __init__(self):
        lane = lax.broadcasted_iota(jnp.int32, (1, CHUNK), 1)
        turn = lane % 4
        self.odd = (turn % 2) == 1
        self.sign = jnp.where(self.odd, -1.0, 1.0)
        self.real = jnp.where(turn < 2, 1.0, -1.0)
        self.imag = jnp.where((turn == 0) | (turn == 3), 1.0, -1.0)
        eighth = lane % 8
        root = np.float32(np.sqrt(0.5))
        self.cos = jnp.where(turn % 4 == 0, 1.0, jnp.where(turn == 2, 0.0, root))
        self.cos = jnp.where((eighth > 2) & (eighth < 6), -self.cos, self.cos)
        self.sin = jnp.where(turn == 2, 1.0, jnp.where(turn == 0, 0.0, root))
        self.sin = jnp.where(eighth < 4, -self.sin, self.sin)

    def quarter(self, ar, ai, br, bi):
        return (
            ar + self.real * jnp.where(self.odd, bi, br),
            ai + self.imag * jnp.where(self.odd, br, bi),
        )

    def half(self, re, im):
        ar, ai = self.quarter(re[0], im[0], re[2], im[2])
        br, bi = self.quarter(re[1], im[1], re[3], im[3])
        return ar + (br * self.cos - bi * self.sin), ai + (br * self.sin + bi * self.cos)


def half_spectra(x, table, channels, halves, turns, f):
    re = slice(f, f + CHUNK)
    im = slice(NF + f, NF + f + CHUNK)
    both = jnp.concatenate([x, x], axis=1)
    dr = dot(both, table[:, re])
    di = dot(both, table[:, im])
    out = []
    for b in range(halves):
        rows = [slice((4 * b + e) * channels, (4 * b + e + 1) * channels) for e in range(4)]
        out.append(turns.half([dr[r] for r in rows], [di[r] for r in rows]))
    return out


def end_terms(taps_wide, shifted, tap_count, ends):
    lag = tap_count - 1
    apart = ends.T
    size = apart.shape[0]
    shifted[...] = jnp.zeros_like(shifted)
    shifted[:tap_count, :] = taps_wide
    total = jnp.zeros((lag, apart.shape[1]), F32)
    for j in range(1, tap_count):
        total = total + shifted[j : j + lag, :] * apart[size - j : size - j + 1, :]
    return stacked_parts(total).T.astype(BF16)


def whiten_rows(re, im):
    rows = re.shape[0]
    place = lax.broadcasted_iota(jnp.int32, (rows, NF), 1)
    power = re * re + im * im
    smooth = power
    for s in (1, 2):
        smooth = smooth + jnp.where(place >= s, pltpu.roll(power, s, 1), 0.0)
        smooth = smooth + jnp.where(place < NF - s, pltpu.roll(power, NF - s, 1), 0.0)
    total = jnp.sum(power, axis=1, keepdims=True)
    scaling = lax.rsqrt(smooth * 0.2 + (total * (0.1 / NF) + 1e-06))
    return (re * scaling).astype(BF16), (im * scaling).astype(BF16)


ROWS = 16


def whiten_all(spectra, white, count):
    def step(i, carry):
        rows = pl.ds(pl.multiple_of(i * ROWS, ROWS), ROWS)
        re, im = whiten_rows(spectra[rows, :NF], spectra[rows, NF:])
        white[rows, :NF] = re
        white[rows, NF:] = im
        return carry

    lax.fori_loop(0, count // ROWS, step, 0, unroll=2)


def tail_kernel(traces, wanted, tail, ids, sems):
    start = traces.shape[1] - tail.shape[1]
    copies = [
        pltpu.make_async_copy(traces.at[:, start:], tail, sems.at[0]),
        pltpu.make_async_copy(wanted, ids, sems.at[1]),
    ]
    for copy in copies:
        copy.start()
    for copy in copies:
        copy.wait()


def pair_kernel(mine, other, out):
    out[:1, :] = mine[...]
    out[1:, :] = other[...]


def own_chunk(windows, f, traces, table, lines, edge, part, response, last):
    channels, samples = traces.shape
    size = lines.shape[1] // 3
    lag = edge.shape[1] // 3
    pieces = samples // PIECE
    x = jnp.concatenate([traces[:, q * PIECE : (q + 1) * PIECE] for q in range(pieces)], axis=0)
    turns = Turns()
    re = slice(f, f + CHUNK)
    im = slice(NF + f, NF + f + CHUNK)
    pr = dot(lines[...], stacked_rows(table, size, re))
    pi = dot(lines[...], stacked_rows(table, size, im))
    response[:, :CHUNK] = pr
    response[:, CHUNK:] = pi
    halves = half_spectra(x, table, channels, windows, turns, f)
    for w in range(windows):
        xr, xi = halves[w]
        xr, xi = turns.sign * xr, turns.sign * xi
        if w > 0:
            xr, xi = xr + halves[w - 1][0], xi + halves[w - 1][1]
        yr = xr * pr - xi * pi
        yi = xr * pi + xi * pr
        if w < windows - 1:
            rows = slice(w * channels, (w + 1) * channels)
            part[rows, :CHUNK] = yr
            part[rows, CHUNK:] = yi
        else:
            last[:, :CHUNK] = yr + dot(edge[...], stacked_rows(table, lag, re))
            last[:, CHUNK:] = yi + dot(edge[...], stacked_rows(table, lag, im))


def first_kernel(
    windows, traces, taps, table, part, response, last, ends, edge, lines, square, shifted
):
    channels, samples = traces.shape
    tap_count = taps.shape[0]
    square[...] = jnp.zeros_like(square)
    high, low = split_two(taps[...])
    high = high.astype(F32)
    size = square.shape[0] // 3
    for i, value in enumerate((high, low.astype(F32), high)):
        square[i * size : i * size + tap_count, :channels] = value
    lines[...] = square[...].T[:channels].astype(BF16)
    tile = 128
    for b in range(1, windows):
        ends[:, (b - 1) * tile : b * tile] = traces[:, b * HALF - tile : b * HALF]
    start = (windows - 2) * HALF
    apart = traces[:, start - tile : start].astype(F32) - traces[:, samples - tile :].astype(F32)
    edge[...] = end_terms(taps[...], shifted, tap_count, apart)
    own_chunk(windows, 0, traces, table, lines, edge, part, response, last)


def second_kernel(
    windows, traces, table, lines, edge, first, part, response, white, second, spectra
):
    own_chunk(windows, CHUNK, traces, table, lines, edge, part, response, second)
    for i, half in enumerate((first, second)):
        spectra[:, i * CHUNK : (i + 1) * CHUNK] = half[:, :CHUNK]
        spectra[:, NF + i * CHUNK : NF + (i + 1) * CHUNK] = half[:, CHUNK:]
    whiten_all(spectra, white, white.shape[0])


def part_rows(windows, pairs):
    return [-(-w * pairs // 8) * 8 for w in (windows - 1, 1)]


def picks_kernel(shape, where, counts, slots, *refs):
    channels, windows, pairs, chips = shape
    wanted, picks, chosen = refs[:-2], refs[-2], refs[-1]
    group = where[0]
    first = jnp.int32(0)
    for g in range(counts.shape[0]):
        first = first + jnp.where(g < group, counts[g], 0)
    owned = counts[group]
    width = windows * channels
    lane = lax.broadcasted_iota(jnp.int32, (1, width), 1)
    columns = [jnp.where(lane // channels == w, lane % channels, -2) for w in range(windows)]
    sizes = part_rows(windows, pairs)
    per = wanted[0].shape[0]
    chosen[...] = jnp.zeros_like(chosen)
    for core in range(2):
        for d in range(chips):
            base = (core * chips + d) * sum(sizes)
            tail = base + sizes[0]
            for p in range(pairs):
                slot = wanted[2 * d // per][(2 * d + core) % per, p] - first
                mine = (slot >= 0) & (slot < owned)
                channel = slots[group, jnp.where(mine, slot, 0)]
                channel = jnp.where(mine, channel, -1)
                for w in range(windows):
                    row = (base + w * pairs if w < windows - 1 else tail) + p
                    chosen[row : row + 1, :] = (columns[w] == channel).astype(F32)
    picks[...] = chosen[...].astype(BF16)


def rest_kernel(
    windows, times, where, halo, ends, taps, table, part_a, part_b, response_a, response_b, *refs
):
    own_white, picks, keep, send = refs[:4]
    blocks = refs[4 : 4 + times]
    shifted, spectra, white = refs[4 + times :]
    channels = response_a.shape[0]
    tap_count = taps.shape[0]
    tile = halo.shape[1] - HALF
    rest = windows - 1

    before = [halo[:, :tile], halo[:, HALF:]]
    before += [ends[:, (b - 1) * tile : b * tile] for b in range(1, windows - 2)]
    after = [ends[:, w * tile : (w + 1) * tile] for w in range(rest)]
    apart = jnp.concatenate([b.astype(F32) - a.astype(F32) for b, a in zip(before, after)], axis=0)
    taps_wide = jnp.concatenate([taps[...]] * rest, axis=1)
    edge = end_terms(taps_wide, shifted, tap_count, apart)
    x = jnp.concatenate(
        [halo[:, tile + q * PIECE : tile + (q + 1) * PIECE] for q in range(HALF // PIECE)],
        axis=0,
    )
    turns = Turns()
    for f in range(0, NF, CHUNK):
        re = slice(f, f + CHUNK)
        im = slice(NF + f, NF + f + CHUNK)
        xr, xi = half_spectra(x, table, channels, 1, turns, f)[0]
        part, response = (part_b, response_b) if f else (part_a, response_a)
        pr, pi = response[:, :CHUNK], response[:, CHUNK:]
        er = dot(edge, stacked_rows(table, tap_count - 1, re))
        ei = dot(edge, stacked_rows(table, tap_count - 1, im))
        spectra[:channels, re] = part[:channels, :CHUNK] + er[:channels] + (xr * pr - xi * pi)
        spectra[:channels, im] = part[:channels, CHUNK:] + ei[:channels] + (xr * pi + xi * pr)
        spectra[channels:, re] = part[channels:, :CHUNK] + er[channels:]
        spectra[channels:, im] = part[channels:, CHUNK:] + ei[channels:]
    count = rest * channels
    whiten_all(spectra, white, count)
    white[count:, :] = own_white[...]
    base = keep.shape[0]
    size = channels // times
    choose = picks[...]
    for f in range(0, 2 * NF, CHUNK):
        cols = slice(f, f + CHUNK)
        out = dot(choose, white[:, cols]).astype(BF16)
        keep[:, cols] = out[:base]
        send[:, cols] = out[base:]
    for d in range(times):
        line = (where[1] ^ d) * size
        for w in range(windows):
            if size % ROWS == 0:
                at = pl.multiple_of(w * channels + line, ROWS)
                blocks[d][w * size : (w + 1) * size, :] = white[pl.ds(at, size), :]
            else:
                row = lax.broadcasted_iota(jnp.int32, (size, channels), 0)
                col = lax.broadcasted_iota(jnp.int32, (size, channels), 1)
                move = (col == row + line).astype(F32).astype(BF16)
                moved = dot(move, white[w * channels : (w + 1) * channels, :])
                blocks[d][w * size : (w + 1) * size, :] = moved.astype(BF16)


def correlate_kernel(windows, factor, count, *refs):
    receivers = refs[:count]
    sources = refs[count : 3 * count]
    last = len(refs) == 3 * count + 6
    total = refs[3 * count] if last else None
    out, line_r, line_s = refs[3 * count + last : 3 * count + last + 3]
    held, sems = refs[-2:] if last else (out, None)
    pairs, part = out.shape[0], out.shape[1]
    for d in range(count):
        for w in range(windows):
            at = d * windows + w
            line_r[at] = receivers[d][w].astype(F32) * factor
            if w < windows - 1:
                rows = sources[2 * d][w * pairs : (w + 1) * pairs, :].astype(F32)
            else:
                rows = sources[2 * d + 1][:pairs, :].astype(F32)
            for p in range(pairs):
                line_s[p, at : at + 1, :] = rows[p : p + 1, :]

    def copy(p):
        return pltpu.make_async_copy(held.at[p], out.at[p], sems.at[p])

    def one(p, carry):
        for f in range(0, NF, 128):
            re = slice(f, f + 128)
            im = slice(NF + f, NF + f + 128)
            if last:
                total_r, total_i = total[p, :, re], total[p, :, im]
            else:
                total_r = jnp.zeros((part, 128), F32)
                total_i = jnp.zeros((part, 128), F32)
            for at in range(count * windows):
                rr = line_r[at, :, re]
                ri = line_r[at, :, im]
                sr = line_s[p, at : at + 1, re]
                si = line_s[p, at : at + 1, im]
                total_r = total_r + (sr * rr + si * ri)
                total_i = total_i + (sr * ri - si * rr)
            held[p, :, re] = total_r
            held[p, :, im] = total_i
        if last:
            copy(p).start()
        return carry

    lax.fori_loop(0, pairs, one, 0)
    if last:
        for p in range(pairs):
            copy(p).wait()


def correlate(receivers, sources, total, pairs, factor):
    windows, part, width = receivers[0].shape
    count = len(receivers)
    vmem = pl.BlockSpec(memory_space=pltpu.VMEM)
    shape = (pairs, part, width)
    last = total is not None
    scratch = [
        pltpu.VMEM((count * windows, part, width), F32),
        pltpu.VMEM((pairs, -(-count * windows // 8) * 8, width), F32),
    ]
    if last:
        scratch += [pltpu.VMEM(shape, F32), pltpu.SemaphoreType.DMA((pairs,))]
    return pl.pallas_call(
        functools.partial(correlate_kernel, windows, factor, count),
        out_shape=jax.ShapeDtypeStruct(shape, F32),
        in_specs=[vmem] * (3 * count + last),
        out_specs=pl.BlockSpec(memory_space=pltpu.HBM) if last else vmem,
        scratch_shapes=scratch,
        compiler_params=pltpu.CompilerParams(vmem_limit_bytes=LIMIT),
        name="correlate",
    )(*receivers, *(part for both in sources for part in both), *([total] if last else []))


def shards(traces, filter_taps, source_counts, source_channel, block_sources):
    channels, samples = traces.shape
    tap_count = filter_taps.shape[1]
    pairs = block_sources.shape[1]
    windows = samples // HALF
    groups = lax.axis_size("chan")
    times = lax.axis_size("tm")
    chips = groups // 2
    part = channels // times
    sizes = part_rows(windows, pairs)
    rows_out = chips * sum(sizes)

    def across(x, axis, distance):
        size = lax.axis_size(axis)
        return lax.ppermute(x, axis, [(i, i ^ distance) for i in range(size)])

    smem = pl.BlockSpec(memory_space=pltpu.SMEM)
    vmem = pl.BlockSpec(memory_space=pltpu.VMEM)
    hbm = pl.BlockSpec(memory_space=pltpu.HBM)
    params = pltpu.CompilerParams(vmem_limit_bytes=LIMIT)
    bits = [1 << b for b in range(chips.bit_length() - 1)]

    other = across(block_sources, "chan", 1)
    tail, ids = pl.pallas_call(
        tail_kernel,
        out_shape=[
            jax.ShapeDtypeStruct((channels, HALF + 128), BF16),
            jax.ShapeDtypeStruct(block_sources.shape, jnp.int32),
        ],
        in_specs=[hbm] * 2,
        out_specs=[vmem] * 2,
        scratch_shapes=[pltpu.SemaphoreType.DMA((2,))],
        compiler_params=params,
        name="tail",
    )(*(pltpu.with_memory_space_constraint(a, pltpu.HBM) for a in (traces, block_sources)))
    taps = filter_taps.T
    traces, taps, table = (
        pltpu.with_memory_space_constraint(a, pltpu.VMEM)
        for a in (traces, taps, jnp.asarray(piece_table()))
    )
    wanted = [
        pl.pallas_call(
            pair_kernel,
            out_shape=jax.ShapeDtypeStruct((2, pairs), jnp.int32),
            in_specs=[vmem] * 2,
            out_specs=vmem,
            compiler_params=params,
            cost_estimate=pl.CostEstimate(flops=HINT, bytes_accessed=8 * pairs, transcendentals=0),
            name="pair",
        )(ids, other)
    ]
    tail, pair = lax.optimization_barrier((tail, wanted[0]))
    wanted = [pair]
    halo = lax.ppermute(tail, "tm", [(i - 1, i) for i in range(1, times)])
    for d in range(1, chips):
        wanted.append(across(pair, "chan", 2 * d))
    where = jnp.stack([lax.axis_index("chan"), lax.axis_index("tm")]).astype(jnp.int32)

    shape = (channels, windows, pairs, chips)
    width = windows * channels
    chunk_shapes = [
        jax.ShapeDtypeStruct((width - channels, 2 * CHUNK), F32),
        jax.ShapeDtypeStruct((channels, 2 * CHUNK), F32),
    ]
    size = -(-tap_count // 16) * 16
    part_a, response_a, last, ends, edge, lines = pl.pallas_call(
        functools.partial(first_kernel, windows),
        out_shape=chunk_shapes
        + [
            chunk_shapes[1],
            jax.ShapeDtypeStruct((channels, (windows - 1) * 128), BF16),
            jax.ShapeDtypeStruct((channels, 3 * (tap_count - 1)), BF16),
            jax.ShapeDtypeStruct((channels, 3 * size), BF16),
        ],
        in_specs=[vmem] * 3,
        out_specs=[vmem] * 6,
        scratch_shapes=[
            pltpu.VMEM((3 * size, 128), F32),
            pltpu.VMEM((2 * tap_count + 6, channels), F32),
        ],
        compiler_params=params,
        name="first",
    )(traces, taps, table)
    part_b, response_b, own_white = pl.pallas_call(
        functools.partial(second_kernel, windows),
        out_shape=chunk_shapes + [jax.ShapeDtypeStruct((channels, 2 * NF), BF16)],
        in_specs=[vmem] * 5,
        out_specs=[vmem] * 3,
        scratch_shapes=[
            pltpu.VMEM((channels, 2 * CHUNK), F32),
            pltpu.VMEM((channels, 2 * NF), F32),
        ],
        compiler_params=params,
        name="second",
    )(traces, table, lines, edge, last)
    picks = pl.pallas_call(
        functools.partial(picks_kernel, shape),
        out_shape=jax.ShapeDtypeStruct((2 * rows_out, width), BF16),
        in_specs=[smem] * (3 + len(wanted)),
        out_specs=vmem,
        scratch_shapes=[pltpu.VMEM((2 * rows_out, width), F32)],
        compiler_params=params,
        name="picks",
    )(where, source_counts, source_channel, *wanted)
    outs = pl.pallas_call(
        functools.partial(rest_kernel, windows, times),
        out_shape=[jax.ShapeDtypeStruct((rows_out, 2 * NF), BF16)] * 2
        + [jax.ShapeDtypeStruct((windows * part, 2 * NF), BF16)] * times,
        in_specs=[smem] + [vmem] * 10,
        out_specs=[vmem] * (2 + times),
        scratch_shapes=[
            pltpu.VMEM((2 * tap_count + 6, width - channels), F32),
            pltpu.VMEM((width - channels, 2 * NF), F32),
            pltpu.VMEM((width, 2 * NF), BF16),
        ],
        compiler_params=params,
        name="rest",
    )(
        where,
        halo,
        ends,
        taps,
        table,
        part_a,
        part_b,
        response_a,
        response_b,
        own_white,
        picks,
    )
    keep, send, blocks = outs[0], outs[1], outs[2:]
    gathered = keep + across(send, "chan", 1)
    rows = sum(sizes)
    pieces = [gathered[d * rows : (d + 1) * rows] for d in range(chips)]
    pieces = list(lax.optimization_barrier(tuple(pieces)))
    for bit in bits:
        onward = [d for d in range(2 * bit, chips) if d & (2 * bit - 1) == bit]
        if onward:
            block = jnp.concatenate([pieces[d] for d in onward], axis=0)
            block = across(block, "chan", 2 * bit)
            for i, d in enumerate(onward):
                pieces[d ^ bit] = pieces[d ^ bit] + block[i * rows : (i + 1) * rows]
    mine = pieces[0]
    for bit in bits[:-1]:
        mine = mine + across(pieces[bit], "chan", 2 * bit)
    mine = [mine[: sizes[0]], mine[sizes[0] :]]
    if bits:
        last = pieces[bits[-1]]
        for i, x in enumerate((last[: sizes[0]], last[sizes[0] :])):
            mine[i] = mine[i] + across(x, "chan", 2 * bits[-1])
    receivers = [blocks[0]]
    for d in range(1, times):
        receivers.append(across(blocks[d], "tm", d))
    receivers = [r.reshape(windows, part, 2 * NF) for r in receivers]
    sources = [mine]
    for d in range(1, times):
        both = []
        for x in mine:
            both.append(across(x, "tm", d))
        sources.append(both)

    factor = 1.0 / (windows * times)
    total = correlate(receivers[:1], sources[:1], None, pairs, factor)
    if times > 1:
        total = correlate(receivers[1:], sources[1:], total, pairs, factor)
    return total.transpose(1, 0, 2)


def solution(mesh):
    in_specs = (P(("seg", "chan"), "tm"), P("chan", None), P(), P(), P("chan", None))
    out_specs = P(("seg", "chan", "tm"), None, None)
    return jax.shard_map(shards, mesh=mesh, in_specs=in_specs, out_specs=out_specs, check_vma=False)
```

```python
import functools

import jax
import jax.numpy as jnp
import ml_dtypes
import numpy as np
from jax import lax
from jax.experimental import pallas as pl
from jax.experimental.pallas import tpu as pltpu
from jax.sharding import PartitionSpec as P


NFFT = 4096
NF = 512
F0 = 8
PIECE = NFFT // 8
HALF = NFFT // 2
CHUNK = 256
F32 = jnp.float32
BF16 = jnp.bfloat16
LIMIT = 24 * 1024 * 1024
HINT = 10**10


def piece_table():
    bins = F0 + np.arange(NF)
    angle = (bins * np.arange(PIECE)[:, None] % NFFT) * (2.0 * np.pi / NFFT)
    exact = np.concatenate([np.cos(angle), -np.sin(angle)], axis=1)
    high = exact.astype(ml_dtypes.bfloat16)
    low = (exact - high.astype(np.float64)).astype(ml_dtypes.bfloat16)
    return np.concatenate([high, low], axis=0)


def split_two(x):
    high = x.astype(BF16)
    low = (x - high.astype(F32)).astype(BF16)
    return high, low


def dot(a, b):
    return jnp.dot(a, b, preferred_element_type=F32)


def stacked_parts(x):
    high, low = split_two(x)
    high = high.astype(F32)
    return jnp.concatenate([high, low.astype(F32), high], axis=0)


def stacked_rows(table, rows, cols):
    first = table[:rows, cols]
    return jnp.concatenate([first, first, table[PIECE : PIECE + rows, cols]], axis=0)


class Turns:
    def __init__(self):
        lane = lax.broadcasted_iota(jnp.int32, (1, CHUNK), 1)
        turn = lane % 4
        self.odd = (turn % 2) == 1
        self.sign = jnp.where(self.odd, -1.0, 1.0)
        self.real = jnp.where(turn < 2, 1.0, -1.0)
        self.imag = jnp.where((turn == 0) | (turn == 3), 1.0, -1.0)
        eighth = lane % 8
        root = np.float32(np.sqrt(0.5))
        self.cos = jnp.where(turn % 4 == 0, 1.0, jnp.where(turn == 2, 0.0, root))
        self.cos = jnp.where((eighth > 2) & (eighth < 6), -self.cos, self.cos)
        self.sin = jnp.where(turn == 2, 1.0, jnp.where(turn == 0, 0.0, root))
        self.sin = jnp.where(eighth < 4, -self.sin, self.sin)

    def quarter(self, ar, ai, br, bi):
        return (
            ar + self.real * jnp.where(self.odd, bi, br),
            ai + self.imag * jnp.where(self.odd, br, bi),
        )

    def half(self, re, im):
        ar, ai = self.quarter(re[0], im[0], re[2], im[2])
        br, bi = self.quarter(re[1], im[1], re[3], im[3])
        return ar + (br * self.cos - bi * self.sin), ai + (br * self.sin + bi * self.cos)


def half_spectra(x, table, channels, halves, turns, f):
    re = slice(f, f + CHUNK)
    im = slice(NF + f, NF + f + CHUNK)
    both = jnp.concatenate([x, x], axis=1)
    dr = dot(both, table[:, re])
    di = dot(both, table[:, im])
    out = []
    for b in range(halves):
        rows = [slice((4 * b + e) * channels, (4 * b + e + 1) * channels) for e in range(4)]
        out.append(turns.half([dr[r] for r in rows], [di[r] for r in rows]))
    return out


def end_terms(taps_wide, shifted, tap_count, ends):
    lag = tap_count - 1
    apart = ends.T
    size = apart.shape[0]
    shifted[...] = jnp.zeros_like(shifted)
    shifted[:tap_count, :] = taps_wide
    total = jnp.zeros((lag, apart.shape[1]), F32)
    for j in range(1, tap_count):
        total = total + shifted[j : j + lag, :] * apart[size - j : size - j + 1, :]
    return stacked_parts(total).T.astype(BF16)


def whiten_rows(re, im):
    rows = re.shape[0]
    place = lax.broadcasted_iota(jnp.int32, (rows, NF), 1)
    power = re * re + im * im
    smooth = power
    for s in (1, 2):
        smooth = smooth + jnp.where(place >= s, pltpu.roll(power, s, 1), 0.0)
        smooth = smooth + jnp.where(place < NF - s, pltpu.roll(power, NF - s, 1), 0.0)
    total = jnp.sum(power, axis=1, keepdims=True)
    scaling = lax.rsqrt(smooth * 0.2 + (total * (0.1 / NF) + 1e-06))
    return (re * scaling).astype(BF16), (im * scaling).astype(BF16)


ROWS = 16


def whiten_all(spectra, white, count):
    def step(i, carry):
        rows = pl.ds(pl.multiple_of(i * ROWS, ROWS), ROWS)
        re, im = whiten_rows(spectra[rows, :NF], spectra[rows, NF:])
        white[rows, :NF] = re
        white[rows, NF:] = im
        return carry

    lax.fori_loop(0, count // ROWS, step, 0, unroll=2)


def tail_kernel(traces, wanted, tail, ids, sems):
    start = traces.shape[1] - tail.shape[1]
    copies = [
        pltpu.make_async_copy(traces.at[:, start:], tail, sems.at[0]),
        pltpu.make_async_copy(wanted, ids, sems.at[1]),
    ]
    for copy in copies:
        copy.start()
    for copy in copies:
        copy.wait()


def pair_kernel(mine, other, out):
    out[:1, :] = mine[...]
    out[1:, :] = other[...]


def own_chunk(windows, f, traces, table, lines, edge, part, response, last):
    channels, samples = traces.shape
    size = lines.shape[1] // 3
    lag = edge.shape[1] // 3
    pieces = samples // PIECE
    x = jnp.concatenate([traces[:, q * PIECE : (q + 1) * PIECE] for q in range(pieces)], axis=0)
    turns = Turns()
    re = slice(f, f + CHUNK)
    im = slice(NF + f, NF + f + CHUNK)
    pr = dot(lines[...], stacked_rows(table, size, re))
    pi = dot(lines[...], stacked_rows(table, size, im))
    response[:, :CHUNK] = pr
    response[:, CHUNK:] = pi
    halves = half_spectra(x, table, channels, windows, turns, f)
    for w in range(windows):
        xr, xi = halves[w]
        xr, xi = turns.sign * xr, turns.sign * xi
        if w > 0:
            xr, xi = xr + halves[w - 1][0], xi + halves[w - 1][1]
        yr = xr * pr - xi * pi
        yi = xr * pi + xi * pr
        if w < windows - 1:
            rows = slice(w * channels, (w + 1) * channels)
            part[rows, :CHUNK] = yr
            part[rows, CHUNK:] = yi
        else:
            last[:, :CHUNK] = yr + dot(edge[...], stacked_rows(table, lag, re))
            last[:, CHUNK:] = yi + dot(edge[...], stacked_rows(table, lag, im))


def first_kernel(
    windows, traces, taps, table, part, response, last, ends, edge, lines, square, shifted
):
    channels, samples = traces.shape
    tap_count = taps.shape[0]
    square[...] = jnp.zeros_like(square)
    high, low = split_two(taps[...])
    high = high.astype(F32)
    size = square.shape[0] // 3
    for i, value in enumerate((high, low.astype(F32), high)):
        square[i * size : i * size + tap_count, :channels] = value
    lines[...] = square[...].T[:channels].astype(BF16)
    tile = 128
    for b in range(1, windows):
        ends[:, (b - 1) * tile : b * tile] = traces[:, b * HALF - tile : b * HALF]
    start = (windows - 2) * HALF
    apart = traces[:, start - tile : start].astype(F32) - traces[:, samples - tile :].astype(F32)
    edge[...] = end_terms(taps[...], shifted, tap_count, apart)
    own_chunk(windows, 0, traces, table, lines, edge, part, response, last)


def second_kernel(
    windows, traces, table, lines, edge, first, part, response, white, second, spectra
):
    own_chunk(windows, CHUNK, traces, table, lines, edge, part, response, second)
    for i, half in enumerate((first, second)):
        spectra[:, i * CHUNK : (i + 1) * CHUNK] = half[:, :CHUNK]
        spectra[:, NF + i * CHUNK : NF + (i + 1) * CHUNK] = half[:, CHUNK:]
    whiten_all(spectra, white, white.shape[0])


def part_rows(windows, pairs):
    return [-(-w * pairs // 8) * 8 for w in (windows - 1, 1)]


def picks_kernel(shape, where, counts, slots, *refs):
    channels, windows, pairs, chips = shape
    wanted, (picks, chosen, lines) = refs[:-3], refs[-3:]
    group = where[0]
    first = jnp.int32(0)
    for g in range(counts.shape[0]):
        first = first + jnp.where(g < group, counts[g], 0)
    owned = counts[group]
    lines[...] = jnp.zeros_like(lines)
    at = 0
    for w in wanted:
        lines[at : at + w.shape[0], :pairs] = w[...]
        at += w.shape[0]
    slot = lines[...] - first
    channel = jnp.full(slot.shape, -1, jnp.int32)
    for s in range(slots.shape[1]):
        channel = jnp.where(slot == s, slots[group, s], channel)
    channel = jnp.where((slot >= 0) & (slot < owned), channel, -1)
    turned = channel.astype(F32).T
    width = windows * channels
    lane = lax.broadcasted_iota(jnp.int32, (1, width), 1)
    columns = [
        jnp.where(lane // channels == w, lane % channels, -2).astype(F32) for w in range(windows)
    ]
    sizes = part_rows(windows, pairs)
    chosen[...] = jnp.zeros_like(chosen)
    for core in range(2):
        for d in range(chips):
            base = (core * chips + d) * sum(sizes)
            one = turned[:pairs, 2 * d + core : 2 * d + core + 1]
            for w in range(windows):
                row = base + (w * pairs if w < windows - 1 else sizes[0])
                chosen[row : row + pairs, :] = (one == columns[w]).astype(F32)
    picks[...] = chosen[...].astype(BF16)


def rest_kernel(
    windows, times, where, halo, ends, taps, table, part_a, part_b, response_a, response_b, *refs
):
    own_white, picks, keep, send = refs[:4]
    blocks = refs[4 : 4 + times]
    shifted, spectra, white = refs[4 + times :]
    channels = response_a.shape[0]
    tap_count = taps.shape[0]
    tile = halo.shape[1] - HALF
    rest = windows - 1

    before = [halo[:, :tile], halo[:, HALF:]]
    before += [ends[:, (b - 1) * tile : b * tile] for b in range(1, windows - 2)]
    after = [ends[:, w * tile : (w + 1) * tile] for w in range(rest)]
    apart = jnp.concatenate([b.astype(F32) - a.astype(F32) for b, a in zip(before, after)], axis=0)
    taps_wide = jnp.concatenate([taps[...]] * rest, axis=1)
    edge = end_terms(taps_wide, shifted, tap_count, apart)
    x = jnp.concatenate(
        [halo[:, tile + q * PIECE : tile + (q + 1) * PIECE] for q in range(HALF // PIECE)],
        axis=0,
    )
    turns = Turns()
    for f in range(0, NF, CHUNK):
        re = slice(f, f + CHUNK)
        im = slice(NF + f, NF + f + CHUNK)
        xr, xi = half_spectra(x, table, channels, 1, turns, f)[0]
        part, response = (part_b, response_b) if f else (part_a, response_a)
        pr, pi = response[:, :CHUNK], response[:, CHUNK:]
        er = dot(edge, stacked_rows(table, tap_count - 1, re))
        ei = dot(edge, stacked_rows(table, tap_count - 1, im))
        spectra[:channels, re] = part[:channels, :CHUNK] + er[:channels] + (xr * pr - xi * pi)
        spectra[:channels, im] = part[:channels, CHUNK:] + ei[:channels] + (xr * pi + xi * pr)
        spectra[channels:, re] = part[channels:, :CHUNK] + er[channels:]
        spectra[channels:, im] = part[channels:, CHUNK:] + ei[channels:]
    count = rest * channels
    whiten_all(spectra, white, count)
    white[count:, :] = own_white[...]
    base = keep.shape[0]
    size = channels // times
    choose = picks[...]
    for f in range(0, 2 * NF, CHUNK):
        cols = slice(f, f + CHUNK)
        out = dot(choose, white[:, cols]).astype(BF16)
        keep[:, cols] = out[:base]
        send[:, cols] = out[base:]
    for d in range(times):
        line = (where[1] ^ d) * size
        for w in range(windows):
            if size % ROWS == 0:
                at = pl.multiple_of(w * channels + line, ROWS)
                blocks[d][w * size : (w + 1) * size, :] = white[pl.ds(at, size), :]
            else:
                row = lax.broadcasted_iota(jnp.int32, (size, channels), 0)
                col = lax.broadcasted_iota(jnp.int32, (size, channels), 1)
                move = (col == row + line).astype(F32).astype(BF16)
                moved = dot(move, white[w * channels : (w + 1) * channels, :])
                blocks[d][w * size : (w + 1) * size, :] = moved.astype(BF16)


def correlate_kernel(spans, pairs, factor, has_total, last, *refs):
    count = len(spans)
    receivers, sources = refs[:count], refs[count : 2 * count]
    total = refs[2 * count] if has_total else None
    out, line_r, line_s = refs[2 * count + has_total : 2 * count + has_total + 3]
    held, sems = refs[-2:] if last else (out, None)
    part = out.shape[1]
    windows = 0
    for receiver, source, span in zip(receivers, sources, spans):
        for i, w in enumerate(span):
            line_r[windows] = receiver[w].astype(F32) * factor
            rows = source[i * pairs : (i + 1) * pairs, :].astype(F32)
            for p in range(pairs):
                line_s[p, windows : windows + 1, :] = rows[p : p + 1, :]
            windows += 1

    def copy(p):
        return pltpu.make_async_copy(held.at[p], out.at[p], sems.at[p])

    def one(p, carry):
        for f in range(0, NF, 128):
            re = slice(f, f + 128)
            im = slice(NF + f, NF + f + 128)
            if has_total:
                total_r, total_i = total[p, :, re], total[p, :, im]
            else:
                total_r = jnp.zeros((part, 128), F32)
                total_i = jnp.zeros((part, 128), F32)
            for at in range(windows):
                rr = line_r[at, :, re]
                ri = line_r[at, :, im]
                sr = line_s[p, at : at + 1, re]
                si = line_s[p, at : at + 1, im]
                total_r = total_r + (sr * rr + si * ri)
                total_i = total_i + (sr * ri - si * rr)
            held[p, :, re] = total_r
            held[p, :, im] = total_i
        if last:
            copy(p).start()
        return carry

    lax.fori_loop(0, pairs, one, 0)
    if last:
        for p in range(pairs):
            copy(p).wait()


def correlate(receivers, sources, spans, total, pairs, factor, last):
    _, part, width = receivers[0].shape
    windows = sum(len(span) for span in spans)
    vmem = pl.BlockSpec(memory_space=pltpu.VMEM)
    shape = (pairs, part, width)
    extra = [] if total is None else [total]
    scratch = [
        pltpu.VMEM((windows, part, width), F32),
        pltpu.VMEM((pairs, -(-windows // 8) * 8, width), F32),
    ]
    if last:
        scratch += [pltpu.VMEM(shape, F32), pltpu.SemaphoreType.DMA((pairs,))]
    return pl.pallas_call(
        functools.partial(correlate_kernel, spans, pairs, factor, len(extra), last),
        out_shape=jax.ShapeDtypeStruct(shape, F32),
        in_specs=[vmem] * (2 * len(spans) + len(extra)),
        out_specs=pl.BlockSpec(memory_space=pltpu.HBM) if last else vmem,
        scratch_shapes=scratch,
        compiler_params=pltpu.CompilerParams(vmem_limit_bytes=LIMIT),
        name="correlate",
    )(*receivers, *sources, *extra)


def shards(traces, filter_taps, source_counts, source_channel, block_sources):
    channels, samples = traces.shape
    tap_count = filter_taps.shape[1]
    pairs = block_sources.shape[1]
    windows = samples // HALF
    groups = lax.axis_size("chan")
    times = lax.axis_size("tm")
    chips = groups // 2
    part = channels // times
    sizes = part_rows(windows, pairs)
    rows_out = chips * sum(sizes)

    def across(x, axis, distance):
        size = lax.axis_size(axis)
        return lax.ppermute(x, axis, [(i, i ^ distance) for i in range(size)])

    smem = pl.BlockSpec(memory_space=pltpu.SMEM)
    vmem = pl.BlockSpec(memory_space=pltpu.VMEM)
    hbm = pl.BlockSpec(memory_space=pltpu.HBM)
    params = pltpu.CompilerParams(vmem_limit_bytes=LIMIT)
    bits = [1 << b for b in range(chips.bit_length() - 1)]

    other = across(block_sources, "chan", 1)
    tail, ids = pl.pallas_call(
        tail_kernel,
        out_shape=[
            jax.ShapeDtypeStruct((channels, HALF + 128), BF16),
            jax.ShapeDtypeStruct(block_sources.shape, jnp.int32),
        ],
        in_specs=[hbm] * 2,
        out_specs=[vmem] * 2,
        scratch_shapes=[pltpu.SemaphoreType.DMA((2,))],
        compiler_params=params,
        name="tail",
    )(*(pltpu.with_memory_space_constraint(a, pltpu.HBM) for a in (traces, block_sources)))
    taps = filter_taps.T
    traces, taps, table = (
        pltpu.with_memory_space_constraint(a, pltpu.VMEM)
        for a in (traces, taps, jnp.asarray(piece_table()))
    )
    wanted = [
        pl.pallas_call(
            pair_kernel,
            out_shape=jax.ShapeDtypeStruct((2, pairs), jnp.int32),
            in_specs=[vmem] * 2,
            out_specs=vmem,
            compiler_params=params,
            cost_estimate=pl.CostEstimate(flops=HINT, bytes_accessed=8 * pairs, transcendentals=0),
            name="pair",
        )(ids, other)
    ]
    tail, pair = lax.optimization_barrier((tail, wanted[0]))
    wanted = [pair]
    halo = lax.ppermute(tail, "tm", [(i - 1, i) for i in range(1, times)])
    for bit in bits:
        known = jnp.concatenate(wanted, axis=0)
        wanted = [known, across(known, "chan", 2 * bit)]
    where = jnp.stack([lax.axis_index("chan"), lax.axis_index("tm")]).astype(jnp.int32)

    shape = (channels, windows, pairs, chips)
    width = windows * channels
    chunk_shapes = [
        jax.ShapeDtypeStruct((width - channels, 2 * CHUNK), F32),
        jax.ShapeDtypeStruct((channels, 2 * CHUNK), F32),
    ]
    size = -(-tap_count // 16) * 16
    part_a, response_a, last, ends, edge, lines = pl.pallas_call(
        functools.partial(first_kernel, windows),
        out_shape=chunk_shapes
        + [
            chunk_shapes[1],
            jax.ShapeDtypeStruct((channels, (windows - 1) * 128), BF16),
            jax.ShapeDtypeStruct((channels, 3 * (tap_count - 1)), BF16),
            jax.ShapeDtypeStruct((channels, 3 * size), BF16),
        ],
        in_specs=[vmem] * 3,
        out_specs=[vmem] * 6,
        scratch_shapes=[
            pltpu.VMEM((3 * size, 128), F32),
            pltpu.VMEM((2 * tap_count + 6, channels), F32),
        ],
        compiler_params=params,
        name="first",
    )(traces, taps, table)
    part_b, response_b, own_white = pl.pallas_call(
        functools.partial(second_kernel, windows),
        out_shape=chunk_shapes + [jax.ShapeDtypeStruct((channels, 2 * NF), BF16)],
        in_specs=[vmem] * 5,
        out_specs=[vmem] * 3,
        scratch_shapes=[
            pltpu.VMEM((channels, 2 * CHUNK), F32),
            pltpu.VMEM((channels, 2 * NF), F32),
        ],
        compiler_params=params,
        name="second",
    )(traces, table, lines, edge, last)
    picks = pl.pallas_call(
        functools.partial(picks_kernel, shape),
        out_shape=jax.ShapeDtypeStruct((2 * rows_out, width), BF16),
        in_specs=[smem] * 3 + [vmem] * len(wanted),
        out_specs=vmem,
        scratch_shapes=[
            pltpu.VMEM((2 * rows_out, width), F32),
            pltpu.VMEM((2 * chips, 128), jnp.int32),
        ],
        compiler_params=params,
        name="picks",
    )(where, source_counts, source_channel, *wanted)
    outs = pl.pallas_call(
        functools.partial(rest_kernel, windows, times),
        out_shape=[jax.ShapeDtypeStruct((rows_out, 2 * NF), BF16)] * 2
        + [jax.ShapeDtypeStruct((windows * part, 2 * NF), BF16)] * times,
        in_specs=[smem] + [vmem] * 10,
        out_specs=[vmem] * (2 + times),
        scratch_shapes=[
            pltpu.VMEM((2 * tap_count + 6, width - channels), F32),
            pltpu.VMEM((width - channels, 2 * NF), F32),
            pltpu.VMEM((width, 2 * NF), BF16),
        ],
        compiler_params=params,
        name="rest",
    )(
        where,
        halo,
        ends,
        taps,
        table,
        part_a,
        part_b,
        response_a,
        response_b,
        own_white,
        picks,
    )
    keep, send, blocks = outs[0], outs[1], outs[2:]
    gathered = keep + across(send, "chan", 1)
    rows = sum(sizes)
    pieces = [gathered[d * rows : (d + 1) * rows] for d in range(chips)]
    pieces = list(lax.optimization_barrier(tuple(pieces)))
    for bit in bits:
        onward = [d for d in range(2 * bit, chips) if d & (2 * bit - 1) == bit]
        if onward:
            block = jnp.concatenate([pieces[d] for d in onward], axis=0)
            block = across(block, "chan", 2 * bit)
            for i, d in enumerate(onward):
                pieces[d ^ bit] = pieces[d ^ bit] + block[i * rows : (i + 1) * rows]
    mine = pieces[0]
    for bit in bits[:-1]:
        mine = mine + across(pieces[bit], "chan", 2 * bit)
    mine = [mine[: sizes[0]], mine[sizes[0] :]]
    if bits:
        last = pieces[bits[-1]]
        for i, x in enumerate((last[: sizes[0]], last[sizes[0] :])):
            mine[i] = mine[i] + across(x, "chan", 2 * bits[-1])
    receivers = [blocks[0]]
    for d in range(1, times):
        receivers.append(across(blocks[d], "tm", d))
    receivers = [r.reshape(windows, part, 2 * NF) for r in receivers]
    sources = [mine]
    for d in range(1, times):
        both = []
        for x in mine:
            both.append(across(x, "tm", d))
        sources.append(both)

    factor = 1.0 / (windows * times)
    early, late = list(range(windows - 1)), [windows - 1]
    total = correlate(
        receivers[:1] * 2, sources[0], (early, late), None, pairs, factor, times == 1
    )
    if times > 1:
        for i, span in enumerate((early, late)):
            total = correlate(
                receivers[1:],
                [both[i] for both in sources[1:]],
                (span,) * (times - 1),
                total,
                pairs,
                factor,
                i == 1,
            )
    return total.transpose(1, 0, 2)


def solution(mesh):
    in_specs = (P(("seg", "chan"), "tm"), P("chan", None), P(), P(), P("chan", None))
    out_specs = P(("seg", "chan", "tm"), None, None)
    return jax.shard_map(shards, mesh=mesh, in_specs=in_specs, out_specs=out_specs, check_vma=False)
```

```python
import functools

import jax
import jax.numpy as jnp
import ml_dtypes
import numpy as np
from jax import lax
from jax.experimental import pallas as pl
from jax.experimental.pallas import tpu as pltpu
from jax.sharding import PartitionSpec as P


NFFT = 4096
NF = 512
F0 = 8
PIECE = NFFT // 8
HALF = NFFT // 2
CHUNK = 256
F32 = jnp.float32
BF16 = jnp.bfloat16
LIMIT = 24 * 1024 * 1024
HINT = 10**10


def piece_table():
    bins = F0 + np.arange(NF)
    angle = (bins * np.arange(PIECE)[:, None] % NFFT) * (2.0 * np.pi / NFFT)
    exact = np.concatenate([np.cos(angle), -np.sin(angle)], axis=1)
    high = exact.astype(ml_dtypes.bfloat16)
    low = (exact - high.astype(np.float64)).astype(ml_dtypes.bfloat16)
    return np.concatenate([high, low], axis=0)


def split_two(x):
    high = x.astype(BF16)
    low = (x - high.astype(F32)).astype(BF16)
    return high, low


def dot(a, b):
    return jnp.dot(a, b, preferred_element_type=F32)


def stacked_parts(x):
    high, low = split_two(x)
    high = high.astype(F32)
    return jnp.concatenate([high, low.astype(F32), high], axis=0)


def stacked_rows(table, rows, cols):
    first = table[:rows, cols]
    return jnp.concatenate([first, first, table[PIECE : PIECE + rows, cols]], axis=0)


class Turns:
    def __init__(self):
        lane = lax.broadcasted_iota(jnp.int32, (1, CHUNK), 1)
        turn = lane % 4
        self.odd = (turn % 2) == 1
        self.sign = jnp.where(self.odd, -1.0, 1.0)
        self.real = jnp.where(turn < 2, 1.0, -1.0)
        self.imag = jnp.where((turn == 0) | (turn == 3), 1.0, -1.0)
        eighth = lane % 8
        root = np.float32(np.sqrt(0.5))
        self.cos = jnp.where(turn % 4 == 0, 1.0, jnp.where(turn == 2, 0.0, root))
        self.cos = jnp.where((eighth > 2) & (eighth < 6), -self.cos, self.cos)
        self.sin = jnp.where(turn == 2, 1.0, jnp.where(turn == 0, 0.0, root))
        self.sin = jnp.where(eighth < 4, -self.sin, self.sin)

    def quarter(self, ar, ai, br, bi):
        return (
            ar + self.real * jnp.where(self.odd, bi, br),
            ai + self.imag * jnp.where(self.odd, br, bi),
        )

    def half(self, re, im):
        ar, ai = self.quarter(re[0], im[0], re[2], im[2])
        br, bi = self.quarter(re[1], im[1], re[3], im[3])
        return ar + (br * self.cos - bi * self.sin), ai + (br * self.sin + bi * self.cos)


def half_spectra(x, table, channels, halves, turns, f):
    re = slice(f, f + CHUNK)
    im = slice(NF + f, NF + f + CHUNK)
    both = jnp.concatenate([x, x], axis=1)
    dr = dot(both, table[:, re])
    di = dot(both, table[:, im])
    out = []
    for b in range(halves):
        rows = [slice((4 * b + e) * channels, (4 * b + e + 1) * channels) for e in range(4)]
        out.append(turns.half([dr[r] for r in rows], [di[r] for r in rows]))
    return out


def end_terms(taps_wide, shifted, tap_count, ends):
    lag = tap_count - 1
    apart = ends.T
    size = apart.shape[0]
    shifted[...] = jnp.zeros_like(shifted)
    shifted[:tap_count, :] = taps_wide
    total = jnp.zeros((lag, apart.shape[1]), F32)
    for j in range(1, tap_count):
        total = total + shifted[j : j + lag, :] * apart[size - j : size - j + 1, :]
    return stacked_parts(total).T.astype(BF16)


def whiten_rows(re, im):
    rows = re.shape[0]
    place = lax.broadcasted_iota(jnp.int32, (rows, NF), 1)
    power = re * re + im * im
    smooth = power
    for s in (1, 2):
        smooth = smooth + jnp.where(place >= s, pltpu.roll(power, s, 1), 0.0)
        smooth = smooth + jnp.where(place < NF - s, pltpu.roll(power, NF - s, 1), 0.0)
    total = jnp.sum(power, axis=1, keepdims=True)
    scaling = lax.rsqrt(smooth * 0.2 + (total * (0.1 / NF) + 1e-06))
    return (re * scaling).astype(BF16), (im * scaling).astype(BF16)


ROWS = 16


def whiten_all(spectra, white, count):
    def step(i, carry):
        rows = pl.ds(pl.multiple_of(i * ROWS, ROWS), ROWS)
        re, im = whiten_rows(spectra[rows, :NF], spectra[rows, NF:])
        white[rows, :NF] = re
        white[rows, NF:] = im
        return carry

    lax.fori_loop(0, count // ROWS, step, 0, unroll=4)


def tail_kernel(traces, wanted, tail, ids, sems):
    start = traces.shape[1] - tail.shape[1]
    copies = [
        pltpu.make_async_copy(traces.at[:, start:], tail, sems.at[0]),
        pltpu.make_async_copy(wanted, ids, sems.at[1]),
    ]
    for copy in copies:
        copy.start()
    for copy in copies:
        copy.wait()


def pair_kernel(mine, other, out):
    out[:1, :] = mine[...]
    out[1:, :] = other[...]


def own_chunk(windows, f, traces, table, lines, edge, part, response, last):
    channels, samples = traces.shape
    size = lines.shape[1] // 3
    lag = edge.shape[1] // 3
    pieces = samples // PIECE
    x = jnp.concatenate([traces[:, q * PIECE : (q + 1) * PIECE] for q in range(pieces)], axis=0)
    turns = Turns()
    re = slice(f, f + CHUNK)
    im = slice(NF + f, NF + f + CHUNK)
    pr = dot(lines[...], stacked_rows(table, size, re))
    pi = dot(lines[...], stacked_rows(table, size, im))
    response[:, :CHUNK] = pr
    response[:, CHUNK:] = pi
    halves = half_spectra(x, table, channels, windows, turns, f)
    for w in range(windows):
        xr, xi = halves[w]
        xr, xi = turns.sign * xr, turns.sign * xi
        if w > 0:
            xr, xi = xr + halves[w - 1][0], xi + halves[w - 1][1]
        yr = xr * pr - xi * pi
        yi = xr * pi + xi * pr
        if w < windows - 1:
            rows = slice(w * channels, (w + 1) * channels)
            part[rows, :CHUNK] = yr
            part[rows, CHUNK:] = yi
        else:
            last[:, :CHUNK] = yr + dot(edge[...], stacked_rows(table, lag, re))
            last[:, CHUNK:] = yi + dot(edge[...], stacked_rows(table, lag, im))


def first_kernel(
    windows, traces, taps, table, part, response, last, ends, edge, lines, square, shifted
):
    channels, samples = traces.shape
    tap_count = taps.shape[0]
    square[...] = jnp.zeros_like(square)
    high, low = split_two(taps[...])
    high = high.astype(F32)
    size = square.shape[0] // 3
    for i, value in enumerate((high, low.astype(F32), high)):
        square[i * size : i * size + tap_count, :channels] = value
    lines[...] = square[...].T[:channels].astype(BF16)
    tile = 128
    for b in range(1, windows):
        ends[:, (b - 1) * tile : b * tile] = traces[:, b * HALF - tile : b * HALF]
    start = (windows - 2) * HALF
    apart = traces[:, start - tile : start].astype(F32) - traces[:, samples - tile :].astype(F32)
    edge[...] = end_terms(taps[...], shifted, tap_count, apart)
    own_chunk(windows, 0, traces, table, lines, edge, part, response, last)


def second_kernel(
    windows, traces, table, lines, edge, first, part, response, white, second, spectra
):
    own_chunk(windows, CHUNK, traces, table, lines, edge, part, response, second)
    for i, half in enumerate((first, second)):
        spectra[:, i * CHUNK : (i + 1) * CHUNK] = half[:, :CHUNK]
        spectra[:, NF + i * CHUNK : NF + (i + 1) * CHUNK] = half[:, CHUNK:]
    whiten_all(spectra, white, white.shape[0])


def part_rows(windows, pairs):
    return [-(-w * pairs // 8) * 8 for w in (windows - 1, 1)]


def picks_kernel(shape, counts, slots, *refs):
    channels, windows, pairs, chips = shape
    wanted, (picks, chosen, lines) = refs[:-3], refs[-3:]
    group = lax.axis_index("chan")
    place = lax.broadcasted_iota(jnp.int32, counts.shape, 1)
    held = counts[...].astype(F32)
    first = jnp.sum(jnp.where(place < group, held, 0.0), axis=1, keepdims=True)
    owned = jnp.sum(jnp.where(place == group, held, 0.0), axis=1, keepdims=True)
    row = lax.broadcasted_iota(jnp.int32, slots.shape, 0)
    own_slots = jnp.where(row == group, slots[...], 0).astype(F32)
    own_slots = jnp.sum(own_slots, axis=0, keepdims=True)
    lines[...] = jnp.zeros_like(lines)
    at = 0
    for w in wanted:
        lines[at : at + w.shape[0], :pairs] = w[...].astype(F32)
        at += w.shape[0]
    slot = lines[...] - first
    channel = jnp.full(slot.shape, -1.0, F32)
    for s in range(slots.shape[1]):
        channel = jnp.where(slot == s, own_slots[:, s : s + 1], channel)
    channel = jnp.where((slot >= 0) & (slot < owned), channel, -1.0)
    turned = channel.T
    width = windows * channels
    lane = lax.broadcasted_iota(jnp.int32, (1, width), 1)
    columns = [
        jnp.where(lane // channels == w, lane % channels, -2).astype(F32) for w in range(windows)
    ]
    sizes = part_rows(windows, pairs)
    chosen[...] = jnp.zeros_like(chosen)
    for core in range(2):
        for d in range(chips):
            base = (core * chips + d) * sum(sizes)
            one = turned[:pairs, 2 * d + core : 2 * d + core + 1]
            for w in range(windows):
                row = base + (w * pairs if w < windows - 1 else sizes[0])
                chosen[row : row + pairs, :] = (one == columns[w]).astype(F32)
    picks[...] = chosen[...].astype(BF16)


def rest_kernel(
    windows, times, halo, ends, taps, table, part_a, part_b, response_a, response_b, *refs
):
    own_white, picks, keep, send = refs[:4]
    blocks = refs[4 : 4 + times]
    shifted, spectra, white = refs[4 + times :]
    channels = response_a.shape[0]
    tap_count = taps.shape[0]
    tile = halo.shape[1] - HALF
    rest = windows - 1

    before = [halo[:, :tile], halo[:, HALF:]]
    before += [ends[:, (b - 1) * tile : b * tile] for b in range(1, windows - 2)]
    after = [ends[:, w * tile : (w + 1) * tile] for w in range(rest)]
    apart = jnp.concatenate([b.astype(F32) - a.astype(F32) for b, a in zip(before, after)], axis=0)
    taps_wide = jnp.concatenate([taps[...]] * rest, axis=1)
    edge = end_terms(taps_wide, shifted, tap_count, apart)
    x = jnp.concatenate(
        [halo[:, tile + q * PIECE : tile + (q + 1) * PIECE] for q in range(HALF // PIECE)],
        axis=0,
    )
    turns = Turns()
    for f in range(0, NF, CHUNK):
        re = slice(f, f + CHUNK)
        im = slice(NF + f, NF + f + CHUNK)
        xr, xi = half_spectra(x, table, channels, 1, turns, f)[0]
        part, response = (part_b, response_b) if f else (part_a, response_a)
        pr, pi = response[:, :CHUNK], response[:, CHUNK:]
        er = dot(edge, stacked_rows(table, tap_count - 1, re))
        ei = dot(edge, stacked_rows(table, tap_count - 1, im))
        spectra[:channels, re] = part[:channels, :CHUNK] + er[:channels] + (xr * pr - xi * pi)
        spectra[:channels, im] = part[:channels, CHUNK:] + ei[:channels] + (xr * pi + xi * pr)
        spectra[channels:, re] = part[channels:, :CHUNK] + er[channels:]
        spectra[channels:, im] = part[channels:, CHUNK:] + ei[channels:]
    count = rest * channels
    whiten_all(spectra, white, count)
    white[count:, :] = own_white[...]
    base = keep.shape[0]
    size = channels // times
    choose = picks[...]
    for f in range(0, 2 * NF, CHUNK):
        cols = slice(f, f + CHUNK)
        out = dot(choose, white[:, cols]).astype(BF16)
        keep[:, cols] = out[:base]
        send[:, cols] = out[base:]
    for d in range(times):
        line = (lax.axis_index("tm") ^ d) * size
        for w in range(windows):
            if size % ROWS == 0:
                at = pl.multiple_of(w * channels + line, ROWS)
                blocks[d][w * size : (w + 1) * size, :] = white[pl.ds(at, size), :]
            else:
                row = lax.broadcasted_iota(jnp.int32, (size, channels), 0)
                col = lax.broadcasted_iota(jnp.int32, (size, channels), 1)
                move = (col == row + line).astype(F32).astype(BF16)
                moved = dot(move, white[w * channels : (w + 1) * channels, :])
                blocks[d][w * size : (w + 1) * size, :] = moved.astype(BF16)


def correlate_kernel(spans, pairs, factor, has_total, last, *refs):
    count = len(spans)
    receivers, sources = refs[:count], refs[count : 2 * count]
    total = refs[2 * count] if has_total else None
    out, line_r, line_s = refs[2 * count + has_total : 2 * count + has_total + 3]
    held, sems = refs[-2:] if last else (out, None)
    part = out.shape[1]
    windows = 0
    for receiver, source, span in zip(receivers, sources, spans):
        for i, w in enumerate(span):
            line_r[windows] = receiver[w].astype(F32) * factor
            rows = source[i * pairs : (i + 1) * pairs, :].astype(F32)
            for p in range(pairs):
                line_s[p, windows : windows + 1, :] = rows[p : p + 1, :]
            windows += 1

    def copy(p):
        return pltpu.make_async_copy(held.at[p], out.at[p], sems.at[p])

    def one(p, carry):
        for f in range(0, NF, 128):
            re = slice(f, f + 128)
            im = slice(NF + f, NF + f + 128)
            if has_total:
                total_r, total_i = total[p, :, re], total[p, :, im]
            else:
                total_r = jnp.zeros((part, 128), F32)
                total_i = jnp.zeros((part, 128), F32)
            for at in range(windows):
                rr = line_r[at, :, re]
                ri = line_r[at, :, im]
                sr = line_s[p, at : at + 1, re]
                si = line_s[p, at : at + 1, im]
                total_r = total_r + (sr * rr + si * ri)
                total_i = total_i + (sr * ri - si * rr)
            held[p, :, re] = total_r
            held[p, :, im] = total_i
        if last:
            copy(p).start()
        return carry

    lax.fori_loop(0, pairs, one, 0)
    if last:
        for p in range(pairs):
            copy(p).wait()


def correlate(receivers, sources, spans, total, pairs, factor, last):
    _, part, width = receivers[0].shape
    windows = sum(len(span) for span in spans)
    vmem = pl.BlockSpec(memory_space=pltpu.VMEM)
    shape = (pairs, part, width)
    extra = [] if total is None else [total]
    scratch = [
        pltpu.VMEM((windows, part, width), F32),
        pltpu.VMEM((pairs, -(-windows // 8) * 8, width), F32),
    ]
    if last:
        scratch += [pltpu.VMEM(shape, F32), pltpu.SemaphoreType.DMA((pairs,))]
    return pl.pallas_call(
        functools.partial(correlate_kernel, spans, pairs, factor, len(extra), last),
        out_shape=jax.ShapeDtypeStruct(shape, F32),
        in_specs=[vmem] * (2 * len(spans) + len(extra)),
        out_specs=pl.BlockSpec(memory_space=pltpu.HBM) if last else vmem,
        scratch_shapes=scratch,
        compiler_params=pltpu.CompilerParams(vmem_limit_bytes=LIMIT),
        name="correlate",
    )(*receivers, *sources, *extra)


def shards(traces, filter_taps, source_counts, source_channel, block_sources):
    channels, samples = traces.shape
    tap_count = filter_taps.shape[1]
    pairs = block_sources.shape[1]
    windows = samples // HALF
    groups = lax.axis_size("chan")
    times = lax.axis_size("tm")
    chips = groups // 2
    part = channels // times
    sizes = part_rows(windows, pairs)
    rows_out = chips * sum(sizes)

    def across(x, axis, distance):
        size = lax.axis_size(axis)
        return lax.ppermute(x, axis, [(i, i ^ distance) for i in range(size)])

    vmem = pl.BlockSpec(memory_space=pltpu.VMEM)
    hbm = pl.BlockSpec(memory_space=pltpu.HBM)
    params = pltpu.CompilerParams(vmem_limit_bytes=LIMIT)
    bits = [1 << b for b in range(chips.bit_length() - 1)]

    other = across(block_sources, "chan", 1)
    tail, ids = pl.pallas_call(
        tail_kernel,
        out_shape=[
            jax.ShapeDtypeStruct((channels, HALF + 128), BF16),
            jax.ShapeDtypeStruct(block_sources.shape, jnp.int32),
        ],
        in_specs=[hbm] * 2,
        out_specs=[vmem] * 2,
        scratch_shapes=[pltpu.SemaphoreType.DMA((2,))],
        compiler_params=params,
        name="tail",
    )(*(pltpu.with_memory_space_constraint(a, pltpu.HBM) for a in (traces, block_sources)))
    taps = filter_taps.T
    traces, taps, table = (
        pltpu.with_memory_space_constraint(a, pltpu.VMEM)
        for a in (traces, taps, jnp.asarray(piece_table()))
    )
    wanted = [
        pl.pallas_call(
            pair_kernel,
            out_shape=jax.ShapeDtypeStruct((2, pairs), jnp.int32),
            in_specs=[vmem] * 2,
            out_specs=vmem,
            compiler_params=params,
            cost_estimate=pl.CostEstimate(flops=HINT, bytes_accessed=8 * pairs, transcendentals=0),
            name="pair",
        )(ids, other)
    ]
    tail, pair = lax.optimization_barrier((tail, wanted[0]))
    wanted = [pair]
    halo = lax.ppermute(tail, "tm", [(i - 1, i) for i in range(1, times)])
    for bit in bits:
        known = jnp.concatenate(wanted, axis=0)
        wanted = [known, across(known, "chan", 2 * bit)]

    shape = (channels, windows, pairs, chips)
    width = windows * channels
    chunk_shapes = [
        jax.ShapeDtypeStruct((width - channels, 2 * CHUNK), F32),
        jax.ShapeDtypeStruct((channels, 2 * CHUNK), F32),
    ]
    size = -(-tap_count // 16) * 16
    part_a, response_a, last, ends, edge, lines = pl.pallas_call(
        functools.partial(first_kernel, windows),
        out_shape=chunk_shapes
        + [
            chunk_shapes[1],
            jax.ShapeDtypeStruct((channels, (windows - 1) * 128), BF16),
            jax.ShapeDtypeStruct((channels, 3 * (tap_count - 1)), BF16),
            jax.ShapeDtypeStruct((channels, 3 * size), BF16),
        ],
        in_specs=[vmem] * 3,
        out_specs=[vmem] * 6,
        scratch_shapes=[
            pltpu.VMEM((3 * size, 128), F32),
            pltpu.VMEM((2 * tap_count + 6, channels), F32),
        ],
        compiler_params=params,
        name="first",
    )(traces, taps, table)
    part_b, response_b, own_white = pl.pallas_call(
        functools.partial(second_kernel, windows),
        out_shape=chunk_shapes + [jax.ShapeDtypeStruct((channels, 2 * NF), BF16)],
        in_specs=[vmem] * 5,
        out_specs=[vmem] * 3,
        scratch_shapes=[
            pltpu.VMEM((channels, 2 * CHUNK), F32),
            pltpu.VMEM((channels, 2 * NF), F32),
        ],
        compiler_params=params,
        name="second",
    )(traces, table, lines, edge, last)
    picks = pl.pallas_call(
        functools.partial(picks_kernel, shape),
        out_shape=jax.ShapeDtypeStruct((2 * rows_out, width), BF16),
        in_specs=[vmem] * (2 + len(wanted)),
        out_specs=vmem,
        scratch_shapes=[pltpu.VMEM((2 * rows_out, width), F32), pltpu.VMEM((2 * chips, 128), F32)],
        compiler_params=params,
        name="picks",
    )(source_counts[None], source_channel, *wanted)
    outs = pl.pallas_call(
        functools.partial(rest_kernel, windows, times),
        out_shape=[jax.ShapeDtypeStruct((rows_out, 2 * NF), BF16)] * 2
        + [jax.ShapeDtypeStruct((windows * part, 2 * NF), BF16)] * times,
        in_specs=[vmem] * 10,
        out_specs=[vmem] * (2 + times),
        scratch_shapes=[
            pltpu.VMEM((2 * tap_count + 6, width - channels), F32),
            pltpu.VMEM((width - channels, 2 * NF), F32),
            pltpu.VMEM((width, 2 * NF), BF16),
        ],
        compiler_params=params,
        name="rest",
    )(
        halo,
        ends,
        taps,
        table,
        part_a,
        part_b,
        response_a,
        response_b,
        own_white,
        picks,
    )
    keep, send, blocks = outs[0], outs[1], outs[2:]
    gathered = keep + across(send, "chan", 1)
    rows = sum(sizes)
    pieces = [gathered[d * rows : (d + 1) * rows] for d in range(chips)]
    pieces = list(lax.optimization_barrier(tuple(pieces)))
    for bit in bits:
        onward = [d for d in range(2 * bit, chips) if d & (2 * bit - 1) == bit]
        if onward:
            block = jnp.concatenate([pieces[d] for d in onward], axis=0)
            block = across(block, "chan", 2 * bit)
            for i, d in enumerate(onward):
                pieces[d ^ bit] = pieces[d ^ bit] + block[i * rows : (i + 1) * rows]
    mine = pieces[0]
    for bit in bits[:-1]:
        mine = mine + across(pieces[bit], "chan", 2 * bit)
    mine = [mine[: sizes[0]], mine[sizes[0] :]]
    if bits:
        last = pieces[bits[-1]]
        for i, x in enumerate((last[: sizes[0]], last[sizes[0] :])):
            mine[i] = mine[i] + across(x, "chan", 2 * bits[-1])
    receivers = [blocks[0]]
    for d in range(1, times):
        receivers.append(across(blocks[d], "tm", d))
    receivers = [r.reshape(windows, part, 2 * NF) for r in receivers]
    sources = [mine]
    for d in range(1, times):
        both = []
        for x in mine:
            both.append(across(x, "tm", d))
        sources.append(both)

    factor = 1.0 / (windows * times)
    early, late = list(range(windows - 1)), [windows - 1]
    total = correlate(
        receivers[:1] * 2, sources[0], (early, late), None, pairs, factor, times == 1
    )
    if times > 1:
        for i, span in enumerate((early, late)):
            total = correlate(
                receivers[1:],
                [both[i] for both in sources[1:]],
                (span,) * (times - 1),
                total,
                pairs,
                factor,
                i == 1,
            )
    return total.transpose(1, 0, 2)


def solution(mesh):
    in_specs = (P(("seg", "chan"), "tm"), P("chan", None), P(), P(), P("chan", None))
    out_specs = P(("seg", "chan", "tm"), None, None)
    return jax.shard_map(shards, mesh=mesh, in_specs=in_specs, out_specs=out_specs, check_vma=False)
```

```python
import functools

import jax
import jax.numpy as jnp
import ml_dtypes
import numpy as np
from jax import lax
from jax.experimental import pallas as pl
from jax.experimental.pallas import tpu as pltpu
from jax.sharding import PartitionSpec as P


NFFT = 4096
NF = 512
F0 = 8
PIECE = NFFT // 8
HALF = NFFT // 2
CHUNK = 256
F32 = jnp.float32
BF16 = jnp.bfloat16
LIMIT = 24 * 1024 * 1024
HINT = 10**10


def piece_table():
    bins = F0 + np.arange(NF)
    angle = (bins * np.arange(PIECE)[:, None] % NFFT) * (2.0 * np.pi / NFFT)
    exact = np.concatenate([np.cos(angle), -np.sin(angle)], axis=1)
    high = exact.astype(ml_dtypes.bfloat16)
    low = (exact - high.astype(np.float64)).astype(ml_dtypes.bfloat16)
    return np.concatenate([high, low], axis=0)


def split_two(x):
    high = x.astype(BF16)
    low = (x - high.astype(F32)).astype(BF16)
    return high, low


def dot(a, b):
    return jnp.dot(a, b, preferred_element_type=F32)


def stacked_parts(x):
    high, low = split_two(x)
    high = high.astype(F32)
    return jnp.concatenate([high, low.astype(F32), high], axis=0)


def stacked_rows(table, rows, cols):
    first = table[:rows, cols]
    return jnp.concatenate([first, first, table[PIECE : PIECE + rows, cols]], axis=0)


class Turns:
    def __init__(self):
        lane = lax.broadcasted_iota(jnp.int32, (1, CHUNK), 1)
        turn = lane % 4
        self.odd = (turn % 2) == 1
        self.sign = jnp.where(self.odd, -1.0, 1.0)
        self.real = jnp.where(turn < 2, 1.0, -1.0)
        self.imag = jnp.where((turn == 0) | (turn == 3), 1.0, -1.0)
        eighth = lane % 8
        root = np.float32(np.sqrt(0.5))
        self.cos = jnp.where(turn % 4 == 0, 1.0, jnp.where(turn == 2, 0.0, root))
        self.cos = jnp.where((eighth > 2) & (eighth < 6), -self.cos, self.cos)
        self.sin = jnp.where(turn == 2, 1.0, jnp.where(turn == 0, 0.0, root))
        self.sin = jnp.where(eighth < 4, -self.sin, self.sin)

    def quarter(self, ar, ai, br, bi):
        return (
            ar + self.real * jnp.where(self.odd, bi, br),
            ai + self.imag * jnp.where(self.odd, br, bi),
        )

    def half(self, re, im):
        ar, ai = self.quarter(re[0], im[0], re[2], im[2])
        br, bi = self.quarter(re[1], im[1], re[3], im[3])
        return ar + (br * self.cos - bi * self.sin), ai + (br * self.sin + bi * self.cos)


def half_spectra(x, table, channels, halves, turns, f):
    re = slice(f, f + CHUNK)
    im = slice(NF + f, NF + f + CHUNK)
    both = jnp.concatenate([x, x], axis=1)
    dr = dot(both, table[:, re])
    di = dot(both, table[:, im])
    out = []
    for b in range(halves):
        rows = [slice((4 * b + e) * channels, (4 * b + e + 1) * channels) for e in range(4)]
        out.append(turns.half([dr[r] for r in rows], [di[r] for r in rows]))
    return out


def end_terms(taps_wide, shifted, tap_count, ends):
    lag = tap_count - 1
    apart = ends.T
    size = apart.shape[0]
    shifted[...] = jnp.zeros_like(shifted)
    shifted[:tap_count, :] = taps_wide
    total = jnp.zeros((lag, apart.shape[1]), F32)
    for j in range(1, tap_count):
        total = total + shifted[j : j + lag, :] * apart[size - j : size - j + 1, :]
    return stacked_parts(total).T.astype(BF16)


def whiten_rows(re, im):
    rows = re.shape[0]
    place = lax.broadcasted_iota(jnp.int32, (rows, NF), 1)
    power = re * re + im * im
    smooth = power
    for s in (1, 2):
        smooth = smooth + jnp.where(place >= s, pltpu.roll(power, s, 1), 0.0)
        smooth = smooth + jnp.where(place < NF - s, pltpu.roll(power, NF - s, 1), 0.0)
    total = jnp.sum(power, axis=1, keepdims=True)
    scaling = lax.rsqrt(smooth * 0.2 + (total * (0.1 / NF) + 1e-06))
    return (re * scaling).astype(BF16), (im * scaling).astype(BF16)


ROWS = 16


def whiten_all(spectra, white, count):
    def step(i, carry):
        rows = pl.ds(pl.multiple_of(i * ROWS, ROWS), ROWS)
        re, im = whiten_rows(spectra[rows, :NF], spectra[rows, NF:])
        white[rows, :NF] = re
        white[rows, NF:] = im
        return carry

    lax.fori_loop(0, count // ROWS, step, 0, unroll=4)


def tail_kernel(traces, wanted, tail, ids, sems):
    start = traces.shape[1] - tail.shape[1]
    copies = [
        pltpu.make_async_copy(traces.at[:, start:], tail, sems.at[0]),
        pltpu.make_async_copy(wanted, ids, sems.at[1]),
    ]
    for copy in copies:
        copy.start()
    for copy in copies:
        copy.wait()


def pair_kernel(mine, other, out):
    out[:1, :] = mine[...]
    out[1:, :] = other[...]


def own_chunk(windows, f, traces, table, lines, edge, part, response, last):
    channels, samples = traces.shape
    size = lines.shape[1] // 3
    lag = edge.shape[1] // 3
    pieces = samples // PIECE
    x = jnp.concatenate([traces[:, q * PIECE : (q + 1) * PIECE] for q in range(pieces)], axis=0)
    turns = Turns()
    re = slice(f, f + CHUNK)
    im = slice(NF + f, NF + f + CHUNK)
    pr = dot(lines[...], stacked_rows(table, size, re))
    pi = dot(lines[...], stacked_rows(table, size, im))
    response[:, :CHUNK] = pr
    response[:, CHUNK:] = pi
    halves = half_spectra(x, table, channels, windows, turns, f)
    for w in range(windows):
        xr, xi = halves[w]
        xr, xi = turns.sign * xr, turns.sign * xi
        if w > 0:
            xr, xi = xr + halves[w - 1][0], xi + halves[w - 1][1]
        yr = xr * pr - xi * pi
        yi = xr * pi + xi * pr
        if w < windows - 1:
            rows = slice(w * channels, (w + 1) * channels)
            part[rows, :CHUNK] = yr
            part[rows, CHUNK:] = yi
        else:
            last[:, :CHUNK] = yr + dot(edge[...], stacked_rows(table, lag, re))
            last[:, CHUNK:] = yi + dot(edge[...], stacked_rows(table, lag, im))


def first_kernel(
    windows, traces, taps, table, part, response, last, ends, edge, lines, square, shifted
):
    channels, samples = traces.shape
    tap_count = taps.shape[0]
    square[...] = jnp.zeros_like(square)
    high, low = split_two(taps[...])
    high = high.astype(F32)
    size = square.shape[0] // 3
    for i, value in enumerate((high, low.astype(F32), high)):
        square[i * size : i * size + tap_count, :channels] = value
    lines[...] = square[...].T[:channels].astype(BF16)
    tile = 128
    for b in range(1, windows):
        ends[:, (b - 1) * tile : b * tile] = traces[:, b * HALF - tile : b * HALF]
    start = (windows - 2) * HALF
    apart = traces[:, start - tile : start].astype(F32) - traces[:, samples - tile :].astype(F32)
    edge[...] = end_terms(taps[...], shifted, tap_count, apart)
    own_chunk(windows, 0, traces, table, lines, edge, part, response, last)


def second_kernel(
    windows, traces, table, lines, edge, first, part, response, white, second, spectra
):
    own_chunk(windows, CHUNK, traces, table, lines, edge, part, response, second)
    for i, half in enumerate((first, second)):
        spectra[:, i * CHUNK : (i + 1) * CHUNK] = half[:, :CHUNK]
        spectra[:, NF + i * CHUNK : NF + (i + 1) * CHUNK] = half[:, CHUNK:]
    whiten_all(spectra, white, white.shape[0])


def part_rows(windows, pairs):
    return [-(-w * pairs // 8) * 8 for w in (windows - 1, 1)]


def picks_kernel(shape, counts, slots, *refs):
    channels, windows, pairs, chips = shape
    wanted, (picks, chosen, lines) = refs[:-3], refs[-3:]
    group = lax.axis_index("chan")
    place = lax.broadcasted_iota(jnp.int32, counts.shape, 1)
    held = counts[...].astype(F32)
    first = jnp.sum(jnp.where(place < group, held, 0.0), axis=1, keepdims=True)
    owned = jnp.sum(jnp.where(place == group, held, 0.0), axis=1, keepdims=True)
    row = lax.broadcasted_iota(jnp.int32, slots.shape, 0)
    own_slots = jnp.where(row == group, slots[...], 0).astype(F32)
    own_slots = jnp.sum(own_slots, axis=0, keepdims=True)
    lines[...] = jnp.zeros_like(lines)
    at = 0
    for w in wanted:
        lines[at : at + w.shape[0], :pairs] = w[...].astype(F32)
        at += w.shape[0]
    slot = lines[...] - first
    channel = jnp.full(slot.shape, -1.0, F32)
    for s in range(slots.shape[1]):
        channel = jnp.where(slot == s, own_slots[:, s : s + 1], channel)
    channel = jnp.where((slot >= 0) & (slot < owned), channel, -1.0)
    turned = channel.T
    width = windows * channels
    lane = lax.broadcasted_iota(jnp.int32, (1, width), 1)
    columns = [
        jnp.where(lane // channels == w, lane % channels, -2).astype(F32) for w in range(windows)
    ]
    sizes = part_rows(windows, pairs)
    chosen[...] = jnp.zeros_like(chosen)
    for core in range(2):
        for d in range(chips):
            base = (core * chips + d) * sum(sizes)
            one = turned[:pairs, 2 * d + core : 2 * d + core + 1]
            for w in range(windows):
                row = base + (w * pairs if w < windows - 1 else sizes[0])
                chosen[row : row + pairs, :] = (one == columns[w]).astype(F32)
    picks[...] = chosen[...].astype(BF16)


def rest_kernel(
    windows, times, halo, ends, taps, table, part_a, part_b, response_a, response_b, *refs
):
    own_white, picks, keep, send = refs[:4]
    blocks = refs[4 : 4 + times]
    shifted, spectra, white = refs[4 + times :]
    channels = response_a.shape[0]
    tap_count = taps.shape[0]
    tile = halo.shape[1] - HALF
    rest = windows - 1

    before = [halo[:, :tile], halo[:, HALF:]]
    before += [ends[:, (b - 1) * tile : b * tile] for b in range(1, windows - 2)]
    after = [ends[:, w * tile : (w + 1) * tile] for w in range(rest)]
    apart = jnp.concatenate([b.astype(F32) - a.astype(F32) for b, a in zip(before, after)], axis=0)
    taps_wide = jnp.concatenate([taps[...]] * rest, axis=1)
    edge = end_terms(taps_wide, shifted, tap_count, apart)
    x = jnp.concatenate(
        [halo[:, tile + q * PIECE : tile + (q + 1) * PIECE] for q in range(HALF // PIECE)],
        axis=0,
    )
    turns = Turns()
    for f in range(0, NF, CHUNK):
        re = slice(f, f + CHUNK)
        im = slice(NF + f, NF + f + CHUNK)
        xr, xi = half_spectra(x, table, channels, 1, turns, f)[0]
        part, response = (part_b, response_b) if f else (part_a, response_a)
        pr, pi = response[:, :CHUNK], response[:, CHUNK:]
        er = dot(edge, stacked_rows(table, tap_count - 1, re))
        ei = dot(edge, stacked_rows(table, tap_count - 1, im))
        spectra[:channels, re] = part[:channels, :CHUNK] + er[:channels] + (xr * pr - xi * pi)
        spectra[:channels, im] = part[:channels, CHUNK:] + ei[:channels] + (xr * pi + xi * pr)
        spectra[channels:, re] = part[channels:, :CHUNK] + er[channels:]
        spectra[channels:, im] = part[channels:, CHUNK:] + ei[channels:]
    count = rest * channels
    whiten_all(spectra, white, count)
    white[count:, :] = own_white[...]
    base = keep.shape[0]
    size = channels // times
    choose = picks[...]
    for f in range(0, 2 * NF, CHUNK):
        cols = slice(f, f + CHUNK)
        out = dot(choose, white[:, cols]).astype(BF16)
        keep[:, cols] = out[:base]
        send[:, cols] = out[base:]
    for d in range(times):
        line = (lax.axis_index("tm") ^ d) * size
        for w in range(windows):
            if size % ROWS == 0:
                at = pl.multiple_of(w * channels + line, ROWS)
                blocks[d][w * size : (w + 1) * size, :] = white[pl.ds(at, size), :]
            else:
                row = lax.broadcasted_iota(jnp.int32, (size, channels), 0)
                col = lax.broadcasted_iota(jnp.int32, (size, channels), 1)
                move = (col == row + line).astype(F32).astype(BF16)
                moved = dot(move, white[w * channels : (w + 1) * channels, :])
                blocks[d][w * size : (w + 1) * size, :] = moved.astype(BF16)


def correlate_kernel(spans, pairs, factor, has_total, last, *refs):
    count = len(spans)
    receivers, sources = refs[:count], refs[count : 2 * count]
    total = refs[2 * count] if has_total else None
    out, line_r, line_s = refs[2 * count + has_total : 2 * count + has_total + 3]
    held, sems = refs[-2:] if last else (out, None)
    part = out.shape[1]
    windows = 0
    for receiver, source, span in zip(receivers, sources, spans):
        for i, w in enumerate(span):
            line_r[windows] = receiver[w].astype(F32) * factor
            rows = source[i * pairs : (i + 1) * pairs, :].astype(F32)
            for p in range(pairs):
                line_s[p, windows : windows + 1, :] = rows[p : p + 1, :]
            windows += 1

    def copy(p):
        return pltpu.make_async_copy(held.at[p], out.at[p], sems.at[p])

    def one(p, carry):
        for f in range(0, NF, 128):
            re = slice(f, f + 128)
            im = slice(NF + f, NF + f + 128)
            if has_total:
                total_r, total_i = total[p, :, re], total[p, :, im]
            else:
                total_r = jnp.zeros((part, 128), F32)
                total_i = jnp.zeros((part, 128), F32)
            for at in range(windows):
                rr = line_r[at, :, re]
                ri = line_r[at, :, im]
                sr = line_s[p, at : at + 1, re]
                si = line_s[p, at : at + 1, im]
                total_r = total_r + (sr * rr + si * ri)
                total_i = total_i + (sr * ri - si * rr)
            held[p, :, re] = total_r
            held[p, :, im] = total_i
        if last:
            copy(p).start()
        return carry

    lax.fori_loop(0, pairs, one, 0)
    if last:
        for p in range(pairs):
            copy(p).wait()


def correlate(receivers, sources, spans, total, pairs, factor, last):
    _, part, width = receivers[0].shape
    windows = sum(len(span) for span in spans)
    vmem = pl.BlockSpec(memory_space=pltpu.VMEM)
    shape = (pairs, part, width)
    extra = [] if total is None else [total]
    scratch = [
        pltpu.VMEM((windows, part, width), F32),
        pltpu.VMEM((pairs, -(-windows // 8) * 8, width), F32),
    ]
    if last:
        scratch += [pltpu.VMEM(shape, F32), pltpu.SemaphoreType.DMA((pairs,))]
    return pl.pallas_call(
        functools.partial(correlate_kernel, spans, pairs, factor, len(extra), last),
        out_shape=jax.ShapeDtypeStruct(shape, F32),
        in_specs=[vmem] * (2 * len(spans) + len(extra)),
        out_specs=pl.BlockSpec(memory_space=pltpu.HBM) if last else vmem,
        scratch_shapes=scratch,
        compiler_params=pltpu.CompilerParams(vmem_limit_bytes=LIMIT),
        name="correlate",
    )(*receivers, *sources, *extra)


def shards(traces, filter_taps, source_counts, source_channel, block_sources):
    channels, samples = traces.shape
    tap_count = filter_taps.shape[1]
    pairs = block_sources.shape[1]
    windows = samples // HALF
    groups = lax.axis_size("chan")
    times = lax.axis_size("tm")
    chips = groups // 2
    part = channels // times
    sizes = part_rows(windows, pairs)
    rows_out = chips * sum(sizes)

    def across(x, axis, distance):
        size = lax.axis_size(axis)
        return lax.ppermute(x, axis, [(i, i ^ distance) for i in range(size)])

    vmem = pl.BlockSpec(memory_space=pltpu.VMEM)
    hbm = pl.BlockSpec(memory_space=pltpu.HBM)
    params = pltpu.CompilerParams(vmem_limit_bytes=LIMIT)
    bits = [1 << b for b in range(chips.bit_length() - 1)]

    other = across(block_sources, "chan", 1)
    tail, ids = pl.pallas_call(
        tail_kernel,
        out_shape=[
            jax.ShapeDtypeStruct((channels, HALF + 128), BF16),
            jax.ShapeDtypeStruct(block_sources.shape, jnp.int32),
        ],
        in_specs=[hbm] * 2,
        out_specs=[vmem] * 2,
        scratch_shapes=[pltpu.SemaphoreType.DMA((2,))],
        compiler_params=params,
        name="tail",
    )(*(pltpu.with_memory_space_constraint(a, pltpu.HBM) for a in (traces, block_sources)))
    taps = filter_taps.T
    traces, taps, table = (
        pltpu.with_memory_space_constraint(a, pltpu.VMEM)
        for a in (traces, taps, jnp.asarray(piece_table()))
    )
    wanted = [
        pl.pallas_call(
            pair_kernel,
            out_shape=jax.ShapeDtypeStruct((2, pairs), jnp.int32),
            in_specs=[vmem] * 2,
            out_specs=vmem,
            compiler_params=params,
            cost_estimate=pl.CostEstimate(flops=HINT, bytes_accessed=8 * pairs, transcendentals=0),
            name="pair",
        )(ids, other)
    ]
    tail, pair = lax.optimization_barrier((tail, wanted[0]))
    wanted = [pair]
    halo = lax.ppermute(tail, "tm", [(i - 1, i) for i in range(1, times)])
    for bit in bits:
        known = jnp.concatenate(wanted, axis=0)
        wanted = [known, across(known, "chan", 2 * bit)]

    shape = (channels, windows, pairs, chips)
    width = windows * channels
    chunk_shapes = [
        jax.ShapeDtypeStruct((width - channels, 2 * CHUNK), F32),
        jax.ShapeDtypeStruct((channels, 2 * CHUNK), F32),
    ]
    size = -(-tap_count // 16) * 16
    part_a, response_a, last, ends, edge, lines = pl.pallas_call(
        functools.partial(first_kernel, windows),
        out_shape=chunk_shapes
        + [
            chunk_shapes[1],
            jax.ShapeDtypeStruct((channels, (windows - 1) * 128), BF16),
            jax.ShapeDtypeStruct((channels, 3 * (tap_count - 1)), BF16),
            jax.ShapeDtypeStruct((channels, 3 * size), BF16),
        ],
        in_specs=[vmem] * 3,
        out_specs=[vmem] * 6,
        scratch_shapes=[
            pltpu.VMEM((3 * size, 128), F32),
            pltpu.VMEM((2 * tap_count + 6, channels), F32),
        ],
        compiler_params=params,
        name="first",
    )(traces, taps, table)
    part_b, response_b, own_white = pl.pallas_call(
        functools.partial(second_kernel, windows),
        out_shape=chunk_shapes + [jax.ShapeDtypeStruct((channels, 2 * NF), BF16)],
        in_specs=[vmem] * 5,
        out_specs=[vmem] * 3,
        scratch_shapes=[
            pltpu.VMEM((channels, 2 * CHUNK), F32),
            pltpu.VMEM((channels, 2 * NF), F32),
        ],
        compiler_params=params,
        name="second",
    )(traces, table, lines, edge, last)
    picks = pl.pallas_call(
        functools.partial(picks_kernel, shape),
        out_shape=jax.ShapeDtypeStruct((2 * rows_out, width), BF16),
        in_specs=[vmem] * (2 + len(wanted)),
        out_specs=vmem,
        scratch_shapes=[pltpu.VMEM((2 * rows_out, width), F32), pltpu.VMEM((2 * chips, 128), F32)],
        compiler_params=params,
        name="picks",
    )(source_counts[None], source_channel, *wanted)
    outs = pl.pallas_call(
        functools.partial(rest_kernel, windows, times),
        out_shape=[jax.ShapeDtypeStruct((rows_out, 2 * NF), BF16)] * 2
        + [jax.ShapeDtypeStruct((windows * part, 2 * NF), BF16)] * times,
        in_specs=[vmem] * 10,
        out_specs=[vmem] * (2 + times),
        scratch_shapes=[
            pltpu.VMEM((2 * tap_count + 6, width - channels), F32),
            pltpu.VMEM((width - channels, 2 * NF), F32),
            pltpu.VMEM((width, 2 * NF), BF16),
        ],
        compiler_params=params,
        name="rest",
    )(
        halo,
        ends,
        taps,
        table,
        part_a,
        part_b,
        response_a,
        response_b,
        own_white,
        picks,
    )
    keep, send, blocks = outs[0], outs[1], outs[2:]
    gathered = keep + across(send, "chan", 1)
    rows = sum(sizes)
    pieces = [gathered[d * rows : (d + 1) * rows] for d in range(chips)]
    pieces = list(lax.optimization_barrier(tuple(pieces)))
    for bit in bits:
        onward = [d for d in range(2 * bit, chips) if d & (2 * bit - 1) == bit]
        if onward:
            block = jnp.concatenate([pieces[d] for d in onward], axis=0)
            block = across(block, "chan", 2 * bit)
            for i, d in enumerate(onward):
                pieces[d ^ bit] = pieces[d ^ bit] + block[i * rows : (i + 1) * rows]
    mine = pieces[0]
    for bit in bits[:-1]:
        mine = mine + across(pieces[bit], "chan", 2 * bit)
    mine = [mine[: sizes[0]], mine[sizes[0] :]]
    if bits:
        last = pieces[bits[-1]]
        for i, x in enumerate((last[: sizes[0]], last[sizes[0] :])):
            mine[i] = mine[i] + across(x, "chan", 2 * bits[-1])
    receivers = [blocks[0]]
    for d in range(1, times):
        receivers.append(across(blocks[d], "tm", d))
    receivers = [r.reshape(windows, part, 2 * NF) for r in receivers]
    sources = [mine]
    for d in range(1, times):
        both = []
        for x in mine:
            both.append(across(x, "tm", d))
        sources.append(both)

    factor = 1.0 / (windows * times)
    early, late = tuple(range(windows - 1)), (windows - 1,)
    total = None
    for which in ([0], list(range(1, times))):
        for i, span in enumerate((early, late)):
            if which:
                last = i == 1 and which[-1] == times - 1
                total = correlate(
                    [receivers[d] for d in which],
                    [sources[d][i] for d in which],
                    (span,) * len(which),
                    total,
                    pairs,
                    factor,
                    last,
                )
    return total.transpose(1, 0, 2)


def solution(mesh):
    in_specs = (P(("seg", "chan"), "tm"), P("chan", None), P(), P(), P("chan", None))
    out_specs = P(("seg", "chan", "tm"), None, None)
    return jax.shard_map(shards, mesh=mesh, in_specs=in_specs, out_specs=out_specs, check_vma=False)
```

```python
import functools

import jax
import jax.numpy as jnp
import ml_dtypes
import numpy as np
from jax import lax
from jax.experimental import pallas as pl
from jax.experimental.pallas import tpu as pltpu
from jax.sharding import PartitionSpec as P


NFFT = 4096
NF = 512
F0 = 8
PIECE = NFFT // 8
HALF = NFFT // 2
CHUNK = 256
F32 = jnp.float32
BF16 = jnp.bfloat16
LIMIT = 24 * 1024 * 1024


def piece_table():
    bins = F0 + np.arange(NF)
    angle = (bins * np.arange(PIECE)[:, None] % NFFT) * (2.0 * np.pi / NFFT)
    exact = np.concatenate([np.cos(angle), -np.sin(angle)], axis=1)
    high = exact.astype(ml_dtypes.bfloat16)
    low = (exact - high.astype(np.float64)).astype(ml_dtypes.bfloat16)
    return np.concatenate([high, low], axis=0)


def split_two(x):
    high = x.astype(BF16)
    low = (x - high.astype(F32)).astype(BF16)
    return high, low


def dot(a, b):
    return jnp.dot(a, b, preferred_element_type=F32)


def stacked_parts(x):
    high, low = split_two(x)
    high = high.astype(F32)
    return jnp.concatenate([high, low.astype(F32), high], axis=0)


def stacked_rows(table, rows, cols):
    first = table[:rows, cols]
    return jnp.concatenate([first, first, table[PIECE : PIECE + rows, cols]], axis=0)


class Turns:
    def __init__(self):
        lane = lax.broadcasted_iota(jnp.int32, (1, CHUNK), 1)
        turn = lane % 4
        self.odd = (turn % 2) == 1
        self.sign = jnp.where(self.odd, -1.0, 1.0)
        self.real = jnp.where(turn < 2, 1.0, -1.0)
        self.imag = jnp.where((turn == 0) | (turn == 3), 1.0, -1.0)
        eighth = lane % 8
        root = np.float32(np.sqrt(0.5))
        self.cos = jnp.where(turn % 4 == 0, 1.0, jnp.where(turn == 2, 0.0, root))
        self.cos = jnp.where((eighth > 2) & (eighth < 6), -self.cos, self.cos)
        self.sin = jnp.where(turn == 2, 1.0, jnp.where(turn == 0, 0.0, root))
        self.sin = jnp.where(eighth < 4, -self.sin, self.sin)

    def quarter(self, ar, ai, br, bi):
        return (
            ar + self.real * jnp.where(self.odd, bi, br),
            ai + self.imag * jnp.where(self.odd, br, bi),
        )

    def half(self, re, im):
        ar, ai = self.quarter(re[0], im[0], re[2], im[2])
        br, bi = self.quarter(re[1], im[1], re[3], im[3])
        return ar + (br * self.cos - bi * self.sin), ai + (br * self.sin + bi * self.cos)


def half_spectra(x, table, channels, halves, turns, f):
    re = slice(f, f + CHUNK)
    im = slice(NF + f, NF + f + CHUNK)
    both = jnp.concatenate([x, x], axis=1)
    dr = dot(both, table[:, re])
    di = dot(both, table[:, im])
    out = []
    for b in range(halves):
        rows = [slice((4 * b + e) * channels, (4 * b + e + 1) * channels) for e in range(4)]
        out.append(turns.half([dr[r] for r in rows], [di[r] for r in rows]))
    return out


def end_terms(taps_wide, shifted, tap_count, ends):
    lag = tap_count - 1
    apart = ends.T
    size = apart.shape[0]
    shifted[...] = jnp.zeros_like(shifted)
    shifted[:tap_count, :] = taps_wide
    total = jnp.zeros((lag, apart.shape[1]), F32)
    for j in range(1, tap_count):
        total = total + shifted[j : j + lag, :] * apart[size - j : size - j + 1, :]
    return stacked_parts(total).T.astype(BF16)


def whiten_rows(re, im):
    rows = re.shape[0]
    place = lax.broadcasted_iota(jnp.int32, (rows, NF), 1)
    power = re * re + im * im
    smooth = power
    for s in (1, 2):
        smooth = smooth + jnp.where(place >= s, pltpu.roll(power, s, 1), 0.0)
        smooth = smooth + jnp.where(place < NF - s, pltpu.roll(power, NF - s, 1), 0.0)
    total = jnp.sum(power, axis=1, keepdims=True)
    scaling = lax.rsqrt(smooth * 0.2 + (total * (0.1 / NF) + 1e-06))
    return (re * scaling).astype(BF16), (im * scaling).astype(BF16)


ROWS = 16


def whiten_all(spectra, white, count):
    def step(i, carry):
        rows = pl.ds(pl.multiple_of(i * ROWS, ROWS), ROWS)
        re, im = whiten_rows(spectra[rows, :NF], spectra[rows, NF:])
        white[rows, :NF] = re
        white[rows, NF:] = im
        return carry

    lax.fori_loop(0, count // ROWS, step, 0, unroll=4)


def load_kernel(
    traces_in, taps_in, table_in, ids_in, message, last_half, traces, taps, table, ids, sems
):
    channels, samples = traces.shape
    begin = samples - HALF - 128
    copies = [pltpu.make_async_copy(traces_in.at[:, begin:], traces.at[:, begin:], sems.at[0])]
    order = [c for f in range(0, NF, CHUNK) for c in (f, NF + f)]
    for i, c in enumerate(order):
        cols = slice(c, c + CHUNK)
        copies.append(
            pltpu.make_async_copy(table_in.at[:, cols], table.at[:, cols], sems.at[1 + i])
        )
    at = 1 + len(order)
    copies += [
        pltpu.make_async_copy(traces_in.at[:, :begin], traces.at[:, :begin], sems.at[at]),
        pltpu.make_async_copy(taps_in, taps, sems.at[at + 1]),
        pltpu.make_async_copy(ids_in, ids, sems.at[at + 2]),
    ]
    for copy in copies:
        copy.start()
    copies[0].wait()
    message[:, 2 * NF : 2 * NF + 128] = traces[:, begin : begin + 128]
    message[:, 2 * NF + 128 :] = traces[:, samples - 128 :]
    pieces = [samples - HALF + q * PIECE for q in range(HALF // PIECE)]
    x = jnp.concatenate([traces[:, p : p + PIECE] for p in pieces], axis=0)
    turns = Turns()
    for i, f in enumerate(range(0, NF, CHUNK)):
        re = slice(f, f + CHUNK)
        im = slice(NF + f, NF + f + CHUNK)
        copies[1 + 2 * i].wait()
        copies[2 + 2 * i].wait()
        xr, xi = half_spectra(x, table, channels, 1, turns, f)[0]
        last_half[:, re] = xr
        last_half[:, im] = xi
        message[:, re] = xr.astype(BF16)
        message[:, im] = xi.astype(BF16)
    for copy in copies[at:]:
        copy.wait()


def pair_kernel(mine, other, out):
    out[:1, :] = mine[...]
    out[1:, :] = other[...]


def own_chunk(windows, f, traces, table, last_half, lines, edge, part, response, last):
    channels, samples = traces.shape
    size = lines.shape[1] // 3
    lag = edge.shape[1] // 3
    pieces = (samples - HALF) // PIECE
    x = jnp.concatenate([traces[:, q * PIECE : (q + 1) * PIECE] for q in range(pieces)], axis=0)
    turns = Turns()
    re = slice(f, f + CHUNK)
    im = slice(NF + f, NF + f + CHUNK)
    pr = dot(lines[...], stacked_rows(table, size, re))
    pi = dot(lines[...], stacked_rows(table, size, im))
    response[:, :CHUNK] = pr
    response[:, CHUNK:] = pi
    halves = half_spectra(x, table, channels, windows - 1, turns, f)
    halves.append((last_half[:, re], last_half[:, im]))
    for w in range(windows):
        xr, xi = halves[w]
        xr, xi = turns.sign * xr, turns.sign * xi
        if w > 0:
            xr, xi = xr + halves[w - 1][0], xi + halves[w - 1][1]
        yr = xr * pr - xi * pi
        yi = xr * pi + xi * pr
        if w < windows - 1:
            rows = slice(w * channels, (w + 1) * channels)
            part[rows, :CHUNK] = yr
            part[rows, CHUNK:] = yi
        else:
            last[:, :CHUNK] = yr + dot(edge[...], stacked_rows(table, lag, re))
            last[:, CHUNK:] = yi + dot(edge[...], stacked_rows(table, lag, im))


def first_kernel(
    windows, traces, taps, table, last_half, part, response, last, ends, edge, lines, square, shifted
):
    channels, samples = traces.shape
    tap_count = taps.shape[0]
    square[...] = jnp.zeros_like(square)
    high, low = split_two(taps[...])
    high = high.astype(F32)
    size = square.shape[0] // 3
    for i, value in enumerate((high, low.astype(F32), high)):
        square[i * size : i * size + tap_count, :channels] = value
    lines[...] = square[...].T[:channels].astype(BF16)
    tile = 128
    for b in range(1, windows):
        ends[:, (b - 1) * tile : b * tile] = traces[:, b * HALF - tile : b * HALF]
    start = (windows - 2) * HALF
    apart = traces[:, start - tile : start].astype(F32) - traces[:, samples - tile :].astype(F32)
    edge[...] = end_terms(taps[...], shifted, tap_count, apart)
    own_chunk(windows, 0, traces, table, last_half, lines, edge, part, response, last)


def second_kernel(
    windows, traces, table, last_half, lines, edge, first, part, response, white, second, spectra
):
    own_chunk(windows, CHUNK, traces, table, last_half, lines, edge, part, response, second)
    for i, half in enumerate((first, second)):
        spectra[:, i * CHUNK : (i + 1) * CHUNK] = half[:, :CHUNK]
        spectra[:, NF + i * CHUNK : NF + (i + 1) * CHUNK] = half[:, CHUNK:]
    whiten_all(spectra, white, white.shape[0])


def part_rows(windows, pairs):
    return [-(-w * pairs // 8) * 8 for w in (windows - 1, 1)]


def picks_kernel(shape, counts, slots, *refs):
    channels, windows, pairs, chips = shape
    wanted, (picks, chosen, lines) = refs[:-3], refs[-3:]
    group = lax.axis_index("chan")
    place = lax.broadcasted_iota(jnp.int32, counts.shape, 1)
    held = counts[...].astype(F32)
    first = jnp.sum(jnp.where(place < group, held, 0.0), axis=1, keepdims=True)
    owned = jnp.sum(jnp.where(place == group, held, 0.0), axis=1, keepdims=True)
    row = lax.broadcasted_iota(jnp.int32, slots.shape, 0)
    own_slots = jnp.where(row == group, slots[...], 0).astype(F32)
    own_slots = jnp.sum(own_slots, axis=0, keepdims=True)
    lines[...] = jnp.zeros_like(lines)
    at = 0
    for w in wanted:
        lines[at : at + w.shape[0], :pairs] = w[...].astype(F32)
        at += w.shape[0]
    slot = lines[...] - first
    channel = jnp.full(slot.shape, -1.0, F32)
    for s in range(slots.shape[1]):
        channel = jnp.where(slot == s, own_slots[:, s : s + 1], channel)
    channel = jnp.where((slot >= 0) & (slot < owned), channel, -1.0)
    turned = channel.T
    width = windows * channels
    lane = lax.broadcasted_iota(jnp.int32, (1, width), 1)
    columns = [
        jnp.where(lane // channels == w, lane % channels, -2).astype(F32) for w in range(windows)
    ]
    sizes = part_rows(windows, pairs)
    chosen[...] = jnp.zeros_like(chosen)
    for core in range(2):
        for d in range(chips):
            base = (core * chips + d) * sum(sizes)
            one = turned[:pairs, 2 * d + core : 2 * d + core + 1]
            for w in range(windows):
                row = base + (w * pairs if w < windows - 1 else sizes[0])
                chosen[row : row + pairs, :] = (one == columns[w]).astype(F32)
    picks[...] = chosen[...].astype(BF16)


def rest_kernel(
    windows, times, halo, ends, taps, table, part_a, part_b, response_a, response_b, *refs
):
    own_white, picks, keep, send = refs[:4]
    blocks = refs[4 : 4 + times]
    shifted, spectra, white = refs[4 + times :]
    channels = response_a.shape[0]
    tap_count = taps.shape[0]
    tile = 128
    rest = windows - 1

    before = [halo[:, 2 * NF : 2 * NF + tile], halo[:, 2 * NF + tile :]]
    before += [ends[:, (b - 1) * tile : b * tile] for b in range(1, windows - 2)]
    after = [ends[:, w * tile : (w + 1) * tile] for w in range(rest)]
    apart = jnp.concatenate([b.astype(F32) - a.astype(F32) for b, a in zip(before, after)], axis=0)
    taps_wide = jnp.concatenate([taps[...]] * rest, axis=1)
    edge = end_terms(taps_wide, shifted, tap_count, apart)
    for f in range(0, NF, CHUNK):
        re = slice(f, f + CHUNK)
        im = slice(NF + f, NF + f + CHUNK)
        xr, xi = halo[:, re].astype(F32), halo[:, im].astype(F32)
        part, response = (part_b, response_b) if f else (part_a, response_a)
        pr, pi = response[:, :CHUNK], response[:, CHUNK:]
        er = dot(edge, stacked_rows(table, tap_count - 1, re))
        ei = dot(edge, stacked_rows(table, tap_count - 1, im))
        spectra[:channels, re] = part[:channels, :CHUNK] + er[:channels] + (xr * pr - xi * pi)
        spectra[:channels, im] = part[:channels, CHUNK:] + ei[:channels] + (xr * pi + xi * pr)
        spectra[channels:, re] = part[channels:, :CHUNK] + er[channels:]
        spectra[channels:, im] = part[channels:, CHUNK:] + ei[channels:]
    count = rest * channels
    whiten_all(spectra, white, count)
    white[count:, :] = own_white[...]
    base = keep.shape[0]
    size = channels // times
    choose = picks[...]
    for f in range(0, 2 * NF, CHUNK):
        cols = slice(f, f + CHUNK)
        out = dot(choose, white[:, cols]).astype(BF16)
        keep[:, cols] = out[:base]
        send[:, cols] = out[base:]
    for d in range(times):
        line = (lax.axis_index("tm") ^ d) * size
        for w in range(windows):
            if size % ROWS == 0:
                at = pl.multiple_of(w * channels + line, ROWS)
                blocks[d][w * size : (w + 1) * size, :] = white[pl.ds(at, size), :]
            else:
                row = lax.broadcasted_iota(jnp.int32, (size, channels), 0)
                col = lax.broadcasted_iota(jnp.int32, (size, channels), 1)
                move = (col == row + line).astype(F32).astype(BF16)
                moved = dot(move, white[w * channels : (w + 1) * channels, :])
                blocks[d][w * size : (w + 1) * size, :] = moved.astype(BF16)


def correlate_kernel(spans, pairs, factor, has_total, last, *refs):
    count = len(spans)
    receivers, sources = refs[:count], refs[count : 2 * count]
    total = refs[2 * count] if has_total else None
    out, line_r, line_s = refs[2 * count + has_total : 2 * count + has_total + 3]
    held, sems = refs[-2:] if last else (out, None)
    part = out.shape[1]
    windows = 0
    for receiver, source, span in zip(receivers, sources, spans):
        for i, w in enumerate(span):
            line_r[windows] = receiver[w].astype(F32) * factor
            rows = source[i * pairs : (i + 1) * pairs, :].astype(F32)
            for p in range(pairs):
                line_s[p, windows : windows + 1, :] = rows[p : p + 1, :]
            windows += 1

    def copy(p):
        return pltpu.make_async_copy(held.at[p], out.at[p], sems.at[p])

    def one(p, carry):
        for f in range(0, NF, 128):
            re = slice(f, f + 128)
            im = slice(NF + f, NF + f + 128)
            if has_total:
                total_r, total_i = total[p, :, re], total[p, :, im]
            else:
                total_r = jnp.zeros((part, 128), F32)
                total_i = jnp.zeros((part, 128), F32)
            for at in range(windows):
                rr = line_r[at, :, re]
                ri = line_r[at, :, im]
                sr = line_s[p, at : at + 1, re]
                si = line_s[p, at : at + 1, im]
                total_r = total_r + (sr * rr + si * ri)
                total_i = total_i + (sr * ri - si * rr)
            held[p, :, re] = total_r
            held[p, :, im] = total_i
        if last:
            copy(p).start()
        return carry

    lax.fori_loop(0, pairs, one, 0)
    if last:
        for p in range(pairs):
            copy(p).wait()


def correlate(receivers, sources, spans, total, pairs, factor, last):
    _, part, width = receivers[0].shape
    windows = sum(len(span) for span in spans)
    vmem = pl.BlockSpec(memory_space=pltpu.VMEM)
    shape = (pairs, part, width)
    extra = [] if total is None else [total]
    scratch = [
        pltpu.VMEM((windows, part, width), F32),
        pltpu.VMEM((pairs, -(-windows // 8) * 8, width), F32),
    ]
    if last:
        scratch += [pltpu.VMEM(shape, F32), pltpu.SemaphoreType.DMA((pairs,))]
    return pl.pallas_call(
        functools.partial(correlate_kernel, spans, pairs, factor, len(extra), last),
        out_shape=jax.ShapeDtypeStruct(shape, F32),
        in_specs=[vmem] * (2 * len(spans) + len(extra)),
        out_specs=pl.BlockSpec(memory_space=pltpu.HBM) if last else vmem,
        scratch_shapes=scratch,
        compiler_params=pltpu.CompilerParams(vmem_limit_bytes=LIMIT),
        name="correlate",
    )(*receivers, *sources, *extra)


def shards(traces, filter_taps, source_counts, source_channel, block_sources):
    channels, samples = traces.shape
    tap_count = filter_taps.shape[1]
    pairs = block_sources.shape[1]
    windows = samples // HALF
    groups = lax.axis_size("chan")
    times = lax.axis_size("tm")
    chips = groups // 2
    part = channels // times
    sizes = part_rows(windows, pairs)
    rows_out = chips * sum(sizes)

    def across(x, axis, distance):
        size = lax.axis_size(axis)
        return lax.ppermute(x, axis, [(i, i ^ distance) for i in range(size)])

    vmem = pl.BlockSpec(memory_space=pltpu.VMEM)
    hbm = pl.BlockSpec(memory_space=pltpu.HBM)
    params = pltpu.CompilerParams(vmem_limit_bytes=LIMIT)
    bits = [1 << b for b in range(chips.bit_length() - 1)]

    other = across(block_sources, "chan", 1)
    inputs = (traces, filter_taps.T, jnp.asarray(piece_table()), block_sources)
    message, last_half, traces, taps, table, ids = pl.pallas_call(
        load_kernel,
        out_shape=[
            jax.ShapeDtypeStruct((channels, 2 * NF + 256), BF16),
            jax.ShapeDtypeStruct((channels, 2 * NF), F32),
        ]
        + [jax.ShapeDtypeStruct(a.shape, a.dtype) for a in inputs],
        in_specs=[hbm] * 4,
        out_specs=[vmem] * 6,
        scratch_shapes=[pltpu.SemaphoreType.DMA((4 + 2 * NF // CHUNK,))],
        compiler_params=params,
        name="load",
    )(*(pltpu.with_memory_space_constraint(a, pltpu.HBM) for a in inputs))
    wanted = [
        pl.pallas_call(
            pair_kernel,
            out_shape=jax.ShapeDtypeStruct((2, pairs), jnp.int32),
            in_specs=[vmem] * 2,
            out_specs=vmem,
            compiler_params=params,
            name="pair",
        )(ids, other)
    ]
    halo = lax.ppermute(message, "tm", [(i - 1, i) for i in range(1, times)])
    for bit in bits:
        known = jnp.concatenate(wanted, axis=0)
        wanted = [known, across(known, "chan", 2 * bit)]

    shape = (channels, windows, pairs, chips)
    width = windows * channels
    chunk_shapes = [
        jax.ShapeDtypeStruct((width - channels, 2 * CHUNK), F32),
        jax.ShapeDtypeStruct((channels, 2 * CHUNK), F32),
    ]
    size = -(-tap_count // 16) * 16
    part_a, response_a, last, ends, edge, lines = pl.pallas_call(
        functools.partial(first_kernel, windows),
        out_shape=chunk_shapes
        + [
            chunk_shapes[1],
            jax.ShapeDtypeStruct((channels, (windows - 1) * 128), BF16),
            jax.ShapeDtypeStruct((channels, 3 * (tap_count - 1)), BF16),
            jax.ShapeDtypeStruct((channels, 3 * size), BF16),
        ],
        in_specs=[vmem] * 4,
        out_specs=[vmem] * 6,
        scratch_shapes=[
            pltpu.VMEM((3 * size, 128), F32),
            pltpu.VMEM((2 * tap_count + 6, channels), F32),
        ],
        compiler_params=params,
        name="first",
    )(traces, taps, table, last_half)
    part_b, response_b, own_white = pl.pallas_call(
        functools.partial(second_kernel, windows),
        out_shape=chunk_shapes + [jax.ShapeDtypeStruct((channels, 2 * NF), BF16)],
        in_specs=[vmem] * 6,
        out_specs=[vmem] * 3,
        scratch_shapes=[
            pltpu.VMEM((channels, 2 * CHUNK), F32),
            pltpu.VMEM((channels, 2 * NF), F32),
        ],
        compiler_params=params,
        name="second",
    )(traces, table, last_half, lines, edge, last)
    picks = pl.pallas_call(
        functools.partial(picks_kernel, shape),
        out_shape=jax.ShapeDtypeStruct((2 * rows_out, width), BF16),
        in_specs=[vmem] * (2 + len(wanted)),
        out_specs=vmem,
        scratch_shapes=[pltpu.VMEM((2 * rows_out, width), F32), pltpu.VMEM((2 * chips, 128), F32)],
        compiler_params=params,
        name="picks",
    )(source_counts[None], source_channel, *wanted)
    outs = pl.pallas_call(
        functools.partial(rest_kernel, windows, times),
        out_shape=[jax.ShapeDtypeStruct((rows_out, 2 * NF), BF16)] * 2
        + [jax.ShapeDtypeStruct((windows * part, 2 * NF), BF16)] * times,
        in_specs=[vmem] * 10,
        out_specs=[vmem] * (2 + times),
        scratch_shapes=[
            pltpu.VMEM((2 * tap_count + 6, width - channels), F32),
            pltpu.VMEM((width - channels, 2 * NF), F32),
            pltpu.VMEM((width, 2 * NF), BF16),
        ],
        compiler_params=params,
        name="rest",
    )(
        halo,
        ends,
        taps,
        table,
        part_a,
        part_b,
        response_a,
        response_b,
        own_white,
        picks,
    )
    keep, send, blocks = outs[0], outs[1], outs[2:]
    gathered = keep + across(send, "chan", 1)
    rows = sum(sizes)
    pieces = [gathered[d * rows : (d + 1) * rows] for d in range(chips)]
    pieces = list(lax.optimization_barrier(tuple(pieces)))
    for bit in bits:
        onward = [d for d in range(2 * bit, chips) if d & (2 * bit - 1) == bit]
        if onward:
            block = jnp.concatenate([pieces[d] for d in onward], axis=0)
            block = across(block, "chan", 2 * bit)
            for i, d in enumerate(onward):
                pieces[d ^ bit] = pieces[d ^ bit] + block[i * rows : (i + 1) * rows]
    mine = pieces[0]
    for bit in bits[:-1]:
        mine = mine + across(pieces[bit], "chan", 2 * bit)
    mine = [mine[: sizes[0]], mine[sizes[0] :]]
    if bits:
        last = pieces[bits[-1]]
        for i, x in enumerate((last[: sizes[0]], last[sizes[0] :])):
            mine[i] = mine[i] + across(x, "chan", 2 * bits[-1])
    receivers = [blocks[0]]
    for d in range(1, times):
        receivers.append(across(blocks[d], "tm", d))
    receivers = [r.reshape(windows, part, 2 * NF) for r in receivers]
    sources = [mine]
    for d in range(1, times):
        both = []
        for x in mine:
            both.append(across(x, "tm", d))
        sources.append(both)

    factor = 1.0 / (windows * times)
    early, late = tuple(range(windows - 1)), (windows - 1,)
    total = None
    for which in ([0], list(range(1, times))):
        for i, span in enumerate((early, late)):
            if which:
                last = i == 1 and which[-1] == times - 1
                total = correlate(
                    [receivers[d] for d in which],
                    [sources[d][i] for d in which],
                    (span,) * len(which),
                    total,
                    pairs,
                    factor,
                    last,
                )
    return total.transpose(1, 0, 2)


def solution(mesh):
    in_specs = (P(("seg", "chan"), "tm"), P("chan", None), P(), P(), P("chan", None))
    out_specs = P(("seg", "chan", "tm"), None, None)
    return jax.shard_map(shards, mesh=mesh, in_specs=in_specs, out_specs=out_specs, check_vma=False)
```

```python
import functools

import jax
import jax.numpy as jnp
import ml_dtypes
import numpy as np
from jax import lax
from jax.experimental import pallas as pl
from jax.experimental.pallas import tpu as pltpu
from jax.sharding import PartitionSpec as P


NFFT = 4096
NF = 512
F0 = 8
PIECE = NFFT // 8
HALF = NFFT // 2
CHUNK = 256
F32 = jnp.float32
BF16 = jnp.bfloat16
LIMIT = 24 * 1024 * 1024
HINT = 10**10


def piece_table():
    bins = F0 + np.arange(NF)
    angle = (bins * np.arange(PIECE)[:, None] % NFFT) * (2.0 * np.pi / NFFT)
    exact = np.concatenate([np.cos(angle), -np.sin(angle)], axis=1)
    high = exact.astype(ml_dtypes.bfloat16)
    low = (exact - high.astype(np.float64)).astype(ml_dtypes.bfloat16)
    return np.concatenate([high, low], axis=0)


def split_two(x):
    high = x.astype(BF16)
    low = (x - high.astype(F32)).astype(BF16)
    return high, low


def dot(a, b):
    return jnp.dot(a, b, preferred_element_type=F32)


def stacked_parts(x):
    high, low = split_two(x)
    high = high.astype(F32)
    return jnp.concatenate([high, low.astype(F32), high], axis=0)


def stacked_rows(table, rows, cols):
    first = table[:rows, cols]
    return jnp.concatenate([first, first, table[PIECE : PIECE + rows, cols]], axis=0)


class Turns:
    def __init__(self):
        lane = lax.broadcasted_iota(jnp.int32, (1, CHUNK), 1)
        turn = lane % 4
        self.odd = (turn % 2) == 1
        self.sign = jnp.where(self.odd, -1.0, 1.0)
        self.real = jnp.where(turn < 2, 1.0, -1.0)
        self.imag = jnp.where((turn == 0) | (turn == 3), 1.0, -1.0)
        eighth = lane % 8
        root = np.float32(np.sqrt(0.5))
        self.cos = jnp.where(turn % 4 == 0, 1.0, jnp.where(turn == 2, 0.0, root))
        self.cos = jnp.where((eighth > 2) & (eighth < 6), -self.cos, self.cos)
        self.sin = jnp.where(turn == 2, 1.0, jnp.where(turn == 0, 0.0, root))
        self.sin = jnp.where(eighth < 4, -self.sin, self.sin)

    def quarter(self, ar, ai, br, bi):
        return (
            ar + self.real * jnp.where(self.odd, bi, br),
            ai + self.imag * jnp.where(self.odd, br, bi),
        )

    def half(self, re, im):
        ar, ai = self.quarter(re[0], im[0], re[2], im[2])
        br, bi = self.quarter(re[1], im[1], re[3], im[3])
        return ar + (br * self.cos - bi * self.sin), ai + (br * self.sin + bi * self.cos)


def half_spectra(x, table, channels, halves, turns, f):
    re = slice(f, f + CHUNK)
    im = slice(NF + f, NF + f + CHUNK)
    both = jnp.concatenate([x, x], axis=1)
    dr = dot(both, table[:, re])
    di = dot(both, table[:, im])
    out = []
    for b in range(halves):
        rows = [slice((4 * b + e) * channels, (4 * b + e + 1) * channels) for e in range(4)]
        out.append(turns.half([dr[r] for r in rows], [di[r] for r in rows]))
    return out


def end_terms(taps_wide, shifted, tap_count, ends):
    lag = tap_count - 1
    apart = ends.T
    size = apart.shape[0]
    shifted[...] = jnp.zeros_like(shifted)
    shifted[:tap_count, :] = taps_wide
    total = jnp.zeros((lag, apart.shape[1]), F32)
    for j in range(1, tap_count):
        total = total + shifted[j : j + lag, :] * apart[size - j : size - j + 1, :]
    return stacked_parts(total).T.astype(BF16)


def whiten_rows(re, im):
    rows = re.shape[0]
    place = lax.broadcasted_iota(jnp.int32, (rows, NF), 1)
    power = re * re + im * im
    smooth = power
    for s in (1, 2):
        smooth = smooth + jnp.where(place >= s, pltpu.roll(power, s, 1), 0.0)
        smooth = smooth + jnp.where(place < NF - s, pltpu.roll(power, NF - s, 1), 0.0)
    total = jnp.sum(power, axis=1, keepdims=True)
    scaling = lax.rsqrt(smooth * 0.2 + (total * (0.1 / NF) + 1e-06))
    return (re * scaling).astype(BF16), (im * scaling).astype(BF16)


ROWS = 16


def whiten_all(spectra, white, count):
    def step(i, carry):
        rows = pl.ds(pl.multiple_of(i * ROWS, ROWS), ROWS)
        re, im = whiten_rows(spectra[rows, :NF], spectra[rows, NF:])
        white[rows, :NF] = re
        white[rows, NF:] = im
        return carry

    lax.fori_loop(0, count // ROWS, step, 0, unroll=4)


def load_kernel(end, traces_in, table_in, ids_in, message, last_half, table, ids, traces, sems):
    channels, samples = traces.shape
    begin = traces_in.shape[1] - samples
    copies = [pltpu.make_async_copy(traces_in.at[:, begin:], traces, sems.at[0])]
    order = [c for f in range(0, NF, CHUNK) for c in (f, NF + f)]
    for i, c in enumerate(order):
        cols = slice(c, c + CHUNK)
        copies.append(
            pltpu.make_async_copy(table_in.at[:, cols], table.at[:, cols], sems.at[1 + i])
        )
    at = 1 + len(order)
    copies.append(pltpu.make_async_copy(ids_in, ids, sems.at[at]))
    for copy in copies:
        copy.start()
    copies[0].wait()
    lane = lax.broadcasted_iota(jnp.int32, (channels, 128), 1)
    final = pltpu.roll(traces[:, samples - 128 :].astype(F32), 128 - end, 1)
    tile = jnp.where(lane < 128 - end, final, traces[:, :128].astype(F32))
    message[:, 2 * NF :] = tile.astype(BF16)
    pieces = [samples - HALF + q * PIECE for q in range(HALF // PIECE)]
    x = jnp.concatenate([traces[:, p : p + PIECE] for p in pieces], axis=0)
    turns = Turns()
    for i, f in enumerate(range(0, NF, CHUNK)):
        re = slice(f, f + CHUNK)
        im = slice(NF + f, NF + f + CHUNK)
        copies[1 + 2 * i].wait()
        copies[2 + 2 * i].wait()
        xr, xi = half_spectra(x, table, channels, 1, turns, f)[0]
        last_half[:, re] = xr
        last_half[:, im] = xi
        message[:, re] = xr.astype(BF16)
        message[:, im] = xi.astype(BF16)
    for copy in copies[at:]:
        copy.wait()


def pair_kernel(mine, other, out):
    out[:1, :] = mine[...]
    out[1:, :] = other[...]


def own_chunk(windows, f, traces, table, last_half, lines, edge, part, response, last):
    channels, samples = traces.shape
    size = lines.shape[1] // 3
    lag = edge.shape[1] // 3
    pieces = (samples - HALF) // PIECE
    x = jnp.concatenate([traces[:, q * PIECE : (q + 1) * PIECE] for q in range(pieces)], axis=0)
    turns = Turns()
    re = slice(f, f + CHUNK)
    im = slice(NF + f, NF + f + CHUNK)
    pr = dot(lines[...], stacked_rows(table, size, re))
    pi = dot(lines[...], stacked_rows(table, size, im))
    response[:, :CHUNK] = pr
    response[:, CHUNK:] = pi
    halves = half_spectra(x, table, channels, windows - 1, turns, f)
    halves.append((last_half[:, re], last_half[:, im]))
    for w in range(windows):
        xr, xi = halves[w]
        xr, xi = turns.sign * xr, turns.sign * xi
        if w > 0:
            xr, xi = xr + halves[w - 1][0], xi + halves[w - 1][1]
        yr = xr * pr - xi * pi
        yi = xr * pi + xi * pr
        if w < windows - 1:
            rows = slice(w * channels, (w + 1) * channels)
            part[rows, :CHUNK] = yr
            part[rows, CHUNK:] = yi
        else:
            last[:, :CHUNK] = yr + dot(edge[...], stacked_rows(table, lag, re))
            last[:, CHUNK:] = yi + dot(edge[...], stacked_rows(table, lag, im))


def first_kernel(
    windows, traces, taps, table, last_half, part, response, last, ends, edge, lines, square, shifted
):
    channels, samples = traces.shape
    tap_count = taps.shape[0]
    square[...] = jnp.zeros_like(square)
    high, low = split_two(taps[...])
    high = high.astype(F32)
    size = square.shape[0] // 3
    for i, value in enumerate((high, low.astype(F32), high)):
        square[i * size : i * size + tap_count, :channels] = value
    lines[...] = square[...].T[:channels].astype(BF16)
    tile = 128
    for b in range(1, windows):
        ends[:, (b - 1) * tile : b * tile] = traces[:, b * HALF - tile : b * HALF]
    start = (windows - 2) * HALF
    apart = traces[:, start - tile : start].astype(F32) - traces[:, samples - tile :].astype(F32)
    edge[...] = end_terms(taps[...], shifted, tap_count, apart)
    own_chunk(windows, 0, traces, table, last_half, lines, edge, part, response, last)


def second_kernel(
    windows, traces, table, last_half, lines, edge, first, part, response, white, second, spectra
):
    own_chunk(windows, CHUNK, traces, table, last_half, lines, edge, part, response, second)
    for i, half in enumerate((first, second)):
        spectra[:, i * CHUNK : (i + 1) * CHUNK] = half[:, :CHUNK]
        spectra[:, NF + i * CHUNK : NF + (i + 1) * CHUNK] = half[:, CHUNK:]
    whiten_all(spectra, white, white.shape[0])


def part_rows(windows, pairs):
    return [-(-w * pairs // 8) * 8 for w in (windows - 1, 1)]


def picks_kernel(shape, counts, slots, *refs):
    channels, windows, pairs, chips = shape
    wanted, (picks, chosen, lines) = refs[:-3], refs[-3:]
    group = lax.axis_index("chan")
    place = lax.broadcasted_iota(jnp.int32, counts.shape, 1)
    held = counts[...].astype(F32)
    first = jnp.sum(jnp.where(place < group, held, 0.0), axis=1, keepdims=True)
    owned = jnp.sum(jnp.where(place == group, held, 0.0), axis=1, keepdims=True)
    row = lax.broadcasted_iota(jnp.int32, slots.shape, 0)
    own_slots = jnp.where(row == group, slots[...], 0).astype(F32)
    own_slots = jnp.sum(own_slots, axis=0, keepdims=True)
    lines[...] = jnp.zeros_like(lines)
    at = 0
    for w in wanted:
        lines[at : at + w.shape[0], :pairs] = w[...].astype(F32)
        at += w.shape[0]
    slot = lines[...] - first
    channel = jnp.full(slot.shape, -1.0, F32)
    for s in range(slots.shape[1]):
        channel = jnp.where(slot == s, own_slots[:, s : s + 1], channel)
    channel = jnp.where((slot >= 0) & (slot < owned), channel, -1.0)
    turned = channel.T
    width = windows * channels
    lane = lax.broadcasted_iota(jnp.int32, (1, width), 1)
    columns = [
        jnp.where(lane // channels == w, lane % channels, -2).astype(F32) for w in range(windows)
    ]
    sizes = part_rows(windows, pairs)
    chosen[...] = jnp.zeros_like(chosen)
    for core in range(2):
        for d in range(chips):
            base = (core * chips + d) * sum(sizes)
            one = turned[:pairs, 2 * d + core : 2 * d + core + 1]
            for w in range(windows):
                row = base + (w * pairs if w < windows - 1 else sizes[0])
                chosen[row : row + pairs, :] = (one == columns[w]).astype(F32)
    picks[...] = chosen[...].astype(BF16)


def rest_kernel(
    windows, times, halo, ends, taps, table, part_a, part_b, response_a, response_b, *refs
):
    own_white, picks, keep, send = refs[:4]
    blocks = refs[4 : 4 + times]
    shifted, spectra, white = refs[4 + times :]
    channels = response_a.shape[0]
    tap_count = taps.shape[0]
    tile = 128
    rest = windows - 1

    arrived = halo[:, 2 * NF :].astype(F32)
    before = [arrived, pltpu.roll(arrived, tap_count - 1, 1)]
    before += [ends[:, (b - 1) * tile : b * tile] for b in range(1, windows - 2)]
    after = [ends[:, w * tile : (w + 1) * tile] for w in range(rest)]
    apart = jnp.concatenate([b.astype(F32) - a.astype(F32) for b, a in zip(before, after)], axis=0)
    taps_wide = jnp.concatenate([taps[...]] * rest, axis=1)
    edge = end_terms(taps_wide, shifted, tap_count, apart)
    for f in range(0, NF, CHUNK):
        re = slice(f, f + CHUNK)
        im = slice(NF + f, NF + f + CHUNK)
        xr, xi = halo[:, re].astype(F32), halo[:, im].astype(F32)
        part, response = (part_b, response_b) if f else (part_a, response_a)
        pr, pi = response[:, :CHUNK], response[:, CHUNK:]
        er = dot(edge, stacked_rows(table, tap_count - 1, re))
        ei = dot(edge, stacked_rows(table, tap_count - 1, im))
        spectra[:channels, re] = part[:channels, :CHUNK] + er[:channels] + (xr * pr - xi * pi)
        spectra[:channels, im] = part[:channels, CHUNK:] + ei[:channels] + (xr * pi + xi * pr)
        spectra[channels:, re] = part[channels:, :CHUNK] + er[channels:]
        spectra[channels:, im] = part[channels:, CHUNK:] + ei[channels:]
    count = rest * channels
    whiten_all(spectra, white, count)
    white[count:, :] = own_white[...]
    base = keep.shape[0]
    size = channels // times
    choose = picks[...]
    for f in range(0, 2 * NF, CHUNK):
        cols = slice(f, f + CHUNK)
        out = dot(choose, white[:, cols]).astype(BF16)
        keep[:, cols] = out[:base]
        send[:, cols] = out[base:]
    for d in range(times):
        line = (lax.axis_index("tm") ^ d) * size
        for w in range(windows):
            if size % ROWS == 0:
                at = pl.multiple_of(w * channels + line, ROWS)
                blocks[d][w * size : (w + 1) * size, :] = white[pl.ds(at, size), :]
            else:
                row = lax.broadcasted_iota(jnp.int32, (size, channels), 0)
                col = lax.broadcasted_iota(jnp.int32, (size, channels), 1)
                move = (col == row + line).astype(F32).astype(BF16)
                moved = dot(move, white[w * channels : (w + 1) * channels, :])
                blocks[d][w * size : (w + 1) * size, :] = moved.astype(BF16)


def correlate_kernel(spans, pairs, factor, has_total, last, *refs):
    count = len(spans)
    receivers, sources = refs[:count], refs[count : 2 * count]
    total = refs[2 * count] if has_total else None
    out, line_r, line_s = refs[2 * count + has_total : 2 * count + has_total + 3]
    held, sems = refs[-2:] if last else (out, None)
    part = out.shape[1]
    windows = 0
    for receiver, source, span in zip(receivers, sources, spans):
        for i, w in enumerate(span):
            line_r[windows] = receiver[w].astype(F32) * factor
            rows = source[i * pairs : (i + 1) * pairs, :].astype(F32)
            for p in range(pairs):
                line_s[p, windows : windows + 1, :] = rows[p : p + 1, :]
            windows += 1

    def copy(p):
        return pltpu.make_async_copy(held.at[p], out.at[p], sems.at[p])

    def one(p, carry):
        for f in range(0, NF, 128):
            re = slice(f, f + 128)
            im = slice(NF + f, NF + f + 128)
            if has_total:
                total_r, total_i = total[p, :, re], total[p, :, im]
            else:
                total_r = jnp.zeros((part, 128), F32)
                total_i = jnp.zeros((part, 128), F32)
            for at in range(windows):
                rr = line_r[at, :, re]
                ri = line_r[at, :, im]
                sr = line_s[p, at : at + 1, re]
                si = line_s[p, at : at + 1, im]
                total_r = total_r + (sr * rr + si * ri)
                total_i = total_i + (sr * ri - si * rr)
            held[p, :, re] = total_r
            held[p, :, im] = total_i
        if last:
            copy(p).start()
        return carry

    lax.fori_loop(0, pairs, one, 0)
    if last:
        for p in range(pairs):
            copy(p).wait()


def correlate(receivers, sources, spans, total, pairs, factor, last):
    _, part, width = receivers[0].shape
    windows = sum(len(span) for span in spans)
    vmem = pl.BlockSpec(memory_space=pltpu.VMEM)
    shape = (pairs, part, width)
    extra = [] if total is None else [total]
    scratch = [
        pltpu.VMEM((windows, part, width), F32),
        pltpu.VMEM((pairs, -(-windows // 8) * 8, width), F32),
    ]
    if last:
        scratch += [pltpu.VMEM(shape, F32), pltpu.SemaphoreType.DMA((pairs,))]
    return pl.pallas_call(
        functools.partial(correlate_kernel, spans, pairs, factor, len(extra), last),
        out_shape=jax.ShapeDtypeStruct(shape, F32),
        in_specs=[vmem] * (2 * len(spans) + len(extra)),
        out_specs=pl.BlockSpec(memory_space=pltpu.HBM) if last else vmem,
        scratch_shapes=scratch,
        compiler_params=pltpu.CompilerParams(vmem_limit_bytes=LIMIT),
        name="correlate",
    )(*receivers, *sources, *extra)


def shards(traces, filter_taps, source_counts, source_channel, block_sources):
    channels, samples = traces.shape
    tap_count = filter_taps.shape[1]
    pairs = block_sources.shape[1]
    windows = samples // HALF
    groups = lax.axis_size("chan")
    times = lax.axis_size("tm")
    chips = groups // 2
    part = channels // times
    sizes = part_rows(windows, pairs)
    rows_out = chips * sum(sizes)

    def across(x, axis, distance):
        size = lax.axis_size(axis)
        return lax.ppermute(x, axis, [(i, i ^ distance) for i in range(size)])

    vmem = pl.BlockSpec(memory_space=pltpu.VMEM)
    hbm = pl.BlockSpec(memory_space=pltpu.HBM)
    params = pltpu.CompilerParams(vmem_limit_bytes=LIMIT)
    bits = [1 << b for b in range(chips.bit_length() - 1)]

    other = across(block_sources, "chan", 1)
    inputs = (traces, jnp.asarray(piece_table()), block_sources)
    message, last_half, table, ids = pl.pallas_call(
        functools.partial(load_kernel, tap_count - 1),
        out_shape=[
            jax.ShapeDtypeStruct((channels, 2 * NF + 128), BF16),
            jax.ShapeDtypeStruct((channels, 2 * NF), F32),
        ]
        + [jax.ShapeDtypeStruct(a.shape, a.dtype) for a in inputs[1:]],
        in_specs=[hbm] * 3,
        out_specs=[vmem] * 4,
        scratch_shapes=[
            pltpu.VMEM((channels, HALF + 128), BF16),
            pltpu.SemaphoreType.DMA((2 + 2 * NF // CHUNK,)),
        ],
        compiler_params=params,
        name="load",
    )(*(pltpu.with_memory_space_constraint(a, pltpu.HBM) for a in inputs))
    traces, taps = (
        pltpu.with_memory_space_constraint(a, pltpu.VMEM) for a in (traces, filter_taps.T)
    )
    wanted = [
        pl.pallas_call(
            pair_kernel,
            out_shape=jax.ShapeDtypeStruct((2, pairs), jnp.int32),
            in_specs=[vmem] * 2,
            out_specs=vmem,
            compiler_params=params,
            cost_estimate=pl.CostEstimate(flops=HINT, bytes_accessed=8 * pairs, transcendentals=0),
            name="pair",
        )(ids, other)
    ]
    halo = lax.ppermute(message, "tm", [(i - 1, i) for i in range(1, times)])
    for bit in bits:
        known = jnp.concatenate(wanted, axis=0)
        wanted = [known, across(known, "chan", 2 * bit)]

    shape = (channels, windows, pairs, chips)
    width = windows * channels
    chunk_shapes = [
        jax.ShapeDtypeStruct((width - channels, 2 * CHUNK), F32),
        jax.ShapeDtypeStruct((channels, 2 * CHUNK), F32),
    ]
    size = -(-tap_count // 16) * 16
    part_a, response_a, last, ends, edge, lines = pl.pallas_call(
        functools.partial(first_kernel, windows),
        out_shape=chunk_shapes
        + [
            chunk_shapes[1],
            jax.ShapeDtypeStruct((channels, (windows - 1) * 128), BF16),
            jax.ShapeDtypeStruct((channels, 3 * (tap_count - 1)), BF16),
            jax.ShapeDtypeStruct((channels, 3 * size), BF16),
        ],
        in_specs=[vmem] * 4,
        out_specs=[vmem] * 6,
        scratch_shapes=[
            pltpu.VMEM((3 * size, 128), F32),
            pltpu.VMEM((2 * tap_count + 6, channels), F32),
        ],
        compiler_params=params,
        name="first",
    )(traces, taps, table, last_half)
    part_b, response_b, own_white = pl.pallas_call(
        functools.partial(second_kernel, windows),
        out_shape=chunk_shapes + [jax.ShapeDtypeStruct((channels, 2 * NF), BF16)],
        in_specs=[vmem] * 6,
        out_specs=[vmem] * 3,
        scratch_shapes=[
            pltpu.VMEM((channels, 2 * CHUNK), F32),
            pltpu.VMEM((channels, 2 * NF), F32),
        ],
        compiler_params=params,
        name="second",
    )(traces, table, last_half, lines, edge, last)
    picks = pl.pallas_call(
        functools.partial(picks_kernel, shape),
        out_shape=jax.ShapeDtypeStruct((2 * rows_out, width), BF16),
        in_specs=[vmem] * (2 + len(wanted)),
        out_specs=vmem,
        scratch_shapes=[pltpu.VMEM((2 * rows_out, width), F32), pltpu.VMEM((2 * chips, 128), F32)],
        compiler_params=params,
        name="picks",
    )(source_counts[None], source_channel, *wanted)
    outs = pl.pallas_call(
        functools.partial(rest_kernel, windows, times),
        out_shape=[jax.ShapeDtypeStruct((rows_out, 2 * NF), BF16)] * 2
        + [jax.ShapeDtypeStruct((windows * part, 2 * NF), BF16)] * times,
        in_specs=[vmem] * 10,
        out_specs=[vmem] * (2 + times),
        scratch_shapes=[
            pltpu.VMEM((2 * tap_count + 6, width - channels), F32),
            pltpu.VMEM((width - channels, 2 * NF), F32),
            pltpu.VMEM((width, 2 * NF), BF16),
        ],
        compiler_params=params,
        name="rest",
    )(
        halo,
        ends,
        taps,
        table,
        part_a,
        part_b,
        response_a,
        response_b,
        own_white,
        picks,
    )
    keep, send, blocks = outs[0], outs[1], outs[2:]
    gathered = keep + across(send, "chan", 1)
    rows = sum(sizes)
    pieces = [gathered[d * rows : (d + 1) * rows] for d in range(chips)]
    pieces = list(lax.optimization_barrier(tuple(pieces)))
    for bit in bits:
        onward = [d for d in range(2 * bit, chips) if d & (2 * bit - 1) == bit]
        if onward:
            block = jnp.concatenate([pieces[d] for d in onward], axis=0)
            block = across(block, "chan", 2 * bit)
            for i, d in enumerate(onward):
                pieces[d ^ bit] = pieces[d ^ bit] + block[i * rows : (i + 1) * rows]
    mine = pieces[0]
    for bit in bits[:-1]:
        mine = mine + across(pieces[bit], "chan", 2 * bit)
    mine = [mine[: sizes[0]], mine[sizes[0] :]]
    if bits:
        last = pieces[bits[-1]]
        for i, x in enumerate((last[: sizes[0]], last[sizes[0] :])):
            mine[i] = mine[i] + across(x, "chan", 2 * bits[-1])
    receivers = [blocks[0]]
    for d in range(1, times):
        receivers.append(across(blocks[d], "tm", d))
    receivers = [r.reshape(windows, part, 2 * NF) for r in receivers]
    sources = [mine]
    for d in range(1, times):
        both = []
        for x in mine:
            both.append(across(x, "tm", d))
        sources.append(both)

    factor = 1.0 / (windows * times)
    early, late = tuple(range(windows - 1)), (windows - 1,)
    total = None
    for which in ([0], list(range(1, times))):
        for i, span in enumerate((early, late)):
            if which:
                last = i == 1 and which[-1] == times - 1
                total = correlate(
                    [receivers[d] for d in which],
                    [sources[d][i] for d in which],
                    (span,) * len(which),
                    total,
                    pairs,
                    factor,
                    last,
                )
    return total.transpose(1, 0, 2)


def solution(mesh):
    in_specs = (P(("seg", "chan"), "tm"), P("chan", None), P(), P(), P("chan", None))
    out_specs = P(("seg", "chan", "tm"), None, None)
    return jax.shard_map(shards, mesh=mesh, in_specs=in_specs, out_specs=out_specs, check_vma=False)
```

```python
import functools

import jax
import jax.numpy as jnp
import ml_dtypes
import numpy as np
from jax import lax
from jax.experimental import pallas as pl
from jax.experimental.pallas import tpu as pltpu
from jax.sharding import PartitionSpec as P


NFFT = 4096
NF = 512
F0 = 8
PIECE = NFFT // 8
HALF = NFFT // 2
CHUNK = 256
F32 = jnp.float32
BF16 = jnp.bfloat16
LIMIT = 24 * 1024 * 1024
HINT = 10**10


def piece_table():
    bins = F0 + np.arange(NF)
    angle = (bins * np.arange(PIECE)[:, None] % NFFT) * (2.0 * np.pi / NFFT)
    exact = np.concatenate([np.cos(angle), -np.sin(angle)], axis=1)
    high = exact.astype(ml_dtypes.bfloat16)
    low = (exact - high.astype(np.float64)).astype(ml_dtypes.bfloat16)
    both = np.concatenate([high, low], axis=0)
    starts = [c for f in range(0, NF, CHUNK) for c in (f, NF + f)]
    return np.stack([both[:, c : c + CHUNK] for c in starts])


def split_two(x):
    high = x.astype(BF16)
    low = (x - high.astype(F32)).astype(BF16)
    return high, low


def dot(a, b):
    return jnp.dot(a, b, preferred_element_type=F32)


def stacked_parts(x):
    high, low = split_two(x)
    high = high.astype(F32)
    return jnp.concatenate([high, low.astype(F32), high], axis=0)


def stacked_rows(table, rows, at):
    first = table[at, :rows, :]
    return jnp.concatenate([first, first, table[at, PIECE : PIECE + rows, :]], axis=0)


class Turns:
    def __init__(self):
        lane = lax.broadcasted_iota(jnp.int32, (1, CHUNK), 1)
        turn = lane % 4
        self.odd = (turn % 2) == 1
        self.sign = jnp.where(self.odd, -1.0, 1.0)
        self.real = jnp.where(turn < 2, 1.0, -1.0)
        self.imag = jnp.where((turn == 0) | (turn == 3), 1.0, -1.0)
        eighth = lane % 8
        root = np.float32(np.sqrt(0.5))
        self.cos = jnp.where(turn % 4 == 0, 1.0, jnp.where(turn == 2, 0.0, root))
        self.cos = jnp.where((eighth > 2) & (eighth < 6), -self.cos, self.cos)
        self.sin = jnp.where(turn == 2, 1.0, jnp.where(turn == 0, 0.0, root))
        self.sin = jnp.where(eighth < 4, -self.sin, self.sin)

    def quarter(self, ar, ai, br, bi):
        return (
            ar + self.real * jnp.where(self.odd, bi, br),
            ai + self.imag * jnp.where(self.odd, br, bi),
        )

    def half(self, re, im):
        ar, ai = self.quarter(re[0], im[0], re[2], im[2])
        br, bi = self.quarter(re[1], im[1], re[3], im[3])
        return ar + (br * self.cos - bi * self.sin), ai + (br * self.sin + bi * self.cos)


def half_spectra(x, table, channels, halves, turns, f):
    both = jnp.concatenate([x, x], axis=1)
    at = 2 * (f // CHUNK)
    dr = dot(both, table[at])
    di = dot(both, table[at + 1])
    out = []
    for b in range(halves):
        rows = [slice((4 * b + e) * channels, (4 * b + e + 1) * channels) for e in range(4)]
        out.append(turns.half([dr[r] for r in rows], [di[r] for r in rows]))
    return out


def end_terms(taps_wide, shifted, tap_count, ends):
    lag = tap_count - 1
    apart = ends.T
    size = apart.shape[0]
    shifted[...] = jnp.zeros_like(shifted)
    shifted[:tap_count, :] = taps_wide
    total = jnp.zeros((lag, apart.shape[1]), F32)
    for j in range(1, tap_count):
        total = total + shifted[j : j + lag, :] * apart[size - j : size - j + 1, :]
    return stacked_parts(total).T.astype(BF16)


def whiten_rows(re, im):
    rows = re.shape[0]
    place = lax.broadcasted_iota(jnp.int32, (rows, NF), 1)
    power = re * re + im * im
    smooth = power
    for s in (1, 2):
        smooth = smooth + jnp.where(place >= s, pltpu.roll(power, s, 1), 0.0)
        smooth = smooth + jnp.where(place < NF - s, pltpu.roll(power, NF - s, 1), 0.0)
    total = jnp.sum(power, axis=1, keepdims=True)
    scaling = lax.rsqrt(smooth * 0.2 + (total * (0.1 / NF) + 1e-06))
    return (re * scaling).astype(BF16), (im * scaling).astype(BF16)


ROWS = 16


def whiten_all(spectra, white, count):
    def step(i, carry):
        rows = pl.ds(pl.multiple_of(i * ROWS, ROWS), ROWS)
        re, im = whiten_rows(spectra[rows, :NF], spectra[rows, NF:])
        white[rows, :NF] = re
        white[rows, NF:] = im
        return carry

    lax.fori_loop(0, count // ROWS, step, 0, unroll=4)


def load_kernel(end, traces_in, table_in, ids_in, message, last_half, table, ids, traces, sems):
    channels, samples = traces.shape
    begin = traces_in.shape[1] - samples
    copies = [pltpu.make_async_copy(traces_in.at[:, begin:], traces, sems.at[0])]
    at = 1 + table.shape[0]
    for i in range(table.shape[0]):
        copies.append(pltpu.make_async_copy(table_in.at[i], table.at[i], sems.at[1 + i]))
    copies.append(pltpu.make_async_copy(ids_in, ids, sems.at[at]))
    for copy in copies:
        copy.start()
    copies[0].wait()
    lane = lax.broadcasted_iota(jnp.int32, (channels, 128), 1)
    final = pltpu.roll(traces[:, samples - 128 :].astype(F32), 128 - end, 1)
    tile = jnp.where(lane < 128 - end, final, traces[:, :128].astype(F32))
    message[:, 2 * NF :] = tile.astype(BF16)
    pieces = [samples - HALF + q * PIECE for q in range(HALF // PIECE)]
    x = jnp.concatenate([traces[:, p : p + PIECE] for p in pieces], axis=0)
    turns = Turns()
    for i, f in enumerate(range(0, NF, CHUNK)):
        re = slice(f, f + CHUNK)
        im = slice(NF + f, NF + f + CHUNK)
        copies[1 + 2 * i].wait()
        copies[2 + 2 * i].wait()
        xr, xi = half_spectra(x, table, channels, 1, turns, f)[0]
        last_half[:, re] = xr
        last_half[:, im] = xi
        message[:, re] = xr.astype(BF16)
        message[:, im] = xi.astype(BF16)
    for copy in copies[at:]:
        copy.wait()


def pair_kernel(mine, other, out):
    out[:1, :] = mine[...]
    out[1:, :] = other[...]


def own_chunk(windows, f, traces, table, last_half, lines, edge, part, response, last):
    channels, samples = traces.shape
    size = lines.shape[1] // 3
    lag = edge.shape[1] // 3
    pieces = (samples - HALF) // PIECE
    x = jnp.concatenate([traces[:, q * PIECE : (q + 1) * PIECE] for q in range(pieces)], axis=0)
    turns = Turns()
    re = slice(f, f + CHUNK)
    im = slice(NF + f, NF + f + CHUNK)
    at = 2 * (f // CHUNK)
    pr = dot(lines[...], stacked_rows(table, size, at))
    pi = dot(lines[...], stacked_rows(table, size, at + 1))
    response[:, :CHUNK] = pr
    response[:, CHUNK:] = pi
    halves = half_spectra(x, table, channels, windows - 1, turns, f)
    halves.append((last_half[:, re], last_half[:, im]))
    for w in range(windows):
        xr, xi = halves[w]
        xr, xi = turns.sign * xr, turns.sign * xi
        if w > 0:
            xr, xi = xr + halves[w - 1][0], xi + halves[w - 1][1]
        yr = xr * pr - xi * pi
        yi = xr * pi + xi * pr
        if w < windows - 1:
            rows = slice(w * channels, (w + 1) * channels)
            part[rows, :CHUNK] = yr
            part[rows, CHUNK:] = yi
        else:
            last[:, :CHUNK] = yr + dot(edge[...], stacked_rows(table, lag, at))
            last[:, CHUNK:] = yi + dot(edge[...], stacked_rows(table, lag, at + 1))


def first_kernel(
    windows, traces, taps, table, last_half, part, response, last, ends, edge, lines, square, shifted
):
    channels, samples = traces.shape
    tap_count = taps.shape[0]
    square[...] = jnp.zeros_like(square)
    high, low = split_two(taps[...])
    high = high.astype(F32)
    size = square.shape[0] // 3
    for i, value in enumerate((high, low.astype(F32), high)):
        square[i * size : i * size + tap_count, :channels] = value
    lines[...] = square[...].T[:channels].astype(BF16)
    tile = 128
    for b in range(1, windows):
        ends[:, (b - 1) * tile : b * tile] = traces[:, b * HALF - tile : b * HALF]
    start = (windows - 2) * HALF
    apart = traces[:, start - tile : start].astype(F32) - traces[:, samples - tile :].astype(F32)
    edge[...] = end_terms(taps[...], shifted, tap_count, apart)
    own_chunk(windows, 0, traces, table, last_half, lines, edge, part, response, last)


def second_kernel(
    windows, traces, table, last_half, lines, edge, first, part, response, white, second, spectra
):
    own_chunk(windows, CHUNK, traces, table, last_half, lines, edge, part, response, second)
    for i, half in enumerate((first, second)):
        spectra[:, i * CHUNK : (i + 1) * CHUNK] = half[:, :CHUNK]
        spectra[:, NF + i * CHUNK : NF + (i + 1) * CHUNK] = half[:, CHUNK:]
    whiten_all(spectra, white, white.shape[0])


def part_rows(windows, pairs):
    return [-(-w * pairs // 8) * 8 for w in (windows - 1, 1)]


def picks_kernel(shape, counts, slots, *refs):
    channels, windows, pairs, chips = shape
    wanted, (picks, chosen, lines) = refs[:-3], refs[-3:]
    group = lax.axis_index("chan")
    place = lax.broadcasted_iota(jnp.int32, counts.shape, 1)
    held = counts[...].astype(F32)
    first = jnp.sum(jnp.where(place < group, held, 0.0), axis=1, keepdims=True)
    owned = jnp.sum(jnp.where(place == group, held, 0.0), axis=1, keepdims=True)
    row = lax.broadcasted_iota(jnp.int32, slots.shape, 0)
    own_slots = jnp.where(row == group, slots[...], 0).astype(F32)
    own_slots = jnp.sum(own_slots, axis=0, keepdims=True)
    lines[...] = jnp.zeros_like(lines)
    at = 0
    for w in wanted:
        lines[at : at + w.shape[0], :pairs] = w[...].astype(F32)
        at += w.shape[0]
    slot = lines[...] - first
    channel = jnp.full(slot.shape, -1.0, F32)
    for s in range(slots.shape[1]):
        channel = jnp.where(slot == s, own_slots[:, s : s + 1], channel)
    channel = jnp.where((slot >= 0) & (slot < owned), channel, -1.0)
    turned = channel.T
    width = windows * channels
    lane = lax.broadcasted_iota(jnp.int32, (1, width), 1)
    columns = [
        jnp.where(lane // channels == w, lane % channels, -2).astype(F32) for w in range(windows)
    ]
    sizes = part_rows(windows, pairs)
    chosen[...] = jnp.zeros_like(chosen)
    for core in range(2):
        for d in range(chips):
            base = (core * chips + d) * sum(sizes)
            one = turned[:pairs, 2 * d + core : 2 * d + core + 1]
            for w in range(windows):
                row = base + (w * pairs if w < windows - 1 else sizes[0])
                chosen[row : row + pairs, :] = (one == columns[w]).astype(F32)
    picks[...] = chosen[...].astype(BF16)


def rest_kernel(
    windows, times, halo, ends, taps, table, part_a, part_b, response_a, response_b, *refs
):
    own_white, picks, keep, send = refs[:4]
    blocks = refs[4 : 4 + times]
    shifted, spectra, white = refs[4 + times :]
    channels = response_a.shape[0]
    tap_count = taps.shape[0]
    tile = 128
    rest = windows - 1

    arrived = halo[:, 2 * NF :].astype(F32)
    before = [arrived, pltpu.roll(arrived, tap_count - 1, 1)]
    before += [ends[:, (b - 1) * tile : b * tile] for b in range(1, windows - 2)]
    after = [ends[:, w * tile : (w + 1) * tile] for w in range(rest)]
    apart = jnp.concatenate([b.astype(F32) - a.astype(F32) for b, a in zip(before, after)], axis=0)
    taps_wide = jnp.concatenate([taps[...]] * rest, axis=1)
    edge = end_terms(taps_wide, shifted, tap_count, apart)
    for f in range(0, NF, CHUNK):
        re = slice(f, f + CHUNK)
        im = slice(NF + f, NF + f + CHUNK)
        xr, xi = halo[:, re].astype(F32), halo[:, im].astype(F32)
        part, response = (part_b, response_b) if f else (part_a, response_a)
        pr, pi = response[:, :CHUNK], response[:, CHUNK:]
        at = 2 * (f // CHUNK)
        er = dot(edge, stacked_rows(table, tap_count - 1, at))
        ei = dot(edge, stacked_rows(table, tap_count - 1, at + 1))
        spectra[:channels, re] = part[:channels, :CHUNK] + er[:channels] + (xr * pr - xi * pi)
        spectra[:channels, im] = part[:channels, CHUNK:] + ei[:channels] + (xr * pi + xi * pr)
        spectra[channels:, re] = part[channels:, :CHUNK] + er[channels:]
        spectra[channels:, im] = part[channels:, CHUNK:] + ei[channels:]
    count = rest * channels
    whiten_all(spectra, white, count)
    white[count:, :] = own_white[...]
    base = keep.shape[0]
    size = channels // times
    choose = picks[...]
    for f in range(0, 2 * NF, CHUNK):
        cols = slice(f, f + CHUNK)
        out = dot(choose, white[:, cols]).astype(BF16)
        keep[:, cols] = out[:base]
        send[:, cols] = out[base:]
    for d in range(times):
        line = (lax.axis_index("tm") ^ d) * size
        for w in range(windows):
            if size % ROWS == 0:
                at = pl.multiple_of(w * channels + line, ROWS)
                blocks[d][w * size : (w + 1) * size, :] = white[pl.ds(at, size), :]
            else:
                row = lax.broadcasted_iota(jnp.int32, (size, channels), 0)
                col = lax.broadcasted_iota(jnp.int32, (size, channels), 1)
                move = (col == row + line).astype(F32).astype(BF16)
                moved = dot(move, white[w * channels : (w + 1) * channels, :])
                blocks[d][w * size : (w + 1) * size, :] = moved.astype(BF16)


def correlate_kernel(spans, pairs, factor, has_total, last, *refs):
    count = len(spans)
    receivers, sources = refs[:count], refs[count : 2 * count]
    total = refs[2 * count] if has_total else None
    out, line_r, line_s = refs[2 * count + has_total : 2 * count + has_total + 3]
    held, sems = refs[-2:] if last else (out, None)
    part = out.shape[1]
    windows = 0
    for receiver, source, span in zip(receivers, sources, spans):
        for i, w in enumerate(span):
            line_r[windows] = receiver[w].astype(F32) * factor
            rows = source[i * pairs : (i + 1) * pairs, :].astype(F32)
            for p in range(pairs):
                line_s[p, windows : windows + 1, :] = rows[p : p + 1, :]
            windows += 1

    def copy(p):
        return pltpu.make_async_copy(held.at[p], out.at[p], sems.at[p])

    def one(p, carry):
        for f in range(0, NF, 128):
            re = slice(f, f + 128)
            im = slice(NF + f, NF + f + 128)
            if has_total:
                total_r, total_i = total[p, :, re], total[p, :, im]
            else:
                total_r = jnp.zeros((part, 128), F32)
                total_i = jnp.zeros((part, 128), F32)
            for at in range(windows):
                rr = line_r[at, :, re]
                ri = line_r[at, :, im]
                sr = line_s[p, at : at + 1, re]
                si = line_s[p, at : at + 1, im]
                total_r = total_r + (sr * rr + si * ri)
                total_i = total_i + (sr * ri - si * rr)
            held[p, :, re] = total_r
            held[p, :, im] = total_i
        if last:
            copy(p).start()
        return carry

    lax.fori_loop(0, pairs, one, 0, unroll=2 if pairs % 2 == 0 else 1)
    if last:
        for p in range(pairs):
            copy(p).wait()


def correlate(receivers, sources, spans, total, pairs, factor, last):
    _, part, width = receivers[0].shape
    windows = sum(len(span) for span in spans)
    vmem = pl.BlockSpec(memory_space=pltpu.VMEM)
    shape = (pairs, part, width)
    extra = [] if total is None else [total]
    scratch = [
        pltpu.VMEM((windows, part, width), F32),
        pltpu.VMEM((pairs, -(-windows // 8) * 8, width), F32),
    ]
    if last:
        scratch += [pltpu.VMEM(shape, F32), pltpu.SemaphoreType.DMA((pairs,))]
    return pl.pallas_call(
        functools.partial(correlate_kernel, spans, pairs, factor, len(extra), last),
        out_shape=jax.ShapeDtypeStruct(shape, F32),
        in_specs=[vmem] * (2 * len(spans) + len(extra)),
        out_specs=pl.BlockSpec(memory_space=pltpu.HBM) if last else vmem,
        scratch_shapes=scratch,
        compiler_params=pltpu.CompilerParams(vmem_limit_bytes=LIMIT),
        name="correlate",
    )(*receivers, *sources, *extra)


def shards(traces, filter_taps, source_counts, source_channel, block_sources):
    channels, samples = traces.shape
    tap_count = filter_taps.shape[1]
    pairs = block_sources.shape[1]
    windows = samples // HALF
    groups = lax.axis_size("chan")
    times = lax.axis_size("tm")
    chips = groups // 2
    part = channels // times
    sizes = part_rows(windows, pairs)
    rows_out = chips * sum(sizes)

    def across(x, axis, distance):
        size = lax.axis_size(axis)
        return lax.ppermute(x, axis, [(i, i ^ distance) for i in range(size)])

    vmem = pl.BlockSpec(memory_space=pltpu.VMEM)
    hbm = pl.BlockSpec(memory_space=pltpu.HBM)
    params = pltpu.CompilerParams(vmem_limit_bytes=LIMIT)
    bits = [1 << b for b in range(chips.bit_length() - 1)]

    other = across(block_sources, "chan", 1)
    inputs = (traces, jnp.asarray(piece_table()), block_sources)
    message, last_half, table, ids = pl.pallas_call(
        functools.partial(load_kernel, tap_count - 1),
        out_shape=[
            jax.ShapeDtypeStruct((channels, 2 * NF + 128), BF16),
            jax.ShapeDtypeStruct((channels, 2 * NF), F32),
        ]
        + [jax.ShapeDtypeStruct(a.shape, a.dtype) for a in inputs[1:]],
        in_specs=[hbm] * 3,
        out_specs=[vmem] * 4,
        scratch_shapes=[
            pltpu.VMEM((channels, HALF + 128), BF16),
            pltpu.SemaphoreType.DMA((2 + 2 * NF // CHUNK,)),
        ],
        compiler_params=params,
        name="load",
    )(*(pltpu.with_memory_space_constraint(a, pltpu.HBM) for a in inputs))
    traces, taps = (
        pltpu.with_memory_space_constraint(a, pltpu.VMEM) for a in (traces, filter_taps.T)
    )
    wanted = [
        pl.pallas_call(
            pair_kernel,
            out_shape=jax.ShapeDtypeStruct((2, pairs), jnp.int32),
            in_specs=[vmem] * 2,
            out_specs=vmem,
            compiler_params=params,
            cost_estimate=pl.CostEstimate(flops=HINT, bytes_accessed=8 * pairs, transcendentals=0),
            name="pair",
        )(ids, other)
    ]
    halo = lax.ppermute(message, "tm", [(i - 1, i) for i in range(1, times)])
    for bit in bits:
        known = jnp.concatenate(wanted, axis=0)
        wanted = [known, across(known, "chan", 2 * bit)]

    shape = (channels, windows, pairs, chips)
    width = windows * channels
    chunk_shapes = [
        jax.ShapeDtypeStruct((width - channels, 2 * CHUNK), F32),
        jax.ShapeDtypeStruct((channels, 2 * CHUNK), F32),
    ]
    size = -(-tap_count // 16) * 16
    part_a, response_a, last, ends, edge, lines = pl.pallas_call(
        functools.partial(first_kernel, windows),
        out_shape=chunk_shapes
        + [
            chunk_shapes[1],
            jax.ShapeDtypeStruct((channels, (windows - 1) * 128), BF16),
            jax.ShapeDtypeStruct((channels, 3 * (tap_count - 1)), BF16),
            jax.ShapeDtypeStruct((channels, 3 * size), BF16),
        ],
        in_specs=[vmem] * 4,
        out_specs=[vmem] * 6,
        scratch_shapes=[
            pltpu.VMEM((3 * size, 128), F32),
            pltpu.VMEM((2 * tap_count + 6, channels), F32),
        ],
        compiler_params=params,
        name="first",
    )(traces, taps, table, last_half)
    part_b, response_b, own_white = pl.pallas_call(
        functools.partial(second_kernel, windows),
        out_shape=chunk_shapes + [jax.ShapeDtypeStruct((channels, 2 * NF), BF16)],
        in_specs=[vmem] * 6,
        out_specs=[vmem] * 3,
        scratch_shapes=[
            pltpu.VMEM((channels, 2 * CHUNK), F32),
            pltpu.VMEM((channels, 2 * NF), F32),
        ],
        compiler_params=params,
        name="second",
    )(traces, table, last_half, lines, edge, last)
    picks = pl.pallas_call(
        functools.partial(picks_kernel, shape),
        out_shape=jax.ShapeDtypeStruct((2 * rows_out, width), BF16),
        in_specs=[vmem] * (2 + len(wanted)),
        out_specs=vmem,
        scratch_shapes=[pltpu.VMEM((2 * rows_out, width), F32), pltpu.VMEM((2 * chips, 128), F32)],
        compiler_params=params,
        name="picks",
    )(source_counts[None], source_channel, *wanted)
    outs = pl.pallas_call(
        functools.partial(rest_kernel, windows, times),
        out_shape=[jax.ShapeDtypeStruct((rows_out, 2 * NF), BF16)] * 2
        + [jax.ShapeDtypeStruct((windows * part, 2 * NF), BF16)] * times,
        in_specs=[vmem] * 10,
        out_specs=[vmem] * (2 + times),
        scratch_shapes=[
            pltpu.VMEM((2 * tap_count + 6, width - channels), F32),
            pltpu.VMEM((width - channels, 2 * NF), F32),
            pltpu.VMEM((width, 2 * NF), BF16),
        ],
        compiler_params=params,
        name="rest",
    )(
        halo,
        ends,
        taps,
        table,
        part_a,
        part_b,
        response_a,
        response_b,
        own_white,
        picks,
    )
    keep, send, blocks = outs[0], outs[1], outs[2:]
    gathered = keep + across(send, "chan", 1)
    rows = sum(sizes)
    pieces = [gathered[d * rows : (d + 1) * rows] for d in range(chips)]
    pieces = list(lax.optimization_barrier(tuple(pieces)))
    for bit in bits:
        onward = [d for d in range(2 * bit, chips) if d & (2 * bit - 1) == bit]
        if onward:
            block = jnp.concatenate([pieces[d] for d in onward], axis=0)
            block = across(block, "chan", 2 * bit)
            for i, d in enumerate(onward):
                pieces[d ^ bit] = pieces[d ^ bit] + block[i * rows : (i + 1) * rows]
    mine = pieces[0]
    for bit in bits[:-1]:
        mine = mine + across(pieces[bit], "chan", 2 * bit)
    mine = [mine[: sizes[0]], mine[sizes[0] :]]
    if bits:
        last = pieces[bits[-1]]
        for i, x in enumerate((last[: sizes[0]], last[sizes[0] :])):
            mine[i] = mine[i] + across(x, "chan", 2 * bits[-1])
    receivers = [blocks[0]]
    for d in range(1, times):
        receivers.append(across(blocks[d], "tm", d))
    receivers = [r.reshape(windows, part, 2 * NF) for r in receivers]
    sources = [mine]
    for d in range(1, times):
        both = []
        for x in mine:
            both.append(across(x, "tm", d))
        sources.append(both)

    factor = 1.0 / (windows * times)
    early, late = tuple(range(windows - 1)), (windows - 1,)
    total = None
    for which in ([0], list(range(1, times))):
        for i, span in enumerate((early, late)):
            if which:
                last = i == 1 and which[-1] == times - 1
                total = correlate(
                    [receivers[d] for d in which],
                    [sources[d][i] for d in which],
                    (span,) * len(which),
                    total,
                    pairs,
                    factor,
                    last,
                )
    return total.transpose(1, 0, 2)


def solution(mesh):
    in_specs = (P(("seg", "chan"), "tm"), P("chan", None), P(), P(), P("chan", None))
    out_specs = P(("seg", "chan", "tm"), None, None)
    return jax.shard_map(shards, mesh=mesh, in_specs=in_specs, out_specs=out_specs, check_vma=False)
```

```python
import functools

import jax
import jax.numpy as jnp
import ml_dtypes
import numpy as np
from jax import lax
from jax.experimental import pallas as pl
from jax.experimental.pallas import tpu as pltpu
from jax.sharding import PartitionSpec as P


NFFT = 4096
NF = 512
F0 = 8
PIECE = NFFT // 8
HALF = NFFT // 2
CHUNK = 256
F32 = jnp.float32
BF16 = jnp.bfloat16
LIMIT = 24 * 1024 * 1024
HINT = 10**10


def piece_table(size):
    bins = F0 + np.arange(NF)
    angle = (bins * np.arange(size)[:, None] % NFFT) * (2.0 * np.pi / NFFT)
    exact = np.concatenate([np.cos(angle), -np.sin(angle)], axis=1)
    high = exact.astype(ml_dtypes.bfloat16)
    low = (exact - high.astype(np.float64)).astype(ml_dtypes.bfloat16)
    both = np.concatenate([high, low], axis=0)
    starts = [c for f in range(0, NF, CHUNK) for c in (f, NF + f)]
    return np.stack([both[:, c : c + CHUNK] for c in starts])


def split_two(x):
    high = x.astype(BF16)
    low = (x - high.astype(F32)).astype(BF16)
    return high, low


def dot(a, b):
    return jnp.dot(a, b, preferred_element_type=F32)


def stacked_parts(x):
    high, low = split_two(x)
    high = high.astype(F32)
    return jnp.concatenate([high, low.astype(F32), high], axis=0)


def stacked_rows(table, rows, at):
    first = table[at, :rows, :]
    return jnp.concatenate([first, first, table[at, PIECE : PIECE + rows, :]], axis=0)


class Turns:
    def __init__(self):
        lane = lax.broadcasted_iota(jnp.int32, (1, CHUNK), 1)
        turn = lane % 4
        self.odd = (turn % 2) == 1
        self.sign = jnp.where(self.odd, -1.0, 1.0)
        self.real = jnp.where(turn < 2, 1.0, -1.0)
        self.imag = jnp.where((turn == 0) | (turn == 3), 1.0, -1.0)
        eighth = lane % 8
        root = np.float32(np.sqrt(0.5))
        self.cos = jnp.where(turn % 4 == 0, 1.0, jnp.where(turn == 2, 0.0, root))
        self.cos = jnp.where((eighth > 2) & (eighth < 6), -self.cos, self.cos)
        self.sin = jnp.where(turn == 2, 1.0, jnp.where(turn == 0, 0.0, root))
        self.sin = jnp.where(eighth < 4, -self.sin, self.sin)

    def quarter(self, ar, ai, br, bi):
        return (
            ar + self.real * jnp.where(self.odd, bi, br),
            ai + self.imag * jnp.where(self.odd, br, bi),
        )

    def eighth(self, ar, ai, br, bi):
        return ar + (br * self.cos - bi * self.sin), ai + (br * self.sin + bi * self.cos)

    def half(self, re, im):
        a = self.quarter(re[0], im[0], re[2], im[2])
        b = self.quarter(re[1], im[1], re[3], im[3])
        return self.eighth(*a, *b)

    def half_of_eight(self, re, im):
        quarters = [self.quarter(re[e], im[e], re[e + 4], im[e + 4]) for e in range(4)]
        ar, ai = self.eighth(*quarters[0], *quarters[2])
        br, bi = self.eighth(*quarters[1], *quarters[3])
        lane = lax.broadcasted_iota(jnp.int32, (1, CHUNK), 1) % 16
        cos, sin = jnp.zeros((1, CHUNK), F32), jnp.zeros((1, CHUNK), F32)
        for k in range(16):
            angle = 2.0 * np.pi * ((F0 + k) % 16) / 16
            cos = jnp.where(lane == k, np.float32(np.cos(angle)), cos)
            sin = jnp.where(lane == k, np.float32(-np.sin(angle)), sin)
        return ar + (br * cos - bi * sin), ai + (br * sin + bi * cos)


def half_spectra(x, table, channels, halves, turns, f):
    both = jnp.concatenate([x, x], axis=1)
    at = 2 * (f // CHUNK)
    dr = dot(both, table[at])
    di = dot(both, table[at + 1])
    out = []
    for b in range(halves):
        rows = [slice((4 * b + e) * channels, (4 * b + e + 1) * channels) for e in range(4)]
        out.append(turns.half([dr[r] for r in rows], [di[r] for r in rows]))
    return out


def end_terms(taps_wide, shifted, tap_count, ends):
    lag = tap_count - 1
    apart = ends.T
    size = apart.shape[0]
    shifted[...] = jnp.zeros_like(shifted)
    shifted[:tap_count, :] = taps_wide
    total = jnp.zeros((lag, apart.shape[1]), F32)
    for j in range(1, tap_count):
        total = total + shifted[j : j + lag, :] * apart[size - j : size - j + 1, :]
    return stacked_parts(total).T.astype(BF16)


def whiten_rows(re, im):
    rows = re.shape[0]
    place = lax.broadcasted_iota(jnp.int32, (rows, NF), 1)
    power = re * re + im * im
    smooth = power
    for s in (1, 2):
        smooth = smooth + jnp.where(place >= s, pltpu.roll(power, s, 1), 0.0)
        smooth = smooth + jnp.where(place < NF - s, pltpu.roll(power, NF - s, 1), 0.0)
    total = jnp.sum(power, axis=1, keepdims=True)
    scaling = lax.rsqrt(smooth * 0.2 + (total * (0.1 / NF) + 1e-06))
    return (re * scaling).astype(BF16), (im * scaling).astype(BF16)


ROWS = 16


def whiten_all(spectra, white, count):
    def step(i, carry):
        rows = pl.ds(pl.multiple_of(i * ROWS, ROWS), ROWS)
        re, im = whiten_rows(spectra[rows, :NF], spectra[rows, NF:])
        white[rows, :NF] = re
        white[rows, NF:] = im
        return carry

    lax.fori_loop(0, count // ROWS, step, 0, unroll=4)


def load_kernel(end, traces_in, table_in, ids_in, message, last_half, ids, traces, table, sems):
    channels, samples = traces.shape
    begin = traces_in.shape[1] - samples
    copies = [pltpu.make_async_copy(traces_in.at[:, begin:], traces, sems.at[0])]
    at = 1 + table.shape[0]
    for i in range(table.shape[0]):
        copies.append(pltpu.make_async_copy(table_in.at[i], table.at[i], sems.at[1 + i]))
    copies.append(pltpu.make_async_copy(ids_in, ids, sems.at[at]))
    for copy in copies:
        copy.start()
    copies[0].wait()
    lane = lax.broadcasted_iota(jnp.int32, (channels, 128), 1)
    final = pltpu.roll(traces[:, samples - 128 :].astype(F32), 128 - end, 1)
    tile = jnp.where(lane < 128 - end, final, traces[:, :128].astype(F32))
    message[:, 2 * NF :] = tile.astype(BF16)
    size = table.shape[1] // 2
    starts = range(samples - HALF, samples, size)
    x = jnp.concatenate([traces[:, p : p + size] for p in starts], axis=0)
    both = jnp.concatenate([x, x], axis=1)
    rows = [slice(e * channels, (e + 1) * channels) for e in range(HALF // size)]
    turns = Turns()
    for i, f in enumerate(range(0, NF, CHUNK)):
        re = slice(f, f + CHUNK)
        im = slice(NF + f, NF + f + CHUNK)
        copies[1 + 2 * i].wait()
        copies[2 + 2 * i].wait()
        dr = dot(both, table[2 * i])
        di = dot(both, table[2 * i + 1])
        xr, xi = turns.half_of_eight([dr[r] for r in rows], [di[r] for r in rows])
        last_half[:, re] = xr
        last_half[:, im] = xi
        message[:, re] = xr.astype(BF16)
        message[:, im] = xi.astype(BF16)
    for copy in copies[at:]:
        copy.wait()


def pair_kernel(mine, other, out):
    out[:1, :] = mine[...]
    out[1:, :] = other[...]


def own_chunk(windows, f, traces, table, last_half, lines, edge, part, response, last):
    channels, samples = traces.shape
    size = lines.shape[1] // 3
    lag = edge.shape[1] // 3
    pieces = (samples - HALF) // PIECE
    x = jnp.concatenate([traces[:, q * PIECE : (q + 1) * PIECE] for q in range(pieces)], axis=0)
    turns = Turns()
    re = slice(f, f + CHUNK)
    im = slice(NF + f, NF + f + CHUNK)
    at = 2 * (f // CHUNK)
    pr = dot(lines[...], stacked_rows(table, size, at))
    pi = dot(lines[...], stacked_rows(table, size, at + 1))
    response[:, :CHUNK] = pr
    response[:, CHUNK:] = pi
    halves = half_spectra(x, table, channels, windows - 1, turns, f)
    halves.append((last_half[:, re], last_half[:, im]))
    for w in range(windows):
        xr, xi = halves[w]
        xr, xi = turns.sign * xr, turns.sign * xi
        if w > 0:
            xr, xi = xr + halves[w - 1][0], xi + halves[w - 1][1]
        yr = xr * pr - xi * pi
        yi = xr * pi + xi * pr
        if w < windows - 1:
            rows = slice(w * channels, (w + 1) * channels)
            part[rows, :CHUNK] = yr
            part[rows, CHUNK:] = yi
        else:
            last[:, :CHUNK] = yr + dot(edge[...], stacked_rows(table, lag, at))
            last[:, CHUNK:] = yi + dot(edge[...], stacked_rows(table, lag, at + 1))


def first_kernel(
    windows, traces, taps, table, last_half, part, response, last, ends, edge, lines, square, shifted
):
    channels, samples = traces.shape
    tap_count = taps.shape[0]
    square[...] = jnp.zeros_like(square)
    high, low = split_two(taps[...])
    high = high.astype(F32)
    size = square.shape[0] // 3
    for i, value in enumerate((high, low.astype(F32), high)):
        square[i * size : i * size + tap_count, :channels] = value
    lines[...] = square[...].T[:channels].astype(BF16)
    tile = 128
    for b in range(1, windows):
        ends[:, (b - 1) * tile : b * tile] = traces[:, b * HALF - tile : b * HALF]
    start = (windows - 2) * HALF
    apart = traces[:, start - tile : start].astype(F32) - traces[:, samples - tile :].astype(F32)
    edge[...] = end_terms(taps[...], shifted, tap_count, apart)
    own_chunk(windows, 0, traces, table, last_half, lines, edge, part, response, last)


def second_kernel(
    windows, traces, table, last_half, lines, edge, first, part, response, white, second, spectra
):
    own_chunk(windows, CHUNK, traces, table, last_half, lines, edge, part, response, second)
    for i, half in enumerate((first, second)):
        spectra[:, i * CHUNK : (i + 1) * CHUNK] = half[:, :CHUNK]
        spectra[:, NF + i * CHUNK : NF + (i + 1) * CHUNK] = half[:, CHUNK:]
    whiten_all(spectra, white, white.shape[0])


def part_rows(windows, pairs):
    return [-(-w * pairs // 8) * 8 for w in (windows - 1, 1)]


def picks_kernel(shape, counts, slots, *refs):
    channels, windows, pairs, chips = shape
    wanted, (picks, chosen, lines) = refs[:-3], refs[-3:]
    group = lax.axis_index("chan")
    place = lax.broadcasted_iota(jnp.int32, counts.shape, 1)
    held = counts[...].astype(F32)
    first = jnp.sum(jnp.where(place < group, held, 0.0), axis=1, keepdims=True)
    owned = jnp.sum(jnp.where(place == group, held, 0.0), axis=1, keepdims=True)
    row = lax.broadcasted_iota(jnp.int32, slots.shape, 0)
    own_slots = jnp.where(row == group, slots[...], 0).astype(F32)
    own_slots = jnp.sum(own_slots, axis=0, keepdims=True)
    lines[...] = jnp.zeros_like(lines)
    at = 0
    for w in wanted:
        lines[at : at + w.shape[0], :pairs] = w[...].astype(F32)
        at += w.shape[0]
    slot = lines[...] - first
    channel = jnp.full(slot.shape, -1.0, F32)
    for s in range(slots.shape[1]):
        channel = jnp.where(slot == s, own_slots[:, s : s + 1], channel)
    channel = jnp.where((slot >= 0) & (slot < owned), channel, -1.0)
    turned = channel.T
    width = windows * channels
    lane = lax.broadcasted_iota(jnp.int32, (1, width), 1)
    columns = [
        jnp.where(lane // channels == w, lane % channels, -2).astype(F32) for w in range(windows)
    ]
    sizes = part_rows(windows, pairs)
    chosen[...] = jnp.zeros_like(chosen)
    for core in range(2):
        for d in range(chips):
            base = (core * chips + d) * sum(sizes)
            one = turned[:pairs, 2 * d + core : 2 * d + core + 1]
            for w in range(windows):
                row = base + (w * pairs if w < windows - 1 else sizes[0])
                chosen[row : row + pairs, :] = (one == columns[w]).astype(F32)
    picks[...] = chosen[...].astype(BF16)


def rest_kernel(
    windows, times, halo, ends, taps, table, part_a, part_b, response_a, response_b, *refs
):
    own_white, picks, keep, send = refs[:4]
    blocks = refs[4 : 4 + times]
    shifted, spectra, white = refs[4 + times :]
    channels = response_a.shape[0]
    tap_count = taps.shape[0]
    tile = 128
    rest = windows - 1

    arrived = halo[:, 2 * NF :].astype(F32)
    before = [arrived, pltpu.roll(arrived, tap_count - 1, 1)]
    before += [ends[:, (b - 1) * tile : b * tile] for b in range(1, windows - 2)]
    after = [ends[:, w * tile : (w + 1) * tile] for w in range(rest)]
    apart = jnp.concatenate([b.astype(F32) - a.astype(F32) for b, a in zip(before, after)], axis=0)
    taps_wide = jnp.concatenate([taps[...]] * rest, axis=1)
    edge = end_terms(taps_wide, shifted, tap_count, apart)
    for f in range(0, NF, CHUNK):
        re = slice(f, f + CHUNK)
        im = slice(NF + f, NF + f + CHUNK)
        xr, xi = halo[:, re].astype(F32), halo[:, im].astype(F32)
        part, response = (part_b, response_b) if f else (part_a, response_a)
        pr, pi = response[:, :CHUNK], response[:, CHUNK:]
        at = 2 * (f // CHUNK)
        er = dot(edge, stacked_rows(table, tap_count - 1, at))
        ei = dot(edge, stacked_rows(table, tap_count - 1, at + 1))
        spectra[:channels, re] = part[:channels, :CHUNK] + er[:channels] + (xr * pr - xi * pi)
        spectra[:channels, im] = part[:channels, CHUNK:] + ei[:channels] + (xr * pi + xi * pr)
        spectra[channels:, re] = part[channels:, :CHUNK] + er[channels:]
        spectra[channels:, im] = part[channels:, CHUNK:] + ei[channels:]
    count = rest * channels
    whiten_all(spectra, white, count)
    white[count:, :] = own_white[...]
    base = keep.shape[0]
    size = channels // times
    choose = picks[...]
    for f in range(0, 2 * NF, CHUNK):
        cols = slice(f, f + CHUNK)
        out = dot(choose, white[:, cols]).astype(BF16)
        keep[:, cols] = out[:base]
        send[:, cols] = out[base:]
    for d in range(times):
        line = (lax.axis_index("tm") ^ d) * size
        for w in range(windows):
            if size % ROWS == 0:
                at = pl.multiple_of(w * channels + line, ROWS)
                blocks[d][w * size : (w + 1) * size, :] = white[pl.ds(at, size), :]
            else:
                row = lax.broadcasted_iota(jnp.int32, (size, channels), 0)
                col = lax.broadcasted_iota(jnp.int32, (size, channels), 1)
                move = (col == row + line).astype(F32).astype(BF16)
                moved = dot(move, white[w * channels : (w + 1) * channels, :])
                blocks[d][w * size : (w + 1) * size, :] = moved.astype(BF16)


def correlate_kernel(spans, pairs, factor, has_total, last, *refs):
    count = len(spans)
    receivers, sources = refs[:count], refs[count : 2 * count]
    total = refs[2 * count] if has_total else None
    out, line_r, line_s = refs[2 * count + has_total : 2 * count + has_total + 3]
    held, sems = refs[-2:] if last else (out, None)
    part = out.shape[1]
    windows = 0
    for receiver, source, span in zip(receivers, sources, spans):
        for i, w in enumerate(span):
            line_r[windows] = receiver[w].astype(F32) * factor
            rows = source[i * pairs : (i + 1) * pairs, :].astype(F32)
            for p in range(pairs):
                line_s[p, windows : windows + 1, :] = rows[p : p + 1, :]
            windows += 1

    def copy(p):
        return pltpu.make_async_copy(held.at[p], out.at[p], sems.at[p])

    def one(p, carry):
        for f in range(0, NF, 128):
            re = slice(f, f + 128)
            im = slice(NF + f, NF + f + 128)
            if has_total:
                total_r, total_i = total[p, :, re], total[p, :, im]
            else:
                total_r = jnp.zeros((part, 128), F32)
                total_i = jnp.zeros((part, 128), F32)
            for at in range(windows):
                rr = line_r[at, :, re]
                ri = line_r[at, :, im]
                sr = line_s[p, at : at + 1, re]
                si = line_s[p, at : at + 1, im]
                total_r = total_r + (sr * rr + si * ri)
                total_i = total_i + (sr * ri - si * rr)
            held[p, :, re] = total_r
            held[p, :, im] = total_i
        if last:
            copy(p).start()
        return carry

    lax.fori_loop(0, pairs, one, 0, unroll=2 if pairs % 2 == 0 else 1)
    if last:
        for p in range(pairs):
            copy(p).wait()


def correlate(receivers, sources, spans, total, pairs, factor, last):
    _, part, width = receivers[0].shape
    windows = sum(len(span) for span in spans)
    vmem = pl.BlockSpec(memory_space=pltpu.VMEM)
    shape = (pairs, part, width)
    extra = [] if total is None else [total]
    scratch = [
        pltpu.VMEM((windows, part, width), F32),
        pltpu.VMEM((pairs, -(-windows // 8) * 8, width), F32),
    ]
    if last:
        scratch += [pltpu.VMEM(shape, F32), pltpu.SemaphoreType.DMA((pairs,))]
    return pl.pallas_call(
        functools.partial(correlate_kernel, spans, pairs, factor, len(extra), last),
        out_shape=jax.ShapeDtypeStruct(shape, F32),
        in_specs=[vmem] * (2 * len(spans) + len(extra)),
        out_specs=pl.BlockSpec(memory_space=pltpu.HBM) if last else vmem,
        scratch_shapes=scratch,
        compiler_params=pltpu.CompilerParams(vmem_limit_bytes=LIMIT),
        name="correlate",
    )(*receivers, *sources, *extra)


def shards(traces, filter_taps, source_counts, source_channel, block_sources):
    channels, samples = traces.shape
    tap_count = filter_taps.shape[1]
    pairs = block_sources.shape[1]
    windows = samples // HALF
    groups = lax.axis_size("chan")
    times = lax.axis_size("tm")
    chips = groups // 2
    part = channels // times
    sizes = part_rows(windows, pairs)
    rows_out = chips * sum(sizes)

    def across(x, axis, distance):
        size = lax.axis_size(axis)
        return lax.ppermute(x, axis, [(i, i ^ distance) for i in range(size)])

    vmem = pl.BlockSpec(memory_space=pltpu.VMEM)
    hbm = pl.BlockSpec(memory_space=pltpu.HBM)
    params = pltpu.CompilerParams(vmem_limit_bytes=LIMIT)
    bits = [1 << b for b in range(chips.bit_length() - 1)]

    other = across(block_sources, "chan", 1)
    inputs = (traces, jnp.asarray(piece_table(PIECE // 2)), block_sources)
    message, last_half, ids = pl.pallas_call(
        functools.partial(load_kernel, tap_count - 1),
        out_shape=[
            jax.ShapeDtypeStruct((channels, 2 * NF + 128), BF16),
            jax.ShapeDtypeStruct((channels, 2 * NF), F32),
            jax.ShapeDtypeStruct(block_sources.shape, jnp.int32),
        ],
        in_specs=[hbm] * 3,
        out_specs=[vmem] * 3,
        scratch_shapes=[
            pltpu.VMEM((channels, HALF + 128), BF16),
            pltpu.VMEM(inputs[1].shape, BF16),
            pltpu.SemaphoreType.DMA((2 + 2 * NF // CHUNK,)),
        ],
        compiler_params=params,
        name="load",
    )(*(pltpu.with_memory_space_constraint(a, pltpu.HBM) for a in inputs))
    traces, taps, table = (
        pltpu.with_memory_space_constraint(a, pltpu.VMEM)
        for a in (traces, filter_taps.T, jnp.asarray(piece_table(PIECE)))
    )
    wanted = [
        pl.pallas_call(
            pair_kernel,
            out_shape=jax.ShapeDtypeStruct((2, pairs), jnp.int32),
            in_specs=[vmem] * 2,
            out_specs=vmem,
            compiler_params=params,
            cost_estimate=pl.CostEstimate(flops=HINT, bytes_accessed=8 * pairs, transcendentals=0),
            name="pair",
        )(ids, other)
    ]
    halo = lax.ppermute(message, "tm", [(i - 1, i) for i in range(1, times)])
    for bit in bits:
        known = jnp.concatenate(wanted, axis=0)
        wanted = [known, across(known, "chan", 2 * bit)]

    shape = (channels, windows, pairs, chips)
    width = windows * channels
    chunk_shapes = [
        jax.ShapeDtypeStruct((width - channels, 2 * CHUNK), F32),
        jax.ShapeDtypeStruct((channels, 2 * CHUNK), F32),
    ]
    size = -(-tap_count // 16) * 16
    part_a, response_a, last, ends, edge, lines = pl.pallas_call(
        functools.partial(first_kernel, windows),
        out_shape=chunk_shapes
        + [
            chunk_shapes[1],
            jax.ShapeDtypeStruct((channels, (windows - 1) * 128), BF16),
            jax.ShapeDtypeStruct((channels, 3 * (tap_count - 1)), BF16),
            jax.ShapeDtypeStruct((channels, 3 * size), BF16),
        ],
        in_specs=[vmem] * 4,
        out_specs=[vmem] * 6,
        scratch_shapes=[
            pltpu.VMEM((3 * size, 128), F32),
            pltpu.VMEM((2 * tap_count + 6, channels), F32),
        ],
        compiler_params=params,
        name="first",
    )(traces, taps, table, last_half)
    part_b, response_b, own_white = pl.pallas_call(
        functools.partial(second_kernel, windows),
        out_shape=chunk_shapes + [jax.ShapeDtypeStruct((channels, 2 * NF), BF16)],
        in_specs=[vmem] * 6,
        out_specs=[vmem] * 3,
        scratch_shapes=[
            pltpu.VMEM((channels, 2 * CHUNK), F32),
            pltpu.VMEM((channels, 2 * NF), F32),
        ],
        compiler_params=params,
        name="second",
    )(traces, table, last_half, lines, edge, last)
    picks = pl.pallas_call(
        functools.partial(picks_kernel, shape),
        out_shape=jax.ShapeDtypeStruct((2 * rows_out, width), BF16),
        in_specs=[vmem] * (2 + len(wanted)),
        out_specs=vmem,
        scratch_shapes=[pltpu.VMEM((2 * rows_out, width), F32), pltpu.VMEM((2 * chips, 128), F32)],
        compiler_params=params,
        name="picks",
    )(source_counts[None], source_channel, *wanted)
    outs = pl.pallas_call(
        functools.partial(rest_kernel, windows, times),
        out_shape=[jax.ShapeDtypeStruct((rows_out, 2 * NF), BF16)] * 2
        + [jax.ShapeDtypeStruct((windows * part, 2 * NF), BF16)] * times,
        in_specs=[vmem] * 10,
        out_specs=[vmem] * (2 + times),
        scratch_shapes=[
            pltpu.VMEM((2 * tap_count + 6, width - channels), F32),
            pltpu.VMEM((width - channels, 2 * NF), F32),
            pltpu.VMEM((width, 2 * NF), BF16),
        ],
        compiler_params=params,
        name="rest",
    )(
        halo,
        ends,
        taps,
        table,
        part_a,
        part_b,
        response_a,
        response_b,
        own_white,
        picks,
    )
    keep, send, blocks = outs[0], outs[1], outs[2:]
    gathered = keep + across(send, "chan", 1)
    rows = sum(sizes)
    pieces = [gathered[d * rows : (d + 1) * rows] for d in range(chips)]
    pieces = list(lax.optimization_barrier(tuple(pieces)))
    for bit in bits:
        onward = [d for d in range(2 * bit, chips) if d & (2 * bit - 1) == bit]
        if onward:
            block = jnp.concatenate([pieces[d] for d in onward], axis=0)
            block = across(block, "chan", 2 * bit)
            for i, d in enumerate(onward):
                pieces[d ^ bit] = pieces[d ^ bit] + block[i * rows : (i + 1) * rows]
    mine = pieces[0]
    for bit in bits[:-1]:
        mine = mine + across(pieces[bit], "chan", 2 * bit)
    mine = [mine[: sizes[0]], mine[sizes[0] :]]
    if bits:
        last = pieces[bits[-1]]
        for i, x in enumerate((last[: sizes[0]], last[sizes[0] :])):
            mine[i] = mine[i] + across(x, "chan", 2 * bits[-1])
    receivers = [blocks[0]]
    for d in range(1, times):
        receivers.append(across(blocks[d], "tm", d))
    receivers = [r.reshape(windows, part, 2 * NF) for r in receivers]
    sources = [mine]
    for d in range(1, times):
        both = []
        for x in mine:
            both.append(across(x, "tm", d))
        sources.append(both)

    factor = 1.0 / (windows * times)
    early, late = tuple(range(windows - 1)), (windows - 1,)
    total = None
    for which in ([0], list(range(1, times))):
        for i, span in enumerate((early, late)):
            if which:
                last = i == 1 and which[-1] == times - 1
                total = correlate(
                    [receivers[d] for d in which],
                    [sources[d][i] for d in which],
                    (span,) * len(which),
                    total,
                    pairs,
                    factor,
                    last,
                )
    return total.transpose(1, 0, 2)


def solution(mesh):
    in_specs = (P(("seg", "chan"), "tm"), P("chan", None), P(), P(), P("chan", None))
    out_specs = P(("seg", "chan", "tm"), None, None)
    return jax.shard_map(shards, mesh=mesh, in_specs=in_specs, out_specs=out_specs, check_vma=False)
```

```python
import functools

import jax
import jax.numpy as jnp
import ml_dtypes
import numpy as np
from jax import lax
from jax.experimental import pallas as pl
from jax.experimental.pallas import tpu as pltpu
from jax.sharding import PartitionSpec as P


NFFT = 4096
NF = 512
F0 = 8
PIECE = NFFT // 8
HALF = NFFT // 2
CHUNK = 256
F32 = jnp.float32
BF16 = jnp.bfloat16
LIMIT = 24 * 1024 * 1024
HINT = 10**10


def piece_table():
    bins = F0 + np.arange(NF)
    angle = (bins * np.arange(PIECE)[:, None] % NFFT) * (2.0 * np.pi / NFFT)
    exact = np.concatenate([np.cos(angle), -np.sin(angle)], axis=1)
    high = exact.astype(ml_dtypes.bfloat16)
    low = (exact - high.astype(np.float64)).astype(ml_dtypes.bfloat16)
    both = np.concatenate([high, low], axis=0)
    starts = [c for f in range(0, NF, CHUNK) for c in (f, NF + f)]
    return np.stack([both[:, c : c + CHUNK] for c in starts])


def split_two(x):
    high = x.astype(BF16)
    low = (x - high.astype(F32)).astype(BF16)
    return high, low


def dot(a, b):
    return jnp.dot(a, b, preferred_element_type=F32)


def stacked_parts(x):
    high, low = split_two(x)
    high = high.astype(F32)
    return jnp.concatenate([high, low.astype(F32), high], axis=0)


def stacked_rows(table, rows, at):
    first = table[at, :rows, :]
    return jnp.concatenate([first, first, table[at, PIECE : PIECE + rows, :]], axis=0)


class Turns:
    def __init__(self):
        lane = lax.broadcasted_iota(jnp.int32, (1, CHUNK), 1)
        turn = lane % 4
        self.odd = (turn % 2) == 1
        self.sign = jnp.where(self.odd, -1.0, 1.0)
        self.real = jnp.where(turn < 2, 1.0, -1.0)
        self.imag = jnp.where((turn == 0) | (turn == 3), 1.0, -1.0)
        eighth = lane % 8
        root = np.float32(np.sqrt(0.5))
        self.cos = jnp.where(turn % 4 == 0, 1.0, jnp.where(turn == 2, 0.0, root))
        self.cos = jnp.where((eighth > 2) & (eighth < 6), -self.cos, self.cos)
        self.sin = jnp.where(turn == 2, 1.0, jnp.where(turn == 0, 0.0, root))
        self.sin = jnp.where(eighth < 4, -self.sin, self.sin)

    def quarter(self, ar, ai, br, bi):
        return (
            ar + self.real * jnp.where(self.odd, bi, br),
            ai + self.imag * jnp.where(self.odd, br, bi),
        )

    def half(self, re, im):
        ar, ai = self.quarter(re[0], im[0], re[2], im[2])
        br, bi = self.quarter(re[1], im[1], re[3], im[3])
        return ar + (br * self.cos - bi * self.sin), ai + (br * self.sin + bi * self.cos)


def half_spectra(x, table, channels, halves, turns, f):
    both = jnp.concatenate([x, x], axis=1)
    at = 2 * (f // CHUNK)
    dr = dot(both, table[at])
    di = dot(both, table[at + 1])
    out = []
    for b in range(halves):
        rows = [slice((4 * b + e) * channels, (4 * b + e + 1) * channels) for e in range(4)]
        out.append(turns.half([dr[r] for r in rows], [di[r] for r in rows]))
    return out


def end_terms(taps_wide, shifted, tap_count, ends):
    lag = tap_count - 1
    apart = ends.T
    size = apart.shape[0]
    shifted[...] = jnp.zeros_like(shifted)
    shifted[:tap_count, :] = taps_wide
    total = jnp.zeros((lag, apart.shape[1]), F32)
    for j in range(1, tap_count):
        total = total + shifted[j : j + lag, :] * apart[size - j : size - j + 1, :]
    return stacked_parts(total).T.astype(BF16)


def whiten_rows(re, im):
    rows = re.shape[0]
    place = lax.broadcasted_iota(jnp.int32, (rows, NF), 1)
    power = re * re + im * im
    smooth = power
    for s in (1, 2):
        smooth = smooth + jnp.where(place >= s, pltpu.roll(power, s, 1), 0.0)
        smooth = smooth + jnp.where(place < NF - s, pltpu.roll(power, NF - s, 1), 0.0)
    total = jnp.sum(power, axis=1, keepdims=True)
    scaling = lax.rsqrt(smooth * 0.2 + (total * (0.1 / NF) + 1e-06))
    return (re * scaling).astype(BF16), (im * scaling).astype(BF16)


ROWS = 16


def whiten_all(spectra, white, count):
    def step(i, carry):
        rows = pl.ds(pl.multiple_of(i * ROWS, ROWS), ROWS)
        re, im = whiten_rows(spectra[rows, :NF], spectra[rows, NF:])
        white[rows, :NF] = re
        white[rows, NF:] = im
        return carry

    lax.fori_loop(0, count // ROWS, step, 0, unroll=4)


def load_kernel(end, traces_in, table_in, ids_in, message, last_half, table, ids, traces, sems):
    channels, samples = traces.shape
    begin = traces_in.shape[1] - samples
    copies = [pltpu.make_async_copy(traces_in.at[:, begin:], traces, sems.at[0])]
    at = 1 + table.shape[0]
    for i in range(table.shape[0]):
        copies.append(pltpu.make_async_copy(table_in.at[i], table.at[i], sems.at[1 + i]))
    copies.append(pltpu.make_async_copy(ids_in, ids, sems.at[at]))
    for copy in copies:
        copy.start()
    copies[0].wait()
    lane = lax.broadcasted_iota(jnp.int32, (channels, 128), 1)
    final = pltpu.roll(traces[:, samples - 128 :].astype(F32), 128 - end, 1)
    tile = jnp.where(lane < 128 - end, final, traces[:, :128].astype(F32))
    message[:, 2 * NF :] = tile.astype(BF16)
    pieces = [samples - HALF + q * PIECE for q in range(HALF // PIECE)]
    x = jnp.concatenate([traces[:, p : p + PIECE] for p in pieces], axis=0)
    turns = Turns()
    for i, f in enumerate(range(0, NF, CHUNK)):
        re = slice(f, f + CHUNK)
        im = slice(NF + f, NF + f + CHUNK)
        copies[1 + 2 * i].wait()
        copies[2 + 2 * i].wait()
        xr, xi = half_spectra(x, table, channels, 1, turns, f)[0]
        last_half[:, re] = xr
        last_half[:, im] = xi
        message[:, re] = xr.astype(BF16)
        message[:, im] = xi.astype(BF16)
    for copy in copies[at:]:
        copy.wait()


def pair_kernel(mine, other, out):
    out[:1, :] = mine[...]
    out[1:, :] = other[...]


def own_chunk(windows, f, traces, table, last_half, lines, edge, part, response, last):
    channels, samples = traces.shape
    size = lines.shape[1] // 3
    lag = edge.shape[1] // 3
    pieces = (samples - HALF) // PIECE
    x = jnp.concatenate([traces[:, q * PIECE : (q + 1) * PIECE] for q in range(pieces)], axis=0)
    turns = Turns()
    re = slice(f, f + CHUNK)
    im = slice(NF + f, NF + f + CHUNK)
    at = 2 * (f // CHUNK)
    pr = dot(lines[...], stacked_rows(table, size, at))
    pi = dot(lines[...], stacked_rows(table, size, at + 1))
    response[:, :CHUNK] = pr
    response[:, CHUNK:] = pi
    halves = half_spectra(x, table, channels, windows - 1, turns, f)
    halves.append((last_half[:, re], last_half[:, im]))
    for w in range(windows):
        xr, xi = halves[w]
        xr, xi = turns.sign * xr, turns.sign * xi
        if w > 0:
            xr, xi = xr + halves[w - 1][0], xi + halves[w - 1][1]
        yr = xr * pr - xi * pi
        yi = xr * pi + xi * pr
        if w < windows - 1:
            rows = slice(w * channels, (w + 1) * channels)
            part[rows, :CHUNK] = yr
            part[rows, CHUNK:] = yi
        else:
            last[:, :CHUNK] = yr + dot(edge[...], stacked_rows(table, lag, at))
            last[:, CHUNK:] = yi + dot(edge[...], stacked_rows(table, lag, at + 1))


def first_kernel(
    windows, traces, taps, table, last_half, part, response, last, ends, edge, lines, square, shifted
):
    channels, samples = traces.shape
    tap_count = taps.shape[0]
    square[...] = jnp.zeros_like(square)
    high, low = split_two(taps[...])
    high = high.astype(F32)
    size = square.shape[0] // 3
    for i, value in enumerate((high, low.astype(F32), high)):
        square[i * size : i * size + tap_count, :channels] = value
    lines[...] = square[...].T[:channels].astype(BF16)
    tile = 128
    for b in range(1, windows):
        ends[:, (b - 1) * tile : b * tile] = traces[:, b * HALF - tile : b * HALF]
    start = (windows - 2) * HALF
    apart = traces[:, start - tile : start].astype(F32) - traces[:, samples - tile :].astype(F32)
    edge[...] = end_terms(taps[...], shifted, tap_count, apart)
    own_chunk(windows, 0, traces, table, last_half, lines, edge, part, response, last)


def second_kernel(
    windows, traces, table, last_half, lines, edge, first, part, response, white, second, spectra
):
    own_chunk(windows, CHUNK, traces, table, last_half, lines, edge, part, response, second)
    for i, half in enumerate((first, second)):
        spectra[:, i * CHUNK : (i + 1) * CHUNK] = half[:, :CHUNK]
        spectra[:, NF + i * CHUNK : NF + (i + 1) * CHUNK] = half[:, CHUNK:]
    whiten_all(spectra, white, white.shape[0])


def part_rows(windows, pairs):
    return [-(-w * pairs // 8) * 8 for w in (windows - 1, 1)]


def picks_kernel(shape, counts, slots, *refs):
    channels, windows, pairs, chips = shape
    wanted, (picks, chosen, lines) = refs[:-3], refs[-3:]
    group = lax.axis_index("chan")
    place = lax.broadcasted_iota(jnp.int32, counts.shape, 1)
    held = counts[...].astype(F32)
    first = jnp.sum(jnp.where(place < group, held, 0.0), axis=1, keepdims=True)
    owned = jnp.sum(jnp.where(place == group, held, 0.0), axis=1, keepdims=True)
    row = lax.broadcasted_iota(jnp.int32, slots.shape, 0)
    own_slots = jnp.where(row == group, slots[...], 0).astype(F32)
    own_slots = jnp.sum(own_slots, axis=0, keepdims=True)
    lines[...] = jnp.zeros_like(lines)
    at = 0
    for w in wanted:
        lines[at : at + w.shape[0], :pairs] = w[...].astype(F32)
        at += w.shape[0]
    slot = lines[...] - first
    channel = jnp.full(slot.shape, -1.0, F32)
    for s in range(slots.shape[1]):
        channel = jnp.where(slot == s, own_slots[:, s : s + 1], channel)
    channel = jnp.where((slot >= 0) & (slot < owned), channel, -1.0)
    turned = channel.T
    width = windows * channels
    lane = lax.broadcasted_iota(jnp.int32, (1, width), 1)
    columns = [
        jnp.where(lane // channels == w, lane % channels, -2).astype(F32) for w in range(windows)
    ]
    sizes = part_rows(windows, pairs)
    chosen[...] = jnp.zeros_like(chosen)
    for core in range(2):
        for d in range(chips):
            base = (core * chips + d) * sum(sizes)
            one = turned[:pairs, 2 * d + core : 2 * d + core + 1]
            for w in range(windows):
                row = base + (w * pairs if w < windows - 1 else sizes[0])
                chosen[row : row + pairs, :] = (one == columns[w]).astype(F32)
    picks[...] = chosen[...].astype(BF16)


def rest_kernel(
    windows, pairs, times, halo, ends, taps, table, part_a, part_b, response_a, response_b, *refs
):
    own_white, picks, keep, send = refs[:4]
    blocks = refs[4 : 4 + times]
    shifted, spectra, white = refs[4 + times :]
    channels = response_a.shape[0]
    tap_count = taps.shape[0]
    tile = 128
    rest = windows - 1

    arrived = halo[:, 2 * NF :].astype(F32)
    before = [arrived, pltpu.roll(arrived, tap_count - 1, 1)]
    before += [ends[:, (b - 1) * tile : b * tile] for b in range(1, windows - 2)]
    after = [ends[:, w * tile : (w + 1) * tile] for w in range(rest)]
    apart = jnp.concatenate([b.astype(F32) - a.astype(F32) for b, a in zip(before, after)], axis=0)
    taps_wide = jnp.concatenate([taps[...]] * rest, axis=1)
    edge = end_terms(taps_wide, shifted, tap_count, apart)
    for f in range(0, NF, CHUNK):
        re = slice(f, f + CHUNK)
        im = slice(NF + f, NF + f + CHUNK)
        xr, xi = halo[:, re].astype(F32), halo[:, im].astype(F32)
        part, response = (part_b, response_b) if f else (part_a, response_a)
        pr, pi = response[:, :CHUNK], response[:, CHUNK:]
        at = 2 * (f // CHUNK)
        er = dot(edge, stacked_rows(table, tap_count - 1, at))
        ei = dot(edge, stacked_rows(table, tap_count - 1, at + 1))
        spectra[:channels, re] = part[:channels, :CHUNK] + er[:channels] + (xr * pr - xi * pi)
        spectra[:channels, im] = part[:channels, CHUNK:] + ei[:channels] + (xr * pi + xi * pr)
        spectra[channels:, re] = part[channels:, :CHUNK] + er[channels:]
        spectra[channels:, im] = part[channels:, CHUNK:] + ei[channels:]
    count = rest * channels
    whiten_all(spectra, white, count)
    white[count:, :] = own_white[...]
    base = picks.shape[0] // 2
    sizes = part_rows(windows, pairs)
    used = [(windows - 1) * pairs, pairs]
    part = channels // times
    choose = picks[...]
    for f in range(0, 2 * NF, CHUNK):
        cols = slice(f, f + CHUNK)
        out = dot(choose, white[:, cols]).astype(BF16)
        imag = f >= NF
        place = slice(f - NF * imag, f - NF * imag + CHUNK)
        for target, first in ((keep, 0), (send, base)):
            for d in range(base // sum(sizes)):
                at, row = first + d * sum(sizes), d * 2 * sum(used)
                for size, n in zip(sizes, used):
                    put = row + imag * n
                    target[put : put + n, place] = out[at : at + n]
                    at, row = at + size, row + 2 * n
    for d in range(times):
        line = (lax.axis_index("tm") ^ d) * part
        for w in range(windows):
            if part % ROWS == 0:
                at = pl.multiple_of(w * channels + line, ROWS)
                blocks[d][w * part : (w + 1) * part, :] = white[pl.ds(at, part), :]
            else:
                row = lax.broadcasted_iota(jnp.int32, (part, channels), 0)
                col = lax.broadcasted_iota(jnp.int32, (part, channels), 1)
                move = (col == row + line).astype(F32).astype(BF16)
                moved = dot(move, white[w * channels : (w + 1) * channels, :])
                blocks[d][w * part : (w + 1) * part, :] = moved.astype(BF16)


def correlate_kernel(spans, pairs, factor, has_total, last, *refs):
    count = len(spans)
    receivers, sources = refs[:count], refs[count : 2 * count]
    total = refs[2 * count] if has_total else None
    out, line_r, line_s = refs[2 * count + has_total : 2 * count + has_total + 3]
    held, sems = refs[-2:] if last else (out, None)
    part = out.shape[1]
    windows = 0
    for receiver, source, span in zip(receivers, sources, spans):
        for i, w in enumerate(span):
            line_r[windows] = receiver[w].astype(F32) * factor
            for c in range(2):
                at = (c * len(span) + i) * pairs
                rows = source[at : at + pairs, :].astype(F32)
                cols = slice(c * NF, (c + 1) * NF)
                for p in range(pairs):
                    line_s[p, windows : windows + 1, cols] = rows[p : p + 1, :]
            windows += 1

    def copy(p):
        return pltpu.make_async_copy(held.at[p], out.at[p], sems.at[p])

    def one(p, carry):
        for f in range(0, NF, 128):
            re = slice(f, f + 128)
            im = slice(NF + f, NF + f + 128)
            if has_total:
                total_r, total_i = total[p, :, re], total[p, :, im]
            else:
                total_r = jnp.zeros((part, 128), F32)
                total_i = jnp.zeros((part, 128), F32)
            for at in range(windows):
                rr = line_r[at, :, re]
                ri = line_r[at, :, im]
                sr = line_s[p, at : at + 1, re]
                si = line_s[p, at : at + 1, im]
                total_r = total_r + (sr * rr + si * ri)
                total_i = total_i + (sr * ri - si * rr)
            held[p, :, re] = total_r
            held[p, :, im] = total_i
        if last:
            copy(p).start()
        return carry

    lax.fori_loop(0, pairs, one, 0, unroll=2 if pairs % 2 == 0 else 1)
    if last:
        for p in range(pairs):
            copy(p).wait()


def correlate(receivers, sources, spans, total, pairs, factor, last):
    _, part, width = receivers[0].shape
    windows = sum(len(span) for span in spans)
    vmem = pl.BlockSpec(memory_space=pltpu.VMEM)
    shape = (pairs, part, width)
    extra = [] if total is None else [total]
    scratch = [
        pltpu.VMEM((windows, part, width), F32),
        pltpu.VMEM((pairs, -(-windows // 8) * 8, width), F32),
    ]
    if last:
        scratch += [pltpu.VMEM(shape, F32), pltpu.SemaphoreType.DMA((pairs,))]
    return pl.pallas_call(
        functools.partial(correlate_kernel, spans, pairs, factor, len(extra), last),
        out_shape=jax.ShapeDtypeStruct(shape, F32),
        in_specs=[vmem] * (2 * len(spans) + len(extra)),
        out_specs=pl.BlockSpec(memory_space=pltpu.HBM) if last else vmem,
        scratch_shapes=scratch,
        compiler_params=pltpu.CompilerParams(vmem_limit_bytes=LIMIT),
        name="correlate",
    )(*receivers, *sources, *extra)


def shards(traces, filter_taps, source_counts, source_channel, block_sources):
    channels, samples = traces.shape
    tap_count = filter_taps.shape[1]
    pairs = block_sources.shape[1]
    windows = samples // HALF
    groups = lax.axis_size("chan")
    times = lax.axis_size("tm")
    chips = groups // 2
    part = channels // times
    sizes = part_rows(windows, pairs)
    rows_out = chips * sum(sizes)
    rows, cut = 2 * windows * pairs, 2 * (windows - 1) * pairs

    def across(x, axis, distance):
        size = lax.axis_size(axis)
        return lax.ppermute(x, axis, [(i, i ^ distance) for i in range(size)])

    vmem = pl.BlockSpec(memory_space=pltpu.VMEM)
    hbm = pl.BlockSpec(memory_space=pltpu.HBM)
    params = pltpu.CompilerParams(vmem_limit_bytes=LIMIT)
    bits = [1 << b for b in range(chips.bit_length() - 1)]

    other = across(block_sources, "chan", 1)
    inputs = (traces, jnp.asarray(piece_table()), block_sources)
    message, last_half, table, ids = pl.pallas_call(
        functools.partial(load_kernel, tap_count - 1),
        out_shape=[
            jax.ShapeDtypeStruct((channels, 2 * NF + 128), BF16),
            jax.ShapeDtypeStruct((channels, 2 * NF), F32),
        ]
        + [jax.ShapeDtypeStruct(a.shape, a.dtype) for a in inputs[1:]],
        in_specs=[hbm] * 3,
        out_specs=[vmem] * 4,
        scratch_shapes=[
            pltpu.VMEM((channels, HALF + 128), BF16),
            pltpu.SemaphoreType.DMA((2 + 2 * NF // CHUNK,)),
        ],
        compiler_params=params,
        name="load",
    )(*(pltpu.with_memory_space_constraint(a, pltpu.HBM) for a in inputs))
    traces, taps = (
        pltpu.with_memory_space_constraint(a, pltpu.VMEM) for a in (traces, filter_taps.T)
    )
    wanted = [
        pl.pallas_call(
            pair_kernel,
            out_shape=jax.ShapeDtypeStruct((2, pairs), jnp.int32),
            in_specs=[vmem] * 2,
            out_specs=vmem,
            compiler_params=params,
            cost_estimate=pl.CostEstimate(flops=HINT, bytes_accessed=8 * pairs, transcendentals=0),
            name="pair",
        )(ids, other)
    ]
    halo = lax.ppermute(message, "tm", [(i - 1, i) for i in range(1, times)])
    for bit in bits:
        known = jnp.concatenate(wanted, axis=0)
        wanted = [known, across(known, "chan", 2 * bit)]

    shape = (channels, windows, pairs, chips)
    width = windows * channels
    chunk_shapes = [
        jax.ShapeDtypeStruct((width - channels, 2 * CHUNK), F32),
        jax.ShapeDtypeStruct((channels, 2 * CHUNK), F32),
    ]
    size = -(-tap_count // 16) * 16
    part_a, response_a, last, ends, edge, lines = pl.pallas_call(
        functools.partial(first_kernel, windows),
        out_shape=chunk_shapes
        + [
            chunk_shapes[1],
            jax.ShapeDtypeStruct((channels, (windows - 1) * 128), BF16),
            jax.ShapeDtypeStruct((channels, 3 * (tap_count - 1)), BF16),
            jax.ShapeDtypeStruct((channels, 3 * size), BF16),
        ],
        in_specs=[vmem] * 4,
        out_specs=[vmem] * 6,
        scratch_shapes=[
            pltpu.VMEM((3 * size, 128), F32),
            pltpu.VMEM((2 * tap_count + 6, channels), F32),
        ],
        compiler_params=params,
        name="first",
    )(traces, taps, table, last_half)
    part_b, response_b, own_white = pl.pallas_call(
        functools.partial(second_kernel, windows),
        out_shape=chunk_shapes + [jax.ShapeDtypeStruct((channels, 2 * NF), BF16)],
        in_specs=[vmem] * 6,
        out_specs=[vmem] * 3,
        scratch_shapes=[
            pltpu.VMEM((channels, 2 * CHUNK), F32),
            pltpu.VMEM((channels, 2 * NF), F32),
        ],
        compiler_params=params,
        name="second",
    )(traces, table, last_half, lines, edge, last)
    picks = pl.pallas_call(
        functools.partial(picks_kernel, shape),
        out_shape=jax.ShapeDtypeStruct((2 * rows_out, width), BF16),
        in_specs=[vmem] * (2 + len(wanted)),
        out_specs=vmem,
        scratch_shapes=[pltpu.VMEM((2 * rows_out, width), F32), pltpu.VMEM((2 * chips, 128), F32)],
        compiler_params=params,
        name="picks",
    )(source_counts[None], source_channel, *wanted)
    outs = pl.pallas_call(
        functools.partial(rest_kernel, windows, pairs, times),
        out_shape=[jax.ShapeDtypeStruct((chips * rows, NF), BF16)] * 2
        + [jax.ShapeDtypeStruct((windows * part, 2 * NF), BF16)] * times,
        in_specs=[vmem] * 10,
        out_specs=[vmem] * (2 + times),
        scratch_shapes=[
            pltpu.VMEM((2 * tap_count + 6, width - channels), F32),
            pltpu.VMEM((width - channels, 2 * NF), F32),
            pltpu.VMEM((width, 2 * NF), BF16),
        ],
        compiler_params=params,
        name="rest",
    )(
        halo,
        ends,
        taps,
        table,
        part_a,
        part_b,
        response_a,
        response_b,
        own_white,
        picks,
    )
    keep, send, blocks = outs[0], outs[1], outs[2:]
    gathered = keep + across(send, "chan", 1)
    pieces = [gathered[d * rows : (d + 1) * rows] for d in range(chips)]
    pieces = list(lax.optimization_barrier(tuple(pieces)))
    for bit in bits:
        onward = [d for d in range(2 * bit, chips) if d & (2 * bit - 1) == bit]
        if onward:
            block = jnp.concatenate([pieces[d] for d in onward], axis=0)
            block = across(block, "chan", 2 * bit)
            for i, d in enumerate(onward):
                pieces[d ^ bit] = pieces[d ^ bit] + block[i * rows : (i + 1) * rows]
    mine = pieces[0]
    for bit in bits[:-1]:
        mine = mine + across(pieces[bit], "chan", 2 * bit)
    mine = [mine[:cut], mine[cut:]]
    if bits:
        last = pieces[bits[-1]]
        for i, x in enumerate((last[:cut], last[cut:])):
            mine[i] = mine[i] + across(x, "chan", 2 * bits[-1])
    receivers = [blocks[0]]
    for d in range(1, times):
        receivers.append(across(blocks[d], "tm", d))
    receivers = [r.reshape(windows, part, 2 * NF) for r in receivers]
    sources = [mine]
    for d in range(1, times):
        both = []
        for x in mine:
            both.append(across(x, "tm", d))
        sources.append(both)

    factor = 1.0 / (windows * times)
    early, late = tuple(range(windows - 1)), (windows - 1,)
    total = None
    for which in ([0], list(range(1, times))):
        for i, span in enumerate((early, late)):
            if which:
                last = i == 1 and which[-1] == times - 1
                total = correlate(
                    [receivers[d] for d in which],
                    [sources[d][i] for d in which],
                    (span,) * len(which),
                    total,
                    pairs,
                    factor,
                    last,
                )
    return total.transpose(1, 0, 2)


def solution(mesh):
    in_specs = (P(("seg", "chan"), "tm"), P("chan", None), P(), P(), P("chan", None))
    out_specs = P(("seg", "chan", "tm"), None, None)
    return jax.shard_map(shards, mesh=mesh, in_specs=in_specs, out_specs=out_specs, check_vma=False)
```

```python
import functools

import jax
import jax.numpy as jnp
import ml_dtypes
import numpy as np
from jax import lax
from jax.experimental import pallas as pl
from jax.experimental.pallas import tpu as pltpu
from jax.sharding import PartitionSpec as P


NFFT = 4096
NF = 512
F0 = 8
PIECE = NFFT // 8
HALF = NFFT // 2
CHUNK = 256
F32 = jnp.float32
BF16 = jnp.bfloat16
LIMIT = 24 * 1024 * 1024
HINT = 10**10


def piece_table():
    bins = F0 + np.arange(NF)
    angle = (bins * np.arange(PIECE)[:, None] % NFFT) * (2.0 * np.pi / NFFT)
    exact = np.concatenate([np.cos(angle), -np.sin(angle)], axis=1)
    high = exact.astype(ml_dtypes.bfloat16)
    low = (exact - high.astype(np.float64)).astype(ml_dtypes.bfloat16)
    both = np.concatenate([high, low], axis=0)
    starts = [c for f in range(0, NF, CHUNK) for c in (f, NF + f)]
    return np.stack([both[:, c : c + CHUNK] for c in starts])


def split_two(x):
    high = x.astype(BF16)
    low = (x - high.astype(F32)).astype(BF16)
    return high, low


def dot(a, b):
    return jnp.dot(a, b, preferred_element_type=F32)


def stacked_parts(x):
    high, low = split_two(x)
    high = high.astype(F32)
    return jnp.concatenate([high, low.astype(F32), high], axis=0)


def stacked_rows(table, rows, at):
    first = table[at, :rows, :]
    return jnp.concatenate([first, first, table[at, PIECE : PIECE + rows, :]], axis=0)


class Turns:
    def __init__(self):
        lane = lax.broadcasted_iota(jnp.int32, (1, CHUNK), 1)
        turn = lane % 4
        self.odd = (turn % 2) == 1
        self.sign = jnp.where(self.odd, -1.0, 1.0)
        self.real = jnp.where(turn < 2, 1.0, -1.0)
        self.imag = jnp.where((turn == 0) | (turn == 3), 1.0, -1.0)
        eighth = lane % 8
        root = np.float32(np.sqrt(0.5))
        self.cos = jnp.where(turn % 4 == 0, 1.0, jnp.where(turn == 2, 0.0, root))
        self.cos = jnp.where((eighth > 2) & (eighth < 6), -self.cos, self.cos)
        self.sin = jnp.where(turn == 2, 1.0, jnp.where(turn == 0, 0.0, root))
        self.sin = jnp.where(eighth < 4, -self.sin, self.sin)

    def quarter(self, ar, ai, br, bi):
        return (
            ar + self.real * jnp.where(self.odd, bi, br),
            ai + self.imag * jnp.where(self.odd, br, bi),
        )

    def half(self, re, im):
        ar, ai = self.quarter(re[0], im[0], re[2], im[2])
        br, bi = self.quarter(re[1], im[1], re[3], im[3])
        return ar + (br * self.cos - bi * self.sin), ai + (br * self.sin + bi * self.cos)


def half_spectra(x, table, channels, halves, turns, f):
    both = jnp.concatenate([x, x], axis=1)
    at = 2 * (f // CHUNK)
    dr = dot(both, table[at])
    di = dot(both, table[at + 1])
    out = []
    for b in range(halves):
        rows = [slice((4 * b + e) * channels, (4 * b + e + 1) * channels) for e in range(4)]
        out.append(turns.half([dr[r] for r in rows], [di[r] for r in rows]))
    return out


def end_terms(taps_wide, shifted, tap_count, ends):
    lag = tap_count - 1
    apart = ends.T
    size = apart.shape[0]
    shifted[...] = jnp.zeros_like(shifted)
    shifted[:tap_count, :] = taps_wide
    total = jnp.zeros((lag, apart.shape[1]), F32)
    for j in range(1, tap_count):
        total = total + shifted[j : j + lag, :] * apart[size - j : size - j + 1, :]
    return stacked_parts(total).T.astype(BF16)


def whiten_rows(re, im):
    rows = re.shape[0]
    place = lax.broadcasted_iota(jnp.int32, (rows, NF), 1)
    power = re * re + im * im
    smooth = power
    for s in (1, 2):
        smooth = smooth + jnp.where(place >= s, pltpu.roll(power, s, 1), 0.0)
        smooth = smooth + jnp.where(place < NF - s, pltpu.roll(power, NF - s, 1), 0.0)
    total = jnp.sum(power, axis=1, keepdims=True)
    scaling = lax.rsqrt(smooth * 0.2 + (total * (0.1 / NF) + 1e-06))
    return (re * scaling).astype(BF16), (im * scaling).astype(BF16)


ROWS = 16


def whiten_all(spectra, white, count):
    def step(i, carry):
        rows = pl.ds(pl.multiple_of(i * ROWS, ROWS), ROWS)
        re, im = whiten_rows(spectra[rows, :NF], spectra[rows, NF:])
        white[rows, :NF] = re
        white[rows, NF:] = im
        return carry

    lax.fori_loop(0, count // ROWS, step, 0, unroll=4)


def load_kernel(end, traces_in, table_in, ids_in, message, last_half, table, ids, traces, sems):
    channels, samples = traces.shape
    begin = traces_in.shape[1] - samples
    copies = [pltpu.make_async_copy(traces_in.at[:, begin:], traces, sems.at[0])]
    at = 1 + 2 * table.shape[0]
    for k in range(0, table.shape[0], 2):
        for part in (slice(0, PIECE), slice(PIECE, 2 * PIECE)):
            for i in (k, k + 1):
                sem = sems.at[len(copies)]
                copies.append(
                    pltpu.make_async_copy(table_in.at[i, part], table.at[i, part], sem)
                )
    copies.append(pltpu.make_async_copy(ids_in, ids, sems.at[at]))
    for copy in copies:
        copy.start()
    copies[0].wait()
    lane = lax.broadcasted_iota(jnp.int32, (channels, 128), 1)
    final = pltpu.roll(traces[:, samples - 128 :].astype(F32), 128 - end, 1)
    tile = jnp.where(lane < 128 - end, final, traces[:, :128].astype(F32))
    message[:, 2 * NF :] = tile.astype(BF16)
    pieces = [samples - HALF + q * PIECE for q in range(HALF // PIECE)]
    x = jnp.concatenate([traces[:, p : p + PIECE] for p in pieces], axis=0)
    turns = Turns()
    rows = [slice(e * channels, (e + 1) * channels) for e in range(HALF // PIECE)]
    for i, f in enumerate(range(0, NF, CHUNK)):
        re = slice(f, f + CHUNK)
        im = slice(NF + f, NF + f + CHUNK)
        sums = []
        for j, part in enumerate((slice(0, PIECE), slice(PIECE, 2 * PIECE))):
            for c in range(2):
                copies[1 + 4 * i + 2 * j + c].wait()
                term = dot(x, table[2 * i + c, part, :])
                if j:
                    sums[c] = sums[c] + term
                else:
                    sums.append(term)
        xr, xi = turns.half(*([total[r] for r in rows] for total in sums))
        last_half[:, re] = xr
        last_half[:, im] = xi
        message[:, re] = xr.astype(BF16)
        message[:, im] = xi.astype(BF16)
    for copy in copies[at:]:
        copy.wait()


def pair_kernel(mine, other, out):
    out[:1, :] = mine[...]
    out[1:, :] = other[...]


def own_chunk(windows, f, traces, table, last_half, lines, edge, part, response, last):
    channels, samples = traces.shape
    size = lines.shape[1] // 3
    lag = edge.shape[1] // 3
    pieces = (samples - HALF) // PIECE
    x = jnp.concatenate([traces[:, q * PIECE : (q + 1) * PIECE] for q in range(pieces)], axis=0)
    turns = Turns()
    re = slice(f, f + CHUNK)
    im = slice(NF + f, NF + f + CHUNK)
    at = 2 * (f // CHUNK)
    pr = dot(lines[...], stacked_rows(table, size, at))
    pi = dot(lines[...], stacked_rows(table, size, at + 1))
    response[:, :CHUNK] = pr
    response[:, CHUNK:] = pi
    halves = half_spectra(x, table, channels, windows - 1, turns, f)
    halves.append((last_half[:, re], last_half[:, im]))
    for w in range(windows):
        xr, xi = halves[w]
        xr, xi = turns.sign * xr, turns.sign * xi
        if w > 0:
            xr, xi = xr + halves[w - 1][0], xi + halves[w - 1][1]
        yr = xr * pr - xi * pi
        yi = xr * pi + xi * pr
        if w < windows - 1:
            rows = slice(w * channels, (w + 1) * channels)
            part[rows, :CHUNK] = yr
            part[rows, CHUNK:] = yi
        else:
            last[:, :CHUNK] = yr + dot(edge[...], stacked_rows(table, lag, at))
            last[:, CHUNK:] = yi + dot(edge[...], stacked_rows(table, lag, at + 1))


def first_kernel(
    windows, traces, taps, table, last_half, part, response, last, ends, edge, lines, square, shifted
):
    channels, samples = traces.shape
    tap_count = taps.shape[0]
    square[...] = jnp.zeros_like(square)
    high, low = split_two(taps[...])
    high = high.astype(F32)
    size = square.shape[0] // 3
    for i, value in enumerate((high, low.astype(F32), high)):
        square[i * size : i * size + tap_count, :channels] = value
    lines[...] = square[...].T[:channels].astype(BF16)
    tile = 128
    for b in range(1, windows):
        ends[:, (b - 1) * tile : b * tile] = traces[:, b * HALF - tile : b * HALF]
    start = (windows - 2) * HALF
    apart = traces[:, start - tile : start].astype(F32) - traces[:, samples - tile :].astype(F32)
    edge[...] = end_terms(taps[...], shifted, tap_count, apart)
    own_chunk(windows, 0, traces, table, last_half, lines, edge, part, response, last)


def second_kernel(
    windows, traces, table, last_half, lines, edge, first, part, response, white, second, spectra
):
    own_chunk(windows, CHUNK, traces, table, last_half, lines, edge, part, response, second)
    for i, half in enumerate((first, second)):
        spectra[:, i * CHUNK : (i + 1) * CHUNK] = half[:, :CHUNK]
        spectra[:, NF + i * CHUNK : NF + (i + 1) * CHUNK] = half[:, CHUNK:]
    whiten_all(spectra, white, white.shape[0])


def part_rows(windows, pairs):
    return [-(-w * pairs // 8) * 8 for w in (windows - 1, 1)]


def picks_kernel(shape, counts, slots, *refs):
    channels, windows, pairs, chips = shape
    wanted, (picks, chosen, lines) = refs[:-3], refs[-3:]
    group = lax.axis_index("chan")
    place = lax.broadcasted_iota(jnp.int32, counts.shape, 1)
    held = counts[...].astype(F32)
    first = jnp.sum(jnp.where(place < group, held, 0.0), axis=1, keepdims=True)
    owned = jnp.sum(jnp.where(place == group, held, 0.0), axis=1, keepdims=True)
    row = lax.broadcasted_iota(jnp.int32, slots.shape, 0)
    own_slots = jnp.where(row == group, slots[...], 0).astype(F32)
    own_slots = jnp.sum(own_slots, axis=0, keepdims=True)
    lines[...] = jnp.zeros_like(lines)
    at = 0
    for w in wanted:
        lines[at : at + w.shape[0], :pairs] = w[...].astype(F32)
        at += w.shape[0]
    slot = lines[...] - first
    channel = jnp.full(slot.shape, -1.0, F32)
    for s in range(slots.shape[1]):
        channel = jnp.where(slot == s, own_slots[:, s : s + 1], channel)
    channel = jnp.where((slot >= 0) & (slot < owned), channel, -1.0)
    turned = channel.T
    width = windows * channels
    lane = lax.broadcasted_iota(jnp.int32, (1, width), 1)
    columns = [
        jnp.where(lane // channels == w, lane % channels, -2).astype(F32) for w in range(windows)
    ]
    sizes = part_rows(windows, pairs)
    chosen[...] = jnp.zeros_like(chosen)
    for core in range(2):
        for d in range(chips):
            base = (core * chips + d) * sum(sizes)
            one = turned[:pairs, 2 * d + core : 2 * d + core + 1]
            for w in range(windows):
                row = base + (w * pairs if w < windows - 1 else sizes[0])
                chosen[row : row + pairs, :] = (one == columns[w]).astype(F32)
    picks[...] = chosen[...].astype(BF16)


def rest_kernel(
    windows, pairs, times, halo, ends, taps, table, part_a, part_b, response_a, response_b, *refs
):
    own_white, picks, keep, send = refs[:4]
    blocks = refs[4 : 4 + times]
    shifted, spectra, white = refs[4 + times :]
    channels = response_a.shape[0]
    tap_count = taps.shape[0]
    tile = 128
    rest = windows - 1

    arrived = halo[:, 2 * NF :].astype(F32)
    before = [arrived, pltpu.roll(arrived, tap_count - 1, 1)]
    before += [ends[:, (b - 1) * tile : b * tile] for b in range(1, windows - 2)]
    after = [ends[:, w * tile : (w + 1) * tile] for w in range(rest)]
    apart = jnp.concatenate([b.astype(F32) - a.astype(F32) for b, a in zip(before, after)], axis=0)
    taps_wide = jnp.concatenate([taps[...]] * rest, axis=1)
    edge = end_terms(taps_wide, shifted, tap_count, apart)
    for f in range(0, NF, CHUNK):
        re = slice(f, f + CHUNK)
        im = slice(NF + f, NF + f + CHUNK)
        xr, xi = halo[:, re].astype(F32), halo[:, im].astype(F32)
        part, response = (part_b, response_b) if f else (part_a, response_a)
        pr, pi = response[:, :CHUNK], response[:, CHUNK:]
        at = 2 * (f // CHUNK)
        er = dot(edge, stacked_rows(table, tap_count - 1, at))
        ei = dot(edge, stacked_rows(table, tap_count - 1, at + 1))
        spectra[:channels, re] = part[:channels, :CHUNK] + er[:channels] + (xr * pr - xi * pi)
        spectra[:channels, im] = part[:channels, CHUNK:] + ei[:channels] + (xr * pi + xi * pr)
        spectra[channels:, re] = part[channels:, :CHUNK] + er[channels:]
        spectra[channels:, im] = part[channels:, CHUNK:] + ei[channels:]
    count = rest * channels
    whiten_all(spectra, white, count)
    white[count:, :] = own_white[...]
    base = picks.shape[0] // 2
    sizes = part_rows(windows, pairs)
    used = [(windows - 1) * pairs, pairs]
    part = channels // times
    choose = picks[...]
    for f in range(0, 2 * NF, CHUNK):
        cols = slice(f, f + CHUNK)
        out = dot(choose, white[:, cols]).astype(BF16)
        imag = f >= NF
        place = slice(f - NF * imag, f - NF * imag + CHUNK)
        for target, first in ((keep, 0), (send, base)):
            for d in range(base // sum(sizes)):
                at, row = first + d * sum(sizes), d * 2 * sum(used)
                for size, n in zip(sizes, used):
                    put = row + imag * n
                    target[put : put + n, place] = out[at : at + n]
                    at, row = at + size, row + 2 * n
    for d in range(times):
        line = (lax.axis_index("tm") ^ d) * part
        for w in range(windows):
            if part % ROWS == 0:
                at = pl.multiple_of(w * channels + line, ROWS)
                blocks[d][w * part : (w + 1) * part, :] = white[pl.ds(at, part), :]
            else:
                row = lax.broadcasted_iota(jnp.int32, (part, channels), 0)
                col = lax.broadcasted_iota(jnp.int32, (part, channels), 1)
                move = (col == row + line).astype(F32).astype(BF16)
                moved = dot(move, white[w * channels : (w + 1) * channels, :])
                blocks[d][w * part : (w + 1) * part, :] = moved.astype(BF16)


def correlate_kernel(spans, pairs, factor, has_total, last, *refs):
    count = len(spans)
    receivers, sources = refs[:count], refs[count : 2 * count]
    total = refs[2 * count] if has_total else None
    out, line_r, line_s = refs[2 * count + has_total : 2 * count + has_total + 3]
    held, sems = refs[-2:] if last else (out, None)
    part = out.shape[1]
    windows = 0
    for receiver, source, span in zip(receivers, sources, spans):
        for i, w in enumerate(span):
            line_r[windows] = receiver[w].astype(F32) * factor
            for c in range(2):
                at = (c * len(span) + i) * pairs
                rows = source[at : at + pairs, :].astype(F32)
                cols = slice(c * NF, (c + 1) * NF)
                for p in range(pairs):
                    line_s[p, windows : windows + 1, cols] = rows[p : p + 1, :]
            windows += 1

    def copy(p):
        return pltpu.make_async_copy(held.at[p], out.at[p], sems.at[p])

    def one(p, carry):
        for f in range(0, NF, 128):
            re = slice(f, f + 128)
            im = slice(NF + f, NF + f + 128)
            if has_total:
                total_r, total_i = total[p, :, re], total[p, :, im]
            else:
                total_r = jnp.zeros((part, 128), F32)
                total_i = jnp.zeros((part, 128), F32)
            for at in range(windows):
                rr = line_r[at, :, re]
                ri = line_r[at, :, im]
                sr = line_s[p, at : at + 1, re]
                si = line_s[p, at : at + 1, im]
                total_r = total_r + (sr * rr + si * ri)
                total_i = total_i + (sr * ri - si * rr)
            held[p, :, re] = total_r
            held[p, :, im] = total_i
        if last:
            copy(p).start()
        return carry

    lax.fori_loop(0, pairs, one, 0, unroll=2 if pairs % 2 == 0 else 1)
    if last:
        for p in range(pairs):
            copy(p).wait()


def correlate(receivers, sources, spans, total, pairs, factor, last):
    _, part, width = receivers[0].shape
    windows = sum(len(span) for span in spans)
    vmem = pl.BlockSpec(memory_space=pltpu.VMEM)
    shape = (pairs, part, width)
    extra = [] if total is None else [total]
    scratch = [
        pltpu.VMEM((windows, part, width), F32),
        pltpu.VMEM((pairs, -(-windows // 8) * 8, width), F32),
    ]
    if last:
        scratch += [pltpu.VMEM(shape, F32), pltpu.SemaphoreType.DMA((pairs,))]
    return pl.pallas_call(
        functools.partial(correlate_kernel, spans, pairs, factor, len(extra), last),
        out_shape=jax.ShapeDtypeStruct(shape, F32),
        in_specs=[vmem] * (2 * len(spans) + len(extra)),
        out_specs=pl.BlockSpec(memory_space=pltpu.HBM) if last else vmem,
        scratch_shapes=scratch,
        compiler_params=pltpu.CompilerParams(vmem_limit_bytes=LIMIT),
        name="correlate",
    )(*receivers, *sources, *extra)


def shards(traces, filter_taps, source_counts, source_channel, block_sources):
    channels, samples = traces.shape
    tap_count = filter_taps.shape[1]
    pairs = block_sources.shape[1]
    windows = samples // HALF
    groups = lax.axis_size("chan")
    times = lax.axis_size("tm")
    chips = groups // 2
    part = channels // times
    sizes = part_rows(windows, pairs)
    rows_out = chips * sum(sizes)
    rows, cut = 2 * windows * pairs, 2 * (windows - 1) * pairs

    def across(x, axis, distance):
        size = lax.axis_size(axis)
        return lax.ppermute(x, axis, [(i, i ^ distance) for i in range(size)])

    vmem = pl.BlockSpec(memory_space=pltpu.VMEM)
    hbm = pl.BlockSpec(memory_space=pltpu.HBM)
    params = pltpu.CompilerParams(vmem_limit_bytes=LIMIT)
    bits = [1 << b for b in range(chips.bit_length() - 1)]

    other = across(block_sources, "chan", 1)
    inputs = (traces, jnp.asarray(piece_table()), block_sources)
    message, last_half, table, ids = pl.pallas_call(
        functools.partial(load_kernel, tap_count - 1),
        out_shape=[
            jax.ShapeDtypeStruct((channels, 2 * NF + 128), BF16),
            jax.ShapeDtypeStruct((channels, 2 * NF), F32),
        ]
        + [jax.ShapeDtypeStruct(a.shape, a.dtype) for a in inputs[1:]],
        in_specs=[hbm] * 3,
        out_specs=[vmem] * 4,
        scratch_shapes=[
            pltpu.VMEM((channels, HALF + 128), BF16),
            pltpu.SemaphoreType.DMA((2 + 4 * NF // CHUNK,)),
        ],
        compiler_params=params,
        name="load",
    )(*(pltpu.with_memory_space_constraint(a, pltpu.HBM) for a in inputs))
    traces, taps = (
        pltpu.with_memory_space_constraint(a, pltpu.VMEM) for a in (traces, filter_taps.T)
    )
    wanted = [
        pl.pallas_call(
            pair_kernel,
            out_shape=jax.ShapeDtypeStruct((2, pairs), jnp.int32),
            in_specs=[vmem] * 2,
            out_specs=vmem,
            compiler_params=params,
            cost_estimate=pl.CostEstimate(flops=HINT, bytes_accessed=8 * pairs, transcendentals=0),
            name="pair",
        )(ids, other)
    ]
    halo = lax.ppermute(message, "tm", [(i - 1, i) for i in range(1, times)])
    for bit in bits:
        known = jnp.concatenate(wanted, axis=0)
        wanted = [known, across(known, "chan", 2 * bit)]

    shape = (channels, windows, pairs, chips)
    width = windows * channels
    chunk_shapes = [
        jax.ShapeDtypeStruct((width - channels, 2 * CHUNK), F32),
        jax.ShapeDtypeStruct((channels, 2 * CHUNK), F32),
    ]
    size = -(-tap_count // 16) * 16
    part_a, response_a, last, ends, edge, lines = pl.pallas_call(
        functools.partial(first_kernel, windows),
        out_shape=chunk_shapes
        + [
            chunk_shapes[1],
            jax.ShapeDtypeStruct((channels, (windows - 1) * 128), BF16),
            jax.ShapeDtypeStruct((channels, 3 * (tap_count - 1)), BF16),
            jax.ShapeDtypeStruct((channels, 3 * size), BF16),
        ],
        in_specs=[vmem] * 4,
        out_specs=[vmem] * 6,
        scratch_shapes=[
            pltpu.VMEM((3 * size, 128), F32),
            pltpu.VMEM((2 * tap_count + 6, channels), F32),
        ],
        compiler_params=params,
        name="first",
    )(traces, taps, table, last_half)
    part_b, response_b, own_white = pl.pallas_call(
        functools.partial(second_kernel, windows),
        out_shape=chunk_shapes + [jax.ShapeDtypeStruct((channels, 2 * NF), BF16)],
        in_specs=[vmem] * 6,
        out_specs=[vmem] * 3,
        scratch_shapes=[
            pltpu.VMEM((channels, 2 * CHUNK), F32),
            pltpu.VMEM((channels, 2 * NF), F32),
        ],
        compiler_params=params,
        name="second",
    )(traces, table, last_half, lines, edge, last)
    picks = pl.pallas_call(
        functools.partial(picks_kernel, shape),
        out_shape=jax.ShapeDtypeStruct((2 * rows_out, width), BF16),
        in_specs=[vmem] * (2 + len(wanted)),
        out_specs=vmem,
        scratch_shapes=[pltpu.VMEM((2 * rows_out, width), F32), pltpu.VMEM((2 * chips, 128), F32)],
        compiler_params=params,
        name="picks",
    )(source_counts[None], source_channel, *wanted)
    outs = pl.pallas_call(
        functools.partial(rest_kernel, windows, pairs, times),
        out_shape=[jax.ShapeDtypeStruct((chips * rows, NF), BF16)] * 2
        + [jax.ShapeDtypeStruct((windows * part, 2 * NF), BF16)] * times,
        in_specs=[vmem] * 10,
        out_specs=[vmem] * (2 + times),
        scratch_shapes=[
            pltpu.VMEM((2 * tap_count + 6, width - channels), F32),
            pltpu.VMEM((width - channels, 2 * NF), F32),
            pltpu.VMEM((width, 2 * NF), BF16),
        ],
        compiler_params=params,
        name="rest",
    )(
        halo,
        ends,
        taps,
        table,
        part_a,
        part_b,
        response_a,
        response_b,
        own_white,
        picks,
    )
    keep, send, blocks = outs[0], outs[1], outs[2:]
    gathered = keep + across(send, "chan", 1)
    pieces = [gathered[d * rows : (d + 1) * rows] for d in range(chips)]
    pieces = list(lax.optimization_barrier(tuple(pieces)))
    for bit in bits:
        onward = [d for d in range(2 * bit, chips) if d & (2 * bit - 1) == bit]
        if onward:
            block = jnp.concatenate([pieces[d] for d in onward], axis=0)
            block = across(block, "chan", 2 * bit)
            for i, d in enumerate(onward):
                pieces[d ^ bit] = pieces[d ^ bit] + block[i * rows : (i + 1) * rows]
    mine = pieces[0]
    for bit in bits[:-1]:
        mine = mine + across(pieces[bit], "chan", 2 * bit)
    mine = [mine[:cut], mine[cut:]]
    if bits:
        last = pieces[bits[-1]]
        for i, x in enumerate((last[:cut], last[cut:])):
            mine[i] = mine[i] + across(x, "chan", 2 * bits[-1])
    receivers = [blocks[0]]
    for d in range(1, times):
        receivers.append(across(blocks[d], "tm", d))
    receivers = [r.reshape(windows, part, 2 * NF) for r in receivers]
    sources = [mine]
    for d in range(1, times):
        both = []
        for x in mine:
            both.append(across(x, "tm", d))
        sources.append(both)

    factor = 1.0 / (windows * times)
    early, late = tuple(range(windows - 1)), (windows - 1,)
    total = None
    for which in ([0], list(range(1, times))):
        for i, span in enumerate((early, late)):
            if which:
                last = i == 1 and which[-1] == times - 1
                total = correlate(
                    [receivers[d] for d in which],
                    [sources[d][i] for d in which],
                    (span,) * len(which),
                    total,
                    pairs,
                    factor,
                    last,
                )
    return total.transpose(1, 0, 2)


def solution(mesh):
    in_specs = (P(("seg", "chan"), "tm"), P("chan", None), P(), P(), P("chan", None))
    out_specs = P(("seg", "chan", "tm"), None, None)
    return jax.shard_map(shards, mesh=mesh, in_specs=in_specs, out_specs=out_specs, check_vma=False)
```

```python
import functools

import jax
import jax.numpy as jnp
import ml_dtypes
import numpy as np
from jax import lax
from jax.experimental import pallas as pl
from jax.experimental.pallas import tpu as pltpu
from jax.sharding import PartitionSpec as P


NFFT = 4096
NF = 512
F0 = 8
PIECE = NFFT // 8
HALF = NFFT // 2
CHUNK = 256
F32 = jnp.float32
BF16 = jnp.bfloat16
LIMIT = 24 * 1024 * 1024
HINT = 10**10


def piece_table():
    bins = F0 + np.arange(NF)
    angle = (bins * np.arange(PIECE)[:, None] % NFFT) * (2.0 * np.pi / NFFT)
    exact = np.concatenate([np.cos(angle), -np.sin(angle)], axis=1)
    high = exact.astype(ml_dtypes.bfloat16)
    low = (exact - high.astype(np.float64)).astype(ml_dtypes.bfloat16)
    both = np.concatenate([high, low], axis=0)
    starts = [c for f in range(0, NF, CHUNK) for c in (f, NF + f)]
    return np.stack([both[:, c : c + CHUNK] for c in starts])


def split_two(x):
    high = x.astype(BF16)
    low = (x - high.astype(F32)).astype(BF16)
    return high, low


def dot(a, b):
    return jnp.dot(a, b, preferred_element_type=F32)


def stacked_parts(x):
    high, low = split_two(x)
    high = high.astype(F32)
    return jnp.concatenate([high, low.astype(F32), high], axis=0)


def stacked_rows(table, rows, at):
    first = table[at, :rows, :]
    return jnp.concatenate([first, first, table[at, PIECE : PIECE + rows, :]], axis=0)


class Turns:
    def __init__(self):
        lane = lax.broadcasted_iota(jnp.int32, (1, CHUNK), 1)
        turn = lane % 4
        self.odd = (turn % 2) == 1
        self.sign = jnp.where(self.odd, -1.0, 1.0)
        self.real = jnp.where(turn < 2, 1.0, -1.0)
        self.imag = jnp.where((turn == 0) | (turn == 3), 1.0, -1.0)
        eighth = lane % 8
        root = np.float32(np.sqrt(0.5))
        self.cos = jnp.where(turn % 4 == 0, 1.0, jnp.where(turn == 2, 0.0, root))
        self.cos = jnp.where((eighth > 2) & (eighth < 6), -self.cos, self.cos)
        self.sin = jnp.where(turn == 2, 1.0, jnp.where(turn == 0, 0.0, root))
        self.sin = jnp.where(eighth < 4, -self.sin, self.sin)

    def quarter(self, ar, ai, br, bi):
        return (
            ar + self.real * jnp.where(self.odd, bi, br),
            ai + self.imag * jnp.where(self.odd, br, bi),
        )

    def half(self, re, im):
        ar, ai = self.quarter(re[0], im[0], re[2], im[2])
        br, bi = self.quarter(re[1], im[1], re[3], im[3])
        return ar + (br * self.cos - bi * self.sin), ai + (br * self.sin + bi * self.cos)


def half_spectra(x, table, channels, halves, turns, f):
    both = jnp.concatenate([x, x], axis=1)
    at = 2 * (f // CHUNK)
    dr = dot(both, table[at])
    di = dot(both, table[at + 1])
    out = []
    for b in range(halves):
        rows = [slice((4 * b + e) * channels, (4 * b + e + 1) * channels) for e in range(4)]
        out.append(turns.half([dr[r] for r in rows], [di[r] for r in rows]))
    return out


def end_terms(taps_wide, shifted, tap_count, ends):
    lag = tap_count - 1
    apart = ends.T
    size = apart.shape[0]
    shifted[...] = jnp.zeros_like(shifted)
    shifted[:tap_count, :] = taps_wide
    total = jnp.zeros((lag, apart.shape[1]), F32)
    for j in range(1, tap_count):
        total = total + shifted[j : j + lag, :] * apart[size - j : size - j + 1, :]
    return stacked_parts(total).T.astype(BF16)


def whiten_rows(re, im):
    rows = re.shape[0]
    place = lax.broadcasted_iota(jnp.int32, (rows, NF), 1)
    power = re * re + im * im
    smooth = power
    for s in (1, 2):
        smooth = smooth + jnp.where(place >= s, pltpu.roll(power, s, 1), 0.0)
        smooth = smooth + jnp.where(place < NF - s, pltpu.roll(power, NF - s, 1), 0.0)
    total = jnp.sum(power, axis=1, keepdims=True)
    scaling = lax.rsqrt(smooth * 0.2 + (total * (0.1 / NF) + 1e-06))
    return (re * scaling).astype(BF16), (im * scaling).astype(BF16)


ROWS = 16


def whiten_all(spectra, white, count):
    def step(i, carry):
        rows = pl.ds(pl.multiple_of(i * ROWS, ROWS), ROWS)
        re, im = whiten_rows(spectra[rows, :NF], spectra[rows, NF:])
        white[rows, :NF] = re
        white[rows, NF:] = im
        return carry

    lax.fori_loop(0, count // ROWS, step, 0, unroll=min(8, count // ROWS))


def load_kernel(end, traces_in, table_in, ids_in, message, last_half, table, ids, traces, sems):
    channels, samples = traces.shape
    begin = traces_in.shape[1] - samples
    copies = [pltpu.make_async_copy(traces_in.at[:, begin:], traces, sems.at[0])]
    at = 1 + table.shape[0]
    for i in range(table.shape[0]):
        copies.append(pltpu.make_async_copy(table_in.at[i], table.at[i], sems.at[1 + i]))
    copies.append(pltpu.make_async_copy(ids_in, ids, sems.at[at]))
    for copy in copies:
        copy.start()
    copies[0].wait()
    lane = lax.broadcasted_iota(jnp.int32, (channels, 128), 1)
    final = pltpu.roll(traces[:, samples - 128 :].astype(F32), 128 - end, 1)
    tile = jnp.where(lane < 128 - end, final, traces[:, :128].astype(F32))
    message[:, 2 * NF :] = tile.astype(BF16)
    pieces = [samples - HALF + q * PIECE for q in range(HALF // PIECE)]
    x = jnp.concatenate([traces[:, p : p + PIECE] for p in pieces], axis=0)
    turns = Turns()
    for i, f in enumerate(range(0, NF, CHUNK)):
        re = slice(f, f + CHUNK)
        im = slice(NF + f, NF + f + CHUNK)
        copies[1 + 2 * i].wait()
        copies[2 + 2 * i].wait()
        xr, xi = half_spectra(x, table, channels, 1, turns, f)[0]
        last_half[:, re] = xr
        last_half[:, im] = xi
        message[:, re] = xr.astype(BF16)
        message[:, im] = xi.astype(BF16)
    for copy in copies[at:]:
        copy.wait()


def pair_kernel(mine, other, out):
    out[:1, :] = mine[...]
    out[1:, :] = other[...]


def own_chunk(windows, f, traces, table, last_half, lines, edge, part, response, last):
    channels, samples = traces.shape
    size = lines.shape[1] // 3
    lag = edge.shape[1] // 3
    pieces = (samples - HALF) // PIECE
    x = jnp.concatenate([traces[:, q * PIECE : (q + 1) * PIECE] for q in range(pieces)], axis=0)
    turns = Turns()
    re = slice(f, f + CHUNK)
    im = slice(NF + f, NF + f + CHUNK)
    at = 2 * (f // CHUNK)
    pr = dot(lines[...], stacked_rows(table, size, at))
    pi = dot(lines[...], stacked_rows(table, size, at + 1))
    response[:, :CHUNK] = pr
    response[:, CHUNK:] = pi
    halves = half_spectra(x, table, channels, windows - 1, turns, f)
    halves.append((last_half[:, re], last_half[:, im]))
    for w in range(windows):
        xr, xi = halves[w]
        xr, xi = turns.sign * xr, turns.sign * xi
        if w > 0:
            xr, xi = xr + halves[w - 1][0], xi + halves[w - 1][1]
        yr = xr * pr - xi * pi
        yi = xr * pi + xi * pr
        if w < windows - 1:
            rows = slice(w * channels, (w + 1) * channels)
            part[rows, :CHUNK] = yr
            part[rows, CHUNK:] = yi
        else:
            last[:, :CHUNK] = yr + dot(edge[...], stacked_rows(table, lag, at))
            last[:, CHUNK:] = yi + dot(edge[...], stacked_rows(table, lag, at + 1))


def first_kernel(
    windows, traces, taps, table, last_half, part, response, last, ends, edge, lines, square, shifted
):
    channels, samples = traces.shape
    tap_count = taps.shape[0]
    square[...] = jnp.zeros_like(square)
    high, low = split_two(taps[...])
    high = high.astype(F32)
    size = square.shape[0] // 3
    for i, value in enumerate((high, low.astype(F32), high)):
        square[i * size : i * size + tap_count, :channels] = value
    lines[...] = square[...].T[:channels].astype(BF16)
    tile = 128
    for b in range(1, windows):
        ends[:, (b - 1) * tile : b * tile] = traces[:, b * HALF - tile : b * HALF]
    start = (windows - 2) * HALF
    apart = traces[:, start - tile : start].astype(F32) - traces[:, samples - tile :].astype(F32)
    edge[...] = end_terms(taps[...], shifted, tap_count, apart)
    own_chunk(windows, 0, traces, table, last_half, lines, edge, part, response, last)


def second_kernel(
    windows, traces, table, last_half, lines, edge, first, part, response, white, second, spectra
):
    own_chunk(windows, CHUNK, traces, table, last_half, lines, edge, part, response, second)
    for i, half in enumerate((first, second)):
        spectra[:, i * CHUNK : (i + 1) * CHUNK] = half[:, :CHUNK]
        spectra[:, NF + i * CHUNK : NF + (i + 1) * CHUNK] = half[:, CHUNK:]
    whiten_all(spectra, white, white.shape[0])


def part_rows(windows, pairs):
    return [-(-w * pairs // 8) * 8 for w in (windows - 1, 1)]


def picks_kernel(shape, counts, slots, *refs):
    channels, windows, pairs, chips = shape
    wanted, (picks, chosen, lines) = refs[:-3], refs[-3:]
    group = lax.axis_index("chan")
    place = lax.broadcasted_iota(jnp.int32, counts.shape, 1)
    held = counts[...].astype(F32)
    first = jnp.sum(jnp.where(place < group, held, 0.0), axis=1, keepdims=True)
    owned = jnp.sum(jnp.where(place == group, held, 0.0), axis=1, keepdims=True)
    row = lax.broadcasted_iota(jnp.int32, slots.shape, 0)
    own_slots = jnp.where(row == group, slots[...], 0).astype(F32)
    own_slots = jnp.sum(own_slots, axis=0, keepdims=True)
    lines[...] = jnp.zeros_like(lines)
    at = 0
    for w in wanted:
        lines[at : at + w.shape[0], :pairs] = w[...].astype(F32)
        at += w.shape[0]
    slot = lines[...] - first
    channel = jnp.full(slot.shape, -1.0, F32)
    for s in range(slots.shape[1]):
        channel = jnp.where(slot == s, own_slots[:, s : s + 1], channel)
    channel = jnp.where((slot >= 0) & (slot < owned), channel, -1.0)
    turned = channel.T
    width = windows * channels
    lane = lax.broadcasted_iota(jnp.int32, (1, width), 1)
    columns = [
        jnp.where(lane // channels == w, lane % channels, -2).astype(F32) for w in range(windows)
    ]
    sizes = part_rows(windows, pairs)
    chosen[...] = jnp.zeros_like(chosen)
    for core in range(2):
        for d in range(chips):
            base = (core * chips + d) * sum(sizes)
            one = turned[:pairs, 2 * d + core : 2 * d + core + 1]
            for w in range(windows):
                row = base + (w * pairs if w < windows - 1 else sizes[0])
                chosen[row : row + pairs, :] = (one == columns[w]).astype(F32)
    picks[...] = chosen[...].astype(BF16)


def rest_kernel(
    windows, pairs, halo, ends, taps, table, part_a, part_b, response_a, response_b, *refs
):
    own_white, picks, send, white, shifted, spectra = refs
    channels = response_a.shape[0]
    tap_count = taps.shape[0]
    tile = 128
    rest = windows - 1

    arrived = halo[:, 2 * NF :].astype(F32)
    before = [arrived, pltpu.roll(arrived, tap_count - 1, 1)]
    before += [ends[:, (b - 1) * tile : b * tile] for b in range(1, windows - 2)]
    after = [ends[:, w * tile : (w + 1) * tile] for w in range(rest)]
    apart = jnp.concatenate([b.astype(F32) - a.astype(F32) for b, a in zip(before, after)], axis=0)
    taps_wide = jnp.concatenate([taps[...]] * rest, axis=1)
    edge = end_terms(taps_wide, shifted, tap_count, apart)
    for f in range(0, NF, CHUNK):
        re = slice(f, f + CHUNK)
        im = slice(NF + f, NF + f + CHUNK)
        xr, xi = halo[:, re].astype(F32), halo[:, im].astype(F32)
        part, response = (part_b, response_b) if f else (part_a, response_a)
        pr, pi = response[:, :CHUNK], response[:, CHUNK:]
        at = 2 * (f // CHUNK)
        er = dot(edge, stacked_rows(table, tap_count - 1, at))
        ei = dot(edge, stacked_rows(table, tap_count - 1, at + 1))
        spectra[:channels, re] = part[:channels, :CHUNK] + er[:channels] + (xr * pr - xi * pi)
        spectra[:channels, im] = part[:channels, CHUNK:] + ei[:channels] + (xr * pi + xi * pr)
        spectra[channels:, re] = part[channels:, :CHUNK] + er[channels:]
        spectra[channels:, im] = part[channels:, CHUNK:] + ei[channels:]
    count = rest * channels
    whiten_all(spectra, white, count)
    white[count:, :] = own_white[...]
    spread(windows, pairs, white, picks, send, picks.shape[0] // 2)


def spread(windows, pairs, white, picks, target, first):
    count = picks.shape[0] // 2
    sizes = part_rows(windows, pairs)
    used = [(windows - 1) * pairs, pairs]
    choose = picks[first : first + count, :]
    for f in range(0, 2 * NF, CHUNK):
        out = dot(choose, white[:, f : f + CHUNK]).astype(BF16)
        imag = f >= NF
        place = slice(f - NF * imag, f - NF * imag + CHUNK)
        for d in range(count // sum(sizes)):
            at, row = d * sum(sizes), d * 2 * sum(used)
            for size, n in zip(sizes, used):
                put = row + imag * n
                target[put : put + n, place] = out[at : at + n]
                at, row = at + size, row + 2 * n


def keep_kernel(windows, pairs, white, picks, keep, *blocks):
    times = len(blocks)
    channels = white.shape[0] // windows
    part = channels // times
    spread(windows, pairs, white, picks, keep, 0)
    for d in range(times):
        line = (lax.axis_index("tm") ^ d) * part
        for w in range(windows):
            if part % ROWS == 0:
                at = pl.multiple_of(w * channels + line, ROWS)
                blocks[d][w * part : (w + 1) * part, :] = white[pl.ds(at, part), :]
            else:
                row = lax.broadcasted_iota(jnp.int32, (part, channels), 0)
                col = lax.broadcasted_iota(jnp.int32, (part, channels), 1)
                move = (col == row + line).astype(F32).astype(BF16)
                moved = dot(move, white[w * channels : (w + 1) * channels, :])
                blocks[d][w * part : (w + 1) * part, :] = moved.astype(BF16)


def correlate_kernel(spans, pairs, factor, has_total, last, *refs):
    count = len(spans)
    receivers, sources = refs[:count], refs[count : 2 * count]
    total = refs[2 * count] if has_total else None
    out, line_r, line_s = refs[2 * count + has_total : 2 * count + has_total + 3]
    held, sems = refs[-2:] if last else (out, None)
    part = out.shape[1]
    windows = 0
    for receiver, source, span in zip(receivers, sources, spans):
        for i, w in enumerate(span):
            line_r[windows] = receiver[w].astype(F32) * factor
            for c in range(2):
                at = (c * len(span) + i) * pairs
                rows = source[at : at + pairs, :].astype(F32)
                cols = slice(c * NF, (c + 1) * NF)
                for p in range(pairs):
                    line_s[p, windows : windows + 1, cols] = rows[p : p + 1, :]
            windows += 1

    def copy(p):
        return pltpu.make_async_copy(held.at[p], out.at[p], sems.at[p])

    def one(p, carry):
        for f in range(0, NF, 128):
            re = slice(f, f + 128)
            im = slice(NF + f, NF + f + 128)
            if has_total:
                total_r, total_i = total[p, :, re], total[p, :, im]
            else:
                total_r = jnp.zeros((part, 128), F32)
                total_i = jnp.zeros((part, 128), F32)
            for at in range(windows):
                rr = line_r[at, :, re]
                ri = line_r[at, :, im]
                sr = line_s[p, at : at + 1, re]
                si = line_s[p, at : at + 1, im]
                total_r = total_r + (sr * rr + si * ri)
                total_i = total_i + (sr * ri - si * rr)
            held[p, :, re] = total_r
            held[p, :, im] = total_i
        if last:
            copy(p).start()
        return carry

    lax.fori_loop(0, pairs, one, 0, unroll=4 if pairs % 4 == 0 else 1)
    if last:
        for p in range(pairs):
            copy(p).wait()


def correlate(receivers, sources, spans, total, pairs, factor, last):
    _, part, width = receivers[0].shape
    windows = sum(len(span) for span in spans)
    vmem = pl.BlockSpec(memory_space=pltpu.VMEM)
    shape = (pairs, part, width)
    extra = [] if total is None else [total]
    scratch = [
        pltpu.VMEM((windows, part, width), F32),
        pltpu.VMEM((pairs, -(-windows // 8) * 8, width), F32),
    ]
    if last:
        scratch += [pltpu.VMEM(shape, F32), pltpu.SemaphoreType.DMA((pairs,))]
    return pl.pallas_call(
        functools.partial(correlate_kernel, spans, pairs, factor, len(extra), last),
        out_shape=jax.ShapeDtypeStruct(shape, F32),
        in_specs=[vmem] * (2 * len(spans) + len(extra)),
        out_specs=pl.BlockSpec(memory_space=pltpu.HBM) if last else vmem,
        scratch_shapes=scratch,
        compiler_params=pltpu.CompilerParams(vmem_limit_bytes=LIMIT),
        name="correlate",
    )(*receivers, *sources, *extra)


def shards(traces, filter_taps, source_counts, source_channel, block_sources):
    channels, samples = traces.shape
    tap_count = filter_taps.shape[1]
    pairs = block_sources.shape[1]
    windows = samples // HALF
    groups = lax.axis_size("chan")
    times = lax.axis_size("tm")
    chips = groups // 2
    part = channels // times
    sizes = part_rows(windows, pairs)
    rows_out = chips * sum(sizes)
    rows, cut = 2 * windows * pairs, 2 * (windows - 1) * pairs

    def across(x, axis, distance):
        size = lax.axis_size(axis)
        return lax.ppermute(x, axis, [(i, i ^ distance) for i in range(size)])

    vmem = pl.BlockSpec(memory_space=pltpu.VMEM)
    hbm = pl.BlockSpec(memory_space=pltpu.HBM)
    params = pltpu.CompilerParams(vmem_limit_bytes=LIMIT)
    bits = [1 << b for b in range(chips.bit_length() - 1)]

    other = across(block_sources, "chan", 1)
    inputs = (traces, jnp.asarray(piece_table()), block_sources)
    message, last_half, table, ids = pl.pallas_call(
        functools.partial(load_kernel, tap_count - 1),
        out_shape=[
            jax.ShapeDtypeStruct((channels, 2 * NF + 128), BF16),
            jax.ShapeDtypeStruct((channels, 2 * NF), F32),
        ]
        + [jax.ShapeDtypeStruct(a.shape, a.dtype) for a in inputs[1:]],
        in_specs=[hbm] * 3,
        out_specs=[vmem] * 4,
        scratch_shapes=[
            pltpu.VMEM((channels, HALF + 128), BF16),
            pltpu.SemaphoreType.DMA((2 + 2 * NF // CHUNK,)),
        ],
        compiler_params=params,
        name="load",
    )(*(pltpu.with_memory_space_constraint(a, pltpu.HBM) for a in inputs))
    traces, taps = (
        pltpu.with_memory_space_constraint(a, pltpu.VMEM) for a in (traces, filter_taps.T)
    )
    wanted = [
        pl.pallas_call(
            pair_kernel,
            out_shape=jax.ShapeDtypeStruct((2, pairs), jnp.int32),
            in_specs=[vmem] * 2,
            out_specs=vmem,
            compiler_params=params,
            cost_estimate=pl.CostEstimate(flops=HINT, bytes_accessed=8 * pairs, transcendentals=0),
            name="pair",
        )(ids, other)
    ]
    halo = lax.ppermute(message, "tm", [(i - 1, i) for i in range(1, times)])
    for bit in bits:
        known = jnp.concatenate(wanted, axis=0)
        wanted = [known, across(known, "chan", 2 * bit)]

    shape = (channels, windows, pairs, chips)
    width = windows * channels
    chunk_shapes = [
        jax.ShapeDtypeStruct((width - channels, 2 * CHUNK), F32),
        jax.ShapeDtypeStruct((channels, 2 * CHUNK), F32),
    ]
    size = -(-tap_count // 16) * 16
    part_a, response_a, last, ends, edge, lines = pl.pallas_call(
        functools.partial(first_kernel, windows),
        out_shape=chunk_shapes
        + [
            chunk_shapes[1],
            jax.ShapeDtypeStruct((channels, (windows - 1) * 128), BF16),
            jax.ShapeDtypeStruct((channels, 3 * (tap_count - 1)), BF16),
            jax.ShapeDtypeStruct((channels, 3 * size), BF16),
        ],
        in_specs=[vmem] * 4,
        out_specs=[vmem] * 6,
        scratch_shapes=[
            pltpu.VMEM((3 * size, 128), F32),
            pltpu.VMEM((2 * tap_count + 6, channels), F32),
        ],
        compiler_params=params,
        name="first",
    )(traces, taps, table, last_half)
    part_b, response_b, own_white = pl.pallas_call(
        functools.partial(second_kernel, windows),
        out_shape=chunk_shapes + [jax.ShapeDtypeStruct((channels, 2 * NF), BF16)],
        in_specs=[vmem] * 6,
        out_specs=[vmem] * 3,
        scratch_shapes=[
            pltpu.VMEM((channels, 2 * CHUNK), F32),
            pltpu.VMEM((channels, 2 * NF), F32),
        ],
        compiler_params=params,
        name="second",
    )(traces, table, last_half, lines, edge, last)
    picks = pl.pallas_call(
        functools.partial(picks_kernel, shape),
        out_shape=jax.ShapeDtypeStruct((2 * rows_out, width), BF16),
        in_specs=[vmem] * (2 + len(wanted)),
        out_specs=vmem,
        scratch_shapes=[pltpu.VMEM((2 * rows_out, width), F32), pltpu.VMEM((2 * chips, 128), F32)],
        compiler_params=params,
        name="picks",
    )(source_counts[None], source_channel, *wanted)
    send, white = pl.pallas_call(
        functools.partial(rest_kernel, windows, pairs),
        out_shape=[
            jax.ShapeDtypeStruct((chips * rows, NF), BF16),
            jax.ShapeDtypeStruct((width, 2 * NF), BF16),
        ],
        in_specs=[vmem] * 10,
        out_specs=[vmem] * 2,
        scratch_shapes=[
            pltpu.VMEM((2 * tap_count + 6, width - channels), F32),
            pltpu.VMEM((width - channels, 2 * NF), F32),
        ],
        compiler_params=params,
        name="rest",
    )(
        halo,
        ends,
        taps,
        table,
        part_a,
        part_b,
        response_a,
        response_b,
        own_white,
        picks,
    )
    keep, *blocks = pl.pallas_call(
        functools.partial(keep_kernel, windows, pairs),
        out_shape=[jax.ShapeDtypeStruct((chips * rows, NF), BF16)]
        + [jax.ShapeDtypeStruct((windows * part, 2 * NF), BF16)] * times,
        in_specs=[vmem] * 2,
        out_specs=[vmem] * (1 + times),
        compiler_params=params,
        name="keep",
    )(white, picks)
    gathered = keep + across(send, "chan", 1)
    pieces = [gathered[d * rows : (d + 1) * rows] for d in range(chips)]
    pieces = list(lax.optimization_barrier(tuple(pieces)))
    for bit in bits:
        onward = [d for d in range(2 * bit, chips) if d & (2 * bit - 1) == bit]
        if onward:
            block = jnp.concatenate([pieces[d] for d in onward], axis=0)
            block = across(block, "chan", 2 * bit)
            for i, d in enumerate(onward):
                pieces[d ^ bit] = pieces[d ^ bit] + block[i * rows : (i + 1) * rows]
    mine = pieces[0]
    for bit in bits[:-1]:
        mine = mine + across(pieces[bit], "chan", 2 * bit)
    mine = [mine[:cut], mine[cut:]]
    if bits:
        last = pieces[bits[-1]]
        for i, x in enumerate((last[:cut], last[cut:])):
            mine[i] = mine[i] + across(x, "chan", 2 * bits[-1])
    receivers = [blocks[0]]
    for d in range(1, times):
        receivers.append(across(blocks[d], "tm", d))
    receivers = [r.reshape(windows, part, 2 * NF) for r in receivers]
    sources = [mine]
    for d in range(1, times):
        both = []
        for x in mine:
            both.append(across(x, "tm", d))
        sources.append(both)

    factor = 1.0 / (windows * times)
    early, late = tuple(range(windows - 1)), (windows - 1,)
    total = None
    for which in ([0], list(range(1, times))):
        for i, span in enumerate((early, late)):
            if which:
                last = i == 1 and which[-1] == times - 1
                total = correlate(
                    [receivers[d] for d in which],
                    [sources[d][i] for d in which],
                    (span,) * len(which),
                    total,
                    pairs,
                    factor,
                    last,
                )
    return total.transpose(1, 0, 2)


def solution(mesh):
    in_specs = (P(("seg", "chan"), "tm"), P("chan", None), P(), P(), P("chan", None))
    out_specs = P(("seg", "chan", "tm"), None, None)
    return jax.shard_map(shards, mesh=mesh, in_specs=in_specs, out_specs=out_specs, check_vma=False)
```
